32 devices in a mesh: stream: 2 (over x), batch: 16 (over z, y, core).
Axes of the slice: x: 2, y: 2, z: 4, core: 2. Of those that a mesh axis runs over, the one named last changes fastest.
Arguments:
- tokens: bfloat16 [2, 32, 1024, 768], P('stream', 'batch'), may hold values from -6 to 6
- cotangent: bfloat16 [2, 32, 1024, 768], P('stream', 'batch'), may hold values from -6 to 6
- lengths: int32 [32], P('batch'), may hold values from 128 to 1024, as said below
- ln1_gain: bfloat16 [768], P('batch'), may hold values from 0.099609375 to 1.8984375
- w_qkv: bfloat16 [768, 2304], P('batch'), may hold values from -0.21875 to 0.21875
- w_out: bfloat16 [768, 768], P('batch'), may hold values from -0.875 to 0.875
- ln2_gain: bfloat16 [768], P('batch'), may hold values from 0.099609375 to 1.8984375
- w_up: bfloat16 [768, 3072], P('batch'), may hold values from -0.21875 to 0.21875
- w_down: bfloat16 [3072, 768], P('batch'), may hold values from -0.109375 to 0.109375
Outputs:
- out: bfloat16 [2, 32, 1024, 768], P('stream', 'batch')
- tokens_grad: float32 [2, 32, 1024, 768], P('stream', 'batch')
- ln1_gain_grad: float32 [768], P(('stream', 'batch'))
- w_qkv_grad: float32 [768, 2304], P(('stream', 'batch'))
- w_out_grad: float32 [768, 768], P(('stream', 'batch'))
- ln2_gain_grad: float32 [768], P(('stream', 'batch'))
- w_up_grad: float32 [768, 3072], P(('stream', 'batch'))
- w_down_grad: float32 [3072, 768], P(('stream', 'batch'))
The draws below stay inside these ranges and needn't reach their ends.
Inputs may be any that keep to these rules, and one draw needn't show every extreme that they name: `lengths`: each length is a multiple of 16; in every draw some row is 1024 long.
All inputs are finite; a program needn't handle non-finite values.
Results may differ from the reference program's by a relative error of at most 0.014.
Values may be sent and summed in bfloat16 or wider, within the bound.
A program may use at most 512 MiB of HBM per device.

```python
import math
import jax
import jax.numpy as jnp
from jax import lax

D = 768
HD = 64
FF = 3072
BLOCK = 16
SEQ = 1024
LMIN = 128
ROWS = 32


def draw_lengths(key, part):
    choices_count = (SEQ - LMIN) // BLOCK + 1
    key_one, key_two, key_three = jax.random.split(key, 3)
    first_draw = jax.random.randint(key_one, (ROWS,), 0, choices_count)
    second_draw = jax.random.randint(key_two, (ROWS,), 0, choices_count)
    shortfall = jnp.minimum(first_draw, second_draw)
    full_row = jax.random.randint(key_three, (), 0, ROWS)
    shortfall = jnp.where(jnp.arange(ROWS) == full_row, 0, shortfall)
    return (SEQ - BLOCK * shortfall).astype(jnp.int32)


def shard_levels(stream_key, extent, cuts, low, largest):
    loudness = 1.0
    for axis_at, blocks in cuts:
        draws = jax.random.uniform(jax.random.fold_in(jax.random.fold_in(stream_key, 6), axis_at), (blocks,), jnp.float32, low / len(cuts), largest / len(cuts))
        loudness = loudness * jnp.repeat(jnp.exp(draws), extent[axis_at] // blocks).reshape((-1,) + (1,) * (len(extent) - 1 - axis_at))
    return loudness


def centred(rng, extent, scale, bound, cuts=(), held_as=jnp.bfloat16):
    level = shard_levels(rng, extent, cuts, -0.22, 0.18) if cuts else 1.0
    array = jax.random.normal(rng, extent, jnp.float32) * scale * level
    return jnp.minimum(jnp.maximum(array, -bound), bound).astype(held_as)


def setup_inputs(seed: int = 0) -> dict:
    keys = jax.random.split(jax.random.key(seed), 10)
    return {
        "tokens": centred(keys[0], (2, ROWS, SEQ, D), 1.0, 6.0, ((0, 2), (1, 16))),
        "cotangent": centred(keys[1], (2, ROWS, SEQ, D), 1.0, 6.0, ((0, 2), (1, 16))),
        "lengths": draw_lengths(jax.random.fold_in(keys[9], 71), 0),
        "ln1_gain": jnp.clip(1.0 + 0.18 * jax.random.normal(keys[3], (D,), jnp.float32), 0.099609375, 1.8984375).astype(jnp.bfloat16),
        "w_qkv": centred(keys[4], (D, 3 * D), D ** -0.5, 0.21875, ((0, 16),)),
        "w_out": centred(keys[5], (D, D), (D // 16) ** -0.5, 0.875, ((0, 16),)),
        "ln2_gain": jnp.clip(1.0 + 0.18 * jax.random.normal(keys[6], (D,), jnp.float32), 0.099609375, 1.8984375).astype(jnp.bfloat16),
        "w_up": centred(keys[7], (D, FF), D ** -0.5, 0.21875, ((0, 16),)),
        "w_down": centred(keys[8], (FF, D), FF ** -0.5, 0.109375, ((0, 16),)),
    }


@jax.custom_vjp
def low(v):
    return lax.optimization_barrier(v.astype(jnp.bfloat16)).astype(jnp.float32)

@jax.custom_vjp
def low_back(v):
    return v

def low_keep(v):
    return (low(v), None)

def low_pass(kept, grad):
    return (grad,)

def back_keep(v):
    return (v, None)

def back_low(kept, grad):
    return (low(grad),)
low.defvjp(low_keep, low_pass)
low_back.defvjp(back_keep, back_low)
exact_precision_flag = lax.Precision.HIGHEST

def rotary_tables(length, width):
    half_width = width // 2
    places = jnp.arange(length).astype(jnp.float32)
    rates = jnp.exp(jnp.arange(half_width).astype(jnp.float32) * (-2.0 * math.log(10000.0) / width))
    angles = places[:, None] * rates[None, :]
    return (jnp.cos(angles)[:, None, :], jnp.sin(angles)[:, None, :])

def rotate(field, cosine, sine):
    half_width = field.shape[-1] // 2
    first_half = field[..., :half_width]
    second_half = field[..., half_width:]
    return jnp.concatenate([first_half * cosine - second_half * sine, second_half * cosine + first_half * sine], axis=-1)

def layer_norm(values, gain_vec):
    center = values - lax.optimization_barrier(jnp.mean(values, axis=-1, keepdims=True))
    spread = lax.optimization_barrier(jnp.mean(center * center, axis=-1, keepdims=True))
    return center * lax.rsqrt(spread + 1e-05) * gain_vec

def attend(queries, keys_all, values_all, allowed):
    raw_scores = jnp.einsum('qhd,khd->hqk', queries, keys_all, precision=exact_precision_flag)
    scores = jnp.where(allowed[None], low_back(raw_scores) * 0.125, -1e+30)
    attn_probs = low(jax.nn.softmax(scores, axis=-1))
    return jnp.einsum('hqk,khd->qhd', attn_probs, values_all, precision=exact_precision_flag)

def row_forward(paired_rows, length_row, params, cosine, sine):
    gain_one, query_key_value_weight, output_weight, gain_two, up_weight, down_weight = params
    length = paired_rows.shape[1]
    width = paired_rows.shape[2]
    heads = width // HD
    first_hidden = low(layer_norm(paired_rows, gain_one))
    query_key_value_rows = low_back(jnp.einsum('bpg,gi->bpi', first_hidden, query_key_value_weight, precision=exact_precision_flag))
    queries = low(rotate(query_key_value_rows[..., :width].reshape(2, length, heads, HD), cosine, sine))
    keys_all = low(rotate(query_key_value_rows[..., width:2 * width].reshape(2, length, heads, HD), cosine, sine))
    values_all = low(query_key_value_rows[..., 2 * width:].reshape(2, length, heads, HD))
    places = jnp.arange(length)
    blocks = places // BLOCK
    live_key = (places < length_row)[None, :]
    earlier = blocks[None, :] < blocks[:, None]
    same_block = blocks[None, :] == blocks[:, None]
    clean_mixed = attend(queries[0], keys_all[0], values_all[0], (earlier | same_block) & live_key)
    noisy_allowed = jnp.concatenate([earlier & live_key, same_block & live_key], axis=1)
    noisy_mixed = attend(queries[1], jnp.concatenate([keys_all[0], keys_all[1]], axis=0), jnp.concatenate([values_all[0], values_all[1]], axis=0), noisy_allowed)
    attention_mixed = low(low_back(jnp.stack([clean_mixed, noisy_mixed]).reshape(2, length, width)))
    residual_middle = paired_rows + low_back(jnp.einsum('brm,mg->brg', attention_mixed, output_weight, precision=exact_precision_flag))
    second_hidden = low(layer_norm(residual_middle, gain_two))
    upper_projection = low_back(jnp.einsum('qzr,rg->qzg', second_hidden, up_weight, precision=exact_precision_flag))
    active_branch = low(low_back(jax.nn.gelu(upper_projection, approximate=True)))
    return residual_middle + low_back(jnp.einsum('itp,ph->ith', active_branch, down_weight, precision=exact_precision_flag))

def reference(tokens, cotangent, lengths, ln1_gain, w_qkv, w_out, ln2_gain, w_up, w_down):
    cosine, sine = rotary_tables(SEQ, HD)
    params = tuple((weight.astype(jnp.float32) for weight in (ln1_gain, w_qkv, w_out, ln2_gain, w_up, w_down)))
    inputs = tokens.astype(jnp.float32)

    def forward(inputs_all, params_all):

        def one_row(row_args):
            return row_forward(row_args[0], row_args[1], params_all, cosine, sine)
        result = lax.map(jax.checkpoint(one_row), (jnp.moveaxis(inputs_all, 1, 0), lengths))
        return jnp.moveaxis(result, 0, 1)
    outputs, pullback = jax.vjp(forward, inputs, params)
    input_grad, param_grads = pullback(cotangent.astype(jnp.float32))
    return (outputs.astype(jnp.bfloat16), input_grad, param_grads[0], param_grads[1], param_grads[2], param_grads[3], param_grads[4], param_grads[5])
```

```python
import functools
import math

import jax
import jax.numpy as jnp
from jax import lax
from jax.experimental import pallas as pl
from jax.experimental.pallas import tpu as pltpu
from jax.sharding import PartitionSpec as P

HD = 64
BLOCK = 16
LANES = 128
TILE = 256
BIG = -1e30
f32, bf16 = jnp.float32, jnp.bfloat16


def mm(a, b):
    return lax.dot_general(a, b, (((1,), (0,)), ((), ())), preferred_element_type=f32)


def mm_t(a, b):
    return lax.dot_general(a, b, (((1,), (1,)), ((), ())), preferred_element_type=f32)


def t_mm(a, b):
    return lax.dot_general(a, b, (((0,), (0,)), ((), ())), preferred_element_type=f32)


def rotary_tables(length):
    half = HD // 2
    places = jnp.arange(length).astype(f32)
    rates = jnp.exp(jnp.arange(half).astype(f32) * (-2.0 * math.log(10000.0) / HD))
    angles = places[:, None] * rates[None, :]
    cosine, sine = jnp.cos(angles), jnp.sin(angles)
    return (
        jnp.concatenate([cosine] * 4, axis=1),
        jnp.concatenate([-sine, sine, -sine, sine], axis=1),
    )


def half_partner(x):
    lane = lax.broadcasted_iota(jnp.int32, x.shape, 1)
    low = lax.rem(lane, HD) < HD // 2
    return jnp.where(low, pltpu.roll(x, LANES - HD // 2, 1), pltpu.roll(x, HD // 2, 1))


def project_kernel(x_ref, gain_ref, w_ref, cos_ref, sin_ref, out_ref):
    x = x_ref[...].astype(f32)
    width = x.shape[1]
    center = x - jnp.mean(x, axis=1, keepdims=True)
    spread = jnp.mean(center * center, axis=1, keepdims=True)
    hidden = (center * lax.rsqrt(spread + 1e-5) * gain_ref[...].astype(f32)).astype(bf16)
    cosine, sine = cos_ref[...], sin_ref[...]
    for part in range(3):
        rows = mm(hidden, w_ref[:, part * width : (part + 1) * width])
        for pair in range(width // LANES):
            cols = slice(pair * LANES, (pair + 1) * LANES)
            field = rows[:, cols]
            if part < 2:
                field = field * cosine + half_partner(field) * sine
            if part == 0:
                field = field * 0.125
            out_ref[part, :, cols] = field.astype(bf16)


def project(x, gain, w, cosine, sine, tile=256):
    tokens, width = x.shape
    length = cosine.shape[0]
    per = length // tile
    return pl.pallas_call(
        project_kernel,
        name="project",
        grid=(tokens // tile,),
        in_specs=[
            pl.BlockSpec((tile, width), lambda i: (i, 0)),
            pl.BlockSpec((1, width), lambda i: (0, 0)),
            pl.BlockSpec((width, 3 * width), lambda i: (0, 0), pipeline_mode=pl.Buffered(1)),
            pl.BlockSpec((tile, LANES), lambda i: (lax.rem(i, per), 0)),
            pl.BlockSpec((tile, LANES), lambda i: (lax.rem(i, per), 0)),
        ],
        out_specs=pl.BlockSpec((3, tile, width), lambda i: (0, i, 0)),
        out_shape=jax.ShapeDtypeStruct((3, tokens, width), bf16),
        compiler_params=pltpu.CompilerParams(vmem_limit_bytes=48 << 20),
        cost_estimate=pl.CostEstimate(
            flops=6 * tokens * width * width, bytes_accessed=tokens * width * 8 + 6 * width * width, transcendentals=0
        ),
    )(x, gain, w, cosine, sine)


def mask_tables(length, row_length):
    pos = jnp.arange(length)
    blk = (pos // BLOCK)[:, None]
    lane = (jnp.arange(LANES) % HD)[None, :]
    dead = (pos >= row_length)[:, None]
    clean_query = (lane == blk).astype(bf16)
    noisy_query = (lane == blk - 1).astype(bf16)
    main_key = jnp.where((blk > lane) | dead, BIG, 0.0).astype(bf16)
    diag_key = jnp.where((blk != lane) | dead, BIG, 0.0).astype(bf16)
    return clean_query, noisy_query, main_key, diag_key


def low_lanes(shape):
    return lax.broadcasted_iota(jnp.int32, shape, 1) < HD


def attend_kernel(side_ref, qkv_ref, cq_ref, nq_ref, mk_ref, dk_ref, out_ref, log_ref,
                  qa, ka, kd, va, s_scr):
    length = out_ref.shape[1]
    clean = side_ref[0]
    noisy = 1 - clean
    tiles = length // TILE
    low = low_lanes((length, LANES))
    ones = jnp.ones((16, length), bf16)
    vc_t = qkv_ref[2, clean].T
    vn_t = qkv_ref[2, noisy].T
    for head in range(2):
        pick = low if head == 0 else jnp.logical_not(low)
        qa[0, head] = jnp.where(pick, qkv_ref[0, clean], cq_ref[...])
        qa[1, head] = jnp.where(pick, qkv_ref[0, noisy], nq_ref[...])
        qa[2, head] = jnp.where(pick, qkv_ref[0, noisy], cq_ref[...])
        ka[head] = jnp.where(pick, qkv_ref[1, clean], mk_ref[...])
        kd[head] = jnp.where(pick, qkv_ref[1, noisy], dk_ref[...])
        va[0, head, :HD] = vc_t[head * HD : (head + 1) * HD]
        va[1, head, :HD] = vn_t[head * HD : (head + 1) * HD]
        va[0, head, HD:] = ones
        va[1, head, HD:] = ones
    for copy in range(2):
        where_to = clean if copy == 0 else noisy
        for tile in range(tiles):
            rows = slice(tile * TILE, (tile + 1) * TILE)
            parts = []
            for head in range(2):
                pieces = [(qa[copy, head, rows, :], ka, 0, t) for t in range(tile + 1)]
                if copy == 1:
                    pieces.append((qa[2, head, rows, :], kd, 1, tile))
                top = None
                for n, (query, keys, vi, t) in enumerate(pieces):
                    s = mm_t(keys[head, t * TILE : (t + 1) * TILE, :], query)
                    if copy == 1 and tile == 0 and n == 0:
                        first = lax.broadcasted_iota(jnp.int32, s.shape, 1) < BLOCK
                        s = jnp.where(first, BIG, s)
                    s_scr[head, n * TILE : (n + 1) * TILE, :] = s
                    m = jnp.max(s, axis=0, keepdims=True)
                    top = m if top is None else jnp.maximum(top, m)
                acc = None
                for n, (query, keys, vi, t) in enumerate(pieces):
                    p = jnp.exp(s_scr[head, n * TILE : (n + 1) * TILE, :] - top).astype(bf16)
                    o = mm(va[vi, head, :, t * TILE : (t + 1) * TILE], p)
                    acc = o if acc is None else acc + o
                total = acc[HD : HD + 1, :]
                parts.append(acc[:HD] / total)
                log_ref[where_to, 0, head : head + 1, rows] = top + jnp.log(total)
            out_ref[where_to, rows, :] = jnp.concatenate(parts, axis=0).T.astype(bf16)


def attend(side, qkv, tables):
    _, copies, length, width = qkv.shape
    pairs = width // LANES
    table_spec = pl.BlockSpec((length, LANES), lambda i, s: (0, 0))
    return pl.pallas_call(
        attend_kernel,
        name="attend",
        grid_spec=pltpu.PrefetchScalarGridSpec(
            num_scalar_prefetch=1,
            grid=(pairs,),
            in_specs=[pl.BlockSpec((3, copies, length, LANES), lambda i, s: (0, 0, 0, i))] + [table_spec] * 4,
            out_specs=[
                pl.BlockSpec((copies, length, LANES), lambda i, s: (0, 0, i)),
                pl.BlockSpec((copies, 1, 2, length), lambda i, s: (0, i, 0, 0)),
            ],
            scratch_shapes=[
                pltpu.VMEM((3, 2, length, LANES), bf16),
                pltpu.VMEM((2, length, LANES), bf16),
                pltpu.VMEM((2, length, LANES), bf16),
                pltpu.VMEM((2, 2, HD + 16, length), bf16),
                pltpu.VMEM((2, length + TILE, TILE), f32),
            ],
        ),
        out_shape=[
            jax.ShapeDtypeStruct((copies, length, width), bf16),
            jax.ShapeDtypeStruct((copies, pairs, 2, length), f32),
        ],
        compiler_params=pltpu.CompilerParams(vmem_limit_bytes=48 << 20),
        cost_estimate=pl.CostEstimate(
            flops=8 * length * length * width, bytes_accessed=16 * length * width, transcendentals=length * length * 12
        ),
    )(side, qkv, *tables)


def split3(x):
    hi = x.astype(bf16)
    rest = x - hi.astype(f32)
    mid = rest.astype(bf16)
    lo = (rest - mid.astype(f32)).astype(bf16)
    return hi, mid, lo


def attend_back_kernel(side_ref, qkv_ref, o_ref, do_ref, log_ref, cq_ref, nq_ref, mk_ref, dk_ref, cos_ref, sin_ref,
                       dqkv_ref, qa, qz, ka, kd, kt, doz, dsum, dq, dkc, dvc):
    length = o_ref.shape[1]
    clean = side_ref[0]
    noisy = 1 - clean
    tiles = length // TILE
    low = low_lanes((length, LANES))
    zero = jnp.zeros((length, LANES), bf16)
    for copy in range(2):
        at = clean if copy == 0 else noisy
        kt[copy] = qkv_ref[1, at].T
        prod = (o_ref[at].astype(f32) * do_ref[at].astype(f32)).T
        dsum[copy, 0:1] = jnp.sum(prod[:HD], axis=0, keepdims=True)
        dsum[copy, 1:2] = jnp.sum(prod[HD:], axis=0, keepdims=True)
        for head in range(2):
            pick = low if head == 0 else jnp.logical_not(low)
            qa[copy, head] = jnp.where(pick, qkv_ref[0, at], (cq_ref, nq_ref)[copy][...])
            qz[copy, head] = jnp.where(pick, qkv_ref[0, at], zero)
            doz[copy, head] = jnp.where(pick, do_ref[at], zero)
            if copy == 0:
                ka[head] = jnp.where(pick, qkv_ref[1, at], mk_ref[...])
            else:
                qa[2, head] = jnp.where(pick, qkv_ref[0, at], cq_ref[...])
                kd[head] = jnp.where(pick, qkv_ref[1, at], dk_ref[...])
    cosine, sine = cos_ref[...], sin_ref[...]

    def piece(copy, tile, query, keys, kv_copy, t, mask_first):
        rows = slice(tile * TILE, (tile + 1) * TILE)
        krows = slice(t * TILE, (t + 1) * TILE)
        kv_at = clean if kv_copy == 0 else noisy
        at = clean if copy == 0 else noisy
        probs, raws = [], []
        for head in range(2):
            s = mm_t(keys[head, krows, :], qa[query, head, rows, :])
            p = jnp.exp(s - log_ref[at, 0, head : head + 1, rows])
            if mask_first:
                first = lax.broadcasted_iota(jnp.int32, s.shape, 1) < BLOCK
                p = jnp.where(first, 0.0, p)
            dp = mm_t(qkv_ref[2, kv_at, krows, :], doz[copy, head, rows, :])
            raw = (p * (dp - dsum[copy, head : head + 1, rows])).astype(bf16)
            p = p.astype(bf16)
            dq[copy, head * HD : (head + 1) * HD, rows] += mm(kt[kv_copy, head * HD : (head + 1) * HD, krows], raw)
            probs.append(p)
            raws.append(raw)
        p2 = jnp.concatenate(probs, axis=1)
        r2 = jnp.concatenate(raws, axis=1)
        do2 = jnp.concatenate([doz[copy, 0, rows, :], doz[copy, 1, rows, :]], axis=0)
        q2 = jnp.concatenate([qz[copy, 0, rows, :], qz[copy, 1, rows, :]], axis=0)
        return mm(p2, do2), mm(r2, q2)

    def finish(field, rotate, scale):
        if rotate:
            c, s = cosine, sine
            field = field * c - half_partner(field) * s
        return (field * scale if scale != 1.0 else field).astype(bf16)

    dq[...] = jnp.zeros_like(dq)
    for t in range(tiles):
        krows = slice(t * TILE, (t + 1) * TILE)
        dv_t, dk_t = piece(1, t, 2, kd, 1, t, False)
        dqkv_ref[2, noisy, krows, :] = dv_t.astype(bf16)
        dkc[krows, :] = dk_t
    dqkv_ref[1, noisy] = finish(dkc[...], True, 1.0)
    for t in range(tiles):
        krows = slice(t * TILE, (t + 1) * TILE)
        dv_acc = dk_acc = None
        for tile in range(t, tiles):
            for copy in range(2):
                dv_t, dk_t = piece(copy, tile, copy, ka, 0, t, copy == 1 and tile == 0)
                dv_acc = dv_t if dv_acc is None else dv_acc + dv_t
                dk_acc = dk_t if dk_acc is None else dk_acc + dk_t
        dqkv_ref[2, clean, krows, :] = dv_acc.astype(bf16)
        dkc[krows, :] = dk_acc
    dqkv_ref[1, clean] = finish(dkc[...], True, 1.0)
    dqkv_ref[0, clean] = finish(dq[0].T, True, 0.125)
    dqkv_ref[0, noisy] = finish(dq[1].T, True, 0.125)


def attend_back(side, qkv, mixed, grad, logs, tables, cosine, sine):
    _, copies, length, width = qkv.shape
    pairs = width // LANES
    table_spec = pl.BlockSpec((length, LANES), lambda i, s: (0, 0), pipeline_mode=pl.Buffered(1))
    row_spec = pl.BlockSpec((copies, length, LANES), lambda i, s: (0, 0, i))
    three = pl.BlockSpec((3, copies, length, LANES), lambda i, s: (0, 0, 0, i))
    return pl.pallas_call(
        attend_back_kernel,
        name="attend_back",
        grid_spec=pltpu.PrefetchScalarGridSpec(
            num_scalar_prefetch=1,
            grid=(pairs,),
            in_specs=[three, row_spec, row_spec, pl.BlockSpec((copies, 1, 2, length), lambda i, s: (0, i, 0, 0))]
            + [table_spec] * 6,
            out_specs=three,
            scratch_shapes=[
                pltpu.VMEM((3, 2, length, LANES), bf16),
                pltpu.VMEM((2, 2, length, LANES), bf16),
                pltpu.VMEM((2, length, LANES), bf16),
                pltpu.VMEM((2, length, LANES), bf16),
                pltpu.VMEM((2, LANES, length), bf16),
                pltpu.VMEM((2, 2, length, LANES), bf16),
                pltpu.VMEM((2, 2, length), f32),
                pltpu.VMEM((2, LANES, length), f32),
                pltpu.VMEM((length, LANES), f32),
                pltpu.VMEM((length, LANES), f32),
            ],
        ),
        out_shape=jax.ShapeDtypeStruct((3, copies, length, width), bf16),
        compiler_params=pltpu.CompilerParams(vmem_limit_bytes=48 << 20),
        cost_estimate=pl.CostEstimate(
            flops=20 * length * length * width, bytes_accessed=30 * length * width, transcendentals=length * length * 12
        ),
    )(side, qkv, mixed, grad, logs, *tables, cosine, sine)


ROOT = math.sqrt(2.0 / math.pi)


def feed_kernel(x_ref, mixed_ref, grad_ref, gain_ref, wo_ref, wu_ref, wd_ref,
                out_ref, act_ref, du_ref, h2_ref, dmid_ref, dbr_ref, dmix_ref, dgain_ref, *, chunk):
    width, ff = wu_ref.shape
    gain = gain_ref[...].astype(f32)
    middle = x_ref[...].astype(f32) + mm(mixed_ref[...], wo_ref[...])
    center = middle - jnp.mean(middle, axis=1, keepdims=True)
    spread = jnp.mean(center * center, axis=1, keepdims=True)
    inv = lax.rsqrt(spread + 1e-5)
    norm = center * inv
    hidden = (norm * gain).astype(bf16)
    h2_ref[...] = hidden
    grad = grad_ref[...]
    out = middle
    dh = jnp.zeros_like(middle)
    for c in range(ff // chunk):
        cols = slice(c * chunk, (c + 1) * chunk)
        u = mm(hidden, wu_ref[:, cols])
        da = mm_t(grad, wd_ref[cols, :]).astype(bf16).astype(f32)
        sq = u * u
        t = jnp.tanh(u * (ROOT + (ROOT * 0.044715) * sq))
        half = 0.5 + 0.5 * t
        act = (u * half).astype(bf16)
        slope = half + (u * (half * (1.0 - t))) * (ROOT + (3 * ROOT * 0.044715) * sq)
        du = (da * slope).astype(bf16)
        act_ref[:, cols] = act
        du_ref[:, cols] = du
        out = out + mm(act, wd_ref[cols, :])
        dh = dh + mm_t(du, wu_ref[:, cols])
    out_ref[...] = out.astype(bf16)

    @pl.when(pl.program_id(0) == 0)
    def _():
        dgain_ref[...] = jnp.zeros_like(dgain_ref)

    dgain_ref[...] += jnp.sum((dh * norm).reshape(-1, 8, width), axis=0)
    e = dh * gain
    dmid = grad.astype(f32) + inv * (
        e - jnp.mean(e, axis=1, keepdims=True) - norm * jnp.mean(e * norm, axis=1, keepdims=True)
    )
    dmid_ref[...] = dmid
    dbr = dmid.astype(bf16)
    dbr_ref[...] = dbr
    dmix_ref[...] = mm_t(dbr, wo_ref[...]).astype(bf16)


def feed(x, mixed, grad, gain, wo, wu, wd, tile=256, chunk=768):
    tokens, width = x.shape
    ff = wu.shape[1]
    row = pl.BlockSpec((tile, width), lambda i: (i, 0))
    wide = pl.BlockSpec((tile, ff), lambda i: (i, 0))
    def keep(shape):
        return pl.BlockSpec(shape, lambda i: (0, 0), pipeline_mode=pl.Buffered(1))
    return pl.pallas_call(
        functools.partial(feed_kernel, chunk=chunk),
        name="feed",
        grid=(tokens // tile,),
        in_specs=[row, row, row, keep((1, width)), keep((width, width)), keep((width, ff)), keep((ff, width))],
        out_specs=[row, wide, wide, row, row, row, row, pl.BlockSpec((8, width), lambda i: (0, 0))],
        out_shape=[
            jax.ShapeDtypeStruct((tokens, width), bf16),
            jax.ShapeDtypeStruct((tokens, ff), bf16),
            jax.ShapeDtypeStruct((tokens, ff), bf16),
            jax.ShapeDtypeStruct((tokens, width), bf16),
            jax.ShapeDtypeStruct((tokens, width), f32),
            jax.ShapeDtypeStruct((tokens, width), bf16),
            jax.ShapeDtypeStruct((tokens, width), bf16),
            jax.ShapeDtypeStruct((8, width), f32),
        ],
        compiler_params=pltpu.CompilerParams(vmem_limit_bytes=60 << 20),
        cost_estimate=pl.CostEstimate(
            flops=tokens * width * (4 * width + 8 * ff), bytes_accessed=tokens * (width * 18 + ff * 4),
            transcendentals=tokens * ff
        ),
    )(x, mixed, grad, gain, wo, wu, wd)


def weight_kernel(left_ref, right_ref, out_ref):
    out_ref[...] = t_mm(left_ref[...], right_ref[...]).astype(bf16)


def weight_grad(left, right, block_l, block_r, name):
    tokens, dl = left.shape
    dr = right.shape[1]
    return pl.pallas_call(
        weight_kernel,
        name=name,
        grid=(dl // block_l, dr // block_r),
        in_specs=[
            pl.BlockSpec((tokens, block_l), lambda i, j: (0, i)),
            pl.BlockSpec((tokens, block_r), lambda i, j: (0, j)),
        ],
        out_specs=pl.BlockSpec((block_l, block_r), lambda i, j: (i, j)),
        out_shape=jax.ShapeDtypeStruct((dl, dr), bf16),
        compiler_params=pltpu.CompilerParams(vmem_limit_bytes=48 << 20),
        cost_estimate=pl.CostEstimate(
            flops=2 * tokens * dl * dr, bytes_accessed=2 * tokens * (dl + dr) + 2 * dl * dr, transcendentals=0
        ),
    )(left, right)


def project_back_kernel(x_ref, gain_ref, w_ref, dqkv_ref, dmid_ref, dx_ref, dgain_ref):
    x = x_ref[...].astype(f32)
    width = x.shape[1]
    center = x - jnp.mean(x, axis=1, keepdims=True)
    spread = jnp.mean(center * center, axis=1, keepdims=True)
    inv = lax.rsqrt(spread + 1e-5)
    norm = center * inv
    dh = mm_t(dqkv_ref[0], w_ref[:, :width])
    dh = dh + mm_t(dqkv_ref[1], w_ref[:, width : 2 * width])
    dh = dh + mm_t(dqkv_ref[2], w_ref[:, 2 * width :])

    @pl.when(pl.program_id(0) == 0)
    def _():
        dgain_ref[...] = jnp.zeros_like(dgain_ref)

    dgain_ref[...] += jnp.sum((dh * norm).reshape(-1, 8, width), axis=0)
    e = dh * gain_ref[...].astype(f32)
    dx_ref[...] = dmid_ref[...] + inv * (
        e - jnp.mean(e, axis=1, keepdims=True) - norm * jnp.mean(e * norm, axis=1, keepdims=True)
    )


def project_back(x, gain, w, dqkv, dmid, tile=256):
    tokens, width = x.shape
    row = pl.BlockSpec((tile, width), lambda i: (i, 0))
    return pl.pallas_call(
        project_back_kernel,
        name="project_back",
        grid=(tokens // tile,),
        in_specs=[
            row,
            pl.BlockSpec((1, width), lambda i: (0, 0)),
            pl.BlockSpec((width, 3 * width), lambda i: (0, 0), pipeline_mode=pl.Buffered(1)),
            pl.BlockSpec((3, tile, width), lambda i: (0, i, 0)),
            row,
        ],
        out_specs=[row, pl.BlockSpec((8, width), lambda i: (0, 0))],
        out_shape=[jax.ShapeDtypeStruct((tokens, width), f32), jax.ShapeDtypeStruct((8, width), f32)],
        compiler_params=pltpu.CompilerParams(vmem_limit_bytes=48 << 20),
        cost_estimate=pl.CostEstimate(
            flops=6 * tokens * width * width, bytes_accessed=tokens * width * 16, transcendentals=0
        ),
    )(x, gain, w, dqkv, dmid)


def norm_kernel(x_ref, gain_ref, out_ref):
    x = x_ref[...].astype(f32)
    center = x - jnp.mean(x, axis=1, keepdims=True)
    spread = jnp.mean(center * center, axis=1, keepdims=True)
    out_ref[...] = (center * lax.rsqrt(spread + 1e-5) * gain_ref[...].astype(f32)).astype(bf16)


def norm_rows(x, gain, tile=512):
    tokens, width = x.shape
    row = pl.BlockSpec((tile, width), lambda i: (i, 0))
    return pl.pallas_call(
        norm_kernel,
        name="norm_rows",
        grid=(tokens // tile,),
        in_specs=[row, pl.BlockSpec((1, width), lambda i: (0, 0))],
        out_specs=row,
        out_shape=jax.ShapeDtypeStruct((tokens, width), bf16),
    )(x, gain)


def shards(tokens, cotangent, lengths, ln1_gain, w_qkv, w_out, ln2_gain, w_up, w_down):
    side = lax.axis_index("stream")
    _, rows_dev, length, width = tokens.shape
    assert rows_dev == 2
    swap = [(0, 1), (1, 0)]

    def pair_up(field):
        own = jnp.take(field[0], side, axis=0)
        away = lax.ppermute(jnp.take(field[0], 1 - side, axis=0), "stream", swap)
        return jnp.concatenate([own, away], axis=0)

    def hand_back(field):
        own, away = field[:length], lax.ppermute(field[length:], "stream", swap)
        first = side == 0
        return jnp.stack([jnp.where(first, own, away), jnp.where(first, away, own)])[None]

    w_qkv_all = lax.all_gather(w_qkv, "batch", axis=0, tiled=True)
    gain_one = lax.all_gather(ln1_gain, "batch", axis=0, tiled=True)[None]
    gain_two = lax.all_gather(ln2_gain, "batch", axis=0, tiled=True)[None]
    w_out_all = lax.all_gather(w_out, "batch", axis=0, tiled=True)
    w_up_all = lax.all_gather(w_up, "batch", axis=0, tiled=True)
    w_down_all = lax.all_gather(w_down, "batch", axis=0, tiled=True)

    x = pair_up(tokens)
    grad = pair_up(cotangent)
    cosine, sine = rotary_tables(length)
    tables = mask_tables(length, jnp.take(lengths, side))
    side_array = side.reshape(1).astype(jnp.int32)

    qkv = project(x, gain_one, w_qkv_all, cosine, sine)
    qkv4 = qkv.reshape(3, 2, length, width)
    mixed, logs = attend(side_array, qkv4, tables)
    mixed2 = mixed.reshape(2 * length, width)
    out, act, du, h2, dmid, dbr, dmix, dgain_two = feed(
        x, mixed2, grad, gain_two, w_out_all, w_up_all, w_down_all, tile=512
    )
    dw_down = weight_grad(act, grad, 768, 768, "grad_down")
    dw_up = weight_grad(h2, du, 768, 768, "grad_up")
    dw_out = weight_grad(mixed2, dbr, 768, 768, "grad_out")
    dqkv = attend_back(side_array, qkv4, mixed, dmix.reshape(2, length, width), logs, tables, cosine, sine)
    hidden = norm_rows(x, gain_one)
    dqkv3 = dqkv.reshape(3, 2 * length, width)
    dw_q = [weight_grad(hidden, dqkv3[i], 768, 768, "grad_qkv") for i in range(3)]
    dx, dgain_one = project_back(x, gain_one, w_qkv_all, dqkv3, dmid)

    both = ("stream", "batch")
    peers = lax.axis_size("stream") * lax.axis_size("batch")
    share = width // peers
    packed = jnp.concatenate(
        [
            *dw_q,
            dw_out,
            dw_up,
            dw_down.reshape(peers, -1, share, width).swapaxes(1, 2).reshape(width, -1),
        ],
        axis=1,
    )
    summed = lax.psum_scatter(packed, both, scatter_dimension=0, tiled=True).astype(f32)
    pieces = jnp.split(summed, [3 * width, 4 * width, 4 * width + w_up.shape[1]], axis=1)
    pieces[3] = pieces[3].reshape(share, -1, width).swapaxes(0, 1)
    gains = lax.psum(jnp.stack([jnp.sum(dgain_one, axis=0), jnp.sum(dgain_two, axis=0)]), both)
    at = (side * lax.axis_size("batch") + lax.axis_index("batch")) * share
    gains = lax.dynamic_slice(gains, (0, at), (2, share))
    return (
        hand_back(out),
        hand_back(dx),
        gains[0],
        pieces[0].reshape(share, 3 * width),
        pieces[1].reshape(share, width),
        gains[1],
        pieces[2].reshape(share, -1),
        pieces[3].reshape(-1, width),
    )


def solution(mesh):
    token = P("stream", "batch", None, None)
    vector, matrix = P("batch"), P("batch", None)
    out_vector, out_matrix = P(("stream", "batch")), P(("stream", "batch"), None)
    return jax.shard_map(
        shards,
        mesh=mesh,
        in_specs=(token, token, vector, vector, matrix, matrix, vector, matrix, matrix),
        out_specs=(token, token, out_vector, out_matrix, out_matrix, out_vector, out_matrix, out_matrix),
        check_vma=False,
    )
```

```python
import functools
import math

import jax
import jax.numpy as jnp
from jax import lax
from jax.experimental import pallas as pl
from jax.experimental.pallas import tpu as pltpu
from jax.sharding import PartitionSpec as P

HD = 64
BLOCK = 16
LANES = 128
TILE = 256
BIG = -1e30
f32, bf16 = jnp.float32, jnp.bfloat16


def mm(a, b):
    return lax.dot_general(a, b, (((1,), (0,)), ((), ())), preferred_element_type=f32)


def mm_t(a, b):
    return lax.dot_general(a, b, (((1,), (1,)), ((), ())), preferred_element_type=f32)


def t_mm(a, b):
    return lax.dot_general(a, b, (((0,), (0,)), ((), ())), preferred_element_type=f32)


def rotary_tables(length):
    half = HD // 2
    places = jnp.arange(length).astype(f32)
    rates = jnp.exp(jnp.arange(half).astype(f32) * (-2.0 * math.log(10000.0) / HD))
    angles = places[:, None] * rates[None, :]
    cosine, sine = jnp.cos(angles), jnp.sin(angles)
    return (
        jnp.concatenate([cosine] * 4, axis=1),
        jnp.concatenate([-sine, sine, -sine, sine], axis=1),
    )


def half_partner(x):
    lane = lax.broadcasted_iota(jnp.int32, x.shape, 1)
    low = lax.rem(lane, HD) < HD // 2
    return jnp.where(low, pltpu.roll(x, LANES - HD // 2, 1), pltpu.roll(x, HD // 2, 1))


def row_specs(tile, width, half):
    own = pl.BlockSpec((None, None, tile, width), lambda i, s: (0, s[0], jnp.minimum(i, half - 1), 0))
    away = pl.BlockSpec((tile, width), lambda i, s: (jnp.maximum(i - half, 0), 0))
    return own, away


def read_rows(own_ref, away_ref, half):
    return jnp.where(pl.program_id(0) < half, own_ref[...], away_ref[...])


def project_kernel(side_ref, own_ref, away_ref, gain_ref, w_ref, cos_ref, sin_ref, out_ref, hidden_ref, *, half):
    x = read_rows(own_ref, away_ref, half).astype(f32)
    width = x.shape[1]
    center = x - jnp.mean(x, axis=1, keepdims=True)
    spread = jnp.mean(center * center, axis=1, keepdims=True)
    hidden = (center * lax.rsqrt(spread + 1e-5) * gain_ref[...].astype(f32)).astype(bf16)
    hidden_ref[...] = hidden
    cosine, sine = cos_ref[...], sin_ref[...]
    for part in range(3):
        rows = mm(hidden, w_ref[:, part * width : (part + 1) * width])
        for pair in range(width // LANES):
            cols = slice(pair * LANES, (pair + 1) * LANES)
            field = rows[:, cols]
            if part < 2:
                field = field * cosine + half_partner(field) * sine
            if part == 0:
                field = field * 0.125
            out_ref[part, :, cols] = field.astype(bf16)


def project(side, own, away, gain, w, cosine, sine, tile=512):
    length, width = away.shape
    tokens, half = 2 * length, length // tile
    table = pl.BlockSpec((tile, LANES), lambda i, s: (lax.rem(i, half), 0))
    return pl.pallas_call(
        functools.partial(project_kernel, half=half),
        name="project",
        grid_spec=pltpu.PrefetchScalarGridSpec(
            num_scalar_prefetch=1,
            grid=(2 * half,),
            in_specs=[
                *row_specs(tile, width, half),
                pl.BlockSpec((1, width), lambda i, s: (0, 0)),
                pl.BlockSpec((width, 3 * width), lambda i, s: (0, 0), pipeline_mode=pl.Buffered(1)),
                table,
                table,
            ],
            out_specs=[
                pl.BlockSpec((3, tile, width), lambda i, s: (0, i, 0)),
                pl.BlockSpec((tile, width), lambda i, s: (i, 0)),
            ],
        ),
        out_shape=[jax.ShapeDtypeStruct((3, tokens, width), bf16), jax.ShapeDtypeStruct((tokens, width), bf16)],
        compiler_params=pltpu.CompilerParams(vmem_limit_bytes=48 << 20),
        cost_estimate=pl.CostEstimate(
            flops=6 * tokens * width * width, bytes_accessed=tokens * width * 10 + 6 * width * width, transcendentals=0
        ),
    )(side, own, away, gain, w, cosine, sine)


def mask_tables(length, row_length):
    pos = jnp.arange(length)
    blk = (pos // BLOCK)[:, None]
    lane = (jnp.arange(LANES) % HD)[None, :]
    dead = (pos >= row_length)[:, None]
    clean_query = (lane == blk).astype(bf16)
    noisy_query = (lane == blk - 1).astype(bf16)
    main_key = jnp.where((blk > lane) | dead, BIG, 0.0).astype(bf16)
    diag_key = jnp.where((blk != lane) | dead, BIG, 0.0).astype(bf16)
    return clean_query, noisy_query, main_key, diag_key


def low_lanes(shape):
    return lax.broadcasted_iota(jnp.int32, shape, 1) < HD


def attend_kernel(side_ref, qkv_ref, cq_ref, nq_ref, mk_ref, dk_ref, out_ref, log_ref,
                  qa, ka, kd, va, s_scr):
    length = out_ref.shape[1]
    clean = side_ref[0]
    noisy = 1 - clean
    tiles = length // TILE
    low = low_lanes((length, LANES))
    ones = jnp.ones((16, length), bf16)
    vc_t = qkv_ref[2, clean].T
    vn_t = qkv_ref[2, noisy].T
    for head in range(2):
        pick = low if head == 0 else jnp.logical_not(low)
        qa[0, head] = jnp.where(pick, qkv_ref[0, clean], cq_ref[...])
        qa[1, head] = jnp.where(pick, qkv_ref[0, noisy], nq_ref[...])
        qa[2, head] = jnp.where(pick, qkv_ref[0, noisy], cq_ref[...])
        ka[head] = jnp.where(pick, qkv_ref[1, clean], mk_ref[...])
        kd[head] = jnp.where(pick, qkv_ref[1, noisy], dk_ref[...])
        va[0, head, :HD] = vc_t[head * HD : (head + 1) * HD]
        va[1, head, :HD] = vn_t[head * HD : (head + 1) * HD]
        va[0, head, HD:] = ones
        va[1, head, HD:] = ones
    for copy in range(2):
        where_to = clean if copy == 0 else noisy
        for tile in range(tiles):
            rows = slice(tile * TILE, (tile + 1) * TILE)
            parts = []
            for head in range(2):
                pieces = [(qa[copy, head, rows, :], ka, 0, t) for t in range(tile + 1)]
                if copy == 1:
                    pieces.append((qa[2, head, rows, :], kd, 1, tile))
                top = None
                for n, (query, keys, vi, t) in enumerate(pieces):
                    s = mm_t(keys[head, t * TILE : (t + 1) * TILE, :], query)
                    if copy == 1 and tile == 0 and n == 0:
                        first = lax.broadcasted_iota(jnp.int32, s.shape, 1) < BLOCK
                        s = jnp.where(first, BIG, s)
                    s_scr[head, n * TILE : (n + 1) * TILE, :] = s
                    m = jnp.max(s, axis=0, keepdims=True)
                    top = m if top is None else jnp.maximum(top, m)
                acc = None
                for n, (query, keys, vi, t) in enumerate(pieces):
                    p = jnp.exp(s_scr[head, n * TILE : (n + 1) * TILE, :] - top).astype(bf16)
                    o = mm(va[vi, head, :, t * TILE : (t + 1) * TILE], p)
                    acc = o if acc is None else acc + o
                total = acc[HD : HD + 1, :]
                parts.append(acc[:HD] / total)
                log_ref[where_to, 0, head : head + 1, rows] = top + jnp.log(total)
            out_ref[where_to, rows, :] = jnp.concatenate(parts, axis=0).T.astype(bf16)


def attend(side, qkv, tables):
    _, copies, length, width = qkv.shape
    pairs = width // LANES
    table_spec = pl.BlockSpec((length, LANES), lambda i, s: (0, 0))
    return pl.pallas_call(
        attend_kernel,
        name="attend",
        grid_spec=pltpu.PrefetchScalarGridSpec(
            num_scalar_prefetch=1,
            grid=(pairs,),
            in_specs=[pl.BlockSpec((3, copies, length, LANES), lambda i, s: (0, 0, 0, i))] + [table_spec] * 4,
            out_specs=[
                pl.BlockSpec((copies, length, LANES), lambda i, s: (0, 0, i)),
                pl.BlockSpec((copies, 1, 2, length), lambda i, s: (0, i, 0, 0)),
            ],
            scratch_shapes=[
                pltpu.VMEM((3, 2, length, LANES), bf16),
                pltpu.VMEM((2, length, LANES), bf16),
                pltpu.VMEM((2, length, LANES), bf16),
                pltpu.VMEM((2, 2, HD + 16, length), bf16),
                pltpu.VMEM((2, length + TILE, TILE), f32),
            ],
        ),
        out_shape=[
            jax.ShapeDtypeStruct((copies, length, width), bf16),
            jax.ShapeDtypeStruct((copies, pairs, 2, length), f32),
        ],
        compiler_params=pltpu.CompilerParams(vmem_limit_bytes=48 << 20),
        cost_estimate=pl.CostEstimate(
            flops=8 * length * length * width, bytes_accessed=16 * length * width, transcendentals=length * length * 12
        ),
    )(side, qkv, *tables)


def attend_back_next(side_ref, _, *refs):
    attend_back_kernel(side_ref, *refs)


def attend_back_kernel(side_ref, qkv_ref, o_ref, do_ref, log_ref, cq_ref, nq_ref, mk_ref, dk_ref, cos_ref, sin_ref,
                       dqkv_ref, qa, qz, ka, kd, kt, doz, dsum, dq, dkc, dvc):
    length = o_ref.shape[1]
    clean = side_ref[0]
    noisy = 1 - clean
    tiles = length // TILE
    low = low_lanes((length, LANES))
    zero = jnp.zeros((length, LANES), bf16)
    for copy in range(2):
        at = clean if copy == 0 else noisy
        kt[copy] = qkv_ref[1, at].T
        prod = (o_ref[at].astype(f32) * do_ref[at].astype(f32)).T
        dsum[copy, 0:1] = jnp.sum(prod[:HD], axis=0, keepdims=True)
        dsum[copy, 1:2] = jnp.sum(prod[HD:], axis=0, keepdims=True)
        for head in range(2):
            pick = low if head == 0 else jnp.logical_not(low)
            qa[copy, head] = jnp.where(pick, qkv_ref[0, at], (cq_ref, nq_ref)[copy][...])
            qz[copy, head] = jnp.where(pick, qkv_ref[0, at], zero)
            doz[copy, head] = jnp.where(pick, do_ref[at], zero)
            if copy == 0:
                ka[head] = jnp.where(pick, qkv_ref[1, at], mk_ref[...])
            else:
                qa[2, head] = jnp.where(pick, qkv_ref[0, at], cq_ref[...])
                kd[head] = jnp.where(pick, qkv_ref[1, at], dk_ref[...])
    cosine, sine = cos_ref[...], sin_ref[...]

    def piece(copy, tile, query, keys, kv_copy, t, mask_first):
        rows = slice(tile * TILE, (tile + 1) * TILE)
        krows = slice(t * TILE, (t + 1) * TILE)
        kv_at = clean if kv_copy == 0 else noisy
        at = clean if copy == 0 else noisy
        probs, raws = [], []
        for head in range(2):
            s = mm_t(keys[head, krows, :], qa[query, head, rows, :])
            p = jnp.exp(s - log_ref[at, 0, head : head + 1, rows])
            if mask_first:
                first = lax.broadcasted_iota(jnp.int32, s.shape, 1) < BLOCK
                p = jnp.where(first, 0.0, p)
            dp = mm_t(qkv_ref[2, kv_at, krows, :], doz[copy, head, rows, :])
            raw = (p * (dp - dsum[copy, head : head + 1, rows])).astype(bf16)
            p = p.astype(bf16)
            dq[copy, head * HD : (head + 1) * HD, rows] += mm(kt[kv_copy, head * HD : (head + 1) * HD, krows], raw)
            probs.append(p)
            raws.append(raw)
        p2 = jnp.concatenate(probs, axis=1)
        r2 = jnp.concatenate(raws, axis=1)
        do2 = jnp.concatenate([doz[copy, 0, rows, :], doz[copy, 1, rows, :]], axis=0)
        q2 = jnp.concatenate([qz[copy, 0, rows, :], qz[copy, 1, rows, :]], axis=0)
        return mm(p2, do2), mm(r2, q2)

    def finish(field, rotate, scale):
        if rotate:
            c, s = cosine, sine
            field = field * c - half_partner(field) * s
        return (field * scale if scale != 1.0 else field).astype(bf16)

    dq[...] = jnp.zeros_like(dq)
    for t in range(tiles):
        krows = slice(t * TILE, (t + 1) * TILE)
        dv_t, dk_t = piece(1, t, 2, kd, 1, t, False)
        dqkv_ref[2, noisy, krows, :] = dv_t.astype(bf16)
        dkc[krows, :] = dk_t
    dqkv_ref[1, noisy] = finish(dkc[...], True, 1.0)
    for t in range(tiles):
        krows = slice(t * TILE, (t + 1) * TILE)
        dv_acc = dk_acc = None
        for tile in range(t, tiles):
            for copy in range(2):
                dv_t, dk_t = piece(copy, tile, copy, ka, 0, t, copy == 1 and tile == 0)
                dv_acc = dv_t if dv_acc is None else dv_acc + dv_t
                dk_acc = dk_t if dk_acc is None else dk_acc + dk_t
        dqkv_ref[2, clean, krows, :] = dv_acc.astype(bf16)
        dkc[krows, :] = dk_acc
    dqkv_ref[1, clean] = finish(dkc[...], True, 1.0)
    dqkv_ref[0, clean] = finish(dq[0].T, True, 0.125)
    dqkv_ref[0, noisy] = finish(dq[1].T, True, 0.125)


def attend_back(side, into, first, pairs, qkv, mixed, grad, logs, tables, cosine, sine):
    _, copies, length, width = qkv.shape
    table_spec = pl.BlockSpec((length, LANES), lambda i, s: (0, 0), pipeline_mode=pl.Buffered(1))
    row_spec = pl.BlockSpec((copies, length, LANES), lambda i, s: (0, 0, i + first))
    three = pl.BlockSpec((3, copies, length, LANES), lambda i, s: (0, 0, 0, i + first))
    begun = [] if into is None else [into]
    return pl.pallas_call(
        attend_back_next if begun else attend_back_kernel,
        name="attend_back",
        grid_spec=pltpu.PrefetchScalarGridSpec(
            num_scalar_prefetch=1,
            grid=(pairs,),
            in_specs=[
                *[pl.BlockSpec(memory_space=pl.ANY)] * len(begun),
                three,
                row_spec,
                row_spec,
                pl.BlockSpec((copies, 1, 2, length), lambda i, s: (0, i + first, 0, 0)),
            ]
            + [table_spec] * 6,
            out_specs=three,
            scratch_shapes=[
                pltpu.VMEM((3, 2, length, LANES), bf16),
                pltpu.VMEM((2, 2, length, LANES), bf16),
                pltpu.VMEM((2, length, LANES), bf16),
                pltpu.VMEM((2, length, LANES), bf16),
                pltpu.VMEM((2, LANES, length), bf16),
                pltpu.VMEM((2, 2, length, LANES), bf16),
                pltpu.VMEM((2, 2, length), f32),
                pltpu.VMEM((2, LANES, length), f32),
                pltpu.VMEM((length, LANES), f32),
                pltpu.VMEM((length, LANES), f32),
            ],
        ),
        out_shape=jax.ShapeDtypeStruct((3, copies, length, width), bf16),
        input_output_aliases={1: 0} if begun else {},
        compiler_params=pltpu.CompilerParams(vmem_limit_bytes=48 << 20),
        cost_estimate=pl.CostEstimate(
            flops=20 * length * length * LANES * pairs,
            bytes_accessed=32 * length * LANES * pairs,
            transcendentals=4 * length * length * pairs,
        ),
    )(side, *begun, qkv, mixed, grad, logs, *tables, cosine, sine)


ROOT = math.sqrt(2.0 / math.pi)


def feed_kernel(side_ref, x_own, x_away, mixed_ref, g_own, g_away, gain_ref, rest_ref,
                out_own, out_away, act_ref, du_ref, h2_ref, dmid_ref, dbr_ref, dmix_ref, dgain_ref,
                wo_ref, wu_ref, wd_ref, sems, *, half):
    groups, rows, width = wo_ref.shape
    fold = wd_ref.shape[1]
    ff = fold * width

    def fetch(n):
        cols = rest_ref.at[:, :, n * width : (n + 1) * width]
        if n == 0:
            into = wo_ref
        elif n <= fold:
            into = wu_ref.at[n - 1]
        else:
            into = wd_ref.at[:, n - 1 - fold]
        return pltpu.make_async_copy(cols, into, sems.at[n])

    @pl.when(pl.program_id(0) == 0)
    def _():
        for n in range(1 + 2 * fold):
            fetch(n).start()
        for n in range(1 + 2 * fold):
            fetch(n).wait()

    def down(c):
        per = groups // fold
        return wd_ref[c * per : (c + 1) * per].reshape(width, width)

    wo = wo_ref[...].reshape(width, width)
    gain = gain_ref[...].astype(f32)
    middle = read_rows(x_own, x_away, half).astype(f32) + mm(mixed_ref[...], wo)
    center = middle - jnp.mean(middle, axis=1, keepdims=True)
    spread = jnp.mean(center * center, axis=1, keepdims=True)
    inv = lax.rsqrt(spread + 1e-5)
    norm = center * inv
    hidden = (norm * gain).astype(bf16)
    h2_ref[...] = hidden
    grad = read_rows(g_own, g_away, half)
    out = middle
    dh = jnp.zeros_like(middle)
    for c in range(fold):
        cols = slice(c * width, (c + 1) * width)
        up = wu_ref[c].reshape(width, width)
        u = mm(hidden, up)
        da = mm_t(grad, down(c)).astype(bf16).astype(f32)
        sq = u * u
        t = jnp.tanh(u * (ROOT + (ROOT * 0.044715) * sq))
        part = 0.5 + 0.5 * t
        act = (u * part).astype(bf16)
        slope = part + (u * (part * (1.0 - t))) * (ROOT + (3 * ROOT * 0.044715) * sq)
        du = (da * slope).astype(bf16)
        act_ref[:, cols] = act
        du_ref[:, cols] = du
        out = out + mm(act, down(c))
        dh = dh + mm_t(du, up)
    low = out.astype(bf16)

    @pl.when(pl.program_id(0) < half)
    def _():
        out_own[...] = low

    @pl.when(pl.program_id(0) >= half)
    def _():
        out_away[...] = low

    @pl.when(pl.program_id(0) == 0)
    def _():
        dgain_ref[...] = jnp.zeros_like(dgain_ref)

    dgain_ref[...] += jnp.sum((dh * norm).reshape(-1, 8, width), axis=0)
    e = dh * gain
    dmid = grad.astype(f32) + inv * (
        e - jnp.mean(e, axis=1, keepdims=True) - norm * jnp.mean(e * norm, axis=1, keepdims=True)
    )
    dmid_ref[...] = dmid
    dbr = dmid.astype(bf16)
    dbr_ref[...] = dbr
    dmix_ref[...] = mm_t(dbr, wo).astype(bf16)


def feed(side, x_own, x_away, mixed, g_own, g_away, gain, rest, tile=512):
    tokens, width = mixed.shape
    groups, rows, columns = rest.shape
    fold = (columns // width - 1) // 2
    ff = fold * width
    half = tokens // 2 // tile
    row = pl.BlockSpec((tile, width), lambda i, s: (i, 0))
    wide = pl.BlockSpec((tile, ff), lambda i, s: (i, 0))
    own, away = row_specs(tile, width, half)

    def keep(shape):
        return pl.BlockSpec(shape, lambda i, s: (0, 0), pipeline_mode=pl.Buffered(1))

    return pl.pallas_call(
        functools.partial(feed_kernel, half=half),
        name="feed",
        grid_spec=pltpu.PrefetchScalarGridSpec(
            num_scalar_prefetch=1,
            grid=(2 * half,),
            in_specs=[own, away, row, own, away, keep((1, width)), pl.BlockSpec(memory_space=pl.ANY)],
            out_specs=[own, away, wide, wide, row, row, row, row, pl.BlockSpec((8, width), lambda i, s: (0, 0))],
            scratch_shapes=[
                pltpu.VMEM((groups, rows, width), bf16),
                pltpu.VMEM((fold, groups, rows, width), bf16),
                pltpu.VMEM((groups, fold, rows, width), bf16),
                pltpu.SemaphoreType.DMA((1 + 2 * fold,)),
            ],
        ),
        out_shape=[
            jax.ShapeDtypeStruct((1, 2, tokens // 2, width), bf16),
            jax.ShapeDtypeStruct((tokens // 2, width), bf16),
            jax.ShapeDtypeStruct((tokens, ff), bf16),
            jax.ShapeDtypeStruct((tokens, ff), bf16),
            jax.ShapeDtypeStruct((tokens, width), bf16),
            jax.ShapeDtypeStruct((tokens, width), f32),
            jax.ShapeDtypeStruct((tokens, width), bf16),
            jax.ShapeDtypeStruct((tokens, width), bf16),
            jax.ShapeDtypeStruct((8, width), f32),
        ],
        compiler_params=pltpu.CompilerParams(vmem_limit_bytes=60 << 20),
        cost_estimate=pl.CostEstimate(
            flops=tokens * width * (4 * width + 8 * ff), bytes_accessed=tokens * (width * 18 + ff * 4),
            transcendentals=tokens * ff
        ),
    )(side, x_own, x_away, mixed, g_own, g_away, gain, rest)


def weight_kernel(me_ref, left_ref, *refs, share, split):
    right_refs, (keep_ref, send_ref, scr) = refs[:-3], refs[-3:]
    if split:
        own_ref, away_ref = right_refs
        half = own_ref.shape[0]
        total = t_mm(left_ref[:half], own_ref[...]) + t_mm(left_ref[half:], away_ref[...])
    else:
        total = t_mm(left_ref[...], right_refs[0][...])
    slabs = total.shape[0] // share
    scr[...] = total.reshape(scr.shape)
    low_me = lax.rem(me_ref[0], slabs)
    for slot in range(slabs):
        source = jnp.bitwise_xor(low_me, slot)
        into = send_ref if slot % 2 else keep_ref
        into[slot // 2] = scr[source].astype(bf16)


def weight_grad_columns(me, left, right, part, block, share, name):
    tokens, dl = left.shape
    dr = right.shape[2]
    peers = dl // share
    shape = (peers // 2, share, dr)
    out = pl.BlockSpec((peers // 2, share, block), lambda j, m: (0, 0, j))
    return pl.pallas_call(
        functools.partial(weight_kernel, share=share, split=False),
        name=name,
        grid_spec=pltpu.PrefetchScalarGridSpec(
            num_scalar_prefetch=1,
            grid=(dr // block,),
            in_specs=[
                pl.BlockSpec((tokens, dl), lambda j, m: (0, 0), pipeline_mode=pl.Buffered(1)),
                pl.BlockSpec((None, tokens, block), lambda j, m: (part, 0, j)),
            ],
            out_specs=[out, out],
            scratch_shapes=[pltpu.VMEM((peers, share, block), f32)],
        ),
        out_shape=[jax.ShapeDtypeStruct(shape, bf16)] * 2,
        compiler_params=pltpu.CompilerParams(vmem_limit_bytes=48 << 20),
        cost_estimate=pl.CostEstimate(
            flops=2 * tokens * dl * dr, bytes_accessed=2 * tokens * (dl + dr) + 2 * dl * dr, transcendentals=0
        ),
    )(me, left, right)


def weight_grad_rows(me, left, own, away, block, share, name):
    tokens, dl = left.shape
    length, dr = away.shape
    slabs = block // share
    steps = dl // block
    shape = (steps * slabs // 2, share, dr)
    out = pl.BlockSpec((slabs // 2, share, dr), lambda j, m: (j, 0, 0))

    def place(j, m):
        return (0, jnp.bitwise_xor(j, lax.div(m[0], slabs)))

    return pl.pallas_call(
        functools.partial(weight_kernel, share=share, split=True),
        name=name,
        grid_spec=pltpu.PrefetchScalarGridSpec(
            num_scalar_prefetch=1,
            grid=(steps,),
            in_specs=[
                pl.BlockSpec((tokens, block), place),
                pl.BlockSpec((None, None, length, dr), lambda j, m: (0, m[1], 0, 0), pipeline_mode=pl.Buffered(1)),
                pl.BlockSpec((length, dr), lambda j, m: (0, 0), pipeline_mode=pl.Buffered(1)),
            ],
            out_specs=[out, out],
            scratch_shapes=[pltpu.VMEM((slabs, share, dr), f32)],
        ),
        out_shape=[jax.ShapeDtypeStruct(shape, bf16)] * 2,
        compiler_params=pltpu.CompilerParams(vmem_limit_bytes=48 << 20),
        cost_estimate=pl.CostEstimate(
            flops=2 * tokens * dl * dr, bytes_accessed=2 * tokens * (dl + dr) + 2 * dl * dr, transcendentals=0
        ),
    )(me, left, own, away)


def project_back_kernel(side_ref, x_ref, gain_ref, w_ref, dqkv_ref, dmid_ref, dx_ref, dgain_ref):
    x = x_ref[...].astype(f32)
    width = x.shape[1]
    center = x - jnp.mean(x, axis=1, keepdims=True)
    spread = jnp.mean(center * center, axis=1, keepdims=True)
    inv = lax.rsqrt(spread + 1e-5)
    norm = center * inv
    dh = mm_t(dqkv_ref[0], w_ref[:, :width])
    dh = dh + mm_t(dqkv_ref[1], w_ref[:, width : 2 * width])
    dh = dh + mm_t(dqkv_ref[2], w_ref[:, 2 * width :])

    @pl.when(pl.program_id(0) == 0)
    def _():
        dgain_ref[...] = jnp.zeros_like(dgain_ref)

    dgain_ref[...] += jnp.sum((dh * norm).reshape(-1, 8, width), axis=0)
    e = dh * gain_ref[...].astype(f32)
    dx_ref[...] = (dmid_ref[...] + inv * (
        e - jnp.mean(e, axis=1, keepdims=True) - norm * jnp.mean(e * norm, axis=1, keepdims=True)
    )).astype(dx_ref.dtype)


def project_back(side, x, gain, w, dqkv, dmid, away, tile=256):
    width = x.shape[-1]
    length = dmid.shape[0] // 2
    half = length // tile
    first = half if away else 0
    if away:
        x_spec = pl.BlockSpec((tile, width), lambda i, s: (i, 0))
        out_spec, out_shape = x_spec, jax.ShapeDtypeStruct((length, width), bf16)
    else:
        x_spec = pl.BlockSpec((None, None, tile, width), lambda i, s: (0, s[0], i, 0))
        out_spec, out_shape = x_spec, jax.ShapeDtypeStruct((1, 2, length, width), f32)
    return pl.pallas_call(
        project_back_kernel,
        name="project_back_away" if away else "project_back_own",
        grid_spec=pltpu.PrefetchScalarGridSpec(
            num_scalar_prefetch=1,
            grid=(half,),
            in_specs=[
                x_spec,
                pl.BlockSpec((1, width), lambda i, s: (0, 0)),
                pl.BlockSpec((width, 3 * width), lambda i, s: (0, 0), pipeline_mode=pl.Buffered(1)),
                pl.BlockSpec((3, tile, width), lambda i, s: (0, i + first, 0)),
                pl.BlockSpec((tile, width), lambda i, s: (i + first, 0)),
            ],
            out_specs=[out_spec, pl.BlockSpec((8, width), lambda i, s: (0, 0))],
        ),
        out_shape=[out_shape, jax.ShapeDtypeStruct((8, width), f32)],
        compiler_params=pltpu.CompilerParams(vmem_limit_bytes=48 << 20),
        cost_estimate=pl.CostEstimate(
            flops=6 * length * width * width, bytes_accessed=length * width * 16, transcendentals=0
        ),
    )(side, x, gain, w, dqkv, dmid)


def flip(x, bit):
    axis, by = ("stream", 1) if bit < 0 else ("batch", 1 << bit)
    return lax.ppermute(x, axis, [(i, i ^ by) for i in range(lax.axis_size(axis))])


class SlabSum:
    def __init__(self, pair, order):
        keep, send = pair
        bits = lax.axis_size("batch").bit_length() - 1
        self.left = [-1, *range(bits - 1, 0, -1)]
        self.order = list(order)
        self.keep = keep.reshape(*[2] * bits, *keep.shape[1:])
        self.got = flip(send.reshape(self.keep.shape), 0)

    def step(self):
        if not self.order:
            self.keep = self.keep.astype(f32) + self.got.astype(f32)
            return self.keep
        bit = self.order.pop(0)
        at = self.left.index(bit)
        self.left.remove(bit)
        halves = [
            lax.index_in_dim(self.keep, i, at, False) + lax.index_in_dim(self.got, i, at, False) for i in range(2)
        ]
        self.keep = halves[0]
        self.got = flip(halves[1], bit)
        return self.keep

    def finish(self):
        while self.keep.dtype != f32:
            self.step()
        return self.keep


def after(value, *others):
    return lax.optimization_barrier((value, *others))[0]


def all_sum(x):
    for bit in range(-1, lax.axis_size("batch").bit_length() - 1):
        x = x + flip(x, bit)
    return x


def gather_kernel(shard_ref, gain_ref, w_ref, gains_ref, local_sems, send_sems, recv_sems, *, plans):
    side, me = lax.axis_index("stream"), lax.axis_index("batch")
    bits = sorted(plans[0][2])
    barrier = pltpu.get_barrier_semaphore()
    for bit in bits:
        pl.semaphore_signal(
            barrier, inc=1, device_id=(side, jnp.bitwise_xor(me, 1 << bit)), device_id_type=pl.DeviceIdType.MESH
        )
    pl.semaphore_wait(barrier, len(bits))
    sources, targets = [shard_ref, gain_ref], [w_ref, gains_ref]
    local = [pltpu.make_async_copy(sources[n], targets[n].at[me], local_sems.at[n]) for n in range(2)]
    for copy in local:
        copy.start()

    def copies(plan, step):
        which, cols, order = plans[plan]
        held = [0]
        for bit in order[:step]:
            held += [h ^ (1 << bit) for h in held]
        done = []
        for n, h in enumerate(held):
            slab = jnp.bitwise_xor(me, h)
            at = targets[which].at[slab, :, cols]
            number = (1 << step) - 1 + n
            done.append(
                pltpu.make_async_remote_copy(
                    src_ref=sources[which].at[:, cols] if h == 0 else at,
                    dst_ref=at,
                    send_sem=send_sems.at[plan, number],
                    recv_sem=recv_sems.at[plan, number],
                    device_id=(side, jnp.bitwise_xor(me, 1 << order[step])),
                    device_id_type=pl.DeviceIdType.MESH,
                )
            )
        return done

    for step in range(len(bits)):
        for plan in range(len(plans)):
            if step:
                for copy in copies(plan, step - 1):
                    copy.wait_recv()
            for copy in copies(plan, step):
                copy.start()
    for plan in range(len(plans)):
        for copy in copies(plan, len(bits) - 1):
            copy.wait_recv()
    for plan in range(len(plans)):
        for step in range(len(bits)):
            for copy in copies(plan, step):
                copy.wait_send()
    for copy in local:
        copy.wait()


def gather(shard, gains):
    peers = lax.axis_size("batch")
    rows, columns = shard.shape
    cut = columns // 1024 * 896
    plans = (
        (0, slice(0, cut), (3, 2, 1, 0)),
        (0, slice(cut, columns), (1, 3, 2, 0)),
        (1, slice(0, gains.shape[1]), (1, 3, 2, 0)),
    )
    anywhere = pl.BlockSpec(memory_space=pl.ANY)
    return pl.pallas_call(
        functools.partial(gather_kernel, plans=plans),
        name="gather",
        in_specs=[anywhere, anywhere],
        out_specs=[anywhere, anywhere],
        out_shape=[
            jax.ShapeDtypeStruct((peers, rows, columns), bf16),
            jax.ShapeDtypeStruct((peers, *gains.shape), bf16),
        ],
        scratch_shapes=[
            pltpu.SemaphoreType.DMA((2,)),
            pltpu.SemaphoreType.DMA((len(plans), peers - 1)),
            pltpu.SemaphoreType.DMA((len(plans), peers - 1)),
        ],
        compiler_params=pltpu.CompilerParams(collective_id=0, has_side_effects=True),
        cost_estimate=pl.CostEstimate(flops=0, bytes_accessed=8 * peers * rows * columns, transcendentals=0),
    )(shard, gains)


def shards(tokens, cotangent, lengths, ln1_gain, w_qkv, w_out, ln2_gain, w_up, w_down):
    side = lax.axis_index("stream")
    at = lax.axis_index("batch")
    _, rows_dev, length, width = tokens.shape
    assert rows_dev == 2
    ff = w_up.shape[1]
    peers = lax.axis_size("batch")
    small = peers == 16 and width % (16 * peers) == 0
    side_array = side.reshape(1).astype(jnp.int32)
    index = side * peers + at
    me = jnp.stack([index if small else 0 * index, side]).astype(jnp.int32)
    share = width // (2 * peers)

    x_away = flip(lax.dynamic_index_in_dim(tokens[0], 1 - side, 0, False), -1)
    g_away = flip(lax.dynamic_index_in_dim(cotangent[0], 1 - side, 0, False), -1)
    if small:
        rows = width // peers
        gains = jnp.zeros((16, LANES), bf16)
        gains = gains.at[0, :rows].set(ln1_gain).at[1, :rows].set(ln2_gain)
        w_qkv_all, gains = gather(w_qkv, gains)
        w_qkv_all = w_qkv_all.reshape(width, 3 * width)
        gain_one, gain_two = (gains[:, n, :rows].reshape(1, width) for n in range(2))
        down = w_down.reshape(-1, rows, width).swapaxes(0, 1).reshape(rows, ff)
        rest = lax.all_gather(jnp.concatenate([w_out, w_up, down], axis=1), "batch", axis=0, tiled=True)
        rest = rest.reshape(peers, rows, -1)
    else:
        def whole(x):
            return lax.all_gather(x, "batch", axis=0, tiled=True)

        w_qkv_all = whole(w_qkv)
        gain_one, gain_two = whole(ln1_gain)[None], whole(ln2_gain)[None]
        down = whole(w_down).reshape(16, -1, width // 16, width).swapaxes(1, 2).reshape(width, ff)
        rest = jnp.concatenate([whole(w_out), whole(w_up), down], axis=1).reshape(16, width // 16, -1)

    cosine, sine = rotary_tables(length)
    tables = mask_tables(length, jnp.take(lengths, side))
    qkv, hidden = project(side_array, tokens, x_away, gain_one, w_qkv_all, cosine, sine)
    qkv4 = qkv.reshape(3, 2, length, width)
    mixed, logs = attend(side_array, qkv4, tables)
    mixed2 = mixed.reshape(2 * length, width)
    out, out_away, act, du, h2, dmid, dbr, dmix, dgain_two = feed(
        side_array, tokens, x_away, mixed2, cotangent, g_away, gain_two, rest
    )

    def place(result, away):
        away = flip(away, -1).astype(result.dtype)
        return lax.dynamic_update_slice(result, away[None, None], (0, 1 - side, 0, 0))

    out = place(out, out_away)
    cols_share = share if small else width // 32
    down = weight_grad_rows(me, act, cotangent, g_away, width, ff // width * cols_share, "grad_down")
    down = weight_grad_rows(me, act, cotangent, g_away, width, ff // width * cols_share, "grad_down")
    if small:
        down = SlabSum(down, (-1, 1, 2, 3))
        h2 = after(h2, down.keep)
    up = weight_grad_columns(me, h2, du[None], 0, width, cols_share, "grad_up")
    if small:
        up = SlabSum(up, (1, -1, 2, 3))
        dbr = after(dbr, up.keep, down.step())
    wo = weight_grad_columns(me, mixed2, dbr[None], 0, width, cols_share, "grad_out")
    dgain_two = all_sum(jnp.sum(dgain_two, axis=0, keepdims=True))
    dqkv = None
    dmix = dmix.reshape(2, length, width)
    if small:
        wo = SlabSum(wo, (2, -1, 1, 3))
        dmix = after(dmix, wo.keep, up.step())
    plan = {1: "wo", 2: "down up wo", 3: "down up wo", 4: "down up wo", 5: "down up wo"}
    for first in range(width // LANES):
        if small and first in plan:
            sums = {"down": down, "up": up, "wo": wo}
            dmix = after(dmix, *[sums[n].step() for n in plan[first].split()])
        dqkv = attend_back(side_array, dqkv, first, 1, qkv4, mixed, dmix, logs, tables, cosine, sine)
    dqkv3 = dqkv.reshape(3, 2 * length, width)
    dx_away, dgain_away = project_back(side_array, x_away, gain_one, w_qkv_all, dqkv3, dmid, True)
    later = after(dqkv3, dx_away)
    parts = []
    for n in range(3):
        pair = weight_grad_columns(me, hidden, later, n, width, cols_share, "grad_qkv")
        parts.append(SlabSum(pair, ((1, 2, -1, 3), (2, 1, -1, 3), (2, -1, 1, 3))[n]) if small else pair)
        later = after(later, parts[-1].keep if small else pair[0])
    dx, dgain_own = project_back(side_array, tokens, gain_one, w_qkv_all, later, dmid, False)
    dgain_one = all_sum(jnp.sum(dgain_own + dgain_away, axis=0, keepdims=True))
    dx = place(dx, dx_away)
    if small:
        wq = jnp.concatenate([part.finish() for part in parts], axis=1)
        down, up, wo = down.finish(), up.finish(), wo.finish()
    else:

        def scatter(pair):
            slots = jnp.stack(pair, axis=1)
            rows = slots.reshape(-1, slots.shape[-1])
            return lax.psum_scatter(rows, ("stream", "batch"), scatter_dimension=0, tiled=True).astype(f32)

        down, up, wo, *parts = (scatter(pair) for pair in (down, up, wo, *parts))
        wq = jnp.concatenate(parts, axis=1)
    begin = index * share
    dgain_one, dgain_two = (lax.dynamic_slice(g[0], (begin,), (share,)) for g in (dgain_one, dgain_two))
    return out, dx, dgain_one, wq, wo, dgain_two, up, down


def solution(mesh):
    token = P("stream", "batch", None, None)
    vector, matrix = P("batch"), P("batch", None)
    out_vector, out_matrix = P(("stream", "batch")), P(("stream", "batch"), None)
    return jax.shard_map(
        shards,
        mesh=mesh,
        in_specs=(token, token, vector, vector, matrix, matrix, vector, matrix, matrix),
        out_specs=(token, token, out_vector, out_matrix, out_matrix, out_vector, out_matrix, out_matrix),
        check_vma=False,
    )
```

```python
import functools
import math

import jax
import jax.numpy as jnp
from jax import lax
from jax.experimental import pallas as pl
from jax.experimental.pallas import tpu as pltpu
from jax.sharding import PartitionSpec as P

HD = 64
BLOCK = 16
LANES = 128
TILE = 256
BIG = -1e30
f32, bf16 = jnp.float32, jnp.bfloat16


def mm(a, b):
    return lax.dot_general(a, b, (((1,), (0,)), ((), ())), preferred_element_type=f32)


def mm_t(a, b):
    return lax.dot_general(a, b, (((1,), (1,)), ((), ())), preferred_element_type=f32)


def t_mm(a, b):
    return lax.dot_general(a, b, (((0,), (0,)), ((), ())), preferred_element_type=f32)


def rotary_tables(length):
    half = HD // 2
    places = jnp.arange(length).astype(f32)
    rates = jnp.exp(jnp.arange(half).astype(f32) * (-2.0 * math.log(10000.0) / HD))
    angles = places[:, None] * rates[None, :]
    cosine, sine = jnp.cos(angles), jnp.sin(angles)
    return (
        jnp.concatenate([cosine] * 4, axis=1),
        jnp.concatenate([-sine, sine, -sine, sine], axis=1),
    )


def half_partner(x):
    lane = lax.broadcasted_iota(jnp.int32, x.shape, 1)
    low = lax.rem(lane, HD) < HD // 2
    return jnp.where(low, pltpu.roll(x, LANES - HD // 2, 1), pltpu.roll(x, HD // 2, 1))


def row_specs(tile, width, half):
    own = pl.BlockSpec((None, None, tile, width), lambda i, s: (0, s[0], jnp.minimum(i, half - 1), 0))
    away = pl.BlockSpec((tile, width), lambda i, s: (jnp.maximum(i - half, 0), 0))
    return own, away


def read_rows(own_ref, away_ref, half):
    return jnp.where(pl.program_id(0) < half, own_ref[...], away_ref[...])


def project_kernel(side_ref, own_ref, away_ref, gain_ref, w_ref, cos_ref, sin_ref, out_ref, hidden_ref, *, half):
    x = read_rows(own_ref, away_ref, half).astype(f32)
    width = x.shape[1]
    center = x - jnp.mean(x, axis=1, keepdims=True)
    spread = jnp.mean(center * center, axis=1, keepdims=True)
    hidden = (center * lax.rsqrt(spread + 1e-5) * gain_ref[...].astype(f32)).astype(bf16)
    hidden_ref[...] = hidden
    cosine, sine = cos_ref[...], sin_ref[...]
    for part in range(3):
        rows = mm(hidden, w_ref[:, part * width : (part + 1) * width])
        for pair in range(width // LANES):
            cols = slice(pair * LANES, (pair + 1) * LANES)
            field = rows[:, cols]
            if part < 2:
                field = field * cosine + half_partner(field) * sine
            if part == 0:
                field = field * 0.125
            out_ref[part, :, cols] = field.astype(bf16)


def project(side, own, away, gain, w, cosine, sine, tile=512):
    length, width = away.shape
    tokens, half = 2 * length, length // tile
    table = pl.BlockSpec((tile, LANES), lambda i, s: (lax.rem(i, half), 0))
    return pl.pallas_call(
        functools.partial(project_kernel, half=half),
        name="project",
        grid_spec=pltpu.PrefetchScalarGridSpec(
            num_scalar_prefetch=1,
            grid=(2 * half,),
            in_specs=[
                *row_specs(tile, width, half),
                pl.BlockSpec((1, width), lambda i, s: (0, 0)),
                pl.BlockSpec((width, 3 * width), lambda i, s: (0, 0), pipeline_mode=pl.Buffered(1)),
                table,
                table,
            ],
            out_specs=[
                pl.BlockSpec((3, tile, width), lambda i, s: (0, i, 0)),
                pl.BlockSpec((tile, width), lambda i, s: (i, 0)),
            ],
        ),
        out_shape=[jax.ShapeDtypeStruct((3, tokens, width), bf16), jax.ShapeDtypeStruct((tokens, width), bf16)],
        compiler_params=pltpu.CompilerParams(vmem_limit_bytes=48 << 20),
        cost_estimate=pl.CostEstimate(
            flops=6 * tokens * width * width, bytes_accessed=tokens * width * 10 + 6 * width * width, transcendentals=0
        ),
    )(side, own, away, gain, w, cosine, sine)


def mask_tables(length, row_length):
    pos = jnp.arange(length)
    blk = (pos // BLOCK)[:, None]
    lane = (jnp.arange(LANES) % HD)[None, :]
    dead = (pos >= row_length)[:, None]
    clean_query = (lane == blk).astype(bf16)
    noisy_query = (lane == blk - 1).astype(bf16)
    main_key = jnp.where((blk > lane) | dead, BIG, 0.0).astype(bf16)
    diag_key = jnp.where((blk != lane) | dead, BIG, 0.0).astype(bf16)
    return clean_query, noisy_query, main_key, diag_key


def low_lanes(shape):
    return lax.broadcasted_iota(jnp.int32, shape, 1) < HD


def attend_kernel(side_ref, qkv_ref, cq_ref, nq_ref, mk_ref, dk_ref, out_ref, log_ref,
                  qa, ka, kd, va, s_scr):
    length = out_ref.shape[1]
    clean = side_ref[0]
    noisy = 1 - clean
    tiles = length // TILE
    low = low_lanes((length, LANES))
    ones = jnp.ones((16, length), bf16)
    vc_t = qkv_ref[2, clean].T
    vn_t = qkv_ref[2, noisy].T
    for head in range(2):
        pick = low if head == 0 else jnp.logical_not(low)
        qa[0, head] = jnp.where(pick, qkv_ref[0, clean], cq_ref[...])
        qa[1, head] = jnp.where(pick, qkv_ref[0, noisy], nq_ref[...])
        qa[2, head] = jnp.where(pick, qkv_ref[0, noisy], cq_ref[...])
        ka[head] = jnp.where(pick, qkv_ref[1, clean], mk_ref[...])
        kd[head] = jnp.where(pick, qkv_ref[1, noisy], dk_ref[...])
        va[0, head, :HD] = vc_t[head * HD : (head + 1) * HD]
        va[1, head, :HD] = vn_t[head * HD : (head + 1) * HD]
        va[0, head, HD:] = ones
        va[1, head, HD:] = ones
    for copy in range(2):
        where_to = clean if copy == 0 else noisy
        for tile in range(tiles):
            rows = slice(tile * TILE, (tile + 1) * TILE)
            parts = []
            for head in range(2):
                pieces = [(qa[copy, head, rows, :], ka, 0, t) for t in range(tile + 1)]
                if copy == 1:
                    pieces.append((qa[2, head, rows, :], kd, 1, tile))
                top = None
                for n, (query, keys, vi, t) in enumerate(pieces):
                    s = mm_t(keys[head, t * TILE : (t + 1) * TILE, :], query)
                    if copy == 1 and tile == 0 and n == 0:
                        first = lax.broadcasted_iota(jnp.int32, s.shape, 1) < BLOCK
                        s = jnp.where(first, BIG, s)
                    s_scr[head, n * TILE : (n + 1) * TILE, :] = s
                    m = jnp.max(s, axis=0, keepdims=True)
                    top = m if top is None else jnp.maximum(top, m)
                acc = None
                for n, (query, keys, vi, t) in enumerate(pieces):
                    p = jnp.exp(s_scr[head, n * TILE : (n + 1) * TILE, :] - top).astype(bf16)
                    o = mm(va[vi, head, :, t * TILE : (t + 1) * TILE], p)
                    acc = o if acc is None else acc + o
                total = acc[HD : HD + 1, :]
                parts.append(acc[:HD] / total)
                log_ref[where_to, 0, head : head + 1, rows] = top + jnp.log(total)
            out_ref[where_to, rows, :] = jnp.concatenate(parts, axis=0).T.astype(bf16)


def attend(side, qkv, tables):
    _, copies, length, width = qkv.shape
    pairs = width // LANES
    table_spec = pl.BlockSpec((length, LANES), lambda i, s: (0, 0))
    return pl.pallas_call(
        attend_kernel,
        name="attend",
        grid_spec=pltpu.PrefetchScalarGridSpec(
            num_scalar_prefetch=1,
            grid=(pairs,),
            in_specs=[pl.BlockSpec((3, copies, length, LANES), lambda i, s: (0, 0, 0, i))] + [table_spec] * 4,
            out_specs=[
                pl.BlockSpec((copies, length, LANES), lambda i, s: (0, 0, i)),
                pl.BlockSpec((copies, 1, 2, length), lambda i, s: (0, i, 0, 0)),
            ],
            scratch_shapes=[
                pltpu.VMEM((3, 2, length, LANES), bf16),
                pltpu.VMEM((2, length, LANES), bf16),
                pltpu.VMEM((2, length, LANES), bf16),
                pltpu.VMEM((2, 2, HD + 16, length), bf16),
                pltpu.VMEM((2, length + TILE, TILE), f32),
            ],
        ),
        out_shape=[
            jax.ShapeDtypeStruct((copies, length, width), bf16),
            jax.ShapeDtypeStruct((copies, pairs, 2, length), f32),
        ],
        compiler_params=pltpu.CompilerParams(vmem_limit_bytes=48 << 20),
        cost_estimate=pl.CostEstimate(
            flops=8 * length * length * width, bytes_accessed=16 * length * width, transcendentals=length * length * 12
        ),
    )(side, qkv, *tables)


MESH = pl.DeviceIdType.MESH


def partner(bit):
    side, at = lax.axis_index("stream"), lax.axis_index("batch")
    return (1 - side, at) if bit < 0 else (side, jnp.bitwise_xor(at, 1 << bit))


def greet(bits):
    barrier = pltpu.get_barrier_semaphore()
    for bit in bits:
        pl.semaphore_signal(barrier, inc=1, device_id=partner(bit), device_id_type=MESH)
    pl.semaphore_wait(barrier, len(bits))


class SlabSum:
    def __init__(self, order, keep, send, got, sems, load=None):
        self.order, self.keep, self.send, self.got, self.sems, self.load = (0, *order), keep, send, got, sems, load

    @staticmethod
    def scratch(slots, share, columns):
        steps = slots.bit_length()
        return [
            *[pltpu.VMEM((max(slots >> n, 1), share, columns), bf16) for n in (0, *range(steps))],
            pltpu.SemaphoreType.DMA((2 * steps + 1,)),
        ]

    def copy(self, step):
        count = self.got[step].shape[0]
        return pltpu.make_async_remote_copy(
            src_ref=self.send if step == 0 else self.keep.at[pl.ds(count, count)],
            dst_ref=self.got[step],
            send_sem=self.sems.at[2 * step],
            recv_sem=self.sems.at[2 * step + 1],
            device_id=partner(self.order[step]),
            device_id_type=MESH,
        )

    def loading(self):
        return pltpu.make_async_copy(self.load, self.keep, self.sems.at[2 * len(self.order)])

    def start(self):
        self.copy(0).start()
        if self.load is not None:
            self.loading().start()

    def step(self, step):
        if step == 1 and self.load is not None:
            self.loading().wait()
        self.copy(step - 1).wait_recv()
        got = self.got[step - 1]

        @pl.loop(0, got.shape[0])
        def _(n):
            self.keep[n] = (self.keep[n].astype(f32) + got[n].astype(f32)).astype(bf16)

        self.copy(step).start()

    def finish(self, out_ref, columns=slice(None)):
        last = len(self.order) - 1
        self.copy(last).wait_recv()
        out_ref[:, columns] = self.keep[0].astype(f32) + self.got[last][0].astype(f32)
        for step in range(len(self.order)):
            self.copy(step).wait_send()


class GainSum:
    bits = (-1, 0, 1, 2, 3)

    def __init__(self, held, got, sems):
        self.held, self.got, self.sems = held, got, sems

    @staticmethod
    def scratch(width):
        steps = len(GainSum.bits)
        return [
            pltpu.VMEM((steps, 8, width), f32),
            pltpu.VMEM((steps, 8, width), f32),
            pltpu.SemaphoreType.DMA((2 * steps,)),
        ]

    def copy(self, step):
        return pltpu.make_async_remote_copy(
            src_ref=self.held.at[step],
            dst_ref=self.got.at[step],
            send_sem=self.sems.at[2 * step],
            recv_sem=self.sems.at[2 * step + 1],
            device_id=partner(self.bits[step]),
            device_id_type=MESH,
        )

    def start(self, value):
        self.held[0] = value
        self.copy(0).start()

    def step(self, step):
        self.copy(step - 1).wait_recv()
        self.held[step] = self.held[step - 1] + self.got[step - 1]
        self.copy(step).start()

    def finish(self, out_ref):
        last = len(self.bits) - 1
        self.copy(last).wait_recv()
        out_ref[...] = self.held[last] + self.got[last]
        for step in range(len(self.bits)):
            self.copy(step).wait_send()


DOWN, UP, OUT = (-1, 1, 2, 3), (1, -1, 2, 3), (2, -1, 1, 3)
QKV = ((1, 2, 3, -1), (2, 1, 3, -1), (2, 3, 1, -1))


def attend_back_sum_kernel(*refs, orders):
    count = len(orders)
    core, refs = refs[:10], refs[10:]
    pairs, gain_ref, refs = refs[: 2 * count], refs[2 * count], refs[2 * count + 1 :]
    dqkv_ref, refs = refs[0], refs[1:]
    outs, gain_out, refs = refs[:count], refs[count], refs[count + 1 :]
    own, refs = refs[:10], refs[10:]
    per = len(refs[:-3]) // count
    sums = []
    for n, order in enumerate(orders):
        keep, *got, sems = refs[n * per : (n + 1) * per]
        sums.append(SlabSum(order, keep, pairs[2 * n + 1], got, sems, load=pairs[2 * n]))
    gain = GainSum(*refs[-3:])
    down, up, wo = sums
    step = pl.program_id(0)

    @pl.when(step == 0)
    def _():
        greet(GainSum.bits)
        for one in sums:
            one.start()
        gain.start(gain_ref[...])

    for at, plan in {
        1: ((down, 1), (up, 1), (wo, 1), (gain, 1)),
        2: ((wo, 2), (gain, 2)),
        3: ((down, 2), (up, 2), (wo, 3), (gain, 3)),
        4: ((down, 3), (up, 3), (wo, 4), (gain, 4)),
        5: ((down, 4), (up, 4)),
    }.items():

        @pl.when(step == at)
        def _():
            for one, number in plan:
                one.step(number)

    attend_back_kernel(*core, dqkv_ref, *own)

    @pl.when(step == pl.num_programs(0) - 1)
    def _():
        for one, out_ref in zip(sums, outs):
            one.finish(out_ref)
        gain.finish(gain_out)


def attend_back_kernel(qkv_ref, o_ref, do_ref, log_ref, cq_ref, nq_ref, mk_ref, dk_ref, cos_ref, sin_ref,
                       dqkv_ref, qa, qz, ka, kd, kt, doz, dsum, dq, dkc, dvc):
    length = o_ref.shape[1]
    clean = lax.axis_index("stream")
    noisy = 1 - clean
    tiles = length // TILE
    low = low_lanes((length, LANES))
    zero = jnp.zeros((length, LANES), bf16)
    for copy in range(2):
        at = clean if copy == 0 else noisy
        kt[copy] = qkv_ref[1, at].T
        prod = (o_ref[at].astype(f32) * do_ref[at].astype(f32)).T
        dsum[copy, 0:1] = jnp.sum(prod[:HD], axis=0, keepdims=True)
        dsum[copy, 1:2] = jnp.sum(prod[HD:], axis=0, keepdims=True)
        for head in range(2):
            pick = low if head == 0 else jnp.logical_not(low)
            qa[copy, head] = jnp.where(pick, qkv_ref[0, at], (cq_ref, nq_ref)[copy][...])
            qz[copy, head] = jnp.where(pick, qkv_ref[0, at], zero)
            doz[copy, head] = jnp.where(pick, do_ref[at], zero)
            if copy == 0:
                ka[head] = jnp.where(pick, qkv_ref[1, at], mk_ref[...])
            else:
                qa[2, head] = jnp.where(pick, qkv_ref[0, at], cq_ref[...])
                kd[head] = jnp.where(pick, qkv_ref[1, at], dk_ref[...])
    cosine, sine = cos_ref[...], sin_ref[...]

    def piece(copy, tile, query, keys, kv_copy, t, mask_first):
        rows = slice(tile * TILE, (tile + 1) * TILE)
        krows = slice(t * TILE, (t + 1) * TILE)
        kv_at = clean if kv_copy == 0 else noisy
        at = clean if copy == 0 else noisy
        probs, raws = [], []
        for head in range(2):
            s = mm_t(keys[head, krows, :], qa[query, head, rows, :])
            p = jnp.exp(s - log_ref[at, 0, head : head + 1, rows])
            if mask_first:
                first = lax.broadcasted_iota(jnp.int32, s.shape, 1) < BLOCK
                p = jnp.where(first, 0.0, p)
            dp = mm_t(qkv_ref[2, kv_at, krows, :], doz[copy, head, rows, :])
            raw = (p * (dp - dsum[copy, head : head + 1, rows])).astype(bf16)
            p = p.astype(bf16)
            dq[copy, head * HD : (head + 1) * HD, rows] += mm(kt[kv_copy, head * HD : (head + 1) * HD, krows], raw)
            probs.append(p)
            raws.append(raw)
        p2 = jnp.concatenate(probs, axis=1)
        r2 = jnp.concatenate(raws, axis=1)
        do2 = jnp.concatenate([doz[copy, 0, rows, :], doz[copy, 1, rows, :]], axis=0)
        q2 = jnp.concatenate([qz[copy, 0, rows, :], qz[copy, 1, rows, :]], axis=0)
        return mm(p2, do2), mm(r2, q2)

    def finish(field, rotate, scale):
        if rotate:
            c, s = cosine, sine
            field = field * c - half_partner(field) * s
        return (field * scale if scale != 1.0 else field).astype(bf16)

    dq[...] = jnp.zeros_like(dq)
    for t in range(tiles):
        krows = slice(t * TILE, (t + 1) * TILE)
        dv_t, dk_t = piece(1, t, 2, kd, 1, t, False)
        dqkv_ref[2, noisy, krows, :] = dv_t.astype(bf16)
        dkc[krows, :] = dk_t
    dqkv_ref[1, noisy] = finish(dkc[...], True, 1.0)
    for t in range(tiles):
        krows = slice(t * TILE, (t + 1) * TILE)
        dv_acc = dk_acc = None
        for tile in range(t, tiles):
            for copy in range(2):
                dv_t, dk_t = piece(copy, tile, copy, ka, 0, t, copy == 1 and tile == 0)
                dv_acc = dv_t if dv_acc is None else dv_acc + dv_t
                dk_acc = dk_t if dk_acc is None else dk_acc + dk_t
        dqkv_ref[2, clean, krows, :] = dv_acc.astype(bf16)
        dkc[krows, :] = dk_acc
    dqkv_ref[1, clean] = finish(dkc[...], True, 1.0)
    dqkv_ref[0, clean] = finish(dq[0].T, True, 0.125)
    dqkv_ref[0, noisy] = finish(dq[1].T, True, 0.125)


def attend_back(qkv, mixed, grad, logs, tables, cosine, sine, pairs=None, gain=None):
    _, copies, length, width = qkv.shape
    steps = width // LANES
    table_spec = pl.BlockSpec((length, LANES), lambda i: (0, 0), pipeline_mode=pl.Buffered(1))
    row_spec = pl.BlockSpec((copies, length, LANES), lambda i: (0, 0, i))
    three = pl.BlockSpec((3, copies, length, LANES), lambda i: (0, 0, 0, i))
    anywhere = pl.BlockSpec(memory_space=pl.ANY)

    def fixed(shape):
        return pl.BlockSpec(shape, lambda i: (0, 0), pipeline_mode=pl.Buffered(1))

    more_in, more_specs, more_shapes, more_out, more_scratch = [], [], [], [], []
    body, params = attend_back_kernel, {}
    if pairs is not None:
        assert steps == 6
        body = functools.partial(attend_back_sum_kernel, orders=(DOWN, UP, OUT))
        params = dict(collective_id=1, has_side_effects=True)
        for keep, send in pairs:
            slots, share, columns = keep.shape
            more_in += [keep, send]
            more_specs += [anywhere] * 2
            more_shapes.append(jax.ShapeDtypeStruct((share, columns), f32))
            more_out.append(fixed((share, columns)))
            more_scratch += SlabSum.scratch(slots, share, columns)
        more_in.append(gain)
        more_specs.append(fixed((8, width)))
        more_shapes.append(jax.ShapeDtypeStruct((8, width), f32))
        more_out.append(fixed((8, width)))
        more_scratch += GainSum.scratch(width)
    return pl.pallas_call(
        body,
        name="attend_back",
        grid_spec=pltpu.PrefetchScalarGridSpec(
            num_scalar_prefetch=0,
            grid=(steps,),
            in_specs=[three, row_spec, row_spec, pl.BlockSpec((copies, 1, 2, length), lambda i: (0, i, 0, 0))]
            + [table_spec] * 6
            + more_specs,
            out_specs=[three, *more_out],
            scratch_shapes=[
                pltpu.VMEM((3, 2, length, LANES), bf16),
                pltpu.VMEM((2, 2, length, LANES), bf16),
                pltpu.VMEM((2, length, LANES), bf16),
                pltpu.VMEM((2, length, LANES), bf16),
                pltpu.VMEM((2, LANES, length), bf16),
                pltpu.VMEM((2, 2, length, LANES), bf16),
                pltpu.VMEM((2, 2, length), f32),
                pltpu.VMEM((2, LANES, length), f32),
                pltpu.VMEM((length, LANES), f32),
                pltpu.VMEM((length, LANES), f32),
                *more_scratch,
            ],
        ),
        out_shape=[jax.ShapeDtypeStruct((3, copies, length, width), bf16), *more_shapes],
        compiler_params=pltpu.CompilerParams(vmem_limit_bytes=60 << 20, **params),
        cost_estimate=pl.CostEstimate(
            flops=20 * length * length * width, bytes_accessed=30 * length * width, transcendentals=length * length * 12
        ),
    )(qkv, mixed, grad, logs, *tables, cosine, sine, *more_in)


ROOT = math.sqrt(2.0 / math.pi)


def feed_kernel(side_ref, x_own, x_away, mixed_ref, g_own, g_away, gain_ref, rest_ref,
                out_own, out_away, act_ref, du_ref, h2_ref, dmid_ref, dbr_ref, dmix_ref, dgain_ref,
                wo_ref, wu_ref, wd_ref, sems, *, half):
    groups, rows, width = wo_ref.shape
    fold = wd_ref.shape[1]
    ff = fold * width

    def fetch(n):
        cols = rest_ref.at[:, :, n * width : (n + 1) * width]
        if n == 0:
            into = wo_ref
        elif n <= fold:
            into = wu_ref.at[n - 1]
        else:
            into = wd_ref.at[:, n - 1 - fold]
        return pltpu.make_async_copy(cols, into, sems.at[n])

    @pl.when(pl.program_id(0) == 0)
    def _():
        for n in range(1 + 2 * fold):
            fetch(n).start()
        for n in range(1 + 2 * fold):
            fetch(n).wait()

    def down(c):
        per = groups // fold
        return wd_ref[c * per : (c + 1) * per].reshape(width, width)

    wo = wo_ref[...].reshape(width, width)
    gain = gain_ref[...].astype(f32)
    middle = read_rows(x_own, x_away, half).astype(f32) + mm(mixed_ref[...], wo)
    center = middle - jnp.mean(middle, axis=1, keepdims=True)
    spread = jnp.mean(center * center, axis=1, keepdims=True)
    inv = lax.rsqrt(spread + 1e-5)
    norm = center * inv
    hidden = (norm * gain).astype(bf16)
    h2_ref[...] = hidden
    grad = read_rows(g_own, g_away, half)
    out = middle
    dh = jnp.zeros_like(middle)
    for c in range(fold):
        cols = slice(c * width, (c + 1) * width)
        up = wu_ref[c].reshape(width, width)
        u = mm(hidden, up)
        da = mm_t(grad, down(c)).astype(bf16).astype(f32)
        sq = u * u
        t = jnp.tanh(u * (ROOT + (ROOT * 0.044715) * sq))
        part = 0.5 + 0.5 * t
        act = (u * part).astype(bf16)
        slope = part + (u * (part * (1.0 - t))) * (ROOT + (3 * ROOT * 0.044715) * sq)
        du = (da * slope).astype(bf16)
        act_ref[:, cols] = act
        du_ref[:, cols] = du
        out = out + mm(act, down(c))
        dh = dh + mm_t(du, up)
    low = out.astype(bf16)

    @pl.when(pl.program_id(0) < half)
    def _():
        out_own[...] = low

    @pl.when(pl.program_id(0) >= half)
    def _():
        out_away[...] = low

    @pl.when(pl.program_id(0) == 0)
    def _():
        dgain_ref[...] = jnp.zeros_like(dgain_ref)

    dgain_ref[...] += jnp.sum((dh * norm).reshape(-1, 8, width), axis=0)
    e = dh * gain
    dmid = grad.astype(f32) + inv * (
        e - jnp.mean(e, axis=1, keepdims=True) - norm * jnp.mean(e * norm, axis=1, keepdims=True)
    )
    dmid_ref[...] = dmid
    dbr = dmid.astype(bf16)
    dbr_ref[...] = dbr
    dmix_ref[...] = mm_t(dbr, wo).astype(bf16)


def feed(side, x_own, x_away, mixed, g_own, g_away, gain, rest, tile=512):
    tokens, width = mixed.shape
    groups, rows, columns = rest.shape
    fold = (columns // width - 1) // 2
    ff = fold * width
    half = tokens // 2 // tile
    row = pl.BlockSpec((tile, width), lambda i, s: (i, 0))
    wide = pl.BlockSpec((tile, ff), lambda i, s: (i, 0))
    own, away = row_specs(tile, width, half)

    def keep(shape):
        return pl.BlockSpec(shape, lambda i, s: (0, 0), pipeline_mode=pl.Buffered(1))

    return pl.pallas_call(
        functools.partial(feed_kernel, half=half),
        name="feed",
        grid_spec=pltpu.PrefetchScalarGridSpec(
            num_scalar_prefetch=1,
            grid=(2 * half,),
            in_specs=[own, away, row, own, away, keep((1, width)), pl.BlockSpec(memory_space=pl.ANY)],
            out_specs=[own, away, wide, wide, row, row, row, row, pl.BlockSpec((8, width), lambda i, s: (0, 0))],
            scratch_shapes=[
                pltpu.VMEM((groups, rows, width), bf16),
                pltpu.VMEM((fold, groups, rows, width), bf16),
                pltpu.VMEM((groups, fold, rows, width), bf16),
                pltpu.SemaphoreType.DMA((1 + 2 * fold,)),
            ],
        ),
        out_shape=[
            jax.ShapeDtypeStruct((1, 2, tokens // 2, width), bf16),
            jax.ShapeDtypeStruct((tokens // 2, width), bf16),
            jax.ShapeDtypeStruct((tokens, ff), bf16),
            jax.ShapeDtypeStruct((tokens, ff), bf16),
            jax.ShapeDtypeStruct((tokens, width), bf16),
            jax.ShapeDtypeStruct((tokens, width), f32),
            jax.ShapeDtypeStruct((tokens, width), bf16),
            jax.ShapeDtypeStruct((tokens, width), bf16),
            jax.ShapeDtypeStruct((8, width), f32),
        ],
        compiler_params=pltpu.CompilerParams(vmem_limit_bytes=60 << 20),
        cost_estimate=pl.CostEstimate(
            flops=tokens * width * (4 * width + 8 * ff), bytes_accessed=tokens * (width * 18 + ff * 4),
            transcendentals=tokens * ff
        ),
    )(side, x_own, x_away, mixed, g_own, g_away, gain, rest)


def arranged(slot, order):
    return sum((slot >> bit & 1) << (len(order) - 1 - n) for n, bit in enumerate(order))


def weight_kernel(me_ref, left_ref, *refs, share, split, order):
    weight_slabs(me_ref[0], left_ref, *refs, share=share, split=split, order=order)


def weight_slabs(me, left_ref, *refs, share, split, order):
    right_refs, (keep_ref, send_ref, scr) = refs[:-3], refs[-3:]
    if split:
        own_ref, away_ref = right_refs
        half = own_ref.shape[0]
        total = t_mm(left_ref[:half], own_ref[...]) + t_mm(left_ref[half:], away_ref[...])
    else:
        total = t_mm(left_ref[...], right_refs[0][...])
    slabs = total.shape[0] // share
    scr[...] = total.reshape(scr.shape)
    low_me = lax.rem(me, slabs)
    for slot in range(slabs):
        source = jnp.bitwise_xor(low_me, slot)
        into = send_ref if slot % 2 else keep_ref
        into[arranged(slot // 2, order)] = scr[source].astype(bf16)


def weight_grad_columns(me, left, right, block, share, order, name):
    tokens, dl = left.shape
    dr = right.shape[1]
    peers = dl // share
    shape = (peers // 2, share, dr)
    out = pl.BlockSpec((peers // 2, share, block), lambda j, m: (0, 0, j))
    return pl.pallas_call(
        functools.partial(weight_kernel, share=share, split=False, order=order),
        name=name,
        grid_spec=pltpu.PrefetchScalarGridSpec(
            num_scalar_prefetch=1,
            grid=(dr // block,),
            in_specs=[
                pl.BlockSpec((tokens, dl), lambda j, m: (0, 0), pipeline_mode=pl.Buffered(1)),
                pl.BlockSpec((tokens, block), lambda j, m: (0, j)),
            ],
            out_specs=[out, out],
            scratch_shapes=[pltpu.VMEM((peers, share, block), f32)],
        ),
        out_shape=[jax.ShapeDtypeStruct(shape, bf16)] * 2,
        compiler_params=pltpu.CompilerParams(vmem_limit_bytes=48 << 20),
        cost_estimate=pl.CostEstimate(
            flops=2 * tokens * dl * dr, bytes_accessed=2 * tokens * (dl + dr) + 2 * dl * dr, transcendentals=0
        ),
    )(me, left, right)


def weight_grad_rows(me, left, own, away, block, share, name):
    tokens, dl = left.shape
    length, dr = away.shape
    slabs = block // share
    steps = dl // block
    assert steps == 4
    shape = (2, slabs // 2, 2, share, dr)
    out = pl.BlockSpec((None, slabs // 2, None, share, dr), lambda j, m: (lax.div(j, 2), 0, lax.rem(j, 2), 0, 0))
    bits = (slabs // 2).bit_length() - 1

    def place(j, m):
        return (0, jnp.bitwise_xor(j, lax.div(m[0], slabs)))

    return pl.pallas_call(
        functools.partial(weight_kernel, share=share, split=True, order=tuple(range(bits))),
        name=name,
        grid_spec=pltpu.PrefetchScalarGridSpec(
            num_scalar_prefetch=1,
            grid=(steps,),
            in_specs=[
                pl.BlockSpec((tokens, block), place),
                pl.BlockSpec((None, None, length, dr), lambda j, m: (0, m[1], 0, 0), pipeline_mode=pl.Buffered(1)),
                pl.BlockSpec((length, dr), lambda j, m: (0, 0), pipeline_mode=pl.Buffered(1)),
            ],
            out_specs=[out, out],
            scratch_shapes=[pltpu.VMEM((slabs, share, dr), f32)],
        ),
        out_shape=[jax.ShapeDtypeStruct(shape, bf16)] * 2,
        compiler_params=pltpu.CompilerParams(vmem_limit_bytes=48 << 20),
        cost_estimate=pl.CostEstimate(
            flops=2 * tokens * dl * dr, bytes_accessed=2 * tokens * (dl + dr) + 2 * dl * dr, transcendentals=0
        ),
    )(me, left, own, away)


def qkv_grad_kernel(hidden_ref, dqkv_ref, gain_ref, out_ref, gain_out, scr, *refs, share):
    count = len(QKV)
    width = scr.shape[-1]
    per = len(refs[:-3]) // count
    sums = []
    for n, order in enumerate(QKV):
        send, keep, *got, sems = refs[n * per : (n + 1) * per]
        sums.append(SlabSum(order, keep, send, got, sems))
    gain = GainSum(*refs[-3:])
    me = lax.axis_index("stream") * lax.axis_size("batch") + lax.axis_index("batch")
    step = pl.program_id(0)

    @pl.when(step == 0)
    def _():
        greet(GainSum.bits)
        gain.start(gain_ref[...])

    for n, one in enumerate(sums):

        @pl.when(step == n)
        def _():
            weight_slabs(me, hidden_ref, dqkv_ref, one.keep, one.send, scr, share=share, split=False, order=tuple(
                {-1: 3, 1: 0, 2: 1, 3: 2}[bit] for bit in QKV[n]
            ))
            one.start()
            for earlier in range(n):
                sums[earlier].step(n - earlier)
            if n:
                gain.step(n)

    @pl.when(step == count - 1)
    def _():
        for number in range(2, 5 + count - 1):
            for n, one in enumerate(sums):
                now = number - n
                if count - 1 - n < now < 5:
                    one.step(now)
            if count - 1 < number < 5:
                gain.step(number)
        for n, one in enumerate(sums):
            one.finish(out_ref, slice(n * width, (n + 1) * width))
        gain.finish(gain_out)


def qkv_grad(hidden, dqkv, gain, share):
    tokens, width = hidden.shape
    slots = width // share // 2
    fixed = pl.BlockSpec((8, width), lambda j: (0, 0), pipeline_mode=pl.Buffered(1))
    scratch = []
    for _ in range(3):
        scratch += [pltpu.VMEM((slots, share, width), bf16), *SlabSum.scratch(slots, share, width)]
    return pl.pallas_call(
        functools.partial(qkv_grad_kernel, share=share),
        name="grad_qkv",
        grid_spec=pltpu.PrefetchScalarGridSpec(
            num_scalar_prefetch=0,
            grid=(3,),
            in_specs=[
                pl.BlockSpec((tokens, width), lambda j: (0, 0), pipeline_mode=pl.Buffered(1)),
                pl.BlockSpec((None, tokens, width), lambda j: (j, 0, 0)),
                fixed,
            ],
            out_specs=[pl.BlockSpec((share, 3 * width), lambda j: (0, 0), pipeline_mode=pl.Buffered(1)), fixed],
            scratch_shapes=[pltpu.VMEM((2 * slots, share, width), f32), *scratch, *GainSum.scratch(width)],
        ),
        out_shape=[jax.ShapeDtypeStruct((share, 3 * width), f32), jax.ShapeDtypeStruct((8, width), f32)],
        compiler_params=pltpu.CompilerParams(vmem_limit_bytes=60 << 20, collective_id=2, has_side_effects=True),
        cost_estimate=pl.CostEstimate(
            flops=6 * tokens * width * width, bytes_accessed=8 * tokens * width, transcendentals=0
        ),
    )(hidden, dqkv, gain)


def project_back_kernel(side_ref, x_ref, gain_ref, w_ref, dqkv_ref, dmid_ref, dx_ref, dgain_ref):
    x = x_ref[...].astype(f32)
    width = x.shape[1]
    center = x - jnp.mean(x, axis=1, keepdims=True)
    spread = jnp.mean(center * center, axis=1, keepdims=True)
    inv = lax.rsqrt(spread + 1e-5)
    norm = center * inv
    dh = mm_t(dqkv_ref[0], w_ref[:, :width])
    dh = dh + mm_t(dqkv_ref[1], w_ref[:, width : 2 * width])
    dh = dh + mm_t(dqkv_ref[2], w_ref[:, 2 * width :])

    @pl.when(pl.program_id(0) == 0)
    def _():
        dgain_ref[...] = jnp.zeros_like(dgain_ref)

    dgain_ref[...] += jnp.sum((dh * norm).reshape(-1, 8, width), axis=0)
    e = dh * gain_ref[...].astype(f32)
    dx_ref[...] = (dmid_ref[...] + inv * (
        e - jnp.mean(e, axis=1, keepdims=True) - norm * jnp.mean(e * norm, axis=1, keepdims=True)
    )).astype(dx_ref.dtype)


def project_back(side, x, gain, w, dqkv, dmid, away, tile=256):
    width = x.shape[-1]
    length = dmid.shape[0] // 2
    half = length // tile
    first = half if away else 0
    if away:
        x_spec = pl.BlockSpec((tile, width), lambda i, s: (i, 0))
        out_spec, out_shape = x_spec, jax.ShapeDtypeStruct((length, width), bf16)
    else:
        x_spec = pl.BlockSpec((None, None, tile, width), lambda i, s: (0, s[0], i, 0))
        out_spec, out_shape = x_spec, jax.ShapeDtypeStruct((1, 2, length, width), f32)
    return pl.pallas_call(
        project_back_kernel,
        name="project_back_away" if away else "project_back_own",
        grid_spec=pltpu.PrefetchScalarGridSpec(
            num_scalar_prefetch=1,
            grid=(half,),
            in_specs=[
                x_spec,
                pl.BlockSpec((1, width), lambda i, s: (0, 0)),
                pl.BlockSpec((width, 3 * width), lambda i, s: (0, 0), pipeline_mode=pl.Buffered(1)),
                pl.BlockSpec((3, tile, width), lambda i, s: (0, i + first, 0)),
                pl.BlockSpec((tile, width), lambda i, s: (i + first, 0)),
            ],
            out_specs=[out_spec, pl.BlockSpec((8, width), lambda i, s: (0, 0))],
        ),
        out_shape=[out_shape, jax.ShapeDtypeStruct((8, width), f32)],
        compiler_params=pltpu.CompilerParams(vmem_limit_bytes=48 << 20),
        cost_estimate=pl.CostEstimate(
            flops=6 * length * width * width, bytes_accessed=length * width * 16, transcendentals=0
        ),
    )(side, x, gain, w, dqkv, dmid)


def flip(x, bit):
    axis, by = ("stream", 1) if bit < 0 else ("batch", 1 << bit)
    return lax.ppermute(x, axis, [(i, i ^ by) for i in range(lax.axis_size(axis))])


def after(value, *others):
    return lax.optimization_barrier((value, *others))[0]


def gather_kernel(shard_ref, gain_ref, w_ref, gains_ref, local_sems, send_sems, recv_sems, *, plans):
    side, me = lax.axis_index("stream"), lax.axis_index("batch")
    bits = sorted(plans[0][2])
    barrier = pltpu.get_barrier_semaphore()
    for bit in bits:
        pl.semaphore_signal(
            barrier, inc=1, device_id=(side, jnp.bitwise_xor(me, 1 << bit)), device_id_type=pl.DeviceIdType.MESH
        )
    pl.semaphore_wait(barrier, len(bits))
    sources, targets = [shard_ref, gain_ref], [w_ref, gains_ref]
    local = [pltpu.make_async_copy(sources[n], targets[n].at[me], local_sems.at[n]) for n in range(2)]
    for copy in local:
        copy.start()

    def copies(plan, step):
        which, cols, order = plans[plan]
        held = [0]
        for bit in order[:step]:
            held += [h ^ (1 << bit) for h in held]
        done = []
        for n, h in enumerate(held):
            slab = jnp.bitwise_xor(me, h)
            at = targets[which].at[slab, :, cols]
            number = (1 << step) - 1 + n
            done.append(
                pltpu.make_async_remote_copy(
                    src_ref=sources[which].at[:, cols] if h == 0 else at,
                    dst_ref=at,
                    send_sem=send_sems.at[plan, number],
                    recv_sem=recv_sems.at[plan, number],
                    device_id=(side, jnp.bitwise_xor(me, 1 << order[step])),
                    device_id_type=pl.DeviceIdType.MESH,
                )
            )
        return done

    for step in range(len(bits)):
        for plan in range(len(plans)):
            if step:
                for copy in copies(plan, step - 1):
                    copy.wait_recv()
            for copy in copies(plan, step):
                copy.start()
    for plan in range(len(plans)):
        for copy in copies(plan, len(bits) - 1):
            copy.wait_recv()
    for plan in range(len(plans)):
        for step in range(len(bits)):
            for copy in copies(plan, step):
                copy.wait_send()
    for copy in local:
        copy.wait()


def gather(shard, gains):
    peers = lax.axis_size("batch")
    rows, columns = shard.shape
    cut = columns // 1024 * 896
    plans = (
        (0, slice(0, cut), (3, 2, 1, 0)),
        (0, slice(cut, columns), (1, 3, 2, 0)),
        (1, slice(0, gains.shape[1]), (1, 3, 2, 0)),
    )
    anywhere = pl.BlockSpec(memory_space=pl.ANY)
    return pl.pallas_call(
        functools.partial(gather_kernel, plans=plans),
        name="gather",
        in_specs=[anywhere, anywhere],
        out_specs=[anywhere, anywhere],
        out_shape=[
            jax.ShapeDtypeStruct((peers, rows, columns), bf16),
            jax.ShapeDtypeStruct((peers, *gains.shape), bf16),
        ],
        scratch_shapes=[
            pltpu.SemaphoreType.DMA((2,)),
            pltpu.SemaphoreType.DMA((len(plans), peers - 1)),
            pltpu.SemaphoreType.DMA((len(plans), peers - 1)),
        ],
        compiler_params=pltpu.CompilerParams(collective_id=0, has_side_effects=True),
        cost_estimate=pl.CostEstimate(flops=0, bytes_accessed=8 * peers * rows * columns, transcendentals=0),
    )(shard, gains)


def shards(tokens, cotangent, lengths, ln1_gain, w_qkv, w_out, ln2_gain, w_up, w_down):
    side = lax.axis_index("stream")
    at = lax.axis_index("batch")
    _, rows_dev, length, width = tokens.shape
    assert rows_dev == 2
    ff = w_up.shape[1]
    peers = lax.axis_size("batch")
    small = peers == 16 and width % (16 * peers) == 0
    side_array = side.reshape(1).astype(jnp.int32)
    index = side * peers + at
    me = jnp.stack([index if small else 0 * index, side]).astype(jnp.int32)
    share = width // (2 * peers)

    x_away = flip(lax.dynamic_index_in_dim(tokens[0], 1 - side, 0, False), -1)
    g_away = flip(lax.dynamic_index_in_dim(cotangent[0], 1 - side, 0, False), -1)
    if small:
        rows = width // peers
        gains = jnp.zeros((16, LANES), bf16)
        gains = gains.at[0, :rows].set(ln1_gain).at[1, :rows].set(ln2_gain)
        w_qkv_all, gains = gather(w_qkv, gains)
        w_qkv_all = w_qkv_all.reshape(width, 3 * width)
        gain_one, gain_two = (gains[:, n, :rows].reshape(1, width) for n in range(2))
        down = w_down.reshape(-1, rows, width).swapaxes(0, 1).reshape(rows, ff)
        rest = lax.all_gather(jnp.concatenate([w_out, w_up, down], axis=1), "batch", axis=0, tiled=True)
        rest = rest.reshape(peers, rows, -1)
    else:
        def whole(x):
            return lax.all_gather(x, "batch", axis=0, tiled=True)

        w_qkv_all = whole(w_qkv)
        gain_one, gain_two = whole(ln1_gain)[None], whole(ln2_gain)[None]
        down = whole(w_down).reshape(16, -1, width // 16, width).swapaxes(1, 2).reshape(width, ff)
        rest = jnp.concatenate([whole(w_out), whole(w_up), down], axis=1).reshape(16, width // 16, -1)

    cosine, sine = rotary_tables(length)
    tables = mask_tables(length, jnp.take(lengths, side))
    qkv, hidden = project(side_array, tokens, x_away, gain_one, w_qkv_all, cosine, sine)
    qkv4 = qkv.reshape(3, 2, length, width)
    mixed, logs = attend(side_array, qkv4, tables)
    mixed2 = mixed.reshape(2 * length, width)
    out, out_away, act, du, h2, dmid, dbr, dmix, dgain_two = feed(
        side_array, tokens, x_away, mixed2, cotangent, g_away, gain_two, rest
    )

    def place(result, away):
        away = flip(away, -1).astype(result.dtype)
        return lax.dynamic_update_slice(result, away[None, None], (0, 1 - side, 0, 0))

    out = place(out, out_away)
    unit = share if small else width // 32
    places = {-1: 3, 1: 0, 2: 1, 3: 2}

    def columns_grad(left, right, order, name):
        return weight_grad_columns(me, left, right, width, unit, [places[bit] for bit in order], name)

    down = weight_grad_rows(me, act, cotangent, g_away, width, ff // width * unit, "grad_down")
    down = [part.reshape(16, -1, width) for part in down]
    up = columns_grad(h2, du, UP, "grad_up")
    wo = columns_grad(mixed2, dbr, OUT, "grad_out")
    dmix = after(dmix.reshape(2, length, width), out)
    common = qkv4, mixed, dmix, logs, tables, cosine, sine
    if small:
        dqkv, down, up, wo, dgain_two = attend_back(*common, (down, up, wo), dgain_two)
    else:
        dqkv, = attend_back(*common)
    dqkv3 = dqkv.reshape(3, 2 * length, width)
    dx_away, dgain_away = project_back(side_array, x_away, gain_one, w_qkv_all, dqkv3, dmid, True)
    dx, dgain_own = project_back(side_array, tokens, gain_one, w_qkv_all, dqkv3, dmid, False)
    dgain_one = dgain_own + dgain_away
    if small:
        wq, dgain_one = qkv_grad(hidden, dqkv3, dgain_one, share)
    dx = place(dx, dx_away)
    dgain_one, dgain_two = (jnp.sum(g, axis=0, keepdims=True) for g in (dgain_one, dgain_two))
    if not small:

        def scatter(pair, order):
            slots = jnp.stack(pair, axis=1)
            natural = [arranged(n, order) for n in range(16)]
            rows = slots[jnp.array(natural)].reshape(-1, slots.shape[-1])
            return lax.psum_scatter(rows, ("stream", "batch"), scatter_dimension=0, tiled=True).astype(f32)

        parts = [columns_grad(hidden, dqkv3[n], QKV[n], "grad_qkv") for n in range(3)]
        down, up, wo, *parts = (
            scatter(pair, [places[bit] for bit in order])
            for pair, order in zip((down, up, wo, *parts), (DOWN, UP, OUT, *QKV))
        )
        wq = jnp.concatenate(parts, axis=1)
        dgain_one, dgain_two = lax.psum((dgain_one, dgain_two), ("stream", "batch"))
    begin = index * share
    dgain_one, dgain_two = (lax.dynamic_slice(g[0], (begin,), (share,)) for g in (dgain_one, dgain_two))
    return out, dx, dgain_one, wq, wo, dgain_two, up, down


def solution(mesh):
    token = P("stream", "batch", None, None)
    vector, matrix = P("batch"), P("batch", None)
    out_vector, out_matrix = P(("stream", "batch")), P(("stream", "batch"), None)
    return jax.shard_map(
        shards,
        mesh=mesh,
        in_specs=(token, token, vector, vector, matrix, matrix, vector, matrix, matrix),
        out_specs=(token, token, out_vector, out_matrix, out_matrix, out_vector, out_matrix, out_matrix),
        check_vma=False,
    )
```

```python
import functools
import math

import jax
import jax.numpy as jnp
from jax import lax
from jax.experimental import pallas as pl
from jax.experimental.pallas import tpu as pltpu
from jax.sharding import PartitionSpec as P

HD = 64
BLOCK = 16
LANES = 128
TILE = 256
BIG = -1e30
f32, bf16 = jnp.float32, jnp.bfloat16


def mm(a, b):
    return lax.dot_general(a, b, (((1,), (0,)), ((), ())), preferred_element_type=f32)


def mm_t(a, b):
    return lax.dot_general(a, b, (((1,), (1,)), ((), ())), preferred_element_type=f32)


def t_mm(a, b):
    return lax.dot_general(a, b, (((0,), (0,)), ((), ())), preferred_element_type=f32)


def rotary_tables(length):
    half = HD // 2
    places = jnp.arange(length).astype(f32)
    rates = jnp.exp(jnp.arange(half).astype(f32) * (-2.0 * math.log(10000.0) / HD))
    angles = places[:, None] * rates[None, :]
    cosine, sine = jnp.cos(angles), jnp.sin(angles)
    return (
        jnp.concatenate([cosine] * 4, axis=1),
        jnp.concatenate([-sine, sine, -sine, sine], axis=1),
    )


def half_partner(x):
    lane = lax.broadcasted_iota(jnp.int32, x.shape, 1)
    low = lax.rem(lane, HD) < HD // 2
    return jnp.where(low, pltpu.roll(x, LANES - HD // 2, 1), pltpu.roll(x, HD // 2, 1))


MESH = pl.DeviceIdType.MESH


def partner(bit):
    side, at = lax.axis_index("stream"), lax.axis_index("batch")
    return (1 - side, at) if bit < 0 else (side, jnp.bitwise_xor(at, 1 << bit))


def greet(others):
    barrier = pltpu.get_barrier_semaphore()
    for other in others:
        pl.semaphore_signal(barrier, inc=1, device_id=other, device_id_type=MESH)
    pl.semaphore_wait(barrier, len(others))


def line_partners():
    side, at = lax.axis_index("stream"), lax.axis_index("batch")
    return [partner(-1)] + [(side, jnp.bitwise_xor(at, mask)) for mask in (1, 2, 4, 8, 12)]


class LineGather:
    SENDS = 29

    def __init__(self, chunks, send_sems, recv_sems, local_sems):
        self.chunks, self.send_sems, self.recv_sems, self.local_sems = chunks, send_sems, recv_sems, local_sems
        self.side, self.at = lax.axis_index("stream"), lax.axis_index("batch")
        self.z = lax.div(self.at, 4)

    @staticmethod
    def scratch(count):
        return [
            pltpu.SemaphoreType.DMA((count, LineGather.SENDS)),
            pltpu.SemaphoreType.DMA((count, 16)),
            pltpu.SemaphoreType.DMA((count,)),
        ]

    def copy(self, chunk, shard, target, number, own=False):
        source, place = self.chunks[chunk]
        return pltpu.make_async_remote_copy(
            src_ref=source if own else place(shard),
            dst_ref=place(shard),
            send_sem=self.send_sems.at[chunk, number],
            recv_sem=self.recv_sems.at[chunk, shard],
            device_id=(self.side, target),
            device_id_type=MESH,
        )

    def local(self, chunk):
        source, place = self.chunks[chunk]
        return pltpu.make_async_copy(source, place(self.at), self.local_sems.at[chunk])

    def sends(self, phase):
        at, z = self.at, self.z
        across, core = jnp.bitwise_xor(at, 2), jnp.bitwise_xor(at, 1)
        up, down = (at + 4, z < 3), (at - 4, z > 0)
        other = jnp.bitwise_xor
        if phase == 0:
            yield None, at, [(*up, 0), (*down, 1), (across, None, 2), (core, None, 3)]
        if 1 <= phase <= 3:
            n = 4 + 6 * (phase - 1)
            yield z >= phase, at - 4 * phase, [(*up, n), (across, None, n + 1), (core, None, n + 2)]
            yield z + phase <= 3, at + 4 * phase, [(*down, n + 3), (across, None, n + 4), (core, None, n + 5)]
        if phase == 1:
            yield None, across, [(core, None, 22)]
        if 2 <= phase <= 4:
            d, n = phase - 1, 23 + 2 * (phase - 2)
            yield z >= d, other(at - 4 * d, 2), [(core, None, n)]
            yield z + d <= 3, other(at + 4 * d, 2), [(core, None, n + 1)]

    def each(self, phase, act):
        for when, shard, sends in self.sends(phase):

            def run():
                act(shard, None, None)
                for target, whether, number in sends:
                    if whether is None:
                        act(shard, target, number)
                    else:
                        pl.when(whether)(lambda: act(shard, target, number))

            if when is None:
                run()
            else:
                pl.when(when)(run)

    def phase(self, chunk, phase):
        def act(shard, target, number):
            if target is None:
                if phase == 0:
                    self.local(chunk).start()
                else:
                    self.copy(chunk, shard, self.at, 0).wait_recv()
            else:
                self.copy(chunk, shard, target, number, own=phase == 0).start()

        self.each(phase, act)

    def finish(self):
        for chunk in range(len(self.chunks)):
            for n in range(8):
                shard = jnp.bitwise_xor(lax.rem(self.at, 2), 1) + 2 * n
                self.copy(chunk, shard, self.at, 0).wait_recv()
            self.local(chunk).wait()
            for phase in range(5):

                def act(shard, target, number):
                    if target is not None:
                        self.copy(chunk, shard, target, number, own=phase == 0).wait_send()

                self.each(phase, act)


class SlabSum:
    def __init__(self, order, keep, send, got, sems, load=None):
        self.order, self.keep, self.send, self.got, self.sems, self.load = (0, *order), keep, send, got, sems, load

    @staticmethod
    def scratch(slots, share, columns):
        steps = slots.bit_length()
        return [
            *[pltpu.VMEM((max(slots >> n, 1), share, columns), bf16) for n in (0, *range(steps))],
            pltpu.SemaphoreType.DMA((2 * steps + 1,)),
        ]

    def copy(self, step):
        count = self.got[step].shape[0]
        return pltpu.make_async_remote_copy(
            src_ref=self.send if step == 0 else self.keep.at[pl.ds(count, count)],
            dst_ref=self.got[step],
            send_sem=self.sems.at[2 * step],
            recv_sem=self.sems.at[2 * step + 1],
            device_id=partner(self.order[step]),
            device_id_type=MESH,
        )

    def loading(self):
        return pltpu.make_async_copy(self.load, self.keep, self.sems.at[2 * len(self.order)])

    def start(self):
        self.copy(0).start()
        if self.load is not None:
            self.loading().start()

    def step(self, step):
        if step == 1 and self.load is not None:
            self.loading().wait()
        self.copy(step - 1).wait_recv()
        got = self.got[step - 1]

        @pl.loop(0, got.shape[0])
        def _(n):
            self.keep[n] = (self.keep[n].astype(f32) + got[n].astype(f32)).astype(bf16)

        self.copy(step).start()

    def finish(self, out_ref, columns=slice(None)):
        last = len(self.order) - 1
        self.copy(last).wait_recv()
        out_ref[:, columns] = self.keep[0].astype(f32) + self.got[last][0].astype(f32)
        for step in range(len(self.order)):
            self.copy(step).wait_send()


ALL = (-1, 0, 1, 2, 3)


class GainSum:
    def __init__(self, bits, held, got, sems):
        self.bits, self.held, self.got, self.sems = bits, held, got, sems

    @staticmethod
    def scratch(bits, width):
        steps = len(bits)
        return [
            pltpu.VMEM((steps, 8, width), f32),
            pltpu.VMEM((steps, 8, width), f32),
            pltpu.SemaphoreType.DMA((2 * steps,)),
        ]

    def copy(self, step):
        return pltpu.make_async_remote_copy(
            src_ref=self.held.at[step],
            dst_ref=self.got.at[step],
            send_sem=self.sems.at[2 * step],
            recv_sem=self.sems.at[2 * step + 1],
            device_id=partner(self.bits[step]),
            device_id_type=MESH,
        )

    def start(self, value):
        self.held[0] = value
        self.copy(0).start()

    def step(self, step):
        self.copy(step - 1).wait_recv()
        self.held[step] = self.held[step - 1] + self.got[step - 1]
        self.copy(step).start()

    def finish(self, out_ref):
        last = len(self.bits) - 1
        self.copy(last).wait_recv()
        out_ref[...] = self.held[last] + self.got[last]
        for step in range(len(self.bits)):
            self.copy(step).wait_send()


def row_specs(tile, width, half):
    own = pl.BlockSpec((None, None, tile, width), lambda i, s: (0, s[0], jnp.minimum(i, half - 1), 0))
    away = pl.BlockSpec((tile, width), lambda i, s: (jnp.maximum(i - half, 0), 0))
    return own, away


def read_rows(own_ref, away_ref, half):
    return jnp.where(pl.program_id(0) < half, own_ref[...], away_ref[...])


def project_kernel(side_ref, own_ref, away_ref, gain_ref, w_ref, cos_ref, sin_ref, out_ref, hidden_ref, *, half):
    width = own_ref.shape[-1]
    project_tile(read_rows(own_ref, away_ref, half), gain_ref[...], lambda part: w_ref[:, part * width : (part + 1) * width],
                 cos_ref, sin_ref, out_ref, hidden_ref)


def project_tile(x, gain, weights, cos_ref, sin_ref, out_ref, hidden_ref):
    x = x.astype(f32)
    width = x.shape[1]
    center = x - jnp.mean(x, axis=1, keepdims=True)
    spread = jnp.mean(center * center, axis=1, keepdims=True)
    hidden = (center * lax.rsqrt(spread + 1e-5) * gain.astype(f32)).astype(bf16)
    hidden_ref[...] = hidden
    cosine, sine = cos_ref[...], sin_ref[...]
    for part in range(3):
        rows = mm(hidden, weights(part))
        for pair in range(width // LANES):
            cols = slice(pair * LANES, (pair + 1) * LANES)
            field = rows[:, cols]
            if part < 2:
                field = field * cosine + half_partner(field) * sine
            if part == 0:
                field = field * 0.125
            out_ref[part, :, cols] = field.astype(bf16)


def project(side, own, away, gain, w, cosine, sine, tile=512):
    length, width = away.shape
    tokens, half = 2 * length, length // tile
    table = pl.BlockSpec((tile, LANES), lambda i, s: (lax.rem(i, half), 0))
    return pl.pallas_call(
        functools.partial(project_kernel, half=half),
        name="project",
        grid_spec=pltpu.PrefetchScalarGridSpec(
            num_scalar_prefetch=1,
            grid=(2 * half,),
            in_specs=[
                *row_specs(tile, width, half),
                pl.BlockSpec((1, width), lambda i, s: (0, 0)),
                pl.BlockSpec((width, 3 * width), lambda i, s: (0, 0), pipeline_mode=pl.Buffered(1)),
                table,
                table,
            ],
            out_specs=[
                pl.BlockSpec((3, tile, width), lambda i, s: (0, i, 0)),
                pl.BlockSpec((tile, width), lambda i, s: (i, 0)),
            ],
        ),
        out_shape=[jax.ShapeDtypeStruct((3, tokens, width), bf16), jax.ShapeDtypeStruct((tokens, width), bf16)],
        compiler_params=pltpu.CompilerParams(vmem_limit_bytes=48 << 20),
        cost_estimate=pl.CostEstimate(
            flops=6 * tokens * width * width, bytes_accessed=tokens * width * 10 + 6 * width * width, transcendentals=0
        ),
    )(side, own, away, gain, w, cosine, sine)


def first_kernel(shard_ref, gain_ref, tokens_ref, own_ref, cos_ref, sin_ref, qkv_ref, hidden_ref, away_out, w_out, gains_out,
                 w_all, away, rows, swap_sems, out_sems, send_sems, recv_sems, local_sems, *gain_scratch, half):
    side, at = lax.axis_index("stream"), lax.axis_index("batch")
    step = pl.program_id(0)
    width = own_ref.shape[-1]
    tile = own_ref.shape[-2]
    swap = pltpu.make_async_remote_copy(
        src_ref=tokens_ref.at[0, 1 - side],
        dst_ref=away,
        send_sem=swap_sems.at[0],
        recv_sem=swap_sems.at[1],
        device_id=(1 - side, at),
        device_id_type=MESH,
    )

    def chunk(n):
        cols = slice(n * width, (n + 1) * width)
        return shard_ref.at[:, cols], lambda shard: w_all.at[shard, :, cols]

    weights = LineGather([chunk(n) for n in range(3)], send_sems, recv_sems, local_sems)
    gain = GainSum((0, 1, 2, 3), *gain_scratch)
    keeps = [
        pltpu.make_async_copy(w_all, w_out, out_sems.at[0]),
        pltpu.make_async_copy(away, away_out, out_sems.at[1]),
    ]

    @pl.when(step == 0)
    def _():
        greet(line_partners())
        swap.start()
        gain.start(gain_ref[...])
        for phase in range(5):
            for n in range(3):
                weights.phase(n, phase)
            if 1 <= phase <= 3:
                gain.step(phase)
        gain.finish(gains_out)
        weights.finish()
        keeps[0].start()

    @pl.when(step == half)
    def _():
        swap.wait()
        keeps[1].start()

    @pl.when(step < half)
    def _():
        rows[...] = own_ref[...]

    @pl.when(step >= half)
    def _():
        rows[...] = away[pl.ds(pl.multiple_of((step - half) * tile, tile), tile), :]

    project_tile(rows[...], gains_out[0:1, :], lambda part: w_all[:, :, part * width : (part + 1) * width].reshape(width, width),
                 cos_ref, sin_ref, qkv_ref, hidden_ref)

    @pl.when(step == pl.num_programs(0) - 1)
    def _():
        for keep in keeps:
            keep.wait()


def first(shard, gain, tokens, cosine, sine, tile=512):
    _, _, length, width = tokens.shape
    rows = shard.shape[0]
    half = length // tile
    anywhere = pl.BlockSpec(memory_space=pl.ANY)
    table = pl.BlockSpec((tile, LANES), lambda i: (lax.rem(i, half), 0))
    small = pl.BlockSpec((8, width), lambda i: (0, 0))
    return pl.pallas_call(
        functools.partial(first_kernel, half=half),
        name="first",
        grid=(2 * half,),
        in_specs=[
            anywhere,
            small,
            anywhere,
            pl.BlockSpec((None, None, tile, width), lambda i: (0, lax.axis_index("stream"), jnp.minimum(i, half - 1), 0)),
            table,
            table,
        ],
        out_specs=[
            pl.BlockSpec((3, tile, width), lambda i: (0, i, 0)),
            pl.BlockSpec((tile, width), lambda i: (i, 0)),
            anywhere,
            anywhere,
            small,
        ],
        out_shape=[
            jax.ShapeDtypeStruct((3, 2 * length, width), bf16),
            jax.ShapeDtypeStruct((2 * length, width), bf16),
            jax.ShapeDtypeStruct((length, width), bf16),
            jax.ShapeDtypeStruct((16, rows, 3 * width), bf16),
            jax.ShapeDtypeStruct((8, width), f32),
        ],
        scratch_shapes=[
            pltpu.VMEM((16, rows, 3 * width), bf16),
            pltpu.VMEM((length, width), bf16),
            pltpu.VMEM((tile, width), bf16),
            pltpu.SemaphoreType.DMA((2,)),
            pltpu.SemaphoreType.DMA((2,)),
            *LineGather.scratch(3),
            *GainSum.scratch((0, 1, 2, 3), width),
        ],
        compiler_params=pltpu.CompilerParams(vmem_limit_bytes=48 << 20, collective_id=0, has_side_effects=True),
        cost_estimate=pl.CostEstimate(
            flops=12 * length * width * width, bytes_accessed=length * width * 24 + 12 * width * width, transcendentals=0
        ),
    )(shard, gain, tokens, tokens, cosine, sine)


def mask_tables(length, row_length):
    pos = jnp.arange(length)
    blk = (pos // BLOCK)[:, None]
    lane = (jnp.arange(LANES) % HD)[None, :]
    dead = (pos >= row_length)[:, None]
    clean_query = (lane == blk).astype(bf16)
    noisy_query = (lane == blk - 1).astype(bf16)
    main_key = jnp.where((blk > lane) | dead, BIG, 0.0).astype(bf16)
    diag_key = jnp.where((blk != lane) | dead, BIG, 0.0).astype(bf16)
    return clean_query, noisy_query, main_key, diag_key


def low_lanes(shape):
    return lax.broadcasted_iota(jnp.int32, shape, 1) < HD


def attend_gather_kernel(qkv_ref, cq_ref, nq_ref, mk_ref, dk_ref, wo_ref, wu_ref, wd_ref, grad_ref,
                         out_ref, log_ref, wo_all, wu_all, wd_all, away_ref,
                         qa, ka, kd, va, s_scr, swap_sems, send_sems, recv_sems, local_sems):
    side, at = lax.axis_index("stream"), lax.axis_index("batch")
    step = pl.program_id(0)
    wide, tall = wu_ref.shape[1] // 2, wd_ref.shape[0] // 2

    def columns(n):
        cols = slice(n * wide, (n + 1) * wide)
        return wu_ref.at[:, cols], lambda shard: wu_all.at[shard, :, cols]

    def rows(n):
        part = slice(n * tall, (n + 1) * tall)
        return wd_ref.at[part, :], lambda shard: wd_all.at[shard, part, :]

    chunks = [(wo_ref, lambda shard: wo_all.at[shard]), columns(0), columns(1), rows(0), rows(1)]
    weights = LineGather(chunks, send_sems, recv_sems, local_sems)
    swap = pltpu.make_async_remote_copy(
        src_ref=grad_ref.at[0, 1 - side],
        dst_ref=away_ref,
        send_sem=swap_sems.at[0],
        recv_sem=swap_sems.at[1],
        device_id=(1 - side, at),
        device_id_type=MESH,
    )
    slots = 2 * SLOT_STEPS
    plan = [[] for _ in range(slots + 1)]
    items = [(chunk, phase) for phase in range(1, 5) for chunk in range(5)]
    for n, item in enumerate(items):
        plan[min(1 + n * SLOT_RATE // 16, slots)].append(item)

    @pl.when(step == 0)
    def _():
        greet(line_partners())
        for chunk in range(5):
            weights.phase(chunk, 0)
        swap.start()

    def pass_on(slot):
        for now in range(SLOT_STEPS):
            if plan[2 * now + slot]:

                @pl.when(step == now)
                def _():
                    for item in plan[2 * now + slot]:
                        weights.phase(*item)

    pass_on(0)
    attend_kernel(qkv_ref, cq_ref, nq_ref, mk_ref, dk_ref, out_ref, log_ref, qa, ka, kd, va, s_scr,
                  between=lambda: pass_on(1))

    @pl.when(step == pl.num_programs(0) - 1)
    def _():
        for item in plan[slots]:
            weights.phase(*item)
        weights.finish()
        swap.wait()


SLOT_STEPS = 6
SLOT_RATE = 11


def attend_kernel(qkv_ref, cq_ref, nq_ref, mk_ref, dk_ref, out_ref, log_ref,
                  qa, ka, kd, va, s_scr, between=lambda: None):
    length = out_ref.shape[1]
    clean = lax.axis_index("stream")
    noisy = 1 - clean
    tiles = length // TILE
    low = low_lanes((length, LANES))
    ones = jnp.ones((16, length), bf16)
    vc_t = qkv_ref[2, clean].T
    vn_t = qkv_ref[2, noisy].T
    for head in range(2):
        pick = low if head == 0 else jnp.logical_not(low)
        qa[0, head] = jnp.where(pick, qkv_ref[0, clean], cq_ref[...])
        qa[1, head] = jnp.where(pick, qkv_ref[0, noisy], nq_ref[...])
        qa[2, head] = jnp.where(pick, qkv_ref[0, noisy], cq_ref[...])
        ka[head] = jnp.where(pick, qkv_ref[1, clean], mk_ref[...])
        kd[head] = jnp.where(pick, qkv_ref[1, noisy], dk_ref[...])
        va[0, head, :HD] = vc_t[head * HD : (head + 1) * HD]
        va[1, head, :HD] = vn_t[head * HD : (head + 1) * HD]
        va[0, head, HD:] = ones
        va[1, head, HD:] = ones
    for copy in range(2):
        if copy:
            between()
        where_to = clean if copy == 0 else noisy
        for tile in range(tiles):
            rows = slice(tile * TILE, (tile + 1) * TILE)
            parts = []
            for head in range(2):
                pieces = [(qa[copy, head, rows, :], ka, 0, t) for t in range(tile + 1)]
                if copy == 1:
                    pieces.append((qa[2, head, rows, :], kd, 1, tile))
                top = None
                for n, (query, keys, vi, t) in enumerate(pieces):
                    s = mm_t(keys[head, t * TILE : (t + 1) * TILE, :], query)
                    if copy == 1 and tile == 0 and n == 0:
                        first = lax.broadcasted_iota(jnp.int32, s.shape, 1) < BLOCK
                        s = jnp.where(first, BIG, s)
                    s_scr[head, n * TILE : (n + 1) * TILE, :] = s
                    m = jnp.max(s, axis=0, keepdims=True)
                    top = m if top is None else jnp.maximum(top, m)
                acc = None
                for n, (query, keys, vi, t) in enumerate(pieces):
                    p = jnp.exp(s_scr[head, n * TILE : (n + 1) * TILE, :] - top).astype(bf16)
                    o = mm(va[vi, head, :, t * TILE : (t + 1) * TILE], p)
                    acc = o if acc is None else acc + o
                total = acc[HD : HD + 1, :]
                parts.append(acc[:HD] / total)
                log_ref[where_to, 0, head : head + 1, rows] = top + jnp.log(total)
            out_ref[where_to, rows, :] = jnp.concatenate(parts, axis=0).T.astype(bf16)


def attend(qkv, tables, shards=None, grad=None):
    _, copies, length, width = qkv.shape
    pairs = width // LANES
    table_spec = pl.BlockSpec((length, LANES), lambda i: (0, 0), pipeline_mode=pl.Buffered(1))
    more_in, more_shapes, more_scratch = [], [], []
    body, params = attend_kernel, {}
    if shards is not None:
        assert pairs == SLOT_STEPS
        body = attend_gather_kernel
        params = dict(collective_id=3, has_side_effects=True)
        more_in = [*shards, grad]
        more_shapes = [jax.ShapeDtypeStruct((16, *shard.shape), bf16) for shard in shards]
        more_shapes.append(jax.ShapeDtypeStruct((length, width), bf16))
        more_scratch = [pltpu.SemaphoreType.DMA((2,)), *LineGather.scratch(5)]
    anywhere = pl.BlockSpec(memory_space=pl.ANY)
    return pl.pallas_call(
        body,
        name="attend",
        grid=(pairs,),
        in_specs=[pl.BlockSpec((3, copies, length, LANES), lambda i: (0, 0, 0, i)), *[table_spec] * 4,
                  *[anywhere] * len(more_in)],
        out_specs=[
            pl.BlockSpec((copies, length, LANES), lambda i: (0, 0, i)),
            pl.BlockSpec((copies, 1, 2, length), lambda i: (0, i, 0, 0)),
            *[anywhere] * len(more_in),
        ],
        scratch_shapes=[
            pltpu.VMEM((3, 2, length, LANES), bf16),
            pltpu.VMEM((2, length, LANES), bf16),
            pltpu.VMEM((2, length, LANES), bf16),
            pltpu.VMEM((2, 2, HD + 16, length), bf16),
            pltpu.VMEM((2, length + TILE, TILE), f32),
            *more_scratch,
        ],
        out_shape=[
            jax.ShapeDtypeStruct((copies, length, width), bf16),
            jax.ShapeDtypeStruct((copies, pairs, 2, length), f32),
            *more_shapes,
        ],
        compiler_params=pltpu.CompilerParams(vmem_limit_bytes=48 << 20, **params),
        cost_estimate=pl.CostEstimate(
            flops=8 * length * length * width, bytes_accessed=16 * length * width, transcendentals=length * length * 12
        ),
    )(qkv, *tables, *more_in)


DOWN, UP, OUT = (-1, 1, 2, 3), (1, -1, 2, 3), (2, -1, 1, 3)
QKV = ((1, 2, 3, -1), (2, 1, 3, -1), (2, 3, 1, -1))


def attend_back_sum_kernel(*refs, orders):
    count = len(orders)
    core, refs = refs[:10], refs[10:]
    pairs, gain_ref, refs = refs[: 2 * count], refs[2 * count], refs[2 * count + 1 :]
    dqkv_ref, refs = refs[0], refs[1:]
    outs, gain_out, refs = refs[:count], refs[count], refs[count + 1 :]
    own, refs = refs[:10], refs[10:]
    per = len(refs[:-3]) // count
    sums = []
    for n, order in enumerate(orders):
        keep, *got, sems = refs[n * per : (n + 1) * per]
        sums.append(SlabSum(order, keep, pairs[2 * n + 1], got, sems, load=pairs[2 * n]))
    gain = GainSum(ALL, *refs[-3:])
    down, up, wo = sums
    step = pl.program_id(0)

    @pl.when(step == 0)
    def _():
        greet([partner(bit) for bit in ALL])
        for one in sums:
            one.start()
        gain.start(gain_ref[...])

    for at, plan in {
        1: ((down, 1), (up, 1), (wo, 1), (gain, 1)),
        2: ((wo, 2), (gain, 2)),
        3: ((down, 2), (up, 2), (wo, 3), (gain, 3)),
        4: ((down, 3), (up, 3), (wo, 4), (gain, 4)),
        5: ((down, 4), (up, 4)),
    }.items():

        @pl.when(step == at)
        def _():
            for one, number in plan:
                one.step(number)

    attend_back_kernel(*core, dqkv_ref, *own)

    @pl.when(step == pl.num_programs(0) - 1)
    def _():
        for one, out_ref in zip(sums, outs):
            one.finish(out_ref)
        gain.finish(gain_out)


def attend_back_kernel(qkv_ref, o_ref, do_ref, log_ref, cq_ref, nq_ref, mk_ref, dk_ref, cos_ref, sin_ref,
                       dqkv_ref, qa, qz, ka, kd, kt, doz, dsum, dq, dkc, dvc):
    length = o_ref.shape[1]
    clean = lax.axis_index("stream")
    noisy = 1 - clean
    tiles = length // TILE
    low = low_lanes((length, LANES))
    zero = jnp.zeros((length, LANES), bf16)
    for copy in range(2):
        at = clean if copy == 0 else noisy
        kt[copy] = qkv_ref[1, at].T
        prod = (o_ref[at].astype(f32) * do_ref[at].astype(f32)).T
        dsum[copy, 0:1] = jnp.sum(prod[:HD], axis=0, keepdims=True)
        dsum[copy, 1:2] = jnp.sum(prod[HD:], axis=0, keepdims=True)
        for head in range(2):
            pick = low if head == 0 else jnp.logical_not(low)
            qa[copy, head] = jnp.where(pick, qkv_ref[0, at], (cq_ref, nq_ref)[copy][...])
            qz[copy, head] = jnp.where(pick, qkv_ref[0, at], zero)
            doz[copy, head] = jnp.where(pick, do_ref[at], zero)
            if copy == 0:
                ka[head] = jnp.where(pick, qkv_ref[1, at], mk_ref[...])
            else:
                qa[2, head] = jnp.where(pick, qkv_ref[0, at], cq_ref[...])
                kd[head] = jnp.where(pick, qkv_ref[1, at], dk_ref[...])
    cosine, sine = cos_ref[...], sin_ref[...]

    def piece(copy, tile, query, keys, kv_copy, t, mask_first):
        rows = slice(tile * TILE, (tile + 1) * TILE)
        krows = slice(t * TILE, (t + 1) * TILE)
        kv_at = clean if kv_copy == 0 else noisy
        at = clean if copy == 0 else noisy
        probs, raws = [], []
        for head in range(2):
            s = mm_t(keys[head, krows, :], qa[query, head, rows, :])
            p = jnp.exp(s - log_ref[at, 0, head : head + 1, rows])
            if mask_first:
                first = lax.broadcasted_iota(jnp.int32, s.shape, 1) < BLOCK
                p = jnp.where(first, 0.0, p)
            dp = mm_t(qkv_ref[2, kv_at, krows, :], doz[copy, head, rows, :])
            raw = (p * (dp - dsum[copy, head : head + 1, rows])).astype(bf16)
            p = p.astype(bf16)
            dq[copy, head * HD : (head + 1) * HD, rows] += mm(kt[kv_copy, head * HD : (head + 1) * HD, krows], raw)
            probs.append(p)
            raws.append(raw)
        p2 = jnp.concatenate(probs, axis=1)
        r2 = jnp.concatenate(raws, axis=1)
        do2 = jnp.concatenate([doz[copy, 0, rows, :], doz[copy, 1, rows, :]], axis=0)
        q2 = jnp.concatenate([qz[copy, 0, rows, :], qz[copy, 1, rows, :]], axis=0)
        return mm(p2, do2), mm(r2, q2)

    def finish(field, rotate, scale):
        if rotate:
            c, s = cosine, sine
            field = field * c - half_partner(field) * s
        return (field * scale if scale != 1.0 else field).astype(bf16)

    dq[...] = jnp.zeros_like(dq)
    for t in range(tiles):
        krows = slice(t * TILE, (t + 1) * TILE)
        dv_t, dk_t = piece(1, t, 2, kd, 1, t, False)
        dqkv_ref[2, noisy, krows, :] = dv_t.astype(bf16)
        dkc[krows, :] = dk_t
    dqkv_ref[1, noisy] = finish(dkc[...], True, 1.0)
    for t in range(tiles):
        krows = slice(t * TILE, (t + 1) * TILE)
        dv_acc = dk_acc = None
        for tile in range(t, tiles):
            for copy in range(2):
                dv_t, dk_t = piece(copy, tile, copy, ka, 0, t, copy == 1 and tile == 0)
                dv_acc = dv_t if dv_acc is None else dv_acc + dv_t
                dk_acc = dk_t if dk_acc is None else dk_acc + dk_t
        dqkv_ref[2, clean, krows, :] = dv_acc.astype(bf16)
        dkc[krows, :] = dk_acc
    dqkv_ref[1, clean] = finish(dkc[...], True, 1.0)
    dqkv_ref[0, clean] = finish(dq[0].T, True, 0.125)
    dqkv_ref[0, noisy] = finish(dq[1].T, True, 0.125)


def attend_back(qkv, mixed, grad, logs, tables, cosine, sine, pairs=None, gain=None):
    _, copies, length, width = qkv.shape
    steps = width // LANES
    table_spec = pl.BlockSpec((length, LANES), lambda i: (0, 0), pipeline_mode=pl.Buffered(1))
    row_spec = pl.BlockSpec((copies, length, LANES), lambda i: (0, 0, i))
    three = pl.BlockSpec((3, copies, length, LANES), lambda i: (0, 0, 0, i))
    anywhere = pl.BlockSpec(memory_space=pl.ANY)

    def fixed(shape):
        return pl.BlockSpec(shape, lambda i: (0, 0), pipeline_mode=pl.Buffered(1))

    more_in, more_specs, more_shapes, more_out, more_scratch = [], [], [], [], []
    body, params = attend_back_kernel, {}
    if pairs is not None:
        assert steps == 6
        body = functools.partial(attend_back_sum_kernel, orders=(DOWN, UP, OUT))
        params = dict(collective_id=1, has_side_effects=True)
        for keep, send in pairs:
            slots, share, columns = keep.shape
            more_in += [keep, send]
            more_specs += [anywhere] * 2
            more_shapes.append(jax.ShapeDtypeStruct((share, columns), f32))
            more_out.append(fixed((share, columns)))
            more_scratch += SlabSum.scratch(slots, share, columns)
        more_in.append(gain)
        more_specs.append(fixed((8, width)))
        more_shapes.append(jax.ShapeDtypeStruct((8, width), f32))
        more_out.append(fixed((8, width)))
        more_scratch += GainSum.scratch(ALL, width)
    return pl.pallas_call(
        body,
        name="attend_back",
        grid_spec=pltpu.PrefetchScalarGridSpec(
            num_scalar_prefetch=0,
            grid=(steps,),
            in_specs=[three, row_spec, row_spec, pl.BlockSpec((copies, 1, 2, length), lambda i: (0, i, 0, 0))]
            + [table_spec] * 6
            + more_specs,
            out_specs=[three, *more_out],
            scratch_shapes=[
                pltpu.VMEM((3, 2, length, LANES), bf16),
                pltpu.VMEM((2, 2, length, LANES), bf16),
                pltpu.VMEM((2, length, LANES), bf16),
                pltpu.VMEM((2, length, LANES), bf16),
                pltpu.VMEM((2, LANES, length), bf16),
                pltpu.VMEM((2, 2, length, LANES), bf16),
                pltpu.VMEM((2, 2, length), f32),
                pltpu.VMEM((2, LANES, length), f32),
                pltpu.VMEM((length, LANES), f32),
                pltpu.VMEM((length, LANES), f32),
                *more_scratch,
            ],
        ),
        out_shape=[jax.ShapeDtypeStruct((3, copies, length, width), bf16), *more_shapes],
        compiler_params=pltpu.CompilerParams(vmem_limit_bytes=60 << 20, **params),
        cost_estimate=pl.CostEstimate(
            flops=20 * length * length * width, bytes_accessed=30 * length * width, transcendentals=length * length * 12
        ),
    )(qkv, mixed, grad, logs, *tables, cosine, sine, *more_in)


ROOT = math.sqrt(2.0 / math.pi)


def feed_kernel(side_ref, x_own, x_away, mixed_ref, g_own, g_away, gain_ref, wo_all, wu_all, wd_all,
                out_own, out_away, act_ref, du_ref, h2_ref, dmid_ref, dbr_ref, dmix_ref, dgain_ref,
                wo_ref, wu_ref, wd_ref, sems, *, half):
    groups, rows, width = wo_ref.shape
    fold = wu_ref.shape[0]

    @pl.when(pl.program_id(0) == 0)
    def _():
        copies = [pltpu.make_async_copy(wo_all, wo_ref, sems.at[0])]
        for n in range(fold):
            cols = wu_all.at[:, :, n * width : (n + 1) * width]
            copies.append(pltpu.make_async_copy(cols, wu_ref.at[n], sems.at[1 + n]))
        copies.append(pltpu.make_async_copy(wd_all, wd_ref, sems.at[1 + fold]))
        for copy in copies:
            copy.start()
        for copy in copies:
            copy.wait()

    def down(c):
        per = groups // fold
        return wd_ref[c * per : (c + 1) * per].reshape(width, width)

    wo = wo_ref[...].reshape(width, width)
    gain = gain_ref[...].astype(f32)
    middle = read_rows(x_own, x_away, half).astype(f32) + mm(mixed_ref[...], wo)
    center = middle - jnp.mean(middle, axis=1, keepdims=True)
    spread = jnp.mean(center * center, axis=1, keepdims=True)
    inv = lax.rsqrt(spread + 1e-5)
    norm = center * inv
    hidden = (norm * gain).astype(bf16)
    h2_ref[...] = hidden
    grad = read_rows(g_own, g_away, half)
    out = middle
    dh = jnp.zeros_like(middle)
    for c in range(fold):
        cols = slice(c * width, (c + 1) * width)
        up = wu_ref[c].reshape(width, width)
        u = mm(hidden, up)
        da = mm_t(grad, down(c)).astype(bf16).astype(f32)
        sq = u * u
        t = jnp.tanh(u * (ROOT + (ROOT * 0.044715) * sq))
        part = 0.5 + 0.5 * t
        act = (u * part).astype(bf16)
        slope = part + (u * (part * (1.0 - t))) * (ROOT + (3 * ROOT * 0.044715) * sq)
        du = (da * slope).astype(bf16)
        act_ref[:, cols] = act
        du_ref[:, cols] = du
        out = out + mm(act, down(c))
        dh = dh + mm_t(du, up)
    low = out.astype(bf16)

    @pl.when(pl.program_id(0) < half)
    def _():
        out_own[...] = low

    @pl.when(pl.program_id(0) >= half)
    def _():
        out_away[...] = low

    @pl.when(pl.program_id(0) == 0)
    def _():
        dgain_ref[...] = jnp.zeros_like(dgain_ref)

    dgain_ref[...] += jnp.sum((dh * norm).reshape(-1, 8, width), axis=0)
    e = dh * gain
    dmid = grad.astype(f32) + inv * (
        e - jnp.mean(e, axis=1, keepdims=True) - norm * jnp.mean(e * norm, axis=1, keepdims=True)
    )
    dmid_ref[...] = dmid
    dbr = dmid.astype(bf16)
    dbr_ref[...] = dbr
    dmix_ref[...] = mm_t(dbr, wo).astype(bf16)


def feed(side, x_own, x_away, mixed, g_own, g_away, gain, weights, tile=512):
    tokens, width = mixed.shape
    groups, rows, ff = weights[1].shape
    fold = ff // width
    half = tokens // 2 // tile
    row = pl.BlockSpec((tile, width), lambda i, s: (i, 0))
    wide = pl.BlockSpec((tile, ff), lambda i, s: (i, 0))
    own, away = row_specs(tile, width, half)

    def keep(shape):
        return pl.BlockSpec(shape, lambda i, s: (0, 0), pipeline_mode=pl.Buffered(1))

    return pl.pallas_call(
        functools.partial(feed_kernel, half=half),
        name="feed",
        grid_spec=pltpu.PrefetchScalarGridSpec(
            num_scalar_prefetch=1,
            grid=(2 * half,),
            in_specs=[own, away, row, own, away, keep((1, width)), *[pl.BlockSpec(memory_space=pl.ANY)] * 3],
            out_specs=[own, away, wide, wide, row, row, row, row, pl.BlockSpec((8, width), lambda i, s: (0, 0))],
            scratch_shapes=[
                pltpu.VMEM((groups, rows, width), bf16),
                pltpu.VMEM((fold, groups, rows, width), bf16),
                pltpu.VMEM((groups, fold * rows, width), bf16),
                pltpu.SemaphoreType.DMA((2 + fold,)),
            ],
        ),
        out_shape=[
            jax.ShapeDtypeStruct((1, 2, tokens // 2, width), bf16),
            jax.ShapeDtypeStruct((tokens // 2, width), bf16),
            jax.ShapeDtypeStruct((tokens, ff), bf16),
            jax.ShapeDtypeStruct((tokens, ff), bf16),
            jax.ShapeDtypeStruct((tokens, width), bf16),
            jax.ShapeDtypeStruct((tokens, width), f32),
            jax.ShapeDtypeStruct((tokens, width), bf16),
            jax.ShapeDtypeStruct((tokens, width), bf16),
            jax.ShapeDtypeStruct((8, width), f32),
        ],
        compiler_params=pltpu.CompilerParams(vmem_limit_bytes=60 << 20),
        cost_estimate=pl.CostEstimate(
            flops=tokens * width * (4 * width + 8 * ff), bytes_accessed=tokens * (width * 18 + ff * 4),
            transcendentals=tokens * ff
        ),
    )(side, x_own, x_away, mixed, g_own, g_away, gain, *weights)


def arranged(slot, order):
    return sum((slot >> bit & 1) << (len(order) - 1 - n) for n, bit in enumerate(order))


def weight_kernel(me_ref, left_ref, *refs, share, split, order):
    weight_slabs(me_ref[0], left_ref, *refs, share=share, split=split, order=order)


def weight_slabs(me, left_ref, *refs, share, split, order):
    right_refs, (keep_ref, send_ref, scr) = refs[:-3], refs[-3:]
    if split:
        own_ref, away_ref = right_refs
        half = own_ref.shape[0]
        total = t_mm(left_ref[:half], own_ref[...]) + t_mm(left_ref[half:], away_ref[...])
    else:
        total = t_mm(left_ref[...], right_refs[0][...])
    slabs = total.shape[0] // share
    scr[...] = total.reshape(scr.shape)
    low_me = lax.rem(me, slabs)
    for slot in range(slabs):
        source = jnp.bitwise_xor(low_me, slot)
        into = send_ref if slot % 2 else keep_ref
        into[arranged(slot // 2, order)] = scr[source].astype(bf16)


def weight_grad_columns(me, left, right, block, share, order, name):
    tokens, dl = left.shape
    dr = right.shape[1]
    peers = dl // share
    shape = (peers // 2, share, dr)
    out = pl.BlockSpec((peers // 2, share, block), lambda j, m: (0, 0, j))
    return pl.pallas_call(
        functools.partial(weight_kernel, share=share, split=False, order=order),
        name=name,
        grid_spec=pltpu.PrefetchScalarGridSpec(
            num_scalar_prefetch=1,
            grid=(dr // block,),
            in_specs=[
                pl.BlockSpec((tokens, dl), lambda j, m: (0, 0), pipeline_mode=pl.Buffered(1)),
                pl.BlockSpec((tokens, block), lambda j, m: (0, j)),
            ],
            out_specs=[out, out],
            scratch_shapes=[pltpu.VMEM((peers, share, block), f32)],
        ),
        out_shape=[jax.ShapeDtypeStruct(shape, bf16)] * 2,
        compiler_params=pltpu.CompilerParams(vmem_limit_bytes=48 << 20),
        cost_estimate=pl.CostEstimate(
            flops=2 * tokens * dl * dr, bytes_accessed=2 * tokens * (dl + dr) + 2 * dl * dr, transcendentals=0
        ),
    )(me, left, right)


def weight_grad_rows(me, left, own, away, block, share, name):
    tokens, dl = left.shape
    length, dr = away.shape
    slabs = block // share
    steps = dl // block
    assert steps == 4
    shape = (2, slabs // 2, 2, share, dr)
    out = pl.BlockSpec((None, slabs // 2, None, share, dr), lambda j, m: (lax.div(j, 2), 0, lax.rem(j, 2), 0, 0))
    bits = (slabs // 2).bit_length() - 1

    def place(j, m):
        return (0, jnp.bitwise_xor(j, lax.div(m[0], slabs)))

    return pl.pallas_call(
        functools.partial(weight_kernel, share=share, split=True, order=tuple(range(bits))),
        name=name,
        grid_spec=pltpu.PrefetchScalarGridSpec(
            num_scalar_prefetch=1,
            grid=(steps,),
            in_specs=[
                pl.BlockSpec((tokens, block), place),
                pl.BlockSpec((None, None, length, dr), lambda j, m: (0, m[1], 0, 0), pipeline_mode=pl.Buffered(1)),
                pl.BlockSpec((length, dr), lambda j, m: (0, 0), pipeline_mode=pl.Buffered(1)),
            ],
            out_specs=[out, out],
            scratch_shapes=[pltpu.VMEM((slabs, share, dr), f32)],
        ),
        out_shape=[jax.ShapeDtypeStruct(shape, bf16)] * 2,
        compiler_params=pltpu.CompilerParams(vmem_limit_bytes=48 << 20),
        cost_estimate=pl.CostEstimate(
            flops=2 * tokens * dl * dr, bytes_accessed=2 * tokens * (dl + dr) + 2 * dl * dr, transcendentals=0
        ),
    )(me, left, own, away)


def qkv_grad_kernel(hidden_ref, dqkv_ref, gain_ref, out_ref, gain_out, scr, *refs, share):
    count = len(QKV)
    width = scr.shape[-1]
    per = len(refs[:-3]) // count
    sums = []
    for n, order in enumerate(QKV):
        send, keep, *got, sems = refs[n * per : (n + 1) * per]
        sums.append(SlabSum(order, keep, send, got, sems))
    gain = GainSum(ALL, *refs[-3:])
    me = lax.axis_index("stream") * lax.axis_size("batch") + lax.axis_index("batch")
    step = pl.program_id(0)

    @pl.when(step == 0)
    def _():
        greet([partner(bit) for bit in ALL])
        gain.start(gain_ref[...])

    for n, one in enumerate(sums):

        @pl.when(step == n)
        def _():
            weight_slabs(me, hidden_ref, dqkv_ref, one.keep, one.send, scr, share=share, split=False, order=tuple(
                {-1: 3, 1: 0, 2: 1, 3: 2}[bit] for bit in QKV[n]
            ))
            one.start()
            for earlier in range(n):
                sums[earlier].step(n - earlier)
            if n:
                gain.step(n)

    @pl.when(step == count - 1)
    def _():
        for number in range(2, 5 + count - 1):
            for n, one in enumerate(sums):
                now = number - n
                if count - 1 - n < now < 5:
                    one.step(now)
            if count - 1 < number < 5:
                gain.step(number)
        for n, one in enumerate(sums):
            one.finish(out_ref, slice(n * width, (n + 1) * width))
        gain.finish(gain_out)


def qkv_grad(hidden, dqkv, gain, share):
    tokens, width = hidden.shape
    slots = width // share // 2
    fixed = pl.BlockSpec((8, width), lambda j: (0, 0), pipeline_mode=pl.Buffered(1))
    scratch = []
    for _ in range(3):
        scratch += [pltpu.VMEM((slots, share, width), bf16), *SlabSum.scratch(slots, share, width)]
    return pl.pallas_call(
        functools.partial(qkv_grad_kernel, share=share),
        name="grad_qkv",
        grid_spec=pltpu.PrefetchScalarGridSpec(
            num_scalar_prefetch=0,
            grid=(3,),
            in_specs=[
                pl.BlockSpec((tokens, width), lambda j: (0, 0), pipeline_mode=pl.Buffered(1)),
                pl.BlockSpec((None, tokens, width), lambda j: (j, 0, 0)),
                fixed,
            ],
            out_specs=[pl.BlockSpec((share, 3 * width), lambda j: (0, 0), pipeline_mode=pl.Buffered(1)), fixed],
            scratch_shapes=[pltpu.VMEM((2 * slots, share, width), f32), *scratch, *GainSum.scratch(ALL, width)],
        ),
        out_shape=[jax.ShapeDtypeStruct((share, 3 * width), f32), jax.ShapeDtypeStruct((8, width), f32)],
        compiler_params=pltpu.CompilerParams(vmem_limit_bytes=60 << 20, collective_id=2, has_side_effects=True),
        cost_estimate=pl.CostEstimate(
            flops=6 * tokens * width * width, bytes_accessed=8 * tokens * width, transcendentals=0
        ),
    )(hidden, dqkv, gain)


def project_back_kernel(side_ref, x_ref, gain_ref, w_ref, dqkv_ref, dmid_ref, dx_ref, dgain_ref):
    x = x_ref[...].astype(f32)
    width = x.shape[1]
    center = x - jnp.mean(x, axis=1, keepdims=True)
    spread = jnp.mean(center * center, axis=1, keepdims=True)
    inv = lax.rsqrt(spread + 1e-5)
    norm = center * inv
    dh = mm_t(dqkv_ref[0], w_ref[:, :width])
    dh = dh + mm_t(dqkv_ref[1], w_ref[:, width : 2 * width])
    dh = dh + mm_t(dqkv_ref[2], w_ref[:, 2 * width :])

    @pl.when(pl.program_id(0) == 0)
    def _():
        dgain_ref[...] = jnp.zeros_like(dgain_ref)

    dgain_ref[...] += jnp.sum((dh * norm).reshape(-1, 8, width), axis=0)
    e = dh * gain_ref[...].astype(f32)
    dx_ref[...] = (dmid_ref[...] + inv * (
        e - jnp.mean(e, axis=1, keepdims=True) - norm * jnp.mean(e * norm, axis=1, keepdims=True)
    )).astype(dx_ref.dtype)


def project_back(side, x, gain, w, dqkv, dmid, away, tile=256):
    width = x.shape[-1]
    length = dmid.shape[0] // 2
    half = length // tile
    first = half if away else 0
    if away:
        x_spec = pl.BlockSpec((tile, width), lambda i, s: (i, 0))
        out_spec, out_shape = x_spec, jax.ShapeDtypeStruct((length, width), bf16)
    else:
        x_spec = pl.BlockSpec((None, None, tile, width), lambda i, s: (0, s[0], i, 0))
        out_spec, out_shape = x_spec, jax.ShapeDtypeStruct((1, 2, length, width), f32)
    return pl.pallas_call(
        project_back_kernel,
        name="project_back_away" if away else "project_back_own",
        grid_spec=pltpu.PrefetchScalarGridSpec(
            num_scalar_prefetch=1,
            grid=(half,),
            in_specs=[
                x_spec,
                pl.BlockSpec((1, width), lambda i, s: (0, 0)),
                pl.BlockSpec((width, 3 * width), lambda i, s: (0, 0), pipeline_mode=pl.Buffered(1)),
                pl.BlockSpec((3, tile, width), lambda i, s: (0, i + first, 0)),
                pl.BlockSpec((tile, width), lambda i, s: (i + first, 0)),
            ],
            out_specs=[out_spec, pl.BlockSpec((8, width), lambda i, s: (0, 0))],
        ),
        out_shape=[out_shape, jax.ShapeDtypeStruct((8, width), f32)],
        compiler_params=pltpu.CompilerParams(vmem_limit_bytes=48 << 20),
        cost_estimate=pl.CostEstimate(
            flops=6 * length * width * width, bytes_accessed=length * width * 16, transcendentals=0
        ),
    )(side, x, gain, w, dqkv, dmid)


def flip(x, bit):
    axis, by = ("stream", 1) if bit < 0 else ("batch", 1 << bit)
    return lax.ppermute(x, axis, [(i, i ^ by) for i in range(lax.axis_size(axis))])


def after(value, *others):
    return lax.optimization_barrier((value, *others))[0]


def shards(tokens, cotangent, lengths, ln1_gain, w_qkv, w_out, ln2_gain, w_up, w_down):
    side = lax.axis_index("stream")
    at = lax.axis_index("batch")
    _, rows_dev, length, width = tokens.shape
    assert rows_dev == 2
    ff = w_up.shape[1]
    peers = lax.axis_size("batch")
    small = peers == 16 and width % (16 * peers) == 0
    side_array = side.reshape(1).astype(jnp.int32)
    index = side * peers + at
    me = jnp.stack([index if small else 0 * index, side]).astype(jnp.int32)
    share = width // (2 * peers)

    cosine, sine = rotary_tables(length)
    tables = mask_tables(length, jnp.take(lengths, side))
    if small:
        rows = width // peers
        gains = jnp.zeros((8, width), f32)
        gains = lax.dynamic_update_slice(gains, jnp.stack([ln1_gain, ln2_gain]).astype(f32), (0, at * rows))
        qkv, hidden, x_away, w_qkv_all, gains = first(w_qkv, gains, tokens, cosine, sine)
        qkv4 = qkv.reshape(3, 2, length, width)
        w_qkv_all = w_qkv_all.reshape(width, 3 * width)
        gain_one, gain_two = gains[0:1], gains[1:2]
        mixed, logs, *weights, g_away = attend(qkv4, tables, (w_out, w_up, w_down), cotangent)
    else:

        def whole(x):
            return lax.all_gather(x, "batch", axis=0, tiled=True)

        x_away = flip(lax.dynamic_index_in_dim(tokens[0], 1 - side, 0, False), -1)
        g_away = flip(lax.dynamic_index_in_dim(cotangent[0], 1 - side, 0, False), -1)
        w_qkv_all = whole(w_qkv)
        gain_one, gain_two = (whole(gain)[None].astype(f32) for gain in (ln1_gain, ln2_gain))
        weights = [whole(w).reshape(16, -1, w.shape[1]) for w in (w_out, w_up, w_down)]
        qkv, hidden = project(side_array, tokens, x_away, gain_one, w_qkv_all, cosine, sine)
        qkv4 = qkv.reshape(3, 2, length, width)
        mixed, logs = attend(qkv4, tables)
    mixed2 = mixed.reshape(2 * length, width)
    out, out_away, act, du, h2, dmid, dbr, dmix, dgain_two = feed(
        side_array, tokens, x_away, mixed2, cotangent, g_away, gain_two, weights
    )

    def place(result, away):
        away = flip(away, -1).astype(result.dtype)
        return lax.dynamic_update_slice(result, away[None, None], (0, 1 - side, 0, 0))

    out = place(out, out_away)
    unit = share if small else width // 32
    places = {-1: 3, 1: 0, 2: 1, 3: 2}

    def columns_grad(left, right, order, name):
        return weight_grad_columns(me, left, right, width, unit, [places[bit] for bit in order], name)

    down = weight_grad_rows(me, act, cotangent, g_away, width, ff // width * unit, "grad_down")
    down = [part.reshape(16, -1, width) for part in down]
    up = columns_grad(h2, du, UP, "grad_up")
    wo = columns_grad(mixed2, dbr, OUT, "grad_out")
    dmix = after(dmix.reshape(2, length, width), out)
    common = qkv4, mixed, dmix, logs, tables, cosine, sine
    if small:
        dqkv, down, up, wo, dgain_two = attend_back(*common, (down, up, wo), dgain_two)
    else:
        dqkv, = attend_back(*common)
    dqkv3 = dqkv.reshape(3, 2 * length, width)
    dx_away, dgain_away = project_back(side_array, x_away, gain_one, w_qkv_all, dqkv3, dmid, True)
    dx, dgain_own = project_back(side_array, tokens, gain_one, w_qkv_all, dqkv3, dmid, False)
    dgain_one = dgain_own + dgain_away
    if small:
        wq, dgain_one = qkv_grad(hidden, dqkv3, dgain_one, share)
    dx = place(dx, dx_away)
    dgain_one, dgain_two = (jnp.sum(g, axis=0, keepdims=True) for g in (dgain_one, dgain_two))
    if not small:

        def scatter(pair, order):
            slots = jnp.stack(pair, axis=1)
            natural = [arranged(n, order) for n in range(16)]
            rows = slots[jnp.array(natural)].reshape(-1, slots.shape[-1])
            return lax.psum_scatter(rows, ("stream", "batch"), scatter_dimension=0, tiled=True).astype(f32)

        parts = [columns_grad(hidden, dqkv3[n], QKV[n], "grad_qkv") for n in range(3)]
        down, up, wo, *parts = (
            scatter(pair, [places[bit] for bit in order])
            for pair, order in zip((down, up, wo, *parts), (DOWN, UP, OUT, *QKV))
        )
        wq = jnp.concatenate(parts, axis=1)
        dgain_one, dgain_two = lax.psum((dgain_one, dgain_two), ("stream", "batch"))
    begin = index * share
    dgain_one, dgain_two = (lax.dynamic_slice(g[0], (begin,), (share,)) for g in (dgain_one, dgain_two))
    return out, dx, dgain_one, wq, wo, dgain_two, up, down


def solution(mesh):
    token = P("stream", "batch", None, None)
    vector, matrix = P("batch"), P("batch", None)
    out_vector, out_matrix = P(("stream", "batch")), P(("stream", "batch"), None)
    return jax.shard_map(
        shards,
        mesh=mesh,
        in_specs=(token, token, vector, vector, matrix, matrix, vector, matrix, matrix),
        out_specs=(token, token, out_vector, out_matrix, out_matrix, out_vector, out_matrix, out_matrix),
        check_vma=False,
    )
```

```python
import functools
import math

import jax
import jax.numpy as jnp
from jax import lax
from jax.experimental import pallas as pl
from jax.experimental.pallas import tpu as pltpu
from jax.sharding import PartitionSpec as P

HD = 64
BLOCK = 16
LANES = 128
TILE = 256
BIG = -1e30
f32, bf16 = jnp.float32, jnp.bfloat16


def mm(a, b):
    return lax.dot_general(a, b, (((1,), (0,)), ((), ())), preferred_element_type=f32)


def mm_t(a, b):
    return lax.dot_general(a, b, (((1,), (1,)), ((), ())), preferred_element_type=f32)


def t_mm(a, b):
    return lax.dot_general(a, b, (((0,), (0,)), ((), ())), preferred_element_type=f32)


def rotary_tables(length):
    half = HD // 2
    places = jnp.arange(length).astype(f32)
    rates = jnp.exp(jnp.arange(half).astype(f32) * (-2.0 * math.log(10000.0) / HD))
    angles = places[:, None] * rates[None, :]
    cosine, sine = jnp.cos(angles), jnp.sin(angles)
    return (
        jnp.concatenate([cosine] * 4, axis=1),
        jnp.concatenate([-sine, sine, -sine, sine], axis=1),
    )


def half_partner(x):
    lane = lax.broadcasted_iota(jnp.int32, x.shape, 1)
    low = lax.rem(lane, HD) < HD // 2
    return jnp.where(low, pltpu.roll(x, LANES - HD // 2, 1), pltpu.roll(x, HD // 2, 1))


MESH = pl.DeviceIdType.MESH


def partner(bit):
    side, at = lax.axis_index("stream"), lax.axis_index("batch")
    return (1 - side, at) if bit < 0 else (side, jnp.bitwise_xor(at, 1 << bit))


def greet(others):
    barrier = pltpu.get_barrier_semaphore()
    for other in others:
        pl.semaphore_signal(barrier, inc=1, device_id=other, device_id_type=MESH)
    pl.semaphore_wait(barrier, len(others))


def line_partners():
    side, at = lax.axis_index("stream"), lax.axis_index("batch")
    return [partner(-1)] + [(side, jnp.bitwise_xor(at, mask)) for mask in (1, 2, 4, 8, 12)]


class LineGather:
    SENDS = 29

    def __init__(self, chunks, send_sems, recv_sems, local_sems):
        self.chunks, self.send_sems, self.recv_sems, self.local_sems = chunks, send_sems, recv_sems, local_sems
        self.side, self.at = lax.axis_index("stream"), lax.axis_index("batch")
        self.z = lax.div(self.at, 4)

    @staticmethod
    def scratch(count):
        return [
            pltpu.SemaphoreType.DMA((count, LineGather.SENDS)),
            pltpu.SemaphoreType.DMA((count, 16)),
            pltpu.SemaphoreType.DMA((count,)),
        ]

    def copy(self, chunk, shard, target, number, own=False):
        source, place = self.chunks[chunk]
        return pltpu.make_async_remote_copy(
            src_ref=source if own else place(shard),
            dst_ref=place(shard),
            send_sem=self.send_sems.at[chunk, number],
            recv_sem=self.recv_sems.at[chunk, shard],
            device_id=(self.side, target),
            device_id_type=MESH,
        )

    def local(self, chunk):
        source, place = self.chunks[chunk]
        return pltpu.make_async_copy(source, place(self.at), self.local_sems.at[chunk])

    def sends(self, phase):
        at, z = self.at, self.z
        across, core = jnp.bitwise_xor(at, 2), jnp.bitwise_xor(at, 1)
        up, down = (at + 4, z < 3), (at - 4, z > 0)
        other = jnp.bitwise_xor
        if phase == 0:
            yield None, at, [(*up, 0), (*down, 1), (across, None, 2), (core, None, 3)]
        if 1 <= phase <= 3:
            n = 4 + 6 * (phase - 1)
            yield z >= phase, at - 4 * phase, [(*up, n), (across, None, n + 1), (core, None, n + 2)]
            yield z + phase <= 3, at + 4 * phase, [(*down, n + 3), (across, None, n + 4), (core, None, n + 5)]
        if phase == 1:
            yield None, across, [(core, None, 22)]
        if 2 <= phase <= 4:
            d, n = phase - 1, 23 + 2 * (phase - 2)
            yield z >= d, other(at - 4 * d, 2), [(core, None, n)]
            yield z + d <= 3, other(at + 4 * d, 2), [(core, None, n + 1)]

    def each(self, phase, act):
        for when, shard, sends in self.sends(phase):

            def run():
                act(shard, None, None)
                for target, whether, number in sends:
                    if whether is None:
                        act(shard, target, number)
                    else:
                        pl.when(whether)(lambda: act(shard, target, number))

            if when is None:
                run()
            else:
                pl.when(when)(run)

    def phase(self, chunk, phase):
        def act(shard, target, number):
            if target is None:
                if phase == 0:
                    self.local(chunk).start()
                else:
                    self.copy(chunk, shard, self.at, 0).wait_recv()
            else:
                self.copy(chunk, shard, target, number, own=phase == 0).start()

        self.each(phase, act)

    def finish(self):
        for chunk in range(len(self.chunks)):
            for n in range(8):
                shard = jnp.bitwise_xor(lax.rem(self.at, 2), 1) + 2 * n
                self.copy(chunk, shard, self.at, 0).wait_recv()
            self.local(chunk).wait()
            for phase in range(5):

                def act(shard, target, number):
                    if target is not None:
                        self.copy(chunk, shard, target, number, own=phase == 0).wait_send()

                self.each(phase, act)


class SlabSum:
    def __init__(self, order, keep, send, got, sems, load=None):
        self.order, self.keep, self.send, self.got, self.sems, self.load = (0, *order), keep, send, got, sems, load

    @staticmethod
    def scratch(slots, share, columns):
        steps = slots.bit_length()
        return [
            *[pltpu.VMEM((max(slots >> n, 1), share, columns), bf16) for n in (0, *range(steps))],
            pltpu.SemaphoreType.DMA((2 * steps + 1,)),
        ]

    def copy(self, step):
        count = self.got[step].shape[0]
        return pltpu.make_async_remote_copy(
            src_ref=self.send if step == 0 else self.keep.at[pl.ds(count, count)],
            dst_ref=self.got[step],
            send_sem=self.sems.at[2 * step],
            recv_sem=self.sems.at[2 * step + 1],
            device_id=partner(self.order[step]),
            device_id_type=MESH,
        )

    def loading(self):
        return pltpu.make_async_copy(self.load, self.keep, self.sems.at[2 * len(self.order)])

    def start(self):
        self.copy(0).start()
        if self.load is not None:
            self.loading().start()

    def step(self, step):
        if step == 1 and self.load is not None:
            self.loading().wait()
        self.copy(step - 1).wait_recv()
        got = self.got[step - 1]

        @pl.loop(0, got.shape[0])
        def _(n):
            self.keep[n] = (self.keep[n].astype(f32) + got[n].astype(f32)).astype(bf16)

        self.copy(step).start()

    def finish(self, out_ref, width, first=0):
        last = len(self.order) - 1
        self.copy(last).wait_recv()
        total = self.keep[0].astype(f32) + self.got[last][0].astype(f32)
        share = out_ref.shape[0]
        by = total.shape[0] // share
        block = out_ref.shape[1] if by == 1 else width // by
        for n in range(total.shape[1] // block):
            for i in range(by):
                at = first + (n * by + i) * block
                out_ref[:, at : at + block] = total[i * share : (i + 1) * share, n * block : (n + 1) * block]
        for step in range(len(self.order)):
            self.copy(step).wait_send()


ALL = (-1, 0, 1, 2, 3)
LATE = (0, 1, 2, 3, -1)


class GainSum:
    def __init__(self, bits, held, got, sems):
        self.bits, self.held, self.got, self.sems = bits, held, got, sems

    @staticmethod
    def scratch(bits, width):
        steps = len(bits)
        return [
            pltpu.VMEM((steps, 8, width), f32),
            pltpu.VMEM((steps, 8, width), f32),
            pltpu.SemaphoreType.DMA((2 * steps,)),
        ]

    def copy(self, step):
        return pltpu.make_async_remote_copy(
            src_ref=self.held.at[step],
            dst_ref=self.got.at[step],
            send_sem=self.sems.at[2 * step],
            recv_sem=self.sems.at[2 * step + 1],
            device_id=partner(self.bits[step]),
            device_id_type=MESH,
        )

    def start(self, value):
        self.held[0] = value
        self.copy(0).start()

    def step(self, step):
        self.copy(step - 1).wait_recv()
        self.held[step] = self.held[step - 1] + self.got[step - 1]
        self.copy(step).start()

    def finish(self, out_ref):
        last = len(self.bits) - 1
        self.copy(last).wait_recv()
        out_ref[...] = self.held[last] + self.got[last]
        for step in range(len(self.bits)):
            self.copy(step).wait_send()


def row_specs(tile, width, half):
    own = pl.BlockSpec((None, None, tile, width), lambda i, s: (0, s[0], jnp.minimum(i, half - 1), 0))
    away = pl.BlockSpec((tile, width), lambda i, s: (jnp.maximum(i - half, 0), 0))
    return own, away


def read_rows(own_ref, away_ref, half):
    return jnp.where(pl.program_id(0) < half, own_ref[...], away_ref[...])


def project_kernel(side_ref, own_ref, away_ref, gain_ref, w_ref, cos_ref, sin_ref, out_ref, hidden_ref, *, half):
    width = own_ref.shape[-1]
    project_tile(read_rows(own_ref, away_ref, half), gain_ref[...], lambda part: w_ref[:, part * width : (part + 1) * width],
                 cos_ref, sin_ref, out_ref, hidden_ref)


def project_tile(x, gain, weights, cos_ref, sin_ref, out_ref, hidden_ref):
    x = x.astype(f32)
    width = x.shape[1]
    center = x - jnp.mean(x, axis=1, keepdims=True)
    spread = jnp.mean(center * center, axis=1, keepdims=True)
    hidden = (center * lax.rsqrt(spread + 1e-5) * gain.astype(f32)).astype(bf16)
    hidden_ref[...] = hidden
    cosine, sine = cos_ref[...], sin_ref[...]
    for part in range(3):
        rows = mm(hidden, weights(part))
        for pair in range(width // LANES):
            cols = slice(pair * LANES, (pair + 1) * LANES)
            field = rows[:, cols]
            if part < 2:
                field = field * cosine + half_partner(field) * sine
            if part == 0:
                field = field * 0.125
            out_ref[part, :, cols] = field.astype(bf16)


def project(side, own, away, gain, w, cosine, sine, tile=512):
    length, width = away.shape
    tokens, half = 2 * length, length // tile
    table = pl.BlockSpec((tile, LANES), lambda i, s: (lax.rem(i, half), 0))
    return pl.pallas_call(
        functools.partial(project_kernel, half=half),
        name="project",
        grid_spec=pltpu.PrefetchScalarGridSpec(
            num_scalar_prefetch=1,
            grid=(2 * half,),
            in_specs=[
                *row_specs(tile, width, half),
                pl.BlockSpec((1, width), lambda i, s: (0, 0)),
                pl.BlockSpec((width, 3 * width), lambda i, s: (0, 0), pipeline_mode=pl.Buffered(1)),
                table,
                table,
            ],
            out_specs=[
                pl.BlockSpec((3, tile, width), lambda i, s: (0, i, 0)),
                pl.BlockSpec((tile, width), lambda i, s: (i, 0)),
            ],
        ),
        out_shape=[jax.ShapeDtypeStruct((3, tokens, width), bf16), jax.ShapeDtypeStruct((tokens, width), bf16)],
        compiler_params=pltpu.CompilerParams(vmem_limit_bytes=48 << 20),
        cost_estimate=pl.CostEstimate(
            flops=6 * tokens * width * width, bytes_accessed=tokens * width * 10 + 6 * width * width, transcendentals=0
        ),
    )(side, own, away, gain, w, cosine, sine)


def first_kernel(shard_ref, gain_ref, tokens_ref, own_ref, cos_ref, sin_ref, qkv_ref, hidden_ref, away_out, w_out, gains_out,
                 w_all, away, rows, swap_sems, out_sems, send_sems, recv_sems, local_sems, *gain_scratch, half):
    side, at = lax.axis_index("stream"), lax.axis_index("batch")
    step = pl.program_id(0)
    width = own_ref.shape[-1]
    tile = own_ref.shape[-2]
    swap = pltpu.make_async_remote_copy(
        src_ref=tokens_ref.at[0, 1 - side],
        dst_ref=away,
        send_sem=swap_sems.at[0],
        recv_sem=swap_sems.at[1],
        device_id=(1 - side, at),
        device_id_type=MESH,
    )

    def chunk(n):
        cols = slice(n * width, (n + 1) * width)
        return shard_ref.at[:, cols], lambda shard: w_all.at[shard, :, cols]

    weights = LineGather([chunk(n) for n in range(3)], send_sems, recv_sems, local_sems)
    gain = GainSum((0, 1, 2, 3), *gain_scratch)
    keeps = [
        pltpu.make_async_copy(w_all, w_out, out_sems.at[0]),
        pltpu.make_async_copy(away, away_out, out_sems.at[1]),
    ]

    @pl.when(step == 0)
    def _():
        greet(line_partners())
        swap.start()
        gain.start(gain_ref[...])
        for phase in range(5):
            for n in range(3):
                weights.phase(n, phase)
            if 1 <= phase <= 3:
                gain.step(phase)
        gain.finish(gains_out)
        weights.finish()
        keeps[0].start()

    @pl.when(step == half)
    def _():
        swap.wait()
        keeps[1].start()

    @pl.when(step < half)
    def _():
        rows[...] = own_ref[...]

    @pl.when(step >= half)
    def _():
        rows[...] = away[pl.ds(pl.multiple_of((step - half) * tile, tile), tile), :]

    project_tile(rows[...], gains_out[0:1, :], lambda part: w_all[:, :, part * width : (part + 1) * width].reshape(width, width),
                 cos_ref, sin_ref, qkv_ref, hidden_ref)

    @pl.when(step == pl.num_programs(0) - 1)
    def _():
        for keep in keeps:
            keep.wait()


def first(shard, gain, tokens, cosine, sine, tile=512):
    _, _, length, width = tokens.shape
    rows = shard.shape[0]
    half = length // tile
    anywhere = pl.BlockSpec(memory_space=pl.ANY)
    table = pl.BlockSpec((tile, LANES), lambda i: (lax.rem(i, half), 0))
    small = pl.BlockSpec((8, width), lambda i: (0, 0))
    return pl.pallas_call(
        functools.partial(first_kernel, half=half),
        name="first",
        grid=(2 * half,),
        in_specs=[
            anywhere,
            small,
            anywhere,
            pl.BlockSpec((None, None, tile, width), lambda i: (0, lax.axis_index("stream"), jnp.minimum(i, half - 1), 0)),
            table,
            table,
        ],
        out_specs=[
            pl.BlockSpec((3, tile, width), lambda i: (0, i, 0)),
            pl.BlockSpec((tile, width), lambda i: (i, 0)),
            anywhere,
            anywhere,
            small,
        ],
        out_shape=[
            jax.ShapeDtypeStruct((3, 2 * length, width), bf16),
            jax.ShapeDtypeStruct((2 * length, width), bf16),
            jax.ShapeDtypeStruct((length, width), bf16),
            jax.ShapeDtypeStruct((16, rows, 3 * width), bf16),
            jax.ShapeDtypeStruct((8, width), f32),
        ],
        scratch_shapes=[
            pltpu.VMEM((16, rows, 3 * width), bf16),
            pltpu.VMEM((length, width), bf16),
            pltpu.VMEM((tile, width), bf16),
            pltpu.SemaphoreType.DMA((2,)),
            pltpu.SemaphoreType.DMA((2,)),
            *LineGather.scratch(3),
            *GainSum.scratch((0, 1, 2, 3), width),
        ],
        compiler_params=pltpu.CompilerParams(vmem_limit_bytes=48 << 20, collective_id=0, has_side_effects=True),
        cost_estimate=pl.CostEstimate(
            flops=12 * length * width * width, bytes_accessed=length * width * 24 + 12 * width * width, transcendentals=0
        ),
    )(shard, gain, tokens, tokens, cosine, sine)


def mask_tables(length, row_length):
    pos = jnp.arange(length)
    blk = (pos // BLOCK)[:, None]
    lane = (jnp.arange(LANES) % HD)[None, :]
    dead = (pos >= row_length)[:, None]
    clean_query = (lane == blk).astype(bf16)
    noisy_query = (lane == blk - 1).astype(bf16)
    main_key = jnp.where((blk > lane) | dead, BIG, 0.0).astype(bf16)
    diag_key = jnp.where((blk != lane) | dead, BIG, 0.0).astype(bf16)
    return clean_query, noisy_query, main_key, diag_key


def low_lanes(shape):
    return lax.broadcasted_iota(jnp.int32, shape, 1) < HD


def attend_gather_kernel(qkv_ref, cq_ref, nq_ref, mk_ref, dk_ref, wo_ref, wu_ref, wd_ref, grad_ref,
                         out_ref, log_ref, wo_all, wu_all, wd_all, away_ref,
                         qa, ka, kd, va, s_scr, swap_sems, send_sems, recv_sems, local_sems):
    side, at = lax.axis_index("stream"), lax.axis_index("batch")
    step = pl.program_id(0)
    wide, tall = wu_ref.shape[1] // 2, wd_ref.shape[0] // 2

    def columns(n):
        cols = slice(n * wide, (n + 1) * wide)
        return wu_ref.at[:, cols], lambda shard: wu_all.at[shard, :, cols]

    def rows(n):
        part = slice(n * tall, (n + 1) * tall)
        return wd_ref.at[part, :], lambda shard: wd_all.at[shard, part, :]

    chunks = [(wo_ref, lambda shard: wo_all.at[shard]), columns(0), columns(1), rows(0), rows(1)]
    weights = LineGather(chunks, send_sems, recv_sems, local_sems)
    swap = pltpu.make_async_remote_copy(
        src_ref=grad_ref.at[0, 1 - side],
        dst_ref=away_ref,
        send_sem=swap_sems.at[0],
        recv_sem=swap_sems.at[1],
        device_id=(1 - side, at),
        device_id_type=MESH,
    )
    slots = 2 * SLOT_STEPS
    plan = [[] for _ in range(slots + 1)]
    items = [(chunk, phase) for phase in range(1, 5) for chunk in range(5)]
    for n, item in enumerate(items):
        plan[min(1 + n * SLOT_RATE // 16, slots)].append(item)

    @pl.when(step == 0)
    def _():
        greet(line_partners())
        for chunk in range(5):
            weights.phase(chunk, 0)
        swap.start()

    def pass_on(slot):
        for now in range(SLOT_STEPS):
            if plan[2 * now + slot]:

                @pl.when(step == now)
                def _():
                    for item in plan[2 * now + slot]:
                        weights.phase(*item)

    pass_on(0)
    attend_kernel(qkv_ref, cq_ref, nq_ref, mk_ref, dk_ref, out_ref, log_ref, qa, ka, kd, va, s_scr,
                  between=lambda: pass_on(1))

    @pl.when(step == pl.num_programs(0) - 1)
    def _():
        for item in plan[slots]:
            weights.phase(*item)
        weights.finish()
        swap.wait()


SLOT_STEPS = 6
SLOT_RATE = 11


def attend_kernel(qkv_ref, cq_ref, nq_ref, mk_ref, dk_ref, out_ref, log_ref,
                  qa, ka, kd, va, s_scr, between=lambda: None):
    length = out_ref.shape[1]
    clean = lax.axis_index("stream")
    noisy = 1 - clean
    tiles = length // TILE
    low = low_lanes((length, LANES))
    ones = jnp.ones((16, length), bf16)
    vc_t = qkv_ref[2, clean].T
    vn_t = qkv_ref[2, noisy].T
    for head in range(2):
        pick = low if head == 0 else jnp.logical_not(low)
        qa[0, head] = jnp.where(pick, qkv_ref[0, clean], cq_ref[...])
        qa[1, head] = jnp.where(pick, qkv_ref[0, noisy], nq_ref[...])
        qa[2, head] = jnp.where(pick, qkv_ref[0, noisy], cq_ref[...])
        ka[head] = jnp.where(pick, qkv_ref[1, clean], mk_ref[...])
        kd[head] = jnp.where(pick, qkv_ref[1, noisy], dk_ref[...])
        va[0, head, :HD] = vc_t[head * HD : (head + 1) * HD]
        va[1, head, :HD] = vn_t[head * HD : (head + 1) * HD]
        va[0, head, HD:] = ones
        va[1, head, HD:] = ones
    for copy in range(2):
        if copy:
            between()
        where_to = clean if copy == 0 else noisy
        for tile in range(tiles):
            rows = slice(tile * TILE, (tile + 1) * TILE)
            parts = []
            for head in range(2):
                pieces = [(qa[copy, head, rows, :], ka, 0, t) for t in range(tile + 1)]
                if copy == 1:
                    pieces.append((qa[2, head, rows, :], kd, 1, tile))
                top = None
                for n, (query, keys, vi, t) in enumerate(pieces):
                    s = mm_t(keys[head, t * TILE : (t + 1) * TILE, :], query)
                    if copy == 1 and tile == 0 and n == 0:
                        first = lax.broadcasted_iota(jnp.int32, s.shape, 1) < BLOCK
                        s = jnp.where(first, BIG, s)
                    s_scr[head, n * TILE : (n + 1) * TILE, :] = s
                    m = jnp.max(s, axis=0, keepdims=True)
                    top = m if top is None else jnp.maximum(top, m)
                acc = None
                for n, (query, keys, vi, t) in enumerate(pieces):
                    p = jnp.exp(s_scr[head, n * TILE : (n + 1) * TILE, :] - top).astype(bf16)
                    o = mm(va[vi, head, :, t * TILE : (t + 1) * TILE], p)
                    acc = o if acc is None else acc + o
                total = acc[HD : HD + 1, :]
                parts.append(acc[:HD] / total)
                log_ref[where_to, 0, head : head + 1, rows] = top + jnp.log(total)
            out_ref[where_to, rows, :] = jnp.concatenate(parts, axis=0).T.astype(bf16)


def attend(qkv, tables, shards=None, grad=None):
    _, copies, length, width = qkv.shape
    pairs = width // LANES
    table_spec = pl.BlockSpec((length, LANES), lambda i: (0, 0), pipeline_mode=pl.Buffered(1))
    more_in, more_shapes, more_scratch = [], [], []
    body, params = attend_kernel, {}
    if shards is not None:
        assert pairs == SLOT_STEPS
        body = attend_gather_kernel
        params = dict(collective_id=3, has_side_effects=True)
        more_in = [*shards, grad]
        more_shapes = [jax.ShapeDtypeStruct((16, *shard.shape), bf16) for shard in shards]
        more_shapes.append(jax.ShapeDtypeStruct((length, width), bf16))
        more_scratch = [pltpu.SemaphoreType.DMA((2,)), *LineGather.scratch(5)]
    anywhere = pl.BlockSpec(memory_space=pl.ANY)
    return pl.pallas_call(
        body,
        name="attend",
        grid=(pairs,),
        in_specs=[pl.BlockSpec((3, copies, length, LANES), lambda i: (0, 0, 0, i)), *[table_spec] * 4,
                  *[anywhere] * len(more_in)],
        out_specs=[
            pl.BlockSpec((copies, length, LANES), lambda i: (0, 0, i)),
            pl.BlockSpec((copies, 1, 2, length), lambda i: (0, i, 0, 0)),
            *[anywhere] * len(more_in),
        ],
        scratch_shapes=[
            pltpu.VMEM((3, 2, length, LANES), bf16),
            pltpu.VMEM((2, length, LANES), bf16),
            pltpu.VMEM((2, length, LANES), bf16),
            pltpu.VMEM((2, 2, HD + 16, length), bf16),
            pltpu.VMEM((2, length + TILE, TILE), f32),
            *more_scratch,
        ],
        out_shape=[
            jax.ShapeDtypeStruct((copies, length, width), bf16),
            jax.ShapeDtypeStruct((copies, pairs, 2, length), f32),
            *more_shapes,
        ],
        compiler_params=pltpu.CompilerParams(vmem_limit_bytes=48 << 20, **params),
        cost_estimate=pl.CostEstimate(
            flops=8 * length * length * width, bytes_accessed=16 * length * width, transcendentals=length * length * 12
        ),
    )(qkv, *tables, *more_in)


DOWN, UP, OUT = (-1, 1, 2, 3), (1, -1, 2, 3), (2, -1, 1, 3)
QKV = ((1, 2, 3, -1), (2, 1, 3, -1), (1, 2, 3, -1))


def attend_back_sum_kernel(*refs, orders):
    count = len(orders)
    core, refs = refs[:10], refs[10:]
    pairs, gain_ref, refs = refs[: 2 * count], refs[2 * count], refs[2 * count + 1 :]
    dqkv_ref, refs = refs[0], refs[1:]
    outs, gain_out, refs = refs[:count], refs[count], refs[count + 1 :]
    own, refs = refs[:10], refs[10:]
    per = len(refs[:-3]) // count
    sums = []
    for n, order in enumerate(orders):
        keep, *got, sems = refs[n * per : (n + 1) * per]
        sums.append(SlabSum(order, keep, pairs[2 * n + 1], got, sems, load=pairs[2 * n]))
    gain = GainSum(ALL, *refs[-3:])
    down, up, wo = sums
    step = pl.program_id(0)

    @pl.when(step == 0)
    def _():
        greet([partner(bit) for bit in ALL])
        for one in sums:
            one.start()
        gain.start(gain_ref[...])

    for at, plan in {
        1: ((down, 1), (up, 1), (wo, 1), (gain, 1)),
        2: ((wo, 2), (gain, 2)),
        3: ((down, 2), (up, 2), (wo, 3), (gain, 3)),
        4: ((down, 3), (up, 3), (wo, 4), (gain, 4)),
        5: ((down, 4), (up, 4)),
    }.items():

        @pl.when(step == at)
        def _():
            for one, number in plan:
                one.step(number)

    attend_back_kernel(*core, dqkv_ref, *own)

    @pl.when(step == pl.num_programs(0) - 1)
    def _():
        for one, out_ref in zip(sums, outs):
            one.finish(out_ref, gain_ref.shape[1])
        gain.finish(gain_out)


def attend_back_kernel(qkv_ref, o_ref, do_ref, log_ref, cq_ref, nq_ref, mk_ref, dk_ref, cos_ref, sin_ref,
                       dqkv_ref, qa, qz, ka, kd, kt, doz, dsum, dq, dkc, dvc):
    length = o_ref.shape[1]
    clean = lax.axis_index("stream")
    noisy = 1 - clean
    tiles = length // TILE
    low = low_lanes((length, LANES))
    zero = jnp.zeros((length, LANES), bf16)
    for copy in range(2):
        at = clean if copy == 0 else noisy
        kt[copy] = qkv_ref[1, at].T
        prod = (o_ref[at].astype(f32) * do_ref[at].astype(f32)).T
        dsum[copy, 0:1] = jnp.sum(prod[:HD], axis=0, keepdims=True)
        dsum[copy, 1:2] = jnp.sum(prod[HD:], axis=0, keepdims=True)
        for head in range(2):
            pick = low if head == 0 else jnp.logical_not(low)
            qa[copy, head] = jnp.where(pick, qkv_ref[0, at], (cq_ref, nq_ref)[copy][...])
            qz[copy, head] = jnp.where(pick, qkv_ref[0, at], zero)
            doz[copy, head] = jnp.where(pick, do_ref[at], zero)
            if copy == 0:
                ka[head] = jnp.where(pick, qkv_ref[1, at], mk_ref[...])
            else:
                qa[2, head] = jnp.where(pick, qkv_ref[0, at], cq_ref[...])
                kd[head] = jnp.where(pick, qkv_ref[1, at], dk_ref[...])
    cosine, sine = cos_ref[...], sin_ref[...]

    def piece(copy, tile, query, keys, kv_copy, t, mask_first):
        rows = slice(tile * TILE, (tile + 1) * TILE)
        krows = slice(t * TILE, (t + 1) * TILE)
        kv_at = clean if kv_copy == 0 else noisy
        at = clean if copy == 0 else noisy
        probs, raws = [], []
        for head in range(2):
            s = mm_t(keys[head, krows, :], qa[query, head, rows, :])
            p = jnp.exp(s - log_ref[at, 0, head : head + 1, rows])
            if mask_first:
                first = lax.broadcasted_iota(jnp.int32, s.shape, 1) < BLOCK
                p = jnp.where(first, 0.0, p)
            dp = mm_t(qkv_ref[2, kv_at, krows, :], doz[copy, head, rows, :])
            raw = (p * (dp - dsum[copy, head : head + 1, rows])).astype(bf16)
            p = p.astype(bf16)
            dq[copy, head * HD : (head + 1) * HD, rows] += mm(kt[kv_copy, head * HD : (head + 1) * HD, krows], raw)
            probs.append(p)
            raws.append(raw)
        p2 = jnp.concatenate(probs, axis=1)
        r2 = jnp.concatenate(raws, axis=1)
        do2 = jnp.concatenate([doz[copy, 0, rows, :], doz[copy, 1, rows, :]], axis=0)
        q2 = jnp.concatenate([qz[copy, 0, rows, :], qz[copy, 1, rows, :]], axis=0)
        return mm(p2, do2), mm(r2, q2)

    def finish(field, rotate, scale):
        if rotate:
            c, s = cosine, sine
            field = field * c - half_partner(field) * s
        return (field * scale if scale != 1.0 else field).astype(bf16)

    dq[...] = jnp.zeros_like(dq)
    for t in range(tiles):
        krows = slice(t * TILE, (t + 1) * TILE)
        dv_t, dk_t = piece(1, t, 2, kd, 1, t, False)
        dqkv_ref[2, noisy, krows, :] = dv_t.astype(bf16)
        dkc[krows, :] = dk_t
    dqkv_ref[1, noisy] = finish(dkc[...], True, 1.0)
    for t in range(tiles):
        krows = slice(t * TILE, (t + 1) * TILE)
        dv_acc = dk_acc = None
        for tile in range(t, tiles):
            for copy in range(2):
                dv_t, dk_t = piece(copy, tile, copy, ka, 0, t, copy == 1 and tile == 0)
                dv_acc = dv_t if dv_acc is None else dv_acc + dv_t
                dk_acc = dk_t if dk_acc is None else dk_acc + dk_t
        dqkv_ref[2, clean, krows, :] = dv_acc.astype(bf16)
        dkc[krows, :] = dk_acc
    dqkv_ref[1, clean] = finish(dkc[...], True, 1.0)
    dqkv_ref[0, clean] = finish(dq[0].T, True, 0.125)
    dqkv_ref[0, noisy] = finish(dq[1].T, True, 0.125)


def attend_back(qkv, mixed, grad, logs, tables, cosine, sine, pairs=None, gain=None, slabs=()):
    _, copies, length, width = qkv.shape
    steps = width // LANES
    table_spec = pl.BlockSpec((length, LANES), lambda i: (0, 0), pipeline_mode=pl.Buffered(1))
    row_spec = pl.BlockSpec((copies, length, LANES), lambda i: (0, 0, i))
    three = pl.BlockSpec((3, copies, length, LANES), lambda i: (0, 0, 0, i))
    anywhere = pl.BlockSpec(memory_space=pl.ANY)

    def fixed(shape):
        return pl.BlockSpec(shape, lambda i: (0, 0), pipeline_mode=pl.Buffered(1))

    more_in, more_specs, more_shapes, more_out, more_scratch = [], [], [], [], []
    body, params = attend_back_kernel, {}
    if pairs is not None:
        assert steps == 6
        body = functools.partial(attend_back_sum_kernel, orders=(DOWN, UP, OUT))
        params = dict(collective_id=1, has_side_effects=True)
        for (keep, send), slab in zip(pairs, slabs):
            slots, share, columns = keep.shape
            more_in += [keep, send]
            more_specs += [anywhere] * 2
            more_shapes.append(jax.ShapeDtypeStruct(slab, f32))
            more_out.append(fixed(slab))
            more_scratch += SlabSum.scratch(slots, share, columns)
        more_in.append(gain)
        more_specs.append(fixed((8, width)))
        more_shapes.append(jax.ShapeDtypeStruct((8, width), f32))
        more_out.append(fixed((8, width)))
        more_scratch += GainSum.scratch(ALL, width)
    return pl.pallas_call(
        body,
        name="attend_back",
        grid_spec=pltpu.PrefetchScalarGridSpec(
            num_scalar_prefetch=0,
            grid=(steps,),
            in_specs=[three, row_spec, row_spec, pl.BlockSpec((copies, 1, 2, length), lambda i: (0, i, 0, 0))]
            + [table_spec] * 6
            + more_specs,
            out_specs=[three, *more_out],
            scratch_shapes=[
                pltpu.VMEM((3, 2, length, LANES), bf16),
                pltpu.VMEM((2, 2, length, LANES), bf16),
                pltpu.VMEM((2, length, LANES), bf16),
                pltpu.VMEM((2, length, LANES), bf16),
                pltpu.VMEM((2, LANES, length), bf16),
                pltpu.VMEM((2, 2, length, LANES), bf16),
                pltpu.VMEM((2, 2, length), f32),
                pltpu.VMEM((2, LANES, length), f32),
                pltpu.VMEM((length, LANES), f32),
                pltpu.VMEM((length, LANES), f32),
                *more_scratch,
            ],
        ),
        out_shape=[jax.ShapeDtypeStruct((3, copies, length, width), bf16), *more_shapes],
        compiler_params=pltpu.CompilerParams(vmem_limit_bytes=60 << 20, **params),
        cost_estimate=pl.CostEstimate(
            flops=20 * length * length * width, bytes_accessed=30 * length * width, transcendentals=length * length * 12
        ),
    )(qkv, mixed, grad, logs, *tables, cosine, sine, *more_in)


ROOT = math.sqrt(2.0 / math.pi)


def feed_kernel(side_ref, x_own, x_away, mixed_ref, g_own, g_away, gain_ref, wo_all, wu_all, wd_all,
                out_own, out_away, act_ref, du_ref, h2_ref, dmid_ref, dbr_ref, dmix_ref, dgain_ref,
                wo_ref, wu_ref, wd_ref, sems, *, half):
    groups, rows, width = wo_ref.shape
    fold = wu_ref.shape[0]

    @pl.when(pl.program_id(0) == 0)
    def _():
        copies = [pltpu.make_async_copy(wo_all, wo_ref, sems.at[0])]
        for n in range(fold):
            cols = wu_all.at[:, :, n * width : (n + 1) * width]
            copies.append(pltpu.make_async_copy(cols, wu_ref.at[n], sems.at[1 + n]))
        copies.append(pltpu.make_async_copy(wd_all, wd_ref, sems.at[1 + fold]))
        for copy in copies:
            copy.start()
        for copy in copies:
            copy.wait()

    def down(c):
        per = groups // fold
        return wd_ref[c * per : (c + 1) * per].reshape(width, width)

    wo = wo_ref[...].reshape(width, width)
    gain = gain_ref[...].astype(f32)
    middle = read_rows(x_own, x_away, half).astype(f32) + mm(mixed_ref[...], wo)
    center = middle - jnp.mean(middle, axis=1, keepdims=True)
    spread = jnp.mean(center * center, axis=1, keepdims=True)
    inv = lax.rsqrt(spread + 1e-5)
    norm = center * inv
    hidden = (norm * gain).astype(bf16)
    h2_ref[...] = hidden
    grad = read_rows(g_own, g_away, half)
    out = middle
    dh = jnp.zeros_like(middle)
    for c in range(fold):
        cols = slice(c * width, (c + 1) * width)
        up = wu_ref[c].reshape(width, width)
        u = mm(hidden, up)
        da = mm_t(grad, down(c)).astype(bf16).astype(f32)
        sq = u * u
        t = jnp.tanh(u * (ROOT + (ROOT * 0.044715) * sq))
        part = 0.5 + 0.5 * t
        act = (u * part).astype(bf16)
        slope = part + (u * (part * (1.0 - t))) * (ROOT + (3 * ROOT * 0.044715) * sq)
        du = (da * slope).astype(bf16)
        act_ref[:, cols] = act
        du_ref[:, cols] = du
        out = out + mm(act, down(c))
        dh = dh + mm_t(du, up)
    low = out.astype(bf16)

    @pl.when(pl.program_id(0) < half)
    def _():
        out_own[...] = low

    @pl.when(pl.program_id(0) >= half)
    def _():
        out_away[...] = low

    @pl.when(pl.program_id(0) == 0)
    def _():
        dgain_ref[...] = jnp.zeros_like(dgain_ref)

    dgain_ref[...] += jnp.sum((dh * norm).reshape(-1, 8, width), axis=0)
    e = dh * gain
    dmid = grad.astype(f32) + inv * (
        e - jnp.mean(e, axis=1, keepdims=True) - norm * jnp.mean(e * norm, axis=1, keepdims=True)
    )
    dmid_ref[...] = dmid
    dbr = dmid.astype(bf16)
    dbr_ref[...] = dbr
    dmix_ref[...] = mm_t(dbr, wo).astype(bf16)


def feed(side, x_own, x_away, mixed, g_own, g_away, gain, weights, tile=512):
    tokens, width = mixed.shape
    groups, rows, ff = weights[1].shape
    fold = ff // width
    half = tokens // 2 // tile
    row = pl.BlockSpec((tile, width), lambda i, s: (i, 0))
    wide = pl.BlockSpec((tile, ff), lambda i, s: (i, 0))
    own, away = row_specs(tile, width, half)

    def keep(shape):
        return pl.BlockSpec(shape, lambda i, s: (0, 0), pipeline_mode=pl.Buffered(1))

    return pl.pallas_call(
        functools.partial(feed_kernel, half=half),
        name="feed",
        grid_spec=pltpu.PrefetchScalarGridSpec(
            num_scalar_prefetch=1,
            grid=(2 * half,),
            in_specs=[own, away, row, own, away, keep((1, width)), *[pl.BlockSpec(memory_space=pl.ANY)] * 3],
            out_specs=[own, away, wide, wide, row, row, row, row, pl.BlockSpec((8, width), lambda i, s: (0, 0))],
            scratch_shapes=[
                pltpu.VMEM((groups, rows, width), bf16),
                pltpu.VMEM((fold, groups, rows, width), bf16),
                pltpu.VMEM((groups, fold * rows, width), bf16),
                pltpu.SemaphoreType.DMA((2 + fold,)),
            ],
        ),
        out_shape=[
            jax.ShapeDtypeStruct((1, 2, tokens // 2, width), bf16),
            jax.ShapeDtypeStruct((tokens // 2, width), bf16),
            jax.ShapeDtypeStruct((tokens, ff), bf16),
            jax.ShapeDtypeStruct((tokens, ff), bf16),
            jax.ShapeDtypeStruct((tokens, width), bf16),
            jax.ShapeDtypeStruct((tokens, width), f32),
            jax.ShapeDtypeStruct((tokens, width), bf16),
            jax.ShapeDtypeStruct((tokens, width), bf16),
            jax.ShapeDtypeStruct((8, width), f32),
        ],
        compiler_params=pltpu.CompilerParams(vmem_limit_bytes=60 << 20),
        cost_estimate=pl.CostEstimate(
            flops=tokens * width * (4 * width + 8 * ff), bytes_accessed=tokens * (width * 18 + ff * 4),
            transcendentals=tokens * ff
        ),
    )(side, x_own, x_away, mixed, g_own, g_away, gain, *weights)


def folds(share):
    return 1 if share % 16 == 0 else 2


def fold(slab):
    if folds(slab.shape[0]) == 1:
        return slab
    middle = slab.shape[1] // 2
    return jnp.concatenate([slab[:, :middle], slab[:, middle:]], axis=0)


def arranged(slot, order):
    return sum((slot >> bit & 1) << (len(order) - 1 - n) for n, bit in enumerate(order))


def weight_kernel(me_ref, left_ref, *refs, share, split, order):
    weight_slabs(me_ref[0], left_ref, *refs, share=share, split=split, order=order)


def weight_slabs(me, left_ref, *refs, share, split, order):
    right_refs, (keep_ref, send_ref, scr) = refs[:-3], refs[-3:]
    if split:
        own_ref, away_ref = right_refs
        half = own_ref.shape[0]
        total = t_mm(left_ref[:half], own_ref[...]) + t_mm(left_ref[half:], away_ref[...])
    else:
        total = t_mm(left_ref[...], right_refs[0][...])
    slabs = total.shape[0] // share
    scr[...] = total.reshape(scr.shape)
    low_me = lax.rem(me, slabs)
    for slot in range(slabs):
        source = jnp.bitwise_xor(low_me, slot)
        into = send_ref if slot % 2 else keep_ref
        into[arranged(slot // 2, order)] = fold(scr[source]).astype(bf16)


def weight_grad_columns(me, left, right, block, share, order, name):
    tokens, dl = left.shape
    dr = right.shape[1]
    peers = dl // share
    by = folds(share)
    shape = (peers // 2, share * by, dr // by)
    out = pl.BlockSpec((peers // 2, share * by, block // by), lambda j, m: (0, 0, j))
    return pl.pallas_call(
        functools.partial(weight_kernel, share=share, split=False, order=order),
        name=name,
        grid_spec=pltpu.PrefetchScalarGridSpec(
            num_scalar_prefetch=1,
            grid=(dr // block,),
            in_specs=[
                pl.BlockSpec((tokens, dl), lambda j, m: (0, 0), pipeline_mode=pl.Buffered(1)),
                pl.BlockSpec((tokens, block), lambda j, m: (0, j)),
            ],
            out_specs=[out, out],
            scratch_shapes=[pltpu.VMEM((peers, share, block), f32)],
        ),
        out_shape=[jax.ShapeDtypeStruct(shape, bf16)] * 2,
        compiler_params=pltpu.CompilerParams(vmem_limit_bytes=48 << 20),
        cost_estimate=pl.CostEstimate(
            flops=2 * tokens * dl * dr, bytes_accessed=2 * tokens * (dl + dr) + 2 * dl * dr, transcendentals=0
        ),
    )(me, left, right)


def weight_grad_rows(me, left, own, away, block, share, name):
    tokens, dl = left.shape
    length, dr = away.shape
    slabs = block // share
    steps = dl // block
    assert steps == 4
    shape = (2, slabs // 2, 2, share, dr)
    out = pl.BlockSpec((None, slabs // 2, None, share, dr), lambda j, m: (lax.div(j, 2), 0, lax.rem(j, 2), 0, 0))
    bits = (slabs // 2).bit_length() - 1

    def place(j, m):
        return (0, jnp.bitwise_xor(j, lax.div(m[0], slabs)))

    return pl.pallas_call(
        functools.partial(weight_kernel, share=share, split=True, order=tuple(range(bits))),
        name=name,
        grid_spec=pltpu.PrefetchScalarGridSpec(
            num_scalar_prefetch=1,
            grid=(steps,),
            in_specs=[
                pl.BlockSpec((tokens, block), place),
                pl.BlockSpec((None, None, length, dr), lambda j, m: (0, m[1], 0, 0), pipeline_mode=pl.Buffered(1)),
                pl.BlockSpec((length, dr), lambda j, m: (0, 0), pipeline_mode=pl.Buffered(1)),
            ],
            out_specs=[out, out],
            scratch_shapes=[pltpu.VMEM((slabs, share, dr), f32)],
        ),
        out_shape=[jax.ShapeDtypeStruct(shape, bf16)] * 2,
        compiler_params=pltpu.CompilerParams(vmem_limit_bytes=48 << 20),
        cost_estimate=pl.CostEstimate(
            flops=2 * tokens * dl * dr, bytes_accessed=2 * tokens * (dl + dr) + 2 * dl * dr, transcendentals=0
        ),
    )(me, left, own, away)


def last_kernel(x_own, x_away, gain_ref, w_hbm, dqkv_hbm, dmid_hbm, hidden_hbm,
                dx_ref, dw_ref, gain_out,
                xv, w_ref, dqkv, dmid, hidden, send, land, dgain, scr,
                load_sems, tile_sems, send_sems, recv_sems, out_sems, *refs, share):
    count = len(QKV)
    per = len(refs[:-3]) // count
    sums = []
    for n, order in enumerate(QKV):
        first, keep, *got, sems = refs[n * per : (n + 1) * per]
        sums.append(SlabSum(order, keep, first, got, sems))
    gain = GainSum(LATE, *refs[-3:])
    side, at = lax.axis_index("stream"), lax.axis_index("batch")
    me = side * lax.axis_size("batch") + at
    step = pl.program_id(0)
    width = w_ref.shape[0]
    length = land.shape[0]
    tiles = pl.num_programs(0)
    tile = 2 * length // 8
    half = 4

    def rows_of(t, base=0):
        return pl.ds(pl.multiple_of((t - base) * tile, tile), tile)

    loads = [
        pltpu.make_async_copy(w_hbm, w_ref, load_sems.at[0]),
        pltpu.make_async_copy(x_away, xv.at[pl.ds(length, length)], load_sems.at[1]),
        pltpu.make_async_copy(hidden_hbm, hidden, load_sems.at[2]),
        pltpu.make_async_copy(x_own.at[0, side], xv.at[pl.ds(0, length)], load_sems.at[3]),
    ]

    def load_grad(t):
        return pltpu.make_async_copy(dqkv_hbm.at[:, rows_of(t), :], dqkv.at[:, rows_of(t), :], tile_sems.at[0, t])

    def load_middle(t):
        return pltpu.make_async_copy(dmid_hbm.at[rows_of(t), :], dmid.at[rows_of(t), :], tile_sems.at[1, t])

    def away(t):
        return pltpu.make_async_remote_copy(
            src_ref=send.at[rows_of(t, half), :],
            dst_ref=land.at[rows_of(t, half), :],
            send_sem=send_sems.at[t - half],
            recv_sem=recv_sems.at[t - half],
            device_id=(1 - side, at),
            device_id_type=MESH,
        )

    def result(t, row):
        return pltpu.make_async_copy(
            dmid.at[rows_of(t), :],
            dx_ref.at[0, row, pl.ds(pl.multiple_of(lax.rem(t, half) * tile, tile), tile), :],
            out_sems.at[t],
        )

    @pl.when(step == 0)
    def _():
        loads[0].start()
        loads[1].start()
        load_grad(4).start()
        load_middle(4).start()
        loads[2].start()
        for t in (5, 6, 7, 0, 1, 2, 3):
            load_grad(t).start()
        loads[3].start()
        for t in (5, 6, 7, 0, 1, 2, 3):
            load_middle(t).start()
        dgain[...] = jnp.zeros_like(dgain)
        greet([partner(bit) for bit in ALL])
        loads[0].wait()
        loads[1].wait()
        load_grad(4).wait()
        load_middle(4).wait()

    @pl.when(step > 0)
    def _():
        load_middle(lax.rem(step + half, 8)).wait()

    @pl.when(step == half)
    def _():
        loads[3].wait()

    for now, plan in {
        1: ((0, 1), (1, 1)),
        2: ((0, 2), (2, 1)),
        3: ((1, 2),),
        4: ((0, 3),),
        6: ((2, 2), (1, 3)),
        7: ((0, 4),),
    }.items():

        @pl.when(step == now)
        def _():
            for n, number in plan:
                sums[n].step(number)

    t = lax.rem(step + half, 8)
    rows = rows_of(t)
    x = xv[rows, :].astype(f32)
    center = x - jnp.mean(x, axis=1, keepdims=True)
    spread = jnp.mean(center * center, axis=1, keepdims=True)
    inv = lax.rsqrt(spread + 1e-5)
    norm = center * inv
    dh = mm_t(dqkv[0, rows, :], w_ref[:, :width])
    dh = dh + mm_t(dqkv[1, rows, :], w_ref[:, width : 2 * width])
    dh = dh + mm_t(dqkv[2, rows, :], w_ref[:, 2 * width :])
    dgain[...] += jnp.sum((dh * norm).reshape(-1, 8, width), axis=0)
    e = dh * gain_ref[...]
    dx = dmid[rows, :] + inv * (
        e - jnp.mean(e, axis=1, keepdims=True) - norm * jnp.mean(e * norm, axis=1, keepdims=True)
    )

    @pl.when(step < half)
    def _():
        send[rows_of(step), :] = dx.astype(bf16)
        away(t).start()

    @pl.when(step >= half)
    def _():
        dmid[rows, :] = dx
        result(t, side).start()

    def part(n):
        order = tuple({-1: 3, 1: 0, 2: 1, 3: 2}[bit] for bit in QKV[n])
        weight_slabs(me, hidden, dqkv.at[n], sums[n].keep, sums[n].send, scr, share=share, split=False, order=order)
        sums[n].start()

    @pl.when(step == 0)
    def _():
        loads[2].wait()
        for other in (5, 6, 7, 0, 1, 2, 3):
            load_grad(other).wait()
        part(0)
        part(1)

    @pl.when(step == 1)
    def _():
        part(2)

    @pl.when(step == tiles - 1)
    def _():
        gain.start(dgain[...])
        sums[2].step(3)
        sums[1].step(4)
        sums[0].finish(dw_ref, width, 0)
        gain.step(1)
        sums[2].step(4)
        gain.step(2)
        sums[1].finish(dw_ref, width, width)
        gain.step(3)
        sums[2].finish(dw_ref, width, 2 * width)
        gain.step(4)
        for other in range(half, 8):
            away(other).wait()
            dmid[rows_of(other), :] = land[rows_of(other, half), :].astype(f32)
            result(other, 1 - side).start()
        gain.finish(gain_out)
        for other in range(8):
            result(other, side).wait()


def last(tokens, x_away, gain, w, dqkv, dmid, hidden, share):
    tokens_all, width = hidden.shape
    length = tokens_all // 2
    slots = width // share // 2
    anywhere = pl.BlockSpec(memory_space=pl.ANY)

    def fixed(shape):
        return pl.BlockSpec(shape, lambda i: (0, 0), pipeline_mode=pl.Buffered(1))

    scratch = []
    for _ in range(3):
        by = folds(share)
        scratch += [
            pltpu.VMEM((slots, share * by, width // by), bf16),
            *SlabSum.scratch(slots, share * by, width // by),
        ]
    return pl.pallas_call(
        functools.partial(last_kernel, share=share),
        name="last",
        grid=(8,),
        in_specs=[anywhere, anywhere, fixed((1, width)), *[anywhere] * 4],
        out_specs=[anywhere, fixed((share, 3 * width)), fixed((8, width))],
        out_shape=[
            jax.ShapeDtypeStruct((1, 2, length, width), f32),
            jax.ShapeDtypeStruct((share, 3 * width), f32),
            jax.ShapeDtypeStruct((8, width), f32),
        ],
        scratch_shapes=[
            pltpu.VMEM((2 * length, width), bf16),
            pltpu.VMEM((width, 3 * width), bf16),
            pltpu.VMEM((3, 2 * length, width), bf16),
            pltpu.VMEM((2 * length, width), f32),
            pltpu.VMEM((2 * length, width), bf16),
            pltpu.VMEM((length, width), bf16),
            pltpu.VMEM((length, width), bf16),
            pltpu.VMEM((8, width), f32),
            pltpu.VMEM((2 * slots, share, width), f32),
            pltpu.SemaphoreType.DMA((4,)),
            pltpu.SemaphoreType.DMA((2, 8)),
            pltpu.SemaphoreType.DMA((4,)),
            pltpu.SemaphoreType.DMA((4,)),
            pltpu.SemaphoreType.DMA((8,)),
            *scratch,
            *GainSum.scratch(LATE, width),
        ],
        compiler_params=pltpu.CompilerParams(vmem_limit_bytes=62 << 20, collective_id=2, has_side_effects=True),
        cost_estimate=pl.CostEstimate(
            flops=24 * length * width * width, bytes_accessed=36 * length * width, transcendentals=0
        ),
    )(tokens, x_away, gain, w, dqkv, dmid, hidden)


def project_back_kernel(side_ref, x_ref, gain_ref, w_ref, dqkv_ref, dmid_ref, dx_ref, dgain_ref):
    x = x_ref[...].astype(f32)
    width = x.shape[1]
    center = x - jnp.mean(x, axis=1, keepdims=True)
    spread = jnp.mean(center * center, axis=1, keepdims=True)
    inv = lax.rsqrt(spread + 1e-5)
    norm = center * inv
    dh = mm_t(dqkv_ref[0], w_ref[:, :width])
    dh = dh + mm_t(dqkv_ref[1], w_ref[:, width : 2 * width])
    dh = dh + mm_t(dqkv_ref[2], w_ref[:, 2 * width :])

    @pl.when(pl.program_id(0) == 0)
    def _():
        dgain_ref[...] = jnp.zeros_like(dgain_ref)

    dgain_ref[...] += jnp.sum((dh * norm).reshape(-1, 8, width), axis=0)
    e = dh * gain_ref[...].astype(f32)
    dx_ref[...] = (dmid_ref[...] + inv * (
        e - jnp.mean(e, axis=1, keepdims=True) - norm * jnp.mean(e * norm, axis=1, keepdims=True)
    )).astype(dx_ref.dtype)


def project_back(side, x, gain, w, dqkv, dmid, away, tile=256):
    width = x.shape[-1]
    length = dmid.shape[0] // 2
    half = length // tile
    first = half if away else 0
    if away:
        x_spec = pl.BlockSpec((tile, width), lambda i, s: (i, 0))
        out_spec, out_shape = x_spec, jax.ShapeDtypeStruct((length, width), bf16)
    else:
        x_spec = pl.BlockSpec((None, None, tile, width), lambda i, s: (0, s[0], i, 0))
        out_spec, out_shape = x_spec, jax.ShapeDtypeStruct((1, 2, length, width), f32)
    return pl.pallas_call(
        project_back_kernel,
        name="project_back_away" if away else "project_back_own",
        grid_spec=pltpu.PrefetchScalarGridSpec(
            num_scalar_prefetch=1,
            grid=(half,),
            in_specs=[
                x_spec,
                pl.BlockSpec((1, width), lambda i, s: (0, 0)),
                pl.BlockSpec((width, 3 * width), lambda i, s: (0, 0), pipeline_mode=pl.Buffered(1)),
                pl.BlockSpec((3, tile, width), lambda i, s: (0, i + first, 0)),
                pl.BlockSpec((tile, width), lambda i, s: (i + first, 0)),
            ],
            out_specs=[out_spec, pl.BlockSpec((8, width), lambda i, s: (0, 0))],
        ),
        out_shape=[out_shape, jax.ShapeDtypeStruct((8, width), f32)],
        compiler_params=pltpu.CompilerParams(vmem_limit_bytes=48 << 20),
        cost_estimate=pl.CostEstimate(
            flops=6 * length * width * width, bytes_accessed=length * width * 16, transcendentals=0
        ),
    )(side, x, gain, w, dqkv, dmid)


def flip(x, bit):
    axis, by = ("stream", 1) if bit < 0 else ("batch", 1 << bit)
    return lax.ppermute(x, axis, [(i, i ^ by) for i in range(lax.axis_size(axis))])


def after(value, *others):
    return lax.optimization_barrier((value, *others))[0]


def shards(tokens, cotangent, lengths, ln1_gain, w_qkv, w_out, ln2_gain, w_up, w_down):
    side = lax.axis_index("stream")
    at = lax.axis_index("batch")
    _, rows_dev, length, width = tokens.shape
    assert rows_dev == 2
    ff = w_up.shape[1]
    peers = lax.axis_size("batch")
    small = peers == 16 and width % (16 * peers) == 0
    side_array = side.reshape(1).astype(jnp.int32)
    index = side * peers + at
    me = jnp.stack([index if small else 0 * index, side]).astype(jnp.int32)
    share = width // (2 * peers)

    cosine, sine = rotary_tables(length)
    tables = mask_tables(length, jnp.take(lengths, side))
    if small:
        rows = width // peers
        gains = jnp.zeros((8, width), f32)
        gains = lax.dynamic_update_slice(gains, jnp.stack([ln1_gain, ln2_gain]).astype(f32), (0, at * rows))
        qkv, hidden, x_away, w_qkv_all, gains = first(w_qkv, gains, tokens, cosine, sine)
        qkv4 = qkv.reshape(3, 2, length, width)
        w_qkv_all = w_qkv_all.reshape(width, 3 * width)
        gain_one, gain_two = gains[0:1], gains[1:2]
        mixed, logs, *weights, g_away = attend(qkv4, tables, (w_out, w_up, w_down), cotangent)
    else:

        def whole(x):
            return lax.all_gather(x, "batch", axis=0, tiled=True)

        x_away = flip(lax.dynamic_index_in_dim(tokens[0], 1 - side, 0, False), -1)
        g_away = flip(lax.dynamic_index_in_dim(cotangent[0], 1 - side, 0, False), -1)
        w_qkv_all = whole(w_qkv)
        gain_one, gain_two = (whole(gain)[None].astype(f32) for gain in (ln1_gain, ln2_gain))
        weights = [whole(w).reshape(16, -1, w.shape[1]) for w in (w_out, w_up, w_down)]
        qkv, hidden = project(side_array, tokens, x_away, gain_one, w_qkv_all, cosine, sine)
        qkv4 = qkv.reshape(3, 2, length, width)
        mixed, logs = attend(qkv4, tables)
    mixed2 = mixed.reshape(2 * length, width)
    out, out_away, act, du, h2, dmid, dbr, dmix, dgain_two = feed(
        side_array, tokens, x_away, mixed2, cotangent, g_away, gain_two, weights
    )

    def place(result, away):
        away = flip(away, -1).astype(result.dtype)
        return lax.dynamic_update_slice(result, away[None, None], (0, 1 - side, 0, 0))

    out = place(out, out_away)
    unit = share if small else width // 32
    places = {-1: 3, 1: 0, 2: 1, 3: 2}

    def columns_grad(left, right, order, name):
        return weight_grad_columns(me, left, right, width, unit, [places[bit] for bit in order], name)

    down = weight_grad_rows(me, act, cotangent, g_away, width, ff // width * unit, "grad_down")
    down = [part.reshape(16, -1, width) for part in down]
    up = columns_grad(h2, du, UP, "grad_up")
    wo = columns_grad(mixed2, dbr, OUT, "grad_out")
    dmix = after(dmix.reshape(2, length, width), out)
    common = qkv4, mixed, dmix, logs, tables, cosine, sine
    if small:
        dqkv, down, up, wo, dgain_two = attend_back(
            *common, (down, up, wo), dgain_two, ((ff // width * share, width), (share, ff), (share, width))
        )
    else:
        dqkv, = attend_back(*common)
    dqkv3 = dqkv.reshape(3, 2 * length, width)
    if small:
        dx, wq, dgain_one = last(tokens, x_away, gain_one, w_qkv_all, dqkv3, dmid, hidden, share)
    else:
        dx_away, dgain_away = project_back(side_array, x_away, gain_one, w_qkv_all, dqkv3, dmid, True)
        dx, dgain_own = project_back(side_array, tokens, gain_one, w_qkv_all, dqkv3, dmid, False)
        dgain_one = dgain_own + dgain_away
        dx = place(dx, dx_away)
    dgain_one, dgain_two = (jnp.sum(g, axis=0, keepdims=True) for g in (dgain_one, dgain_two))
    if not small:

        def scatter(pair, order):
            slots = jnp.stack(pair, axis=1)
            natural = [arranged(n, order) for n in range(16)]
            slots = slots[jnp.array(natural)]
            by = folds(unit) if slots.shape[2] == 2 * unit else 1
            slots = slots.reshape(32, by, slots.shape[2] // by, -1, width // by).transpose(0, 2, 3, 1, 4)
            rows = slots.reshape(32 * slots.shape[1], -1)
            return lax.psum_scatter(rows, ("stream", "batch"), scatter_dimension=0, tiled=True).astype(f32)

        parts = [columns_grad(hidden, dqkv3[n], QKV[n], "grad_qkv") for n in range(3)]
        down, up, wo, *parts = (
            scatter(pair, [places[bit] for bit in order])
            for pair, order in zip((down, up, wo, *parts), (DOWN, UP, OUT, *QKV))
        )
        wq = jnp.concatenate(parts, axis=1)
        dgain_one, dgain_two = lax.psum((dgain_one, dgain_two), ("stream", "batch"))
    begin = index * share
    dgain_one, dgain_two = (lax.dynamic_slice(g[0], (begin,), (share,)) for g in (dgain_one, dgain_two))
    return out, dx, dgain_one, wq, wo, dgain_two, up, down


def solution(mesh):
    token = P("stream", "batch", None, None)
    vector, matrix = P("batch"), P("batch", None)
    out_vector, out_matrix = P(("stream", "batch")), P(("stream", "batch"), None)
    return jax.shard_map(
        shards,
        mesh=mesh,
        in_specs=(token, token, vector, vector, matrix, matrix, vector, matrix, matrix),
        out_specs=(token, token, out_vector, out_matrix, out_matrix, out_vector, out_matrix, out_matrix),
        check_vma=False,
    )
```

```python
import functools
import math

import jax
import jax.numpy as jnp
from jax import lax
from jax.experimental import pallas as pl
from jax.experimental.pallas import tpu as pltpu
from jax.sharding import PartitionSpec as P

HD = 64
BLOCK = 16
LANES = 128
TILE = 256
BIG = -1e30
f32, bf16 = jnp.float32, jnp.bfloat16


def mm(a, b):
    return lax.dot_general(a, b, (((1,), (0,)), ((), ())), preferred_element_type=f32)


def mm_t(a, b):
    return lax.dot_general(a, b, (((1,), (1,)), ((), ())), preferred_element_type=f32)


def t_mm(a, b):
    return lax.dot_general(a, b, (((0,), (0,)), ((), ())), preferred_element_type=f32)


def rotary_tables(length):
    half = HD // 2
    places = jnp.arange(length).astype(f32)
    rates = jnp.exp(jnp.arange(half).astype(f32) * (-2.0 * math.log(10000.0) / HD))
    angles = places[:, None] * rates[None, :]
    cosine, sine = jnp.cos(angles), jnp.sin(angles)
    return (
        jnp.concatenate([cosine] * 4, axis=1),
        jnp.concatenate([-sine, sine, -sine, sine], axis=1),
    )


def half_partner(x):
    lane = lax.broadcasted_iota(jnp.int32, x.shape, 1)
    low = lax.rem(lane, HD) < HD // 2
    return jnp.where(low, pltpu.roll(x, LANES - HD // 2, 1), pltpu.roll(x, HD // 2, 1))


MESH = pl.DeviceIdType.MESH


def partner(bit):
    side, at = lax.axis_index("stream"), lax.axis_index("batch")
    return (1 - side, at) if bit < 0 else (side, jnp.bitwise_xor(at, 1 << bit))


def greet(others):
    barrier = pltpu.get_barrier_semaphore()
    for other in others:
        pl.semaphore_signal(barrier, inc=1, device_id=other, device_id_type=MESH)
    pl.semaphore_wait(barrier, len(others))


def line_partners():
    side, at = lax.axis_index("stream"), lax.axis_index("batch")
    return [partner(-1)] + [(side, jnp.bitwise_xor(at, mask)) for mask in (1, 2, 4, 8, 12)]


class LineGather:
    SENDS = 29

    def __init__(self, chunks, send_sems, recv_sems, local_sems):
        self.chunks, self.send_sems, self.recv_sems, self.local_sems = chunks, send_sems, recv_sems, local_sems
        self.side, self.at = lax.axis_index("stream"), lax.axis_index("batch")
        self.z = lax.div(self.at, 4)

    @staticmethod
    def scratch(count):
        return [
            pltpu.SemaphoreType.DMA((count, LineGather.SENDS)),
            pltpu.SemaphoreType.DMA((count, 16)),
            pltpu.SemaphoreType.DMA((count,)),
        ]

    def copy(self, chunk, shard, target, number, own=False):
        source, place = self.chunks[chunk]
        return pltpu.make_async_remote_copy(
            src_ref=source if own else place(shard),
            dst_ref=place(shard),
            send_sem=self.send_sems.at[chunk, number],
            recv_sem=self.recv_sems.at[chunk, shard],
            device_id=(self.side, target),
            device_id_type=MESH,
        )

    def local(self, chunk):
        source, place = self.chunks[chunk]
        return pltpu.make_async_copy(source, place(self.at), self.local_sems.at[chunk])

    def sends(self, phase):
        at, z = self.at, self.z
        across, core = jnp.bitwise_xor(at, 2), jnp.bitwise_xor(at, 1)
        up, down = (at + 4, z < 3), (at - 4, z > 0)
        other = jnp.bitwise_xor
        if phase == 0:
            yield None, at, [(*up, 0), (*down, 1), (across, None, 2), (core, None, 3)]
        if 1 <= phase <= 3:
            n = 4 + 6 * (phase - 1)
            yield z >= phase, at - 4 * phase, [(*up, n), (across, None, n + 1), (core, None, n + 2)]
            yield z + phase <= 3, at + 4 * phase, [(*down, n + 3), (across, None, n + 4), (core, None, n + 5)]
        if phase == 1:
            yield None, across, [(core, None, 22)]
        if 2 <= phase <= 4:
            d, n = phase - 1, 23 + 2 * (phase - 2)
            yield z >= d, other(at - 4 * d, 2), [(core, None, n)]
            yield z + d <= 3, other(at + 4 * d, 2), [(core, None, n + 1)]

    def each(self, phase, act):
        for when, shard, sends in self.sends(phase):

            def run():
                act(shard, None, None)
                for target, whether, number in sends:
                    if whether is None:
                        act(shard, target, number)
                    else:
                        pl.when(whether)(lambda: act(shard, target, number))

            if when is None:
                run()
            else:
                pl.when(when)(run)

    def phase(self, chunk, phase):
        def act(shard, target, number):
            if target is None:
                if phase == 0:
                    self.local(chunk).start()
                else:
                    self.copy(chunk, shard, self.at, 0).wait_recv()
            else:
                self.copy(chunk, shard, target, number, own=phase == 0).start()

        self.each(phase, act)

    def finish(self):
        for chunk in range(len(self.chunks)):
            for n in range(8):
                shard = jnp.bitwise_xor(lax.rem(self.at, 2), 1) + 2 * n
                self.copy(chunk, shard, self.at, 0).wait_recv()
            self.local(chunk).wait()
            for phase in range(5):

                def act(shard, target, number):
                    if target is not None:
                        self.copy(chunk, shard, target, number, own=phase == 0).wait_send()

                self.each(phase, act)


class SlabSum:
    def __init__(self, order, keep, send, got, sems, load=None):
        self.order, self.keep, self.send, self.got, self.sems, self.load = (0, *order), keep, send, got, sems, load

    @staticmethod
    def scratch(slots, share, columns):
        steps = slots.bit_length()
        return [
            *[pltpu.VMEM((max(slots >> n, 1), share, columns), bf16) for n in (0, *range(steps))],
            pltpu.SemaphoreType.DMA((2 * steps + 1,)),
        ]

    def copy(self, step):
        count = self.got[step].shape[0]
        return pltpu.make_async_remote_copy(
            src_ref=self.send if step == 0 else self.keep.at[pl.ds(count, count)],
            dst_ref=self.got[step],
            send_sem=self.sems.at[2 * step],
            recv_sem=self.sems.at[2 * step + 1],
            device_id=partner(self.order[step]),
            device_id_type=MESH,
        )

    def loading(self):
        return pltpu.make_async_copy(self.load, self.keep, self.sems.at[2 * len(self.order)])

    def start(self):
        self.copy(0).start()
        if self.load is not None:
            self.loading().start()

    def step(self, step):
        if step == 1 and self.load is not None:
            self.loading().wait()
        self.copy(step - 1).wait_recv()
        got = self.got[step - 1]

        @pl.loop(0, got.shape[0])
        def _(n):
            self.keep[n] = (self.keep[n].astype(f32) + got[n].astype(f32)).astype(bf16)

        self.copy(step).start()

    def finish(self, out_ref, width, first=0):
        last = len(self.order) - 1
        self.copy(last).wait_recv()
        total = self.keep[0].astype(f32) + self.got[last][0].astype(f32)
        share = out_ref.shape[0]
        by = total.shape[0] // share
        block = out_ref.shape[1] if by == 1 else width // by
        for n in range(total.shape[1] // block):
            for i in range(by):
                at = first + (n * by + i) * block
                out_ref[:, at : at + block] = total[i * share : (i + 1) * share, n * block : (n + 1) * block]
        for step in range(len(self.order)):
            self.copy(step).wait_send()


ALL = (-1, 0, 1, 2, 3)
LATE = (0, 1, 2, 3, -1)


class GainSum:
    def __init__(self, bits, held, got, sems):
        self.bits, self.held, self.got, self.sems = bits, held, got, sems

    @staticmethod
    def scratch(bits, width):
        steps = len(bits)
        return [
            pltpu.VMEM((steps, 8, width), f32),
            pltpu.VMEM((steps, 8, width), f32),
            pltpu.SemaphoreType.DMA((2 * steps,)),
        ]

    def copy(self, step):
        return pltpu.make_async_remote_copy(
            src_ref=self.held.at[step],
            dst_ref=self.got.at[step],
            send_sem=self.sems.at[2 * step],
            recv_sem=self.sems.at[2 * step + 1],
            device_id=partner(self.bits[step]),
            device_id_type=MESH,
        )

    def start(self, value):
        self.held[0] = value
        self.copy(0).start()

    def step(self, step):
        self.copy(step - 1).wait_recv()
        self.held[step] = self.held[step - 1] + self.got[step - 1]
        self.copy(step).start()

    def finish(self, out_ref):
        last = len(self.bits) - 1
        self.copy(last).wait_recv()
        out_ref[...] = self.held[last] + self.got[last]
        for step in range(len(self.bits)):
            self.copy(step).wait_send()


def row_specs(tile, width, half):
    own = pl.BlockSpec((None, None, tile, width), lambda i, s: (0, s[0], jnp.minimum(i, half - 1), 0))
    away = pl.BlockSpec((tile, width), lambda i, s: (jnp.maximum(i - half, 0), 0))
    return own, away


def read_rows(own_ref, away_ref, half):
    return jnp.where(pl.program_id(0) < half, own_ref[...], away_ref[...])


def project_kernel(side_ref, own_ref, away_ref, gain_ref, w_ref, cos_ref, sin_ref, out_ref, hidden_ref, *, half):
    width = own_ref.shape[-1]
    project_tile(read_rows(own_ref, away_ref, half), gain_ref[...], lambda part: w_ref[:, part * width : (part + 1) * width],
                 cos_ref, sin_ref, out_ref, hidden_ref)


def project_tile(x, gain, weights, cos_ref, sin_ref, out_ref, hidden_ref):
    x = x.astype(f32)
    width = x.shape[1]
    center = x - jnp.mean(x, axis=1, keepdims=True)
    spread = jnp.mean(center * center, axis=1, keepdims=True)
    hidden = (center * lax.rsqrt(spread + 1e-5) * gain.astype(f32)).astype(bf16)
    hidden_ref[...] = hidden
    cosine, sine = cos_ref[...], sin_ref[...]
    for part in range(3):
        rows = mm(hidden, weights(part))
        for pair in range(width // LANES):
            cols = slice(pair * LANES, (pair + 1) * LANES)
            field = rows[:, cols]
            if part < 2:
                field = field * cosine + half_partner(field) * sine
            if part == 0:
                field = field * 0.125
            out_ref[part, :, cols] = field.astype(bf16)


def project(side, own, away, gain, w, cosine, sine, tile=512):
    length, width = away.shape
    tokens, half = 2 * length, length // tile
    table = pl.BlockSpec((tile, LANES), lambda i, s: (lax.rem(i, half), 0))
    return pl.pallas_call(
        functools.partial(project_kernel, half=half),
        name="project",
        grid_spec=pltpu.PrefetchScalarGridSpec(
            num_scalar_prefetch=1,
            grid=(2 * half,),
            in_specs=[
                *row_specs(tile, width, half),
                pl.BlockSpec((1, width), lambda i, s: (0, 0)),
                pl.BlockSpec((width, 3 * width), lambda i, s: (0, 0), pipeline_mode=pl.Buffered(1)),
                table,
                table,
            ],
            out_specs=[
                pl.BlockSpec((3, tile, width), lambda i, s: (0, i, 0)),
                pl.BlockSpec((tile, width), lambda i, s: (i, 0)),
            ],
        ),
        out_shape=[jax.ShapeDtypeStruct((3, tokens, width), bf16), jax.ShapeDtypeStruct((tokens, width), bf16)],
        compiler_params=pltpu.CompilerParams(vmem_limit_bytes=62 << 20),
        cost_estimate=pl.CostEstimate(
            flops=6 * tokens * width * width, bytes_accessed=tokens * width * 10 + 6 * width * width, transcendentals=0
        ),
    )(side, own, away, gain, w, cosine, sine)


def first_kernel(shard_ref, wo_ref, wu_ref, gain_ref, tokens_ref, own_ref, cos_ref, sin_ref,
                 qkv_ref, hidden_ref, away_out, w_out, wo_all, wu_all, gains_out,
                 w_all, away, rows, swap_sems, out_sems, *refs, half):
    side, at = lax.axis_index("stream"), lax.axis_index("batch")
    step = pl.program_id(0)
    width = own_ref.shape[-1]
    tile = own_ref.shape[-2]
    def swap(n):
        part = pl.ds(n * tile, tile)
        return pltpu.make_async_remote_copy(
            src_ref=tokens_ref.at[0, 1 - side, part],
            dst_ref=away.at[part],
            send_sem=swap_sems.at[0, n],
            recv_sem=swap_sems.at[1, n],
            device_id=(1 - side, at),
            device_id_type=MESH,
        )

    def chunk(n):
        cols = slice(n * width, (n + 1) * width)
        return shard_ref.at[:, cols], lambda shard: w_all.at[shard, :, cols]

    weights = LineGather([chunk(n) for n in range(3)], *refs[:3])
    part = wu_ref.at[:, : wu_all.shape[2]]
    others = LineGather([(wo_ref, lambda shard: wo_all.at[shard]), (part, lambda shard: wu_all.at[shard])], *refs[3:6])
    gain = GainSum((0, 1, 2, 3), *refs[6:])
    keeps = [
        pltpu.make_async_copy(w_all, w_out, out_sems.at[0]),
        pltpu.make_async_copy(away, away_out, out_sems.at[1]),
    ]

    @pl.when(step == 0)
    def _():
        greet(line_partners())
        for n in range(half):
            swap(n).start()
        gain.start(gain_ref[...])
        for phase in range(5):
            for n in range(3):
                weights.phase(n, phase)
            if 1 <= phase <= 3:
                gain.step(phase)
        gain.finish(gains_out)
        weights.finish()
        for n in range(2):
            others.phase(n, 0)
        keeps[0].start()

    for now in range(1, 4):

        @pl.when(step == now)
        def _():
            for n in range(2):
                others.phase(n, now)
            if now >= half:
                swap(now - half).wait()
            if now == 2 * half - 1:
                keeps[1].start()

    @pl.when(step < half)
    def _():
        rows[...] = own_ref[...]

    @pl.when(step >= half)
    def _():
        rows[...] = away[pl.ds(pl.multiple_of((step - half) * tile, tile), tile), :]

    project_tile(rows[...], gains_out[0:1, :], lambda part: w_all[:, :, part * width : (part + 1) * width].reshape(width, width),
                 cos_ref, sin_ref, qkv_ref, hidden_ref)

    @pl.when(step == pl.num_programs(0) - 1)
    def _():
        for n in range(2):
            others.phase(n, 4)
        others.finish()
        for keep in keeps:
            keep.wait()


def first(shard, wo, wu, cut, gain, tokens, cosine, sine, tile=512):
    _, _, length, width = tokens.shape
    rows = shard.shape[0]
    half = length // tile
    assert half == 2
    anywhere = pl.BlockSpec(memory_space=pl.ANY)
    table = pl.BlockSpec((tile, LANES), lambda i: (lax.rem(i, half), 0))
    small = pl.BlockSpec((8, width), lambda i: (0, 0))
    return pl.pallas_call(
        functools.partial(first_kernel, half=half),
        name="first",
        grid=(2 * half,),
        in_specs=[
            anywhere,
            anywhere,
            anywhere,
            small,
            anywhere,
            pl.BlockSpec((None, None, tile, width), lambda i: (0, lax.axis_index("stream"), jnp.minimum(i, half - 1), 0)),
            table,
            table,
        ],
        out_specs=[
            pl.BlockSpec((3, tile, width), lambda i: (0, i, 0)),
            pl.BlockSpec((tile, width), lambda i: (i, 0)),
            anywhere,
            anywhere,
            anywhere,
            anywhere,
            small,
        ],
        out_shape=[
            jax.ShapeDtypeStruct((3, 2 * length, width), bf16),
            jax.ShapeDtypeStruct((2 * length, width), bf16),
            jax.ShapeDtypeStruct((length, width), bf16),
            jax.ShapeDtypeStruct((16, rows, 3 * width), bf16),
            jax.ShapeDtypeStruct((16, rows, width), bf16),
            jax.ShapeDtypeStruct((16, rows, cut), bf16),
            jax.ShapeDtypeStruct((8, width), f32),
        ],
        scratch_shapes=[
            pltpu.VMEM((16, rows, 3 * width), bf16),
            pltpu.VMEM((length, width), bf16),
            pltpu.VMEM((tile, width), bf16),
            pltpu.SemaphoreType.DMA((2, half)),
            pltpu.SemaphoreType.DMA((2,)),
            *LineGather.scratch(3),
            *LineGather.scratch(2),
            *GainSum.scratch((0, 1, 2, 3), width),
        ],
        compiler_params=pltpu.CompilerParams(vmem_limit_bytes=62 << 20, collective_id=0, has_side_effects=True),
        cost_estimate=pl.CostEstimate(
            flops=12 * length * width * width, bytes_accessed=length * width * 24 + 12 * width * width, transcendentals=0
        ),
    )(shard, wo, wu, gain, tokens, tokens, cosine, sine)


def mask_tables(length, row_length):
    pos = jnp.arange(length)
    blk = (pos // BLOCK)[:, None]
    lane = (jnp.arange(LANES) % HD)[None, :]
    dead = (pos >= row_length)[:, None]
    clean_query = (lane == blk).astype(bf16)
    noisy_query = (lane == blk - 1).astype(bf16)
    main_key = jnp.where((blk > lane) | dead, BIG, 0.0).astype(bf16)
    diag_key = jnp.where((blk != lane) | dead, BIG, 0.0).astype(bf16)
    return clean_query, noisy_query, main_key, diag_key


def low_lanes(shape):
    return lax.broadcasted_iota(jnp.int32, shape, 1) < HD


def attend_gather_kernel(qkv_ref, cq_ref, nq_ref, mk_ref, dk_ref, wu_ref, wd_ref, grad_ref,
                         out_ref, log_ref, wu_all, wd_all, away_ref,
                         qa, ka, kd, va, s_scr, swap_sems, send_sems, recv_sems, local_sems):
    side, at = lax.axis_index("stream"), lax.axis_index("batch")
    step = pl.program_id(0)
    wide, tall = wu_all.shape[2] // 2, wd_ref.shape[0] // 2
    cut = wu_ref.shape[1] - 2 * wide

    def columns(n):
        cols = slice(n * wide, (n + 1) * wide)
        return wu_ref.at[:, cut + n * wide : cut + (n + 1) * wide], lambda shard: wu_all.at[shard, :, cols]

    def rows(n):
        part = slice(n * tall, (n + 1) * tall)
        return wd_ref.at[part, :], lambda shard: wd_all.at[shard, part, :]

    chunks = [columns(0), columns(1), rows(0), rows(1)]
    weights = LineGather(chunks, send_sems, recv_sems, local_sems)
    swap = pltpu.make_async_remote_copy(
        src_ref=grad_ref.at[0, 1 - side],
        dst_ref=away_ref,
        send_sem=swap_sems.at[0],
        recv_sem=swap_sems.at[1],
        device_id=(1 - side, at),
        device_id_type=MESH,
    )
    slots = 2 * SLOT_STEPS
    plan = [[] for _ in range(slots + 1)]
    items = [(chunk, phase) for phase in range(1, 5) for chunk in range(4)]
    for n, item in enumerate(items):
        plan[min(1 + n * SLOT_RATE // 16, slots)].append(item)

    @pl.when(step == 0)
    def _():
        greet(line_partners())
        for chunk in range(4):
            weights.phase(chunk, 0)
        swap.start()

    def pass_on(slot):
        for now in range(SLOT_STEPS):
            if plan[2 * now + slot]:

                @pl.when(step == now)
                def _():
                    for item in plan[2 * now + slot]:
                        weights.phase(*item)

    pass_on(0)
    attend_kernel(qkv_ref, cq_ref, nq_ref, mk_ref, dk_ref, out_ref, log_ref, qa, ka, kd, va, s_scr,
                  between=lambda: pass_on(1))

    @pl.when(step == pl.num_programs(0) - 1)
    def _():
        for item in plan[slots]:
            weights.phase(*item)
        weights.finish()
        swap.wait()


SLOT_STEPS = 6
SLOT_RATE = 12


def attend_kernel(qkv_ref, cq_ref, nq_ref, mk_ref, dk_ref, out_ref, log_ref,
                  qa, ka, kd, va, s_scr, between=lambda: None):
    length = out_ref.shape[1]
    clean = lax.axis_index("stream")
    noisy = 1 - clean
    tiles = length // TILE
    low = low_lanes((length, LANES))
    ones = jnp.ones((16, length), bf16)
    vc_t = qkv_ref[2, clean].T
    vn_t = qkv_ref[2, noisy].T
    for head in range(2):
        pick = low if head == 0 else jnp.logical_not(low)
        qa[0, head] = jnp.where(pick, qkv_ref[0, clean], cq_ref[...])
        qa[1, head] = jnp.where(pick, qkv_ref[0, noisy], nq_ref[...])
        qa[2, head] = jnp.where(pick, qkv_ref[0, noisy], cq_ref[...])
        ka[head] = jnp.where(pick, qkv_ref[1, clean], mk_ref[...])
        kd[head] = jnp.where(pick, qkv_ref[1, noisy], dk_ref[...])
        va[0, head, :HD] = vc_t[head * HD : (head + 1) * HD]
        va[1, head, :HD] = vn_t[head * HD : (head + 1) * HD]
        va[0, head, HD:] = ones
        va[1, head, HD:] = ones
    for copy in range(2):
        if copy:
            between()
        where_to = clean if copy == 0 else noisy
        for tile in range(tiles):
            rows = slice(tile * TILE, (tile + 1) * TILE)
            parts = []
            for head in range(2):
                pieces = [(qa[copy, head, rows, :], ka, 0, t) for t in range(tile + 1)]
                if copy == 1:
                    pieces.append((qa[2, head, rows, :], kd, 1, tile))
                top = None
                for n, (query, keys, vi, t) in enumerate(pieces):
                    s = mm_t(keys[head, t * TILE : (t + 1) * TILE, :], query)
                    if copy == 1 and tile == 0 and n == 0:
                        first = lax.broadcasted_iota(jnp.int32, s.shape, 1) < BLOCK
                        s = jnp.where(first, BIG, s)
                    s_scr[head, n * TILE : (n + 1) * TILE, :] = s
                    m = jnp.max(s, axis=0, keepdims=True)
                    top = m if top is None else jnp.maximum(top, m)
                acc = None
                for n, (query, keys, vi, t) in enumerate(pieces):
                    p = jnp.exp(s_scr[head, n * TILE : (n + 1) * TILE, :] - top).astype(bf16)
                    o = mm(va[vi, head, :, t * TILE : (t + 1) * TILE], p)
                    acc = o if acc is None else acc + o
                total = acc[HD : HD + 1, :]
                parts.append(acc[:HD] / total)
                log_ref[where_to, 0, head : head + 1, rows] = top + jnp.log(total)
            out_ref[where_to, rows, :] = jnp.concatenate(parts, axis=0).T.astype(bf16)


def attend(qkv, tables, shards=None, cut=0, grad=None):
    _, copies, length, width = qkv.shape
    pairs = width // LANES
    table_spec = pl.BlockSpec((length, LANES), lambda i: (0, 0), pipeline_mode=pl.Buffered(1))
    more_in, more_shapes, more_scratch = [], [], []
    body, params = attend_kernel, {}
    if shards is not None:
        assert pairs == SLOT_STEPS
        body = attend_gather_kernel
        params = dict(collective_id=3, has_side_effects=True)
        more_in = [*shards, grad]
        up, down = (shard.shape for shard in shards)
        more_shapes = [jax.ShapeDtypeStruct(s, bf16) for s in ((16, up[0], up[1] - cut), (16, *down))]
        more_shapes.append(jax.ShapeDtypeStruct((length, width), bf16))
        more_scratch = [pltpu.SemaphoreType.DMA((2,)), *LineGather.scratch(4)]
    anywhere = pl.BlockSpec(memory_space=pl.ANY)
    return pl.pallas_call(
        body,
        name="attend",
        grid=(pairs,),
        in_specs=[pl.BlockSpec((3, copies, length, LANES), lambda i: (0, 0, 0, i)), *[table_spec] * 4,
                  *[anywhere] * len(more_in)],
        out_specs=[
            pl.BlockSpec((copies, length, LANES), lambda i: (0, 0, i)),
            pl.BlockSpec((copies, 1, 2, length), lambda i: (0, i, 0, 0)),
            *[anywhere] * len(more_shapes),
        ],
        scratch_shapes=[
            pltpu.VMEM((3, 2, length, LANES), bf16),
            pltpu.VMEM((2, length, LANES), bf16),
            pltpu.VMEM((2, length, LANES), bf16),
            pltpu.VMEM((2, 2, HD + 16, length), bf16),
            pltpu.VMEM((2, length + TILE, TILE), f32),
            *more_scratch,
        ],
        out_shape=[
            jax.ShapeDtypeStruct((copies, length, width), bf16),
            jax.ShapeDtypeStruct((copies, pairs, 2, length), f32),
            *more_shapes,
        ],
        compiler_params=pltpu.CompilerParams(vmem_limit_bytes=62 << 20, **params),
        cost_estimate=pl.CostEstimate(
            flops=8 * length * length * width, bytes_accessed=16 * length * width, transcendentals=length * length * 12
        ),
    )(qkv, *tables, *more_in)


DOWN, UP, OUT = (-1, 1, 2, 3), (1, -1, 2, 3), (2, -1, 1, 3)
QKV = ((1, 2, 3, -1), (2, 1, 3, -1), (1, 2, 3, -1))


def attend_back_sum_kernel(*refs, orders):
    count = len(orders)
    core, refs = refs[:10], refs[10:]
    pairs, gain_ref, refs = refs[: 2 * count], refs[2 * count], refs[2 * count + 1 :]
    dqkv_ref, refs = refs[0], refs[1:]
    outs, gain_out, refs = refs[:count], refs[count], refs[count + 1 :]
    own, refs = refs[:10], refs[10:]
    per = len(refs[:-3]) // count
    sums = []
    for n, order in enumerate(orders):
        keep, *got, sems = refs[n * per : (n + 1) * per]
        sums.append(SlabSum(order, keep, pairs[2 * n + 1], got, sems, load=pairs[2 * n]))
    gain = GainSum(ALL, *refs[-3:])
    down, up, wo = sums
    step = pl.program_id(0)

    @pl.when(step == 0)
    def _():
        greet([partner(bit) for bit in ALL])
        for one in sums:
            one.start()
        gain.start(gain_ref[...])

    for at, plan in {
        1: ((down, 1), (up, 1), (wo, 1), (gain, 1)),
        2: ((wo, 2), (gain, 2)),
        3: ((down, 2), (up, 2), (wo, 3), (gain, 3)),
        4: ((down, 3), (up, 3), (wo, 4), (gain, 4)),
        5: ((down, 4), (up, 4)),
    }.items():

        @pl.when(step == at)
        def _():
            for one, number in plan:
                one.step(number)

    attend_back_kernel(*core, dqkv_ref, *own)

    @pl.when(step == pl.num_programs(0) - 1)
    def _():
        for one, out_ref in zip(sums, outs):
            one.finish(out_ref, gain_ref.shape[1])
        gain.finish(gain_out)


def attend_back_kernel(qkv_ref, o_ref, do_ref, log_ref, cq_ref, nq_ref, mk_ref, dk_ref, cos_ref, sin_ref,
                       dqkv_ref, qa, qz, ka, kd, kt, doz, dsum, dq, dkc, dvc):
    length = o_ref.shape[1]
    clean = lax.axis_index("stream")
    noisy = 1 - clean
    tiles = length // TILE
    low = low_lanes((length, LANES))
    zero = jnp.zeros((length, LANES), bf16)
    for copy in range(2):
        at = clean if copy == 0 else noisy
        kt[copy] = qkv_ref[1, at].T
        prod = (o_ref[at].astype(f32) * do_ref[at].astype(f32)).T
        dsum[copy, 0:1] = jnp.sum(prod[:HD], axis=0, keepdims=True)
        dsum[copy, 1:2] = jnp.sum(prod[HD:], axis=0, keepdims=True)
        for head in range(2):
            pick = low if head == 0 else jnp.logical_not(low)
            qa[copy, head] = jnp.where(pick, qkv_ref[0, at], (cq_ref, nq_ref)[copy][...])
            qz[copy, head] = jnp.where(pick, qkv_ref[0, at], zero)
            doz[copy, head] = jnp.where(pick, do_ref[at], zero)
            if copy == 0:
                ka[head] = jnp.where(pick, qkv_ref[1, at], mk_ref[...])
            else:
                qa[2, head] = jnp.where(pick, qkv_ref[0, at], cq_ref[...])
                kd[head] = jnp.where(pick, qkv_ref[1, at], dk_ref[...])
    cosine, sine = cos_ref[...], sin_ref[...]

    def piece(copy, tile, query, keys, kv_copy, krows):
        rows = slice(tile * TILE, (tile + 1) * TILE)
        kv_at = clean if kv_copy == 0 else noisy
        at = clean if copy == 0 else noisy
        probs, raws, dqs = [], [], []
        for head in range(2):
            s = mm_t(keys[head, krows, :], qa[query, head, rows, :])
            p = jnp.exp(s - log_ref[at, 0, head : head + 1, rows])
            if kv_copy == 0 and copy == 1 and tile == 0:
                first = lax.broadcasted_iota(jnp.int32, s.shape, 1) < BLOCK
                p = jnp.where(first, 0.0, p)
            dp = mm_t(qkv_ref[2, kv_at, krows, :], doz[copy, head, rows, :])
            raw = (p * (dp - dsum[copy, head : head + 1, rows])).astype(bf16)
            dqs.append(mm(kt[kv_copy, head * HD : (head + 1) * HD, krows], raw))
            probs.append(p.astype(bf16))
            raws.append(raw)
        p2 = jnp.concatenate(probs, axis=1)
        r2 = jnp.concatenate(raws, axis=1)
        do2 = jnp.concatenate([doz[copy, 0, rows, :], doz[copy, 1, rows, :]], axis=0)
        q2 = jnp.concatenate([qz[copy, 0, rows, :], qz[copy, 1, rows, :]], axis=0)
        return jnp.concatenate(dqs, axis=0), mm(r2, q2), mm(p2, do2)

    def finish(field, rotate, scale):
        if rotate:
            c, s = cosine, sine
            field = field * c - half_partner(field) * s
        return (field * scale if scale != 1.0 else field).astype(bf16)

    for tile in range(tiles):
        rows = slice(tile * TILE, (tile + 1) * TILE)
        dq_t, dk_t, dv_t = piece(1, tile, 2, kd, 1, rows)
        dq[1, :, rows] = dq_t
        dkc[rows, :] = dk_t
        dqkv_ref[2, noisy, rows, :] = dv_t.astype(bf16)
    dqkv_ref[1, noisy] = finish(dkc[...], True, 1.0)
    for tile in reversed(range(tiles)):
        rows = slice(tile * TILE, (tile + 1) * TILE)
        seen = slice(0, (tile + 1) * TILE)
        for copy in range(2):
            dq_t, dk_t, dv_t = piece(copy, tile, copy, ka, 0, seen)
            if copy == 0:
                dq[0, :, rows] = dq_t
            else:
                dq[1, :, rows] += dq_t
            if copy == 0 and tile == tiles - 1:
                dkc[...] = dk_t
                dvc[...] = dv_t
            else:
                dkc[seen, :] += dk_t
                dvc[seen, :] += dv_t
    dqkv_ref[2, clean] = dvc[...].astype(bf16)
    dqkv_ref[1, clean] = finish(dkc[...], True, 1.0)
    dqkv_ref[0, clean] = finish(dq[0].T, True, 0.125)
    dqkv_ref[0, noisy] = finish(dq[1].T, True, 0.125)


def attend_back(qkv, mixed, grad, logs, tables, cosine, sine, pairs=None, gain=None, slabs=()):
    _, copies, length, width = qkv.shape
    steps = width // LANES
    table_spec = pl.BlockSpec((length, LANES), lambda i: (0, 0), pipeline_mode=pl.Buffered(1))
    row_spec = pl.BlockSpec((copies, length, LANES), lambda i: (0, 0, i))
    three = pl.BlockSpec((3, copies, length, LANES), lambda i: (0, 0, 0, i))
    anywhere = pl.BlockSpec(memory_space=pl.ANY)

    def fixed(shape):
        return pl.BlockSpec(shape, lambda i: (0, 0), pipeline_mode=pl.Buffered(1))

    more_in, more_specs, more_shapes, more_out, more_scratch = [], [], [], [], []
    body, params = attend_back_kernel, {}
    if pairs is not None:
        assert steps == 6
        body = functools.partial(attend_back_sum_kernel, orders=(DOWN, UP, OUT))
        params = dict(collective_id=1, has_side_effects=True)
        for (keep, send), slab in zip(pairs, slabs):
            slots, share, columns = keep.shape
            more_in += [keep, send]
            more_specs += [anywhere] * 2
            more_shapes.append(jax.ShapeDtypeStruct(slab, f32))
            more_out.append(fixed(slab))
            more_scratch += SlabSum.scratch(slots, share, columns)
        more_in.append(gain)
        more_specs.append(fixed((8, width)))
        more_shapes.append(jax.ShapeDtypeStruct((8, width), f32))
        more_out.append(fixed((8, width)))
        more_scratch += GainSum.scratch(ALL, width)
    return pl.pallas_call(
        body,
        name="attend_back",
        grid_spec=pltpu.PrefetchScalarGridSpec(
            num_scalar_prefetch=0,
            grid=(steps,),
            in_specs=[three, row_spec, row_spec, pl.BlockSpec((copies, 1, 2, length), lambda i: (0, i, 0, 0))]
            + [table_spec] * 6
            + more_specs,
            out_specs=[three, *more_out],
            scratch_shapes=[
                pltpu.VMEM((3, 2, length, LANES), bf16),
                pltpu.VMEM((2, 2, length, LANES), bf16),
                pltpu.VMEM((2, length, LANES), bf16),
                pltpu.VMEM((2, length, LANES), bf16),
                pltpu.VMEM((2, LANES, length), bf16),
                pltpu.VMEM((2, 2, length, LANES), bf16),
                pltpu.VMEM((2, 2, length), f32),
                pltpu.VMEM((2, LANES, length), f32),
                pltpu.VMEM((length, LANES), f32),
                pltpu.VMEM((length, LANES), f32),
                *more_scratch,
            ],
        ),
        out_shape=[jax.ShapeDtypeStruct((3, copies, length, width), bf16), *more_shapes],
        compiler_params=pltpu.CompilerParams(vmem_limit_bytes=62 << 20, **params),
        cost_estimate=pl.CostEstimate(
            flops=20 * length * length * width, bytes_accessed=30 * length * width, transcendentals=length * length * 12
        ),
    )(qkv, mixed, grad, logs, *tables, cosine, sine, *more_in)


ROOT = math.sqrt(2.0 / math.pi)


def feed_kernel(side_ref, x_own, x_away, mixed_ref, g_own, g_away, gain_ref, wo_all, wu_all, wu_more, wd_all,
                out_own, out_away, act_ref, du_ref, h2_ref, dmid_ref, dbr_ref, dmix_ref, dgain_ref,
                wo_ref, wu_ref, wd_ref, sems, *, half):
    groups, rows, width = wo_ref.shape
    fold = wu_ref.shape[0]

    @pl.when(pl.program_id(0) == 0)
    def _():
        copies = [pltpu.make_async_copy(wo_all, wo_ref, sems.at[0])]
        begin = 0
        for array in (wu_all, wu_more):
            end = begin + array.shape[2]
            for n in range(fold):
                low, high = max(begin, n * width), min(end, (n + 1) * width)
                if low < high:
                    copies.append(
                        pltpu.make_async_copy(
                            array.at[:, :, low - begin : high - begin],
                            wu_ref.at[n, :, :, low - n * width : high - n * width],
                            sems.at[len(copies)],
                        )
                    )
            begin = end
        copies.append(pltpu.make_async_copy(wd_all, wd_ref, sems.at[len(copies)]))
        for copy in copies:
            copy.start()
        for copy in copies:
            copy.wait()

    def down(c):
        per = groups // fold
        return wd_ref[c * per : (c + 1) * per].reshape(width, width)

    wo = wo_ref[...].reshape(width, width)
    gain = gain_ref[...].astype(f32)
    middle = read_rows(x_own, x_away, half).astype(f32) + mm(mixed_ref[...], wo)
    center = middle - jnp.mean(middle, axis=1, keepdims=True)
    spread = jnp.mean(center * center, axis=1, keepdims=True)
    inv = lax.rsqrt(spread + 1e-5)
    norm = center * inv
    hidden = (norm * gain).astype(bf16)
    h2_ref[...] = hidden
    grad = read_rows(g_own, g_away, half)
    out = middle
    dh = jnp.zeros_like(middle)
    for c in range(fold):
        cols = slice(c * width, (c + 1) * width)
        up = wu_ref[c].reshape(width, width)
        u = mm(hidden, up)
        da = mm_t(grad, down(c)).astype(bf16).astype(f32)
        sq = u * u
        t = jnp.tanh(u * (ROOT + (ROOT * 0.044715) * sq))
        part = 0.5 + 0.5 * t
        act = (u * part).astype(bf16)
        slope = part + (u * (part * (1.0 - t))) * (ROOT + (3 * ROOT * 0.044715) * sq)
        du = (da * slope).astype(bf16)
        act_ref[:, cols] = act
        du_ref[:, cols] = du
        out = out + mm(act, down(c))
        dh = dh + mm_t(du, up)
    low = out.astype(bf16)

    @pl.when(pl.program_id(0) < half)
    def _():
        out_own[...] = low

    @pl.when(pl.program_id(0) >= half)
    def _():
        out_away[...] = low

    @pl.when(pl.program_id(0) == 0)
    def _():
        dgain_ref[...] = jnp.zeros_like(dgain_ref)

    dgain_ref[...] += jnp.sum((dh * norm).reshape(-1, 8, width), axis=0)
    e = dh * gain
    dmid = grad.astype(f32) + inv * (
        e - jnp.mean(e, axis=1, keepdims=True) - norm * jnp.mean(e * norm, axis=1, keepdims=True)
    )
    dmid_ref[...] = dmid
    dbr = dmid.astype(bf16)
    dbr_ref[...] = dbr
    dmix_ref[...] = mm_t(dbr, wo).astype(bf16)


def feed(side, x_own, x_away, mixed, g_own, g_away, gain, weights, tile=512):
    tokens, width = mixed.shape
    groups, rows, _ = weights[0].shape
    ff = weights[1].shape[2] + weights[2].shape[2]
    fold = ff // width
    half = tokens // 2 // tile
    row = pl.BlockSpec((tile, width), lambda i, s: (i, 0))
    wide = pl.BlockSpec((tile, ff), lambda i, s: (i, 0))
    own, away = row_specs(tile, width, half)

    def keep(shape):
        return pl.BlockSpec(shape, lambda i, s: (0, 0), pipeline_mode=pl.Buffered(1))

    return pl.pallas_call(
        functools.partial(feed_kernel, half=half),
        name="feed",
        grid_spec=pltpu.PrefetchScalarGridSpec(
            num_scalar_prefetch=1,
            grid=(2 * half,),
            in_specs=[own, away, row, own, away, keep((1, width)), *[pl.BlockSpec(memory_space=pl.ANY)] * 4],
            out_specs=[own, away, wide, wide, row, row, row, row, pl.BlockSpec((8, width), lambda i, s: (0, 0))],
            scratch_shapes=[
                pltpu.VMEM((groups, rows, width), bf16),
                pltpu.VMEM((fold, groups, rows, width), bf16),
                pltpu.VMEM((groups, fold * rows, width), bf16),
                pltpu.SemaphoreType.DMA((3 + fold,)),
            ],
        ),
        out_shape=[
            jax.ShapeDtypeStruct((1, 2, tokens // 2, width), bf16),
            jax.ShapeDtypeStruct((tokens // 2, width), bf16),
            jax.ShapeDtypeStruct((tokens, ff), bf16),
            jax.ShapeDtypeStruct((tokens, ff), bf16),
            jax.ShapeDtypeStruct((tokens, width), bf16),
            jax.ShapeDtypeStruct((tokens, width), f32),
            jax.ShapeDtypeStruct((tokens, width), bf16),
            jax.ShapeDtypeStruct((tokens, width), bf16),
            jax.ShapeDtypeStruct((8, width), f32),
        ],
        compiler_params=pltpu.CompilerParams(vmem_limit_bytes=62 << 20),
        cost_estimate=pl.CostEstimate(
            flops=tokens * width * (4 * width + 8 * ff), bytes_accessed=tokens * (width * 18 + ff * 4),
            transcendentals=tokens * ff
        ),
    )(side, x_own, x_away, mixed, g_own, g_away, gain, *weights)


def folds(share):
    return 1 if share % 16 == 0 else 2


def fold(slab):
    if folds(slab.shape[0]) == 1:
        return slab
    middle = slab.shape[1] // 2
    return jnp.concatenate([slab[:, :middle], slab[:, middle:]], axis=0)


def arranged(slot, order):
    return sum((slot >> bit & 1) << (len(order) - 1 - n) for n, bit in enumerate(order))


def weight_kernel(me_ref, left_ref, *refs, share, split, order):
    weight_slabs(me_ref[0], left_ref, *refs, share=share, split=split, order=order)


def weight_slabs(me, left_ref, *refs, share, split, order):
    right_refs, (keep_ref, send_ref, scr) = refs[:-3], refs[-3:]
    if split:
        own_ref, away_ref = right_refs
        half = own_ref.shape[0]
        total = t_mm(left_ref[:half], own_ref[...]) + t_mm(left_ref[half:], away_ref[...])
    else:
        total = t_mm(left_ref[...], right_refs[0][...])
    slabs = total.shape[0] // share
    scr[...] = total.reshape(scr.shape)
    low_me = lax.rem(me, slabs)
    for slot in range(slabs):
        source = jnp.bitwise_xor(low_me, slot)
        into = send_ref if slot % 2 else keep_ref
        into[arranged(slot // 2, order)] = fold(scr[source]).astype(bf16)


def weight_grad_columns(me, left, right, block, share, order, name):
    tokens, dl = left.shape
    dr = right.shape[1]
    peers = dl // share
    by = folds(share)
    shape = (peers // 2, share * by, dr // by)
    out = pl.BlockSpec((peers // 2, share * by, block // by), lambda j, m: (0, 0, j))
    return pl.pallas_call(
        functools.partial(weight_kernel, share=share, split=False, order=order),
        name=name,
        grid_spec=pltpu.PrefetchScalarGridSpec(
            num_scalar_prefetch=1,
            grid=(dr // block,),
            in_specs=[
                pl.BlockSpec((tokens, dl), lambda j, m: (0, 0), pipeline_mode=pl.Buffered(1)),
                pl.BlockSpec((tokens, block), lambda j, m: (0, j)),
            ],
            out_specs=[out, out],
            scratch_shapes=[pltpu.VMEM((peers, share, block), f32)],
        ),
        out_shape=[jax.ShapeDtypeStruct(shape, bf16)] * 2,
        compiler_params=pltpu.CompilerParams(vmem_limit_bytes=62 << 20),
        cost_estimate=pl.CostEstimate(
            flops=2 * tokens * dl * dr, bytes_accessed=2 * tokens * (dl + dr) + 2 * dl * dr, transcendentals=0
        ),
    )(me, left, right)


def weight_grad_rows(me, left, own, away, block, share, name):
    tokens, dl = left.shape
    length, dr = away.shape
    slabs = block // share
    steps = dl // block
    assert steps == 4
    shape = (2, slabs // 2, 2, share, dr)
    out = pl.BlockSpec((None, slabs // 2, None, share, dr), lambda j, m: (lax.div(j, 2), 0, lax.rem(j, 2), 0, 0))
    bits = (slabs // 2).bit_length() - 1

    def place(j, m):
        return (0, jnp.bitwise_xor(j, lax.div(m[0], slabs)))

    return pl.pallas_call(
        functools.partial(weight_kernel, share=share, split=True, order=tuple(range(bits))),
        name=name,
        grid_spec=pltpu.PrefetchScalarGridSpec(
            num_scalar_prefetch=1,
            grid=(steps,),
            in_specs=[
                pl.BlockSpec((tokens, block), place),
                pl.BlockSpec((None, None, length, dr), lambda j, m: (0, m[1], 0, 0), pipeline_mode=pl.Buffered(1)),
                pl.BlockSpec((length, dr), lambda j, m: (0, 0), pipeline_mode=pl.Buffered(1)),
            ],
            out_specs=[out, out],
            scratch_shapes=[pltpu.VMEM((slabs, share, dr), f32)],
        ),
        out_shape=[jax.ShapeDtypeStruct(shape, bf16)] * 2,
        compiler_params=pltpu.CompilerParams(vmem_limit_bytes=62 << 20),
        cost_estimate=pl.CostEstimate(
            flops=2 * tokens * dl * dr, bytes_accessed=2 * tokens * (dl + dr) + 2 * dl * dr, transcendentals=0
        ),
    )(me, left, own, away)


def last_kernel(x_own, x_away, gain_ref, w_hbm, dqkv_hbm, dmid_hbm, hidden_hbm,
                dx_ref, dw_ref, gain_out,
                xv, w_ref, dqkv, dmid, hidden, send, land, dgain, scr,
                load_sems, tile_sems, send_sems, recv_sems, out_sems, *refs, share):
    count = len(QKV)
    per = len(refs[:-3]) // count
    sums = []
    for n, order in enumerate(QKV):
        first, keep, *got, sems = refs[n * per : (n + 1) * per]
        sums.append(SlabSum(order, keep, first, got, sems))
    gain = GainSum(LATE, *refs[-3:])
    side, at = lax.axis_index("stream"), lax.axis_index("batch")
    me = side * lax.axis_size("batch") + at
    step = pl.program_id(0)
    width = w_ref.shape[0]
    length = land.shape[0]
    tiles = pl.num_programs(0)
    tile = 2 * length // 8
    half = 4

    def rows_of(t, base=0):
        return pl.ds(pl.multiple_of((t - base) * tile, tile), tile)

    loads = [
        pltpu.make_async_copy(w_hbm, w_ref, load_sems.at[0]),
        pltpu.make_async_copy(x_away, xv.at[pl.ds(length, length)], load_sems.at[1]),
        pltpu.make_async_copy(hidden_hbm, hidden, load_sems.at[2]),
        pltpu.make_async_copy(x_own.at[0, side], xv.at[pl.ds(0, length)], load_sems.at[3]),
    ]

    def load_grad(t):
        return pltpu.make_async_copy(dqkv_hbm.at[:, rows_of(t), :], dqkv.at[:, rows_of(t), :], tile_sems.at[0, t])

    def load_middle(t):
        return pltpu.make_async_copy(dmid_hbm.at[rows_of(t), :], dmid.at[rows_of(t), :], tile_sems.at[1, t])

    def away(t):
        return pltpu.make_async_remote_copy(
            src_ref=send.at[rows_of(t, half), :],
            dst_ref=land.at[rows_of(t, half), :],
            send_sem=send_sems.at[t - half],
            recv_sem=recv_sems.at[t - half],
            device_id=(1 - side, at),
            device_id_type=MESH,
        )

    def result(t, row):
        return pltpu.make_async_copy(
            dmid.at[rows_of(t), :],
            dx_ref.at[0, row, pl.ds(pl.multiple_of(lax.rem(t, half) * tile, tile), tile), :],
            out_sems.at[t],
        )

    @pl.when(step == 0)
    def _():
        loads[0].start()
        loads[1].start()
        load_grad(4).start()
        load_middle(4).start()
        loads[2].start()
        for t in (5, 6, 7, 0, 1, 2, 3):
            load_grad(t).start()
        loads[3].start()
        for t in (5, 6, 7, 0, 1, 2, 3):
            load_middle(t).start()
        dgain[...] = jnp.zeros_like(dgain)
        greet([partner(bit) for bit in ALL])
        loads[0].wait()
        loads[1].wait()
        load_grad(4).wait()
        load_middle(4).wait()

    @pl.when(step > 0)
    def _():
        load_middle(lax.rem(step + half, 8)).wait()

    @pl.when(step == half)
    def _():
        loads[3].wait()

    for now, plan in {
        1: ((0, 1), (1, 1)),
        2: ((0, 2), (2, 1)),
        3: ((1, 2),),
        4: ((0, 3),),
        6: ((2, 2), (1, 3)),
        7: ((0, 4),),
    }.items():

        @pl.when(step == now)
        def _():
            for n, number in plan:
                sums[n].step(number)

    t = lax.rem(step + half, 8)
    rows = rows_of(t)
    x = xv[rows, :].astype(f32)
    center = x - jnp.mean(x, axis=1, keepdims=True)
    spread = jnp.mean(center * center, axis=1, keepdims=True)
    inv = lax.rsqrt(spread + 1e-5)
    norm = center * inv
    dh = mm_t(dqkv[0, rows, :], w_ref[:, :width])
    dh = dh + mm_t(dqkv[1, rows, :], w_ref[:, width : 2 * width])
    dh = dh + mm_t(dqkv[2, rows, :], w_ref[:, 2 * width :])
    dgain[...] += jnp.sum((dh * norm).reshape(-1, 8, width), axis=0)
    e = dh * gain_ref[...]
    dx = dmid[rows, :] + inv * (
        e - jnp.mean(e, axis=1, keepdims=True) - norm * jnp.mean(e * norm, axis=1, keepdims=True)
    )

    @pl.when(step < half)
    def _():
        send[rows_of(step), :] = dx.astype(bf16)
        away(t).start()

    @pl.when(step >= half)
    def _():
        dmid[rows, :] = dx
        result(t, side).start()

    def part(n):
        order = tuple({-1: 3, 1: 0, 2: 1, 3: 2}[bit] for bit in QKV[n])
        weight_slabs(me, hidden, dqkv.at[n], sums[n].keep, sums[n].send, scr, share=share, split=False, order=order)
        sums[n].start()

    @pl.when(step == 0)
    def _():
        loads[2].wait()
        for other in (5, 6, 7, 0, 1, 2, 3):
            load_grad(other).wait()
        part(0)
        part(1)

    @pl.when(step == 1)
    def _():
        part(2)

    @pl.when(step == tiles - 1)
    def _():
        gain.start(dgain[...])
        sums[2].step(3)
        sums[1].step(4)
        sums[0].finish(dw_ref, width, 0)
        gain.step(1)
        sums[2].step(4)
        gain.step(2)
        sums[1].finish(dw_ref, width, width)
        gain.step(3)
        sums[2].finish(dw_ref, width, 2 * width)
        gain.step(4)
        for other in range(half, 8):
            away(other).wait()
            dmid[rows_of(other), :] = land[rows_of(other, half), :].astype(f32)
            result(other, 1 - side).start()
        gain.finish(gain_out)
        for other in range(8):
            result(other, side).wait()


def last(tokens, x_away, gain, w, dqkv, dmid, hidden, share):
    tokens_all, width = hidden.shape
    length = tokens_all // 2
    slots = width // share // 2
    anywhere = pl.BlockSpec(memory_space=pl.ANY)

    def fixed(shape):
        return pl.BlockSpec(shape, lambda i: (0, 0), pipeline_mode=pl.Buffered(1))

    scratch = []
    for _ in range(3):
        by = folds(share)
        scratch += [
            pltpu.VMEM((slots, share * by, width // by), bf16),
            *SlabSum.scratch(slots, share * by, width // by),
        ]
    return pl.pallas_call(
        functools.partial(last_kernel, share=share),
        name="last",
        grid=(8,),
        in_specs=[anywhere, anywhere, fixed((1, width)), *[anywhere] * 4],
        out_specs=[anywhere, fixed((share, 3 * width)), fixed((8, width))],
        out_shape=[
            jax.ShapeDtypeStruct((1, 2, length, width), f32),
            jax.ShapeDtypeStruct((share, 3 * width), f32),
            jax.ShapeDtypeStruct((8, width), f32),
        ],
        scratch_shapes=[
            pltpu.VMEM((2 * length, width), bf16),
            pltpu.VMEM((width, 3 * width), bf16),
            pltpu.VMEM((3, 2 * length, width), bf16),
            pltpu.VMEM((2 * length, width), f32),
            pltpu.VMEM((2 * length, width), bf16),
            pltpu.VMEM((length, width), bf16),
            pltpu.VMEM((length, width), bf16),
            pltpu.VMEM((8, width), f32),
            pltpu.VMEM((2 * slots, share, width), f32),
            pltpu.SemaphoreType.DMA((4,)),
            pltpu.SemaphoreType.DMA((2, 8)),
            pltpu.SemaphoreType.DMA((4,)),
            pltpu.SemaphoreType.DMA((4,)),
            pltpu.SemaphoreType.DMA((8,)),
            *scratch,
            *GainSum.scratch(LATE, width),
        ],
        compiler_params=pltpu.CompilerParams(vmem_limit_bytes=62 << 20, collective_id=2, has_side_effects=True),
        cost_estimate=pl.CostEstimate(
            flops=24 * length * width * width, bytes_accessed=36 * length * width, transcendentals=0
        ),
    )(tokens, x_away, gain, w, dqkv, dmid, hidden)


def project_back_kernel(side_ref, x_ref, gain_ref, w_ref, dqkv_ref, dmid_ref, dx_ref, dgain_ref):
    x = x_ref[...].astype(f32)
    width = x.shape[1]
    center = x - jnp.mean(x, axis=1, keepdims=True)
    spread = jnp.mean(center * center, axis=1, keepdims=True)
    inv = lax.rsqrt(spread + 1e-5)
    norm = center * inv
    dh = mm_t(dqkv_ref[0], w_ref[:, :width])
    dh = dh + mm_t(dqkv_ref[1], w_ref[:, width : 2 * width])
    dh = dh + mm_t(dqkv_ref[2], w_ref[:, 2 * width :])

    @pl.when(pl.program_id(0) == 0)
    def _():
        dgain_ref[...] = jnp.zeros_like(dgain_ref)

    dgain_ref[...] += jnp.sum((dh * norm).reshape(-1, 8, width), axis=0)
    e = dh * gain_ref[...].astype(f32)
    dx_ref[...] = (dmid_ref[...] + inv * (
        e - jnp.mean(e, axis=1, keepdims=True) - norm * jnp.mean(e * norm, axis=1, keepdims=True)
    )).astype(dx_ref.dtype)


def project_back(side, x, gain, w, dqkv, dmid, away, tile=256):
    width = x.shape[-1]
    length = dmid.shape[0] // 2
    half = length // tile
    first = half if away else 0
    if away:
        x_spec = pl.BlockSpec((tile, width), lambda i, s: (i, 0))
        out_spec, out_shape = x_spec, jax.ShapeDtypeStruct((length, width), bf16)
    else:
        x_spec = pl.BlockSpec((None, None, tile, width), lambda i, s: (0, s[0], i, 0))
        out_spec, out_shape = x_spec, jax.ShapeDtypeStruct((1, 2, length, width), f32)
    return pl.pallas_call(
        project_back_kernel,
        name="project_back_away" if away else "project_back_own",
        grid_spec=pltpu.PrefetchScalarGridSpec(
            num_scalar_prefetch=1,
            grid=(half,),
            in_specs=[
                x_spec,
                pl.BlockSpec((1, width), lambda i, s: (0, 0)),
                pl.BlockSpec((width, 3 * width), lambda i, s: (0, 0), pipeline_mode=pl.Buffered(1)),
                pl.BlockSpec((3, tile, width), lambda i, s: (0, i + first, 0)),
                pl.BlockSpec((tile, width), lambda i, s: (i + first, 0)),
            ],
            out_specs=[out_spec, pl.BlockSpec((8, width), lambda i, s: (0, 0))],
        ),
        out_shape=[out_shape, jax.ShapeDtypeStruct((8, width), f32)],
        compiler_params=pltpu.CompilerParams(vmem_limit_bytes=62 << 20),
        cost_estimate=pl.CostEstimate(
            flops=6 * length * width * width, bytes_accessed=length * width * 16, transcendentals=0
        ),
    )(side, x, gain, w, dqkv, dmid)


def flip(x, bit):
    axis, by = ("stream", 1) if bit < 0 else ("batch", 1 << bit)
    return lax.ppermute(x, axis, [(i, i ^ by) for i in range(lax.axis_size(axis))])


def after(value, *others):
    return lax.optimization_barrier((value, *others))[0]


def shards(tokens, cotangent, lengths, ln1_gain, w_qkv, w_out, ln2_gain, w_up, w_down):
    side = lax.axis_index("stream")
    at = lax.axis_index("batch")
    _, rows_dev, length, width = tokens.shape
    assert rows_dev == 2
    ff = w_up.shape[1]
    peers = lax.axis_size("batch")
    small = peers == 16 and width % (16 * peers) == 0
    side_array = side.reshape(1).astype(jnp.int32)
    index = side * peers + at
    me = jnp.stack([index if small else 0 * index, side]).astype(jnp.int32)
    share = width // (2 * peers)
    cut = ff // 3 // LANES * LANES

    cosine, sine = rotary_tables(length)
    tables = mask_tables(length, jnp.take(lengths, side))
    if small:
        rows = width // peers
        gains = jnp.zeros((8, width), f32)
        gains = lax.dynamic_update_slice(gains, jnp.stack([ln1_gain, ln2_gain]).astype(f32), (0, at * rows))
        qkv, hidden, x_away, w_qkv_all, wo_all, wu_all, gains = first(
            w_qkv, w_out, w_up, cut, gains, tokens, cosine, sine
        )
        qkv4 = qkv.reshape(3, 2, length, width)
        w_qkv_all = w_qkv_all.reshape(width, 3 * width)
        gain_one, gain_two = gains[0:1], gains[1:2]
        mixed, logs, wu_more, wd_all, g_away = attend(qkv4, tables, (w_up, w_down), cut, cotangent)
        weights = [wo_all, wu_all, wu_more, wd_all]
    else:

        def whole(x):
            return lax.all_gather(x, "batch", axis=0, tiled=True)

        x_away = flip(lax.dynamic_index_in_dim(tokens[0], 1 - side, 0, False), -1)
        g_away = flip(lax.dynamic_index_in_dim(cotangent[0], 1 - side, 0, False), -1)
        w_qkv_all = whole(w_qkv)
        gain_one, gain_two = (whole(gain)[None].astype(f32) for gain in (ln1_gain, ln2_gain))
        weights = [whole(w).reshape(16, -1, w.shape[1]) for w in (w_out, w_up, w_down)]
        weights[1:2] = [weights[1][:, :, :cut], weights[1][:, :, cut:]]
        qkv, hidden = project(side_array, tokens, x_away, gain_one, w_qkv_all, cosine, sine)
        qkv4 = qkv.reshape(3, 2, length, width)
        mixed, logs = attend(qkv4, tables)
    mixed2 = mixed.reshape(2 * length, width)
    out, out_away, act, du, h2, dmid, dbr, dmix, dgain_two = feed(
        side_array, tokens, x_away, mixed2, cotangent, g_away, gain_two, weights
    )

    def place(result, away):
        away = flip(away, -1).astype(result.dtype)
        return lax.dynamic_update_slice(result, away[None, None], (0, 1 - side, 0, 0))

    out = place(out, out_away)
    unit = share if small else width // 32
    places = {-1: 3, 1: 0, 2: 1, 3: 2}

    def columns_grad(left, right, order, name):
        return weight_grad_columns(me, left, right, width, unit, [places[bit] for bit in order], name)

    down = weight_grad_rows(me, act, cotangent, g_away, width, ff // width * unit, "grad_down")
    down = [part.reshape(16, -1, width) for part in down]
    up = columns_grad(h2, du, UP, "grad_up")
    wo = columns_grad(mixed2, dbr, OUT, "grad_out")
    dmix = after(dmix.reshape(2, length, width), out)
    common = qkv4, mixed, dmix, logs, tables, cosine, sine
    if small:
        dqkv, down, up, wo, dgain_two = attend_back(
            *common, (down, up, wo), dgain_two, ((ff // width * share, width), (share, ff), (share, width))
        )
    else:
        dqkv, = attend_back(*common)
    dqkv3 = dqkv.reshape(3, 2 * length, width)
    if small:
        dx, wq, dgain_one = last(tokens, x_away, gain_one, w_qkv_all, dqkv3, dmid, hidden, share)
    else:
        dx_away, dgain_away = project_back(side_array, x_away, gain_one, w_qkv_all, dqkv3, dmid, True)
        dx, dgain_own = project_back(side_array, tokens, gain_one, w_qkv_all, dqkv3, dmid, False)
        dgain_one = dgain_own + dgain_away
        dx = place(dx, dx_away)
    dgain_one, dgain_two = (jnp.sum(g, axis=0, keepdims=True) for g in (dgain_one, dgain_two))
    if not small:

        def scatter(pair, order):
            slots = jnp.stack(pair, axis=1)
            natural = [arranged(n, order) for n in range(16)]
            slots = slots[jnp.array(natural)]
            by = folds(unit) if slots.shape[2] == 2 * unit else 1
            slots = slots.reshape(32, by, slots.shape[2] // by, -1, width // by).transpose(0, 2, 3, 1, 4)
            rows = slots.reshape(32 * slots.shape[1], -1)
            return lax.psum_scatter(rows, ("stream", "batch"), scatter_dimension=0, tiled=True).astype(f32)

        parts = [columns_grad(hidden, dqkv3[n], QKV[n], "grad_qkv") for n in range(3)]
        down, up, wo, *parts = (
            scatter(pair, [places[bit] for bit in order])
            for pair, order in zip((down, up, wo, *parts), (DOWN, UP, OUT, *QKV))
        )
        wq = jnp.concatenate(parts, axis=1)
        dgain_one, dgain_two = lax.psum((dgain_one, dgain_two), ("stream", "batch"))
    begin = index * share
    dgain_one, dgain_two = (lax.dynamic_slice(g[0], (begin,), (share,)) for g in (dgain_one, dgain_two))
    return out, dx, dgain_one, wq, wo, dgain_two, up, down


def solution(mesh):
    token = P("stream", "batch", None, None)
    vector, matrix = P("batch"), P("batch", None)
    out_vector, out_matrix = P(("stream", "batch")), P(("stream", "batch"), None)
    return jax.shard_map(
        shards,
        mesh=mesh,
        in_specs=(token, token, vector, vector, matrix, matrix, vector, matrix, matrix),
        out_specs=(token, token, out_vector, out_matrix, out_matrix, out_vector, out_matrix, out_matrix),
        check_vma=False,
    )
```

```python
import functools
import math

import jax
import jax.numpy as jnp
from jax import lax
from jax.experimental import pallas as pl
from jax.experimental.pallas import tpu as pltpu
from jax.sharding import PartitionSpec as P

HD = 64
BLOCK = 16
LANES = 128
TILE = 256
BIG = -1e30
f32, bf16 = jnp.float32, jnp.bfloat16


def mm(a, b):
    return lax.dot_general(a, b, (((1,), (0,)), ((), ())), preferred_element_type=f32)


def mm_t(a, b):
    return lax.dot_general(a, b, (((1,), (1,)), ((), ())), preferred_element_type=f32)


def t_mm(a, b):
    return lax.dot_general(a, b, (((0,), (0,)), ((), ())), preferred_element_type=f32)


def rotary_tables(length):
    half = HD // 2
    places = jnp.arange(length).astype(f32)
    rates = jnp.exp(jnp.arange(half).astype(f32) * (-2.0 * math.log(10000.0) / HD))
    angles = places[:, None] * rates[None, :]
    cosine, sine = jnp.cos(angles), jnp.sin(angles)
    return (
        jnp.concatenate([cosine] * 4, axis=1),
        jnp.concatenate([-sine, sine, -sine, sine], axis=1),
    )


def half_partner(x):
    lane = lax.broadcasted_iota(jnp.int32, x.shape, 1)
    low = lax.rem(lane, HD) < HD // 2
    return jnp.where(low, pltpu.roll(x, LANES - HD // 2, 1), pltpu.roll(x, HD // 2, 1))


MESH = pl.DeviceIdType.MESH


def partner(bit):
    side, at = lax.axis_index("stream"), lax.axis_index("batch")
    return (1 - side, at) if bit < 0 else (side, jnp.bitwise_xor(at, 1 << bit))


def greet(others):
    barrier = pltpu.get_barrier_semaphore()
    for other in others:
        pl.semaphore_signal(barrier, inc=1, device_id=other, device_id_type=MESH)
    pl.semaphore_wait(barrier, len(others))


def line_partners():
    side, at = lax.axis_index("stream"), lax.axis_index("batch")
    return [partner(-1)] + [(side, jnp.bitwise_xor(at, mask)) for mask in (1, 2, 4, 8, 12)]


class LineGather:
    SENDS = 37

    def __init__(self, chunks, send_sems, recv_sems, local_sems, across_first=()):
        self.across_first = across_first
        self.chunks, self.send_sems, self.recv_sems, self.local_sems = chunks, send_sems, recv_sems, local_sems
        self.side, self.at = lax.axis_index("stream"), lax.axis_index("batch")
        self.z = lax.div(self.at, 4)

    @staticmethod
    def scratch(count):
        return [
            pltpu.SemaphoreType.DMA((count, LineGather.SENDS)),
            pltpu.SemaphoreType.DMA((count, 16)),
            pltpu.SemaphoreType.DMA((count,)),
        ]

    def copy(self, chunk, shard, target, number, own=False):
        source, place = self.chunks[chunk]
        return pltpu.make_async_remote_copy(
            src_ref=source if own else place(shard),
            dst_ref=place(shard),
            send_sem=self.send_sems.at[chunk, number],
            recv_sem=self.recv_sems.at[chunk, shard],
            device_id=(self.side, target),
            device_id_type=MESH,
        )

    def local(self, chunk):
        source, place = self.chunks[chunk]
        return pltpu.make_async_copy(source, place(self.at), self.local_sems.at[chunk])

    def sends(self, chunk, phase):
        at, z = self.at, self.z
        across, core = jnp.bitwise_xor(at, 2), jnp.bitwise_xor(at, 1)
        up, down = (at + 4, z < 3), (at - 4, z > 0)
        other = jnp.bitwise_xor
        early = chunk in self.across_first
        if phase == 0:
            yield None, at, [(*up, 0), (*down, 1), (across, None, 2), (core, None, 3)]
        if 1 <= phase <= 3:
            n = 4 + 6 * (phase - 1)
            below, above = [(*up, n), (core, None, n + 2)], [(*down, n + 3), (core, None, n + 5)]
            if not early:
                below.append((across, None, n + 1))
                above.append((across, None, n + 4))
            yield z >= phase, at - 4 * phase, below
            yield z + phase <= 3, at + 4 * phase, above
        if phase == 1:
            yield None, across, [(*up, 22), (*down, 23), (core, None, 24)] if early else [(core, None, 24)]
        if 2 <= phase <= 4:
            d, n = phase - 1, 25 + 4 * (phase - 2)
            below, above = [(core, None, n + 1)], [(core, None, n + 3)]
            if early:
                below.append((*up, n))
                above.append((*down, n + 2))
            yield z >= d, other(at - 4 * d, 2), below
            yield z + d <= 3, other(at + 4 * d, 2), above

    def each(self, chunk, phase, act):
        for when, shard, sends in self.sends(chunk, phase):

            def run():
                act(shard, None, None)
                for target, whether, number in sends:
                    if whether is None:
                        act(shard, target, number)
                    else:
                        pl.when(whether)(lambda: act(shard, target, number))

            if when is None:
                run()
            else:
                pl.when(when)(run)

    def phase(self, chunk, phase):
        def act(shard, target, number):
            if target is None:
                if phase == 0:
                    self.local(chunk).start()
                else:
                    self.copy(chunk, shard, self.at, 0).wait_recv()
            else:
                self.copy(chunk, shard, target, number, own=phase == 0).start()

        self.each(chunk, phase, act)

    def finish(self):
        for chunk in range(len(self.chunks)):
            for n in range(8):
                shard = jnp.bitwise_xor(lax.rem(self.at, 2), 1) + 2 * n
                self.copy(chunk, shard, self.at, 0).wait_recv()
            self.local(chunk).wait()
            for phase in range(5):

                def act(shard, target, number):
                    if target is not None:
                        self.copy(chunk, shard, target, number, own=phase == 0).wait_send()

                self.each(chunk, phase, act)


class SlabSum:
    def __init__(self, order, keep, send, got, sems, load=None):
        self.order, self.keep, self.send, self.got, self.sems, self.load = (0, *order), keep, send, got, sems, load

    @staticmethod
    def scratch(slots, share, columns):
        steps = slots.bit_length()
        return [
            *[pltpu.VMEM((max(slots >> n, 1), share, columns), bf16) for n in (0, *range(steps))],
            pltpu.SemaphoreType.DMA((2 * steps + 1,)),
        ]

    def copy(self, step):
        count = self.got[step].shape[0]
        return pltpu.make_async_remote_copy(
            src_ref=self.send if step == 0 else self.keep.at[pl.ds(count, count)],
            dst_ref=self.got[step],
            send_sem=self.sems.at[2 * step],
            recv_sem=self.sems.at[2 * step + 1],
            device_id=partner(self.order[step]),
            device_id_type=MESH,
        )

    def loading(self):
        return pltpu.make_async_copy(self.load, self.keep, self.sems.at[2 * len(self.order)])

    def start(self):
        self.copy(0).start()
        if self.load is not None:
            self.loading().start()

    def step(self, step):
        if step == 1 and self.load is not None:
            self.loading().wait()
        self.copy(step - 1).wait_recv()
        got = self.got[step - 1]

        @pl.loop(0, got.shape[0])
        def _(n):
            self.keep[n] = (self.keep[n].astype(f32) + got[n].astype(f32)).astype(bf16)

        self.copy(step).start()

    def finish(self, out_ref, width, first=0):
        last = len(self.order) - 1
        self.copy(last).wait_recv()
        total = self.keep[0].astype(f32) + self.got[last][0].astype(f32)
        share = out_ref.shape[0]
        by = total.shape[0] // share
        block = out_ref.shape[1] if by == 1 else width // by
        for n in range(total.shape[1] // block):
            for i in range(by):
                at = first + (n * by + i) * block
                out_ref[:, at : at + block] = total[i * share : (i + 1) * share, n * block : (n + 1) * block]
        for step in range(len(self.order)):
            self.copy(step).wait_send()


ALL = (-1, 0, 1, 2, 3)
LATE = (0, 1, 2, 3, -1)


class GainSum:
    def __init__(self, bits, held, got, sems):
        self.bits, self.held, self.got, self.sems = bits, held, got, sems

    @staticmethod
    def scratch(bits, width):
        steps = len(bits)
        return [
            pltpu.VMEM((steps, 8, width), f32),
            pltpu.VMEM((steps, 8, width), f32),
            pltpu.SemaphoreType.DMA((2 * steps,)),
        ]

    def copy(self, step):
        return pltpu.make_async_remote_copy(
            src_ref=self.held.at[step],
            dst_ref=self.got.at[step],
            send_sem=self.sems.at[2 * step],
            recv_sem=self.sems.at[2 * step + 1],
            device_id=partner(self.bits[step]),
            device_id_type=MESH,
        )

    def start(self, value):
        self.held[0] = value
        self.copy(0).start()

    def step(self, step):
        self.copy(step - 1).wait_recv()
        self.held[step] = self.held[step - 1] + self.got[step - 1]
        self.copy(step).start()

    def finish(self, out_ref):
        last = len(self.bits) - 1
        self.copy(last).wait_recv()
        out_ref[...] = self.held[last] + self.got[last]
        for step in range(len(self.bits)):
            self.copy(step).wait_send()


def row_specs(tile, width, half):
    own = pl.BlockSpec((None, None, tile, width), lambda i, s: (0, s[0], jnp.minimum(i, half - 1), 0))
    away = pl.BlockSpec((tile, width), lambda i, s: (jnp.maximum(i - half, 0), 0))
    return own, away


def read_rows(own_ref, away_ref, half):
    return jnp.where(pl.program_id(0) < half, own_ref[...], away_ref[...])


def project_kernel(side_ref, own_ref, away_ref, gain_ref, w_ref, cos_ref, sin_ref, out_ref, hidden_ref, *, half):
    width = own_ref.shape[-1]
    project_tile(read_rows(own_ref, away_ref, half), gain_ref[...], lambda part: w_ref[:, part * width : (part + 1) * width],
                 cos_ref, sin_ref, out_ref, hidden_ref)


def project_tile(x, gain, weights, cos_ref, sin_ref, out_ref, hidden_ref):
    x = x.astype(f32)
    width = x.shape[1]
    center = x - jnp.mean(x, axis=1, keepdims=True)
    spread = jnp.mean(center * center, axis=1, keepdims=True)
    hidden = (center * lax.rsqrt(spread + 1e-5) * gain.astype(f32)).astype(bf16)
    hidden_ref[...] = hidden
    cosine, sine = cos_ref[...], sin_ref[...]
    for part in range(3):
        rows = mm(hidden, weights(part))
        for pair in range(width // LANES):
            cols = slice(pair * LANES, (pair + 1) * LANES)
            field = rows[:, cols]
            if part < 2:
                field = field * cosine + half_partner(field) * sine
            if part == 0:
                field = field * 0.125
            out_ref[part, :, cols] = field.astype(bf16)


def project(side, own, away, gain, w, cosine, sine, tile=512):
    length, width = away.shape
    tokens, half = 2 * length, length // tile
    table = pl.BlockSpec((tile, LANES), lambda i, s: (lax.rem(i, half), 0))
    return pl.pallas_call(
        functools.partial(project_kernel, half=half),
        name="project",
        grid_spec=pltpu.PrefetchScalarGridSpec(
            num_scalar_prefetch=1,
            grid=(2 * half,),
            in_specs=[
                *row_specs(tile, width, half),
                pl.BlockSpec((1, width), lambda i, s: (0, 0)),
                pl.BlockSpec((width, 3 * width), lambda i, s: (0, 0), pipeline_mode=pl.Buffered(1)),
                table,
                table,
            ],
            out_specs=[
                pl.BlockSpec((3, tile, width), lambda i, s: (0, i, 0)),
                pl.BlockSpec((tile, width), lambda i, s: (i, 0)),
            ],
        ),
        out_shape=[jax.ShapeDtypeStruct((3, tokens, width), bf16), jax.ShapeDtypeStruct((tokens, width), bf16)],
        compiler_params=pltpu.CompilerParams(vmem_limit_bytes=62 << 20),
        cost_estimate=pl.CostEstimate(
            flops=6 * tokens * width * width, bytes_accessed=tokens * width * 10 + 6 * width * width, transcendentals=0
        ),
    )(side, own, away, gain, w, cosine, sine)


def first_kernel(shard_ref, wo_ref, wu_ref, gain_ref, tokens_ref, own_ref, cos_ref, sin_ref,
                 qkv_ref, hidden_ref, away_out, w_out, wo_all, wu_all, gains_out,
                 w_all, away, rows, swap_sems, out_sems, *refs, half):
    side, at = lax.axis_index("stream"), lax.axis_index("batch")
    step = pl.program_id(0)
    width = own_ref.shape[-1]
    tile = own_ref.shape[-2]
    def swap(n):
        part = pl.ds(n * tile, tile)
        return pltpu.make_async_remote_copy(
            src_ref=tokens_ref.at[0, 1 - side, part],
            dst_ref=away.at[part],
            send_sem=swap_sems.at[0, n],
            recv_sem=swap_sems.at[1, n],
            device_id=(1 - side, at),
            device_id_type=MESH,
        )

    def chunk(n):
        cols = slice(n * width, (n + 1) * width)
        return shard_ref.at[:, cols], lambda shard: w_all.at[shard, :, cols]

    weights = LineGather([chunk(n) for n in range(3)], *refs[:3])
    part = wu_ref.at[:, : wu_all.shape[2]]
    others = LineGather([(wo_ref, lambda shard: wo_all.at[shard]), (part, lambda shard: wu_all.at[shard])], *refs[3:6])
    gain = GainSum((0, 1, 2, 3), *refs[6:])
    keeps = [
        pltpu.make_async_copy(w_all, w_out, out_sems.at[0]),
        pltpu.make_async_copy(away, away_out, out_sems.at[1]),
    ]

    @pl.when(step == 0)
    def _():
        greet(line_partners())
        for n in range(half):
            swap(n).start()
        gain.start(gain_ref[...])
        for phase in range(5):
            for n in range(3):
                weights.phase(n, phase)
            if 1 <= phase <= 3:
                gain.step(phase)
        gain.finish(gains_out)
        weights.finish()
        for n in range(2):
            others.phase(n, 0)
        keeps[0].start()

    for now in range(1, 4):

        @pl.when(step == now)
        def _():
            for n in range(2):
                others.phase(n, now)
            if now >= half:
                swap(now - half).wait()
            if now == 2 * half - 1:
                keeps[1].start()

    @pl.when(step < half)
    def _():
        rows[...] = own_ref[...]

    @pl.when(step >= half)
    def _():
        rows[...] = away[pl.ds(pl.multiple_of((step - half) * tile, tile), tile), :]

    project_tile(rows[...], gains_out[0:1, :], lambda part: w_all[:, :, part * width : (part + 1) * width].reshape(width, width),
                 cos_ref, sin_ref, qkv_ref, hidden_ref)

    @pl.when(step == pl.num_programs(0) - 1)
    def _():
        for n in range(2):
            others.phase(n, 4)
        others.finish()
        for keep in keeps:
            keep.wait()


def first(shard, wo, wu, cut, gain, tokens, cosine, sine, tile=512):
    _, _, length, width = tokens.shape
    rows = shard.shape[0]
    half = length // tile
    assert half == 2
    anywhere = pl.BlockSpec(memory_space=pl.ANY)
    table = pl.BlockSpec((tile, LANES), lambda i: (lax.rem(i, half), 0))
    small = pl.BlockSpec((8, width), lambda i: (0, 0))
    return pl.pallas_call(
        functools.partial(first_kernel, half=half),
        name="first",
        grid=(2 * half,),
        in_specs=[
            anywhere,
            anywhere,
            anywhere,
            small,
            anywhere,
            pl.BlockSpec((None, None, tile, width), lambda i: (0, lax.axis_index("stream"), jnp.minimum(i, half - 1), 0)),
            table,
            table,
        ],
        out_specs=[
            pl.BlockSpec((3, tile, width), lambda i: (0, i, 0)),
            pl.BlockSpec((tile, width), lambda i: (i, 0)),
            anywhere,
            anywhere,
            anywhere,
            anywhere,
            small,
        ],
        out_shape=[
            jax.ShapeDtypeStruct((3, 2 * length, width), bf16),
            jax.ShapeDtypeStruct((2 * length, width), bf16),
            jax.ShapeDtypeStruct((length, width), bf16),
            jax.ShapeDtypeStruct((16, rows, 3 * width), bf16),
            jax.ShapeDtypeStruct((16, rows, width), bf16),
            jax.ShapeDtypeStruct((16, rows, cut), bf16),
            jax.ShapeDtypeStruct((8, width), f32),
        ],
        scratch_shapes=[
            pltpu.VMEM((16, rows, 3 * width), bf16),
            pltpu.VMEM((length, width), bf16),
            pltpu.VMEM((tile, width), bf16),
            pltpu.SemaphoreType.DMA((2, half)),
            pltpu.SemaphoreType.DMA((2,)),
            *LineGather.scratch(3),
            *LineGather.scratch(2),
            *GainSum.scratch((0, 1, 2, 3), width),
        ],
        compiler_params=pltpu.CompilerParams(vmem_limit_bytes=62 << 20, collective_id=0, has_side_effects=True),
        cost_estimate=pl.CostEstimate(
            flops=12 * length * width * width, bytes_accessed=length * width * 24 + 12 * width * width, transcendentals=0
        ),
    )(shard, wo, wu, gain, tokens, tokens, cosine, sine)


def mask_tables(length, row_length):
    pos = jnp.arange(length)
    blk = (pos // BLOCK)[:, None]
    lane = (jnp.arange(LANES) % HD)[None, :]
    dead = (pos >= row_length)[:, None]
    clean_query = (lane == blk).astype(bf16)
    noisy_query = (lane == blk - 1).astype(bf16)
    main_key = jnp.where((blk > lane) | dead, BIG, 0.0).astype(bf16)
    diag_key = jnp.where((blk != lane) | dead, BIG, 0.0).astype(bf16)
    return clean_query, noisy_query, main_key, diag_key


def low_lanes(shape):
    return lax.broadcasted_iota(jnp.int32, shape, 1) < HD


def attend_gather_kernel(qkv_ref, cq_ref, nq_ref, mk_ref, dk_ref, wu_ref, wd_ref, grad_ref,
                         out_ref, log_ref, wu_all, wd_all, away_ref,
                         qa, ka, kd, va, s_scr, swap_sems, send_sems, recv_sems, local_sems):
    side, at = lax.axis_index("stream"), lax.axis_index("batch")
    step = pl.program_id(0)
    wide, tall = wu_all.shape[2] // 2, wd_ref.shape[0] // 2
    cut = wu_ref.shape[1] - 2 * wide

    def columns(n):
        cols = slice(n * wide, (n + 1) * wide)
        return wu_ref.at[:, cut + n * wide : cut + (n + 1) * wide], lambda shard: wu_all.at[shard, :, cols]

    def rows(n):
        part = slice(n * tall, (n + 1) * tall)
        return wd_ref.at[part, :], lambda shard: wd_all.at[shard, part, :]

    chunks = [columns(0), columns(1), rows(0), rows(1)]
    weights = LineGather(chunks, send_sems, recv_sems, local_sems, EARLY)
    swap = pltpu.make_async_remote_copy(
        src_ref=grad_ref.at[0, 1 - side],
        dst_ref=away_ref,
        send_sem=swap_sems.at[0],
        recv_sem=swap_sems.at[1],
        device_id=(1 - side, at),
        device_id_type=MESH,
    )
    slots = 2 * SLOT_STEPS
    plan = [[] for _ in range(slots + 1)]
    items = SLOT_ORDER
    for n, item in enumerate(items):
        plan[min(1 + n * SLOT_RATE // 16, slots)].append(item)

    @pl.when(step == 0)
    def _():
        greet(line_partners())
        for chunk in range(4):
            weights.phase(chunk, 0)
        swap.start()

    def pass_on(slot):
        for now in range(SLOT_STEPS):
            if plan[2 * now + slot]:

                @pl.when(step == now)
                def _():
                    for item in plan[2 * now + slot]:
                        weights.phase(*item)

    pass_on(0)
    attend_kernel(qkv_ref, cq_ref, nq_ref, mk_ref, dk_ref, out_ref, log_ref, qa, ka, kd, va, s_scr,
                  between=lambda: pass_on(1))

    @pl.when(step == pl.num_programs(0) - 1)
    def _():
        for item in plan[slots]:
            weights.phase(*item)
        weights.finish()
        swap.wait()


EARLY = (0,)
SLOT_STEPS = 6
SLOT_RATE = 14
SLOT_ORDER = [(chunk, phase) for phase in range(1, 5) for chunk in range(4)]


def attend_kernel(qkv_ref, cq_ref, nq_ref, mk_ref, dk_ref, out_ref, log_ref,
                  qa, ka, kd, va, s_scr, between=lambda: None):
    length = out_ref.shape[1]
    clean = lax.axis_index("stream")
    noisy = 1 - clean
    tiles = length // TILE
    low = low_lanes((length, LANES))
    ones = jnp.ones((16, length), bf16)
    vc_t = qkv_ref[2, clean].T
    vn_t = qkv_ref[2, noisy].T
    for head in range(2):
        pick = low if head == 0 else jnp.logical_not(low)
        qa[0, head] = jnp.where(pick, qkv_ref[0, clean], cq_ref[...])
        qa[1, head] = jnp.where(pick, qkv_ref[0, noisy], nq_ref[...])
        qa[2, head] = jnp.where(pick, qkv_ref[0, noisy], cq_ref[...])
        ka[head] = jnp.where(pick, qkv_ref[1, clean], mk_ref[...])
        kd[head] = jnp.where(pick, qkv_ref[1, noisy], dk_ref[...])
        va[0, head, :HD] = vc_t[head * HD : (head + 1) * HD]
        va[1, head, :HD] = vn_t[head * HD : (head + 1) * HD]
        va[0, head, HD:] = ones
        va[1, head, HD:] = ones
    for copy in range(2):
        if copy:
            between()
        where_to = clean if copy == 0 else noisy
        for tile in range(tiles):
            rows = slice(tile * TILE, (tile + 1) * TILE)
            parts = []
            for head in range(2):
                pieces = [(qa[copy, head, rows, :], ka, 0, t) for t in range(tile + 1)]
                if copy == 1:
                    pieces.append((qa[2, head, rows, :], kd, 1, tile))
                top = None
                for n, (query, keys, vi, t) in enumerate(pieces):
                    s = mm_t(keys[head, t * TILE : (t + 1) * TILE, :], query)
                    if copy == 1 and tile == 0 and n == 0:
                        first = lax.broadcasted_iota(jnp.int32, s.shape, 1) < BLOCK
                        s = jnp.where(first, BIG, s)
                    s_scr[head, n * TILE : (n + 1) * TILE, :] = s
                    m = jnp.max(s, axis=0, keepdims=True)
                    top = m if top is None else jnp.maximum(top, m)
                acc = None
                for n, (query, keys, vi, t) in enumerate(pieces):
                    p = jnp.exp(s_scr[head, n * TILE : (n + 1) * TILE, :] - top).astype(bf16)
                    o = mm(va[vi, head, :, t * TILE : (t + 1) * TILE], p)
                    acc = o if acc is None else acc + o
                total = acc[HD : HD + 1, :]
                parts.append(acc[:HD] / total)
                log_ref[where_to, 0, head : head + 1, rows] = top + jnp.log(total)
            out_ref[where_to, rows, :] = jnp.concatenate(parts, axis=0).T.astype(bf16)


def attend(qkv, tables, shards=None, cut=0, grad=None):
    _, copies, length, width = qkv.shape
    pairs = width // LANES
    table_spec = pl.BlockSpec((length, LANES), lambda i: (0, 0), pipeline_mode=pl.Buffered(1))
    more_in, more_shapes, more_scratch = [], [], []
    body, params = attend_kernel, {}
    if shards is not None:
        assert pairs == SLOT_STEPS
        body = attend_gather_kernel
        params = dict(collective_id=3, has_side_effects=True)
        more_in = [*shards, grad]
        up, down = (shard.shape for shard in shards)
        more_shapes = [jax.ShapeDtypeStruct(s, bf16) for s in ((16, up[0], up[1] - cut), (16, *down))]
        more_shapes.append(jax.ShapeDtypeStruct((length, width), bf16))
        more_scratch = [pltpu.SemaphoreType.DMA((2,)), *LineGather.scratch(4)]
    anywhere = pl.BlockSpec(memory_space=pl.ANY)
    return pl.pallas_call(
        body,
        name="attend",
        grid=(pairs,),
        in_specs=[pl.BlockSpec((3, copies, length, LANES), lambda i: (0, 0, 0, i)), *[table_spec] * 4,
                  *[anywhere] * len(more_in)],
        out_specs=[
            pl.BlockSpec((copies, length, LANES), lambda i: (0, 0, i)),
            pl.BlockSpec((copies, 1, 2, length), lambda i: (0, i, 0, 0)),
            *[anywhere] * len(more_shapes),
        ],
        scratch_shapes=[
            pltpu.VMEM((3, 2, length, LANES), bf16),
            pltpu.VMEM((2, length, LANES), bf16),
            pltpu.VMEM((2, length, LANES), bf16),
            pltpu.VMEM((2, 2, HD + 16, length), bf16),
            pltpu.VMEM((2, length + TILE, TILE), f32),
            *more_scratch,
        ],
        out_shape=[
            jax.ShapeDtypeStruct((copies, length, width), bf16),
            jax.ShapeDtypeStruct((copies, pairs, 2, length), f32),
            *more_shapes,
        ],
        compiler_params=pltpu.CompilerParams(vmem_limit_bytes=62 << 20, **params),
        cost_estimate=pl.CostEstimate(
            flops=8 * length * length * width, bytes_accessed=16 * length * width, transcendentals=length * length * 12
        ),
    )(qkv, *tables, *more_in)


DOWN, UP, OUT = (-1, 1, 2, 3), (1, -1, 2, 3), (2, -1, 1, 3)
QKV = ((1, 2, 3, -1), (2, 1, 3, -1), (1, 2, 3, -1))


def attend_back_sum_kernel(*refs, orders):
    count = len(orders)
    core, refs = refs[:10], refs[10:]
    pairs, gain_ref, refs = refs[: 2 * count], refs[2 * count], refs[2 * count + 1 :]
    dqkv_ref, refs = refs[0], refs[1:]
    outs, gain_out, refs = refs[:count], refs[count], refs[count + 1 :]
    own, refs = refs[:10], refs[10:]
    per = len(refs[:-3]) // count
    sums = []
    for n, order in enumerate(orders):
        keep, *got, sems = refs[n * per : (n + 1) * per]
        sums.append(SlabSum(order, keep, pairs[2 * n + 1], got, sems, load=pairs[2 * n]))
    gain = GainSum(ALL, *refs[-3:])
    down, up, wo = sums
    step = pl.program_id(0)

    @pl.when(step == 0)
    def _():
        greet([partner(bit) for bit in ALL])
        for one in sums:
            one.start()
        gain.start(gain_ref[...])

    for at, plan in {
        1: ((down, 1), (up, 1), (wo, 1), (gain, 1)),
        2: ((wo, 2), (gain, 2)),
        3: ((down, 2), (up, 2), (wo, 3), (gain, 3)),
        4: ((down, 3), (up, 3), (wo, 4), (gain, 4)),
        5: ((down, 4), (up, 4)),
    }.items():

        @pl.when(step == at)
        def _():
            for one, number in plan:
                one.step(number)

    attend_back_kernel(*core, dqkv_ref, *own)

    @pl.when(step == pl.num_programs(0) - 1)
    def _():
        for one, out_ref in zip(sums, outs):
            one.finish(out_ref, gain_ref.shape[1])
        gain.finish(gain_out)


def attend_back_kernel(qkv_ref, o_ref, do_ref, log_ref, cq_ref, nq_ref, mk_ref, dk_ref, cos_ref, sin_ref,
                       dqkv_ref, qa, qz, ka, kd, kt, doz, dsum, dq, dkc, dvc):
    length = o_ref.shape[1]
    clean = lax.axis_index("stream")
    noisy = 1 - clean
    tiles = length // TILE
    low = low_lanes((length, LANES))
    zero = jnp.zeros((length, LANES), bf16)
    for copy in range(2):
        at = clean if copy == 0 else noisy
        kt[copy] = qkv_ref[1, at].T
        prod = (o_ref[at].astype(f32) * do_ref[at].astype(f32)).T
        dsum[copy, 0:1] = jnp.sum(prod[:HD], axis=0, keepdims=True)
        dsum[copy, 1:2] = jnp.sum(prod[HD:], axis=0, keepdims=True)
        for head in range(2):
            pick = low if head == 0 else jnp.logical_not(low)
            qa[copy, head] = jnp.where(pick, qkv_ref[0, at], (cq_ref, nq_ref)[copy][...])
            qz[copy, head] = jnp.where(pick, qkv_ref[0, at], zero)
            doz[copy, head] = jnp.where(pick, do_ref[at], zero)
            if copy == 0:
                ka[head] = jnp.where(pick, qkv_ref[1, at], mk_ref[...])
            else:
                qa[2, head] = jnp.where(pick, qkv_ref[0, at], cq_ref[...])
                kd[head] = jnp.where(pick, qkv_ref[1, at], dk_ref[...])
    cosine, sine = cos_ref[...], sin_ref[...]

    def piece(copy, tile, query, keys, kv_copy, krows):
        rows = slice(tile * TILE, (tile + 1) * TILE)
        kv_at = clean if kv_copy == 0 else noisy
        at = clean if copy == 0 else noisy
        probs, raws, dqs = [], [], []
        for head in range(2):
            s = mm_t(keys[head, krows, :], qa[query, head, rows, :])
            p = jnp.exp(s - log_ref[at, 0, head : head + 1, rows])
            if kv_copy == 0 and copy == 1 and tile == 0:
                first = lax.broadcasted_iota(jnp.int32, s.shape, 1) < BLOCK
                p = jnp.where(first, 0.0, p)
            dp = mm_t(qkv_ref[2, kv_at, krows, :], doz[copy, head, rows, :])
            raw = (p * (dp - dsum[copy, head : head + 1, rows])).astype(bf16)
            dqs.append(mm(kt[kv_copy, head * HD : (head + 1) * HD, krows], raw))
            probs.append(p.astype(bf16))
            raws.append(raw)
        grads = [doz[copy, head, rows, :] for head in range(2)]
        queries = [qz[copy, head, rows, :] for head in range(2)]
        return jnp.concatenate(dqs, axis=0), (raws, queries), (probs, grads)

    def product(pair):
        return mm(jnp.concatenate(pair[0], axis=1), jnp.concatenate(pair[1], axis=0))

    def finish(field, rotate, scale):
        if rotate:
            c, s = cosine, sine
            field = field * c - half_partner(field) * s
        return (field * scale if scale != 1.0 else field).astype(bf16)

    for tile in range(tiles):
        rows = slice(tile * TILE, (tile + 1) * TILE)
        dq_t, dk_t, dv_t = piece(1, tile, 2, kd, 1, rows)
        dq[1, :, rows] = dq_t
        dkc[rows, :] = product(dk_t)
        dqkv_ref[2, noisy, rows, :] = product(dv_t).astype(bf16)
    dqkv_ref[1, noisy] = finish(dkc[...], True, 1.0)
    for tile in reversed(range(tiles)):
        rows = slice(tile * TILE, (tile + 1) * TILE)
        seen = slice(0, (tile + 1) * TILE)
        dq_t, dk_c, dv_c = piece(0, tile, 0, ka, 0, seen)
        dq[0, :, rows] = dq_t
        dq_t, dk_n, dv_n = piece(1, tile, 1, ka, 0, seen)
        dq[1, :, rows] += dq_t
        dk_t = product((dk_c[0] + dk_n[0], dk_c[1] + dk_n[1]))
        dv_t = product((dv_c[0] + dv_n[0], dv_c[1] + dv_n[1]))
        if tile == tiles - 1:
            dkc[...] = dk_t
            dvc[...] = dv_t
        else:
            dkc[seen, :] += dk_t
            dvc[seen, :] += dv_t
    dqkv_ref[2, clean] = dvc[...].astype(bf16)
    dqkv_ref[1, clean] = finish(dkc[...], True, 1.0)
    dqkv_ref[0, clean] = finish(dq[0].T, True, 0.125)
    dqkv_ref[0, noisy] = finish(dq[1].T, True, 0.125)


def attend_back(qkv, mixed, grad, logs, tables, cosine, sine, pairs=None, gain=None, slabs=()):
    _, copies, length, width = qkv.shape
    steps = width // LANES
    table_spec = pl.BlockSpec((length, LANES), lambda i: (0, 0), pipeline_mode=pl.Buffered(1))
    row_spec = pl.BlockSpec((copies, length, LANES), lambda i: (0, 0, i))
    three = pl.BlockSpec((3, copies, length, LANES), lambda i: (0, 0, 0, i))
    anywhere = pl.BlockSpec(memory_space=pl.ANY)

    def fixed(shape):
        return pl.BlockSpec(shape, lambda i: (0, 0), pipeline_mode=pl.Buffered(1))

    more_in, more_specs, more_shapes, more_out, more_scratch = [], [], [], [], []
    body, params = attend_back_kernel, {}
    if pairs is not None:
        assert steps == 6
        body = functools.partial(attend_back_sum_kernel, orders=(DOWN, UP, OUT))
        params = dict(collective_id=1, has_side_effects=True)
        for (keep, send), slab in zip(pairs, slabs):
            slots, share, columns = keep.shape
            more_in += [keep, send]
            more_specs += [anywhere] * 2
            more_shapes.append(jax.ShapeDtypeStruct(slab, f32))
            more_out.append(fixed(slab))
            more_scratch += SlabSum.scratch(slots, share, columns)
        more_in.append(gain)
        more_specs.append(fixed((8, width)))
        more_shapes.append(jax.ShapeDtypeStruct((8, width), f32))
        more_out.append(fixed((8, width)))
        more_scratch += GainSum.scratch(ALL, width)
    return pl.pallas_call(
        body,
        name="attend_back",
        grid_spec=pltpu.PrefetchScalarGridSpec(
            num_scalar_prefetch=0,
            grid=(steps,),
            in_specs=[three, row_spec, row_spec, pl.BlockSpec((copies, 1, 2, length), lambda i: (0, i, 0, 0))]
            + [table_spec] * 6
            + more_specs,
            out_specs=[three, *more_out],
            scratch_shapes=[
                pltpu.VMEM((3, 2, length, LANES), bf16),
                pltpu.VMEM((2, 2, length, LANES), bf16),
                pltpu.VMEM((2, length, LANES), bf16),
                pltpu.VMEM((2, length, LANES), bf16),
                pltpu.VMEM((2, LANES, length), bf16),
                pltpu.VMEM((2, 2, length, LANES), bf16),
                pltpu.VMEM((2, 2, length), f32),
                pltpu.VMEM((2, LANES, length), f32),
                pltpu.VMEM((length, LANES), f32),
                pltpu.VMEM((length, LANES), f32),
                *more_scratch,
            ],
        ),
        out_shape=[jax.ShapeDtypeStruct((3, copies, length, width), bf16), *more_shapes],
        compiler_params=pltpu.CompilerParams(vmem_limit_bytes=62 << 20, **params),
        cost_estimate=pl.CostEstimate(
            flops=20 * length * length * width, bytes_accessed=30 * length * width, transcendentals=length * length * 12
        ),
    )(qkv, mixed, grad, logs, *tables, cosine, sine, *more_in)


ROOT = math.sqrt(2.0 / math.pi)


def feed_kernel(side_ref, x_own, x_away, mixed_ref, g_own, g_away, gain_ref, wo_all, wu_all, wu_more, wd_all,
                out_own, out_away, act_ref, du_ref, h2_ref, dmid_ref, dbr_ref, dmix_ref, dgain_ref,
                wo_ref, wu_ref, wd_ref, sems, *, half):
    groups, rows, width = wo_ref.shape
    fold = wu_ref.shape[0]

    @pl.when(pl.program_id(0) == 0)
    def _():
        copies = [pltpu.make_async_copy(wo_all, wo_ref, sems.at[0])]
        begin = 0
        for array in (wu_all, wu_more):
            end = begin + array.shape[2]
            for n in range(fold):
                low, high = max(begin, n * width), min(end, (n + 1) * width)
                if low < high:
                    copies.append(
                        pltpu.make_async_copy(
                            array.at[:, :, low - begin : high - begin],
                            wu_ref.at[n, :, :, low - n * width : high - n * width],
                            sems.at[len(copies)],
                        )
                    )
            begin = end
        copies.append(pltpu.make_async_copy(wd_all, wd_ref, sems.at[len(copies)]))
        for copy in copies:
            copy.start()
        for copy in copies:
            copy.wait()

    def down(c):
        per = groups // fold
        return wd_ref[c * per : (c + 1) * per].reshape(width, width)

    wo = wo_ref[...].reshape(width, width)
    gain = gain_ref[...].astype(f32)
    middle = read_rows(x_own, x_away, half).astype(f32) + mm(mixed_ref[...], wo)
    center = middle - jnp.mean(middle, axis=1, keepdims=True)
    spread = jnp.mean(center * center, axis=1, keepdims=True)
    inv = lax.rsqrt(spread + 1e-5)
    norm = center * inv
    hidden = (norm * gain).astype(bf16)
    h2_ref[...] = hidden
    grad = read_rows(g_own, g_away, half)
    out = middle
    dh = jnp.zeros_like(middle)
    for c in range(fold):
        cols = slice(c * width, (c + 1) * width)
        up = wu_ref[c].reshape(width, width)
        u = mm(hidden, up)
        da = mm_t(grad, down(c)).astype(bf16).astype(f32)
        sq = u * u
        t = jnp.tanh(u * (ROOT + (ROOT * 0.044715) * sq))
        part = 0.5 + 0.5 * t
        act = (u * part).astype(bf16)
        slope = part + (u * (part * (1.0 - t))) * (ROOT + (3 * ROOT * 0.044715) * sq)
        du = (da * slope).astype(bf16)
        act_ref[:, cols] = act
        du_ref[:, cols] = du
        out = out + mm(act, down(c))
        dh = dh + mm_t(du, up)
    low = out.astype(bf16)

    @pl.when(pl.program_id(0) < half)
    def _():
        out_own[...] = low

    @pl.when(pl.program_id(0) >= half)
    def _():
        out_away[...] = low

    @pl.when(pl.program_id(0) == 0)
    def _():
        dgain_ref[...] = jnp.zeros_like(dgain_ref)

    dgain_ref[...] += jnp.sum((dh * norm).reshape(-1, 8, width), axis=0)
    e = dh * gain
    dmid = grad.astype(f32) + inv * (
        e - jnp.mean(e, axis=1, keepdims=True) - norm * jnp.mean(e * norm, axis=1, keepdims=True)
    )
    dmid_ref[...] = dmid
    dbr = dmid.astype(bf16)
    dbr_ref[...] = dbr
    dmix_ref[...] = mm_t(dbr, wo).astype(bf16)


def feed(side, x_own, x_away, mixed, g_own, g_away, gain, weights, tile=512):
    tokens, width = mixed.shape
    groups, rows, _ = weights[0].shape
    ff = weights[1].shape[2] + weights[2].shape[2]
    fold = ff // width
    half = tokens // 2 // tile
    row = pl.BlockSpec((tile, width), lambda i, s: (i, 0))
    wide = pl.BlockSpec((tile, ff), lambda i, s: (i, 0))
    own, away = row_specs(tile, width, half)

    def keep(shape):
        return pl.BlockSpec(shape, lambda i, s: (0, 0), pipeline_mode=pl.Buffered(1))

    return pl.pallas_call(
        functools.partial(feed_kernel, half=half),
        name="feed",
        grid_spec=pltpu.PrefetchScalarGridSpec(
            num_scalar_prefetch=1,
            grid=(2 * half,),
            in_specs=[own, away, row, own, away, keep((1, width)), *[pl.BlockSpec(memory_space=pl.ANY)] * 4],
            out_specs=[own, away, wide, wide, row, row, row, row, pl.BlockSpec((8, width), lambda i, s: (0, 0))],
            scratch_shapes=[
                pltpu.VMEM((groups, rows, width), bf16),
                pltpu.VMEM((fold, groups, rows, width), bf16),
                pltpu.VMEM((groups, fold * rows, width), bf16),
                pltpu.SemaphoreType.DMA((3 + fold,)),
            ],
        ),
        out_shape=[
            jax.ShapeDtypeStruct((1, 2, tokens // 2, width), bf16),
            jax.ShapeDtypeStruct((tokens // 2, width), bf16),
            jax.ShapeDtypeStruct((tokens, ff), bf16),
            jax.ShapeDtypeStruct((tokens, ff), bf16),
            jax.ShapeDtypeStruct((tokens, width), bf16),
            jax.ShapeDtypeStruct((tokens, width), f32),
            jax.ShapeDtypeStruct((tokens, width), bf16),
            jax.ShapeDtypeStruct((tokens, width), bf16),
            jax.ShapeDtypeStruct((8, width), f32),
        ],
        compiler_params=pltpu.CompilerParams(vmem_limit_bytes=62 << 20),
        cost_estimate=pl.CostEstimate(
            flops=tokens * width * (4 * width + 8 * ff), bytes_accessed=tokens * (width * 18 + ff * 4),
            transcendentals=tokens * ff
        ),
    )(side, x_own, x_away, mixed, g_own, g_away, gain, *weights)


def folds(share):
    return 1 if share % 16 == 0 else 2


def fold(slab):
    if folds(slab.shape[0]) == 1:
        return slab
    middle = slab.shape[1] // 2
    return jnp.concatenate([slab[:, :middle], slab[:, middle:]], axis=0)


def arranged(slot, order):
    return sum((slot >> bit & 1) << (len(order) - 1 - n) for n, bit in enumerate(order))


def weight_kernel(me_ref, left_ref, *refs, share, split, order):
    weight_slabs(me_ref[0], left_ref, *refs, share=share, split=split, order=order)


def weight_slabs(me, left_ref, *refs, share, split, order):
    right_refs, (keep_ref, send_ref, scr) = refs[:-3], refs[-3:]
    if split:
        own_ref, away_ref = right_refs
        half = own_ref.shape[0]
        total = t_mm(left_ref[:half], own_ref[...]) + t_mm(left_ref[half:], away_ref[...])
    else:
        total = t_mm(left_ref[...], right_refs[0][...])
    slabs = total.shape[0] // share
    scr[...] = total.reshape(scr.shape)
    low_me = lax.rem(me, slabs)
    for slot in range(slabs):
        source = jnp.bitwise_xor(low_me, slot)
        into = send_ref if slot % 2 else keep_ref
        into[arranged(slot // 2, order)] = fold(scr[source]).astype(bf16)


def weight_grad_columns(me, left, right, block, share, order, name):
    tokens, dl = left.shape
    dr = right.shape[1]
    peers = dl // share
    by = folds(share)
    shape = (peers // 2, share * by, dr // by)
    out = pl.BlockSpec((peers // 2, share * by, block // by), lambda j, m: (0, 0, j))
    return pl.pallas_call(
        functools.partial(weight_kernel, share=share, split=False, order=order),
        name=name,
        grid_spec=pltpu.PrefetchScalarGridSpec(
            num_scalar_prefetch=1,
            grid=(dr // block,),
            in_specs=[
                pl.BlockSpec((tokens, dl), lambda j, m: (0, 0), pipeline_mode=pl.Buffered(1)),
                pl.BlockSpec((tokens, block), lambda j, m: (0, j)),
            ],
            out_specs=[out, out],
            scratch_shapes=[pltpu.VMEM((peers, share, block), f32)],
        ),
        out_shape=[jax.ShapeDtypeStruct(shape, bf16)] * 2,
        compiler_params=pltpu.CompilerParams(vmem_limit_bytes=62 << 20),
        cost_estimate=pl.CostEstimate(
            flops=2 * tokens * dl * dr, bytes_accessed=2 * tokens * (dl + dr) + 2 * dl * dr, transcendentals=0
        ),
    )(me, left, right)


def weight_grad_rows(me, left, own, away, block, share, name):
    tokens, dl = left.shape
    length, dr = away.shape
    slabs = block // share
    steps = dl // block
    assert steps == 4
    shape = (2, slabs // 2, 2, share, dr)
    out = pl.BlockSpec((None, slabs // 2, None, share, dr), lambda j, m: (lax.div(j, 2), 0, lax.rem(j, 2), 0, 0))
    bits = (slabs // 2).bit_length() - 1

    def place(j, m):
        return (0, jnp.bitwise_xor(j, lax.div(m[0], slabs)))

    return pl.pallas_call(
        functools.partial(weight_kernel, share=share, split=True, order=tuple(range(bits))),
        name=name,
        grid_spec=pltpu.PrefetchScalarGridSpec(
            num_scalar_prefetch=1,
            grid=(steps,),
            in_specs=[
                pl.BlockSpec((tokens, block), place),
                pl.BlockSpec((None, None, length, dr), lambda j, m: (0, m[1], 0, 0), pipeline_mode=pl.Buffered(1)),
                pl.BlockSpec((length, dr), lambda j, m: (0, 0), pipeline_mode=pl.Buffered(1)),
            ],
            out_specs=[out, out],
            scratch_shapes=[pltpu.VMEM((slabs, share, dr), f32)],
        ),
        out_shape=[jax.ShapeDtypeStruct(shape, bf16)] * 2,
        compiler_params=pltpu.CompilerParams(vmem_limit_bytes=62 << 20),
        cost_estimate=pl.CostEstimate(
            flops=2 * tokens * dl * dr, bytes_accessed=2 * tokens * (dl + dr) + 2 * dl * dr, transcendentals=0
        ),
    )(me, left, own, away)


def last_kernel(x_own, x_away, gain_ref, w_hbm, dqkv_hbm, dmid_hbm, hidden_hbm,
                dx_ref, dw_ref, gain_out,
                xv, w_ref, dqkv, dmid, hidden, send, land, dgain, scr,
                load_sems, tile_sems, send_sems, recv_sems, out_sems, *refs, share):
    count = len(QKV)
    per = len(refs[:-3]) // count
    sums = []
    for n, order in enumerate(QKV):
        first, keep, *got, sems = refs[n * per : (n + 1) * per]
        sums.append(SlabSum(order, keep, first, got, sems))
    gain = GainSum(LATE, *refs[-3:])
    side, at = lax.axis_index("stream"), lax.axis_index("batch")
    me = side * lax.axis_size("batch") + at
    step = pl.program_id(0)
    width = w_ref.shape[0]
    length = land.shape[0]
    tiles = pl.num_programs(0)
    tile = 2 * length // 8
    half = 4

    def rows_of(t, base=0):
        return pl.ds(pl.multiple_of((t - base) * tile, tile), tile)

    loads = [
        pltpu.make_async_copy(w_hbm, w_ref, load_sems.at[0]),
        pltpu.make_async_copy(x_away, xv.at[pl.ds(length, length)], load_sems.at[1]),
        pltpu.make_async_copy(hidden_hbm, hidden, load_sems.at[2]),
        pltpu.make_async_copy(x_own.at[0, side], xv.at[pl.ds(0, length)], load_sems.at[3]),
    ]

    def load_grad(t):
        return pltpu.make_async_copy(dqkv_hbm.at[:, rows_of(t), :], dqkv.at[:, rows_of(t), :], tile_sems.at[0, t])

    def load_middle(t):
        return pltpu.make_async_copy(dmid_hbm.at[rows_of(t), :], dmid.at[rows_of(t), :], tile_sems.at[1, t])

    def away(t):
        return pltpu.make_async_remote_copy(
            src_ref=send.at[rows_of(t, half), :],
            dst_ref=land.at[rows_of(t, half), :],
            send_sem=send_sems.at[t - half],
            recv_sem=recv_sems.at[t - half],
            device_id=(1 - side, at),
            device_id_type=MESH,
        )

    def result(t, row):
        return pltpu.make_async_copy(
            dmid.at[rows_of(t), :],
            dx_ref.at[0, row, pl.ds(pl.multiple_of(lax.rem(t, half) * tile, tile), tile), :],
            out_sems.at[t],
        )

    @pl.when(step == 0)
    def _():
        loads[0].start()
        loads[1].start()
        load_grad(4).start()
        load_middle(4).start()
        loads[2].start()
        for t in (5, 6, 7, 0, 1, 2, 3):
            load_grad(t).start()
        loads[3].start()
        for t in (5, 6, 7, 0, 1, 2, 3):
            load_middle(t).start()
        dgain[...] = jnp.zeros_like(dgain)
        greet([partner(bit) for bit in ALL])
        loads[0].wait()
        loads[1].wait()
        load_grad(4).wait()
        load_middle(4).wait()

    @pl.when(step > 0)
    def _():
        load_middle(lax.rem(step + half, 8)).wait()

    @pl.when(step == half)
    def _():
        loads[3].wait()

    for now, plan in {
        1: ((0, 1), (1, 1)),
        2: ((0, 2), (2, 1)),
        3: ((1, 2),),
        4: ((0, 3),),
        6: ((2, 2), (1, 3)),
        7: ((0, 4),),
    }.items():

        @pl.when(step == now)
        def _():
            for n, number in plan:
                sums[n].step(number)

    t = lax.rem(step + half, 8)
    rows = rows_of(t)
    x = xv[rows, :].astype(f32)
    center = x - jnp.mean(x, axis=1, keepdims=True)
    spread = jnp.mean(center * center, axis=1, keepdims=True)
    inv = lax.rsqrt(spread + 1e-5)
    norm = center * inv
    dh = mm_t(dqkv[0, rows, :], w_ref[:, :width])
    dh = dh + mm_t(dqkv[1, rows, :], w_ref[:, width : 2 * width])
    dh = dh + mm_t(dqkv[2, rows, :], w_ref[:, 2 * width :])
    dgain[...] += jnp.sum((dh * norm).reshape(-1, 8, width), axis=0)
    e = dh * gain_ref[...]
    dx = dmid[rows, :] + inv * (
        e - jnp.mean(e, axis=1, keepdims=True) - norm * jnp.mean(e * norm, axis=1, keepdims=True)
    )

    @pl.when(step < half)
    def _():
        send[rows_of(step), :] = dx.astype(bf16)
        away(t).start()

    @pl.when(step >= half)
    def _():
        dmid[rows, :] = dx
        result(t, side).start()

    def part(n):
        order = tuple({-1: 3, 1: 0, 2: 1, 3: 2}[bit] for bit in QKV[n])
        weight_slabs(me, hidden, dqkv.at[n], sums[n].keep, sums[n].send, scr, share=share, split=False, order=order)
        sums[n].start()

    @pl.when(step == 0)
    def _():
        loads[2].wait()
        for other in (5, 6, 7, 0, 1, 2, 3):
            load_grad(other).wait()
        part(0)
        part(1)

    @pl.when(step == 1)
    def _():
        part(2)

    @pl.when(step == tiles - 1)
    def _():
        gain.start(dgain[...])
        sums[2].step(3)
        sums[1].step(4)
        sums[0].finish(dw_ref, width, 0)
        gain.step(1)
        sums[2].step(4)
        gain.step(2)
        sums[1].finish(dw_ref, width, width)
        gain.step(3)
        sums[2].finish(dw_ref, width, 2 * width)
        gain.step(4)
        for other in range(half, 8):
            away(other).wait()
            dmid[rows_of(other), :] = land[rows_of(other, half), :].astype(f32)
            result(other, 1 - side).start()
        gain.finish(gain_out)
        for other in range(8):
            result(other, side).wait()


def last(tokens, x_away, gain, w, dqkv, dmid, hidden, share):
    tokens_all, width = hidden.shape
    length = tokens_all // 2
    slots = width // share // 2
    anywhere = pl.BlockSpec(memory_space=pl.ANY)

    def fixed(shape):
        return pl.BlockSpec(shape, lambda i: (0, 0), pipeline_mode=pl.Buffered(1))

    scratch = []
    for _ in range(3):
        by = folds(share)
        scratch += [
            pltpu.VMEM((slots, share * by, width // by), bf16),
            *SlabSum.scratch(slots, share * by, width // by),
        ]
    return pl.pallas_call(
        functools.partial(last_kernel, share=share),
        name="last",
        grid=(8,),
        in_specs=[anywhere, anywhere, fixed((1, width)), *[anywhere] * 4],
        out_specs=[anywhere, fixed((share, 3 * width)), fixed((8, width))],
        out_shape=[
            jax.ShapeDtypeStruct((1, 2, length, width), f32),
            jax.ShapeDtypeStruct((share, 3 * width), f32),
            jax.ShapeDtypeStruct((8, width), f32),
        ],
        scratch_shapes=[
            pltpu.VMEM((2 * length, width), bf16),
            pltpu.VMEM((width, 3 * width), bf16),
            pltpu.VMEM((3, 2 * length, width), bf16),
            pltpu.VMEM((2 * length, width), f32),
            pltpu.VMEM((2 * length, width), bf16),
            pltpu.VMEM((length, width), bf16),
            pltpu.VMEM((length, width), bf16),
            pltpu.VMEM((8, width), f32),
            pltpu.VMEM((2 * slots, share, width), f32),
            pltpu.SemaphoreType.DMA((4,)),
            pltpu.SemaphoreType.DMA((2, 8)),
            pltpu.SemaphoreType.DMA((4,)),
            pltpu.SemaphoreType.DMA((4,)),
            pltpu.SemaphoreType.DMA((8,)),
            *scratch,
            *GainSum.scratch(LATE, width),
        ],
        compiler_params=pltpu.CompilerParams(vmem_limit_bytes=62 << 20, collective_id=2, has_side_effects=True),
        cost_estimate=pl.CostEstimate(
            flops=24 * length * width * width, bytes_accessed=36 * length * width, transcendentals=0
        ),
    )(tokens, x_away, gain, w, dqkv, dmid, hidden)


def project_back_kernel(side_ref, x_ref, gain_ref, w_ref, dqkv_ref, dmid_ref, dx_ref, dgain_ref):
    x = x_ref[...].astype(f32)
    width = x.shape[1]
    center = x - jnp.mean(x, axis=1, keepdims=True)
    spread = jnp.mean(center * center, axis=1, keepdims=True)
    inv = lax.rsqrt(spread + 1e-5)
    norm = center * inv
    dh = mm_t(dqkv_ref[0], w_ref[:, :width])
    dh = dh + mm_t(dqkv_ref[1], w_ref[:, width : 2 * width])
    dh = dh + mm_t(dqkv_ref[2], w_ref[:, 2 * width :])

    @pl.when(pl.program_id(0) == 0)
    def _():
        dgain_ref[...] = jnp.zeros_like(dgain_ref)

    dgain_ref[...] += jnp.sum((dh * norm).reshape(-1, 8, width), axis=0)
    e = dh * gain_ref[...].astype(f32)
    dx_ref[...] = (dmid_ref[...] + inv * (
        e - jnp.mean(e, axis=1, keepdims=True) - norm * jnp.mean(e * norm, axis=1, keepdims=True)
    )).astype(dx_ref.dtype)


def project_back(side, x, gain, w, dqkv, dmid, away, tile=256):
    width = x.shape[-1]
    length = dmid.shape[0] // 2
    half = length // tile
    first = half if away else 0
    if away:
        x_spec = pl.BlockSpec((tile, width), lambda i, s: (i, 0))
        out_spec, out_shape = x_spec, jax.ShapeDtypeStruct((length, width), bf16)
    else:
        x_spec = pl.BlockSpec((None, None, tile, width), lambda i, s: (0, s[0], i, 0))
        out_spec, out_shape = x_spec, jax.ShapeDtypeStruct((1, 2, length, width), f32)
    return pl.pallas_call(
        project_back_kernel,
        name="project_back_away" if away else "project_back_own",
        grid_spec=pltpu.PrefetchScalarGridSpec(
            num_scalar_prefetch=1,
            grid=(half,),
            in_specs=[
                x_spec,
                pl.BlockSpec((1, width), lambda i, s: (0, 0)),
                pl.BlockSpec((width, 3 * width), lambda i, s: (0, 0), pipeline_mode=pl.Buffered(1)),
                pl.BlockSpec((3, tile, width), lambda i, s: (0, i + first, 0)),
                pl.BlockSpec((tile, width), lambda i, s: (i + first, 0)),
            ],
            out_specs=[out_spec, pl.BlockSpec((8, width), lambda i, s: (0, 0))],
        ),
        out_shape=[out_shape, jax.ShapeDtypeStruct((8, width), f32)],
        compiler_params=pltpu.CompilerParams(vmem_limit_bytes=62 << 20),
        cost_estimate=pl.CostEstimate(
            flops=6 * length * width * width, bytes_accessed=length * width * 16, transcendentals=0
        ),
    )(side, x, gain, w, dqkv, dmid)


def flip(x, bit):
    axis, by = ("stream", 1) if bit < 0 else ("batch", 1 << bit)
    return lax.ppermute(x, axis, [(i, i ^ by) for i in range(lax.axis_size(axis))])


def after(value, *others):
    return lax.optimization_barrier((value, *others))[0]


def shards(tokens, cotangent, lengths, ln1_gain, w_qkv, w_out, ln2_gain, w_up, w_down):
    side = lax.axis_index("stream")
    at = lax.axis_index("batch")
    _, rows_dev, length, width = tokens.shape
    assert rows_dev == 2
    ff = w_up.shape[1]
    peers = lax.axis_size("batch")
    small = peers == 16 and width % (16 * peers) == 0
    side_array = side.reshape(1).astype(jnp.int32)
    index = side * peers + at
    me = jnp.stack([index if small else 0 * index, side]).astype(jnp.int32)
    share = width // (2 * peers)
    cut = ff // 3 // LANES * LANES

    cosine, sine = rotary_tables(length)
    tables = mask_tables(length, jnp.take(lengths, side))
    if small:
        rows = width // peers
        gains = jnp.zeros((8, width), f32)
        gains = lax.dynamic_update_slice(gains, jnp.stack([ln1_gain, ln2_gain]).astype(f32), (0, at * rows))
        qkv, hidden, x_away, w_qkv_all, wo_all, wu_all, gains = first(
            w_qkv, w_out, w_up, cut, gains, tokens, cosine, sine
        )
        qkv4 = qkv.reshape(3, 2, length, width)
        w_qkv_all = w_qkv_all.reshape(width, 3 * width)
        gain_one, gain_two = gains[0:1], gains[1:2]
        mixed, logs, wu_more, wd_all, g_away = attend(qkv4, tables, (w_up, w_down), cut, cotangent)
        weights = [wo_all, wu_all, wu_more, wd_all]
    else:

        def whole(x):
            return lax.all_gather(x, "batch", axis=0, tiled=True)

        x_away = flip(lax.dynamic_index_in_dim(tokens[0], 1 - side, 0, False), -1)
        g_away = flip(lax.dynamic_index_in_dim(cotangent[0], 1 - side, 0, False), -1)
        w_qkv_all = whole(w_qkv)
        gain_one, gain_two = (whole(gain)[None].astype(f32) for gain in (ln1_gain, ln2_gain))
        weights = [whole(w).reshape(16, -1, w.shape[1]) for w in (w_out, w_up, w_down)]
        weights[1:2] = [weights[1][:, :, :cut], weights[1][:, :, cut:]]
        qkv, hidden = project(side_array, tokens, x_away, gain_one, w_qkv_all, cosine, sine)
        qkv4 = qkv.reshape(3, 2, length, width)
        mixed, logs = attend(qkv4, tables)
    mixed2 = mixed.reshape(2 * length, width)
    out, out_away, act, du, h2, dmid, dbr, dmix, dgain_two = feed(
        side_array, tokens, x_away, mixed2, cotangent, g_away, gain_two, weights
    )

    def place(result, away):
        away = flip(away, -1).astype(result.dtype)
        return lax.dynamic_update_slice(result, away[None, None], (0, 1 - side, 0, 0))

    out = place(out, out_away)
    unit = share if small else width // 32
    places = {-1: 3, 1: 0, 2: 1, 3: 2}

    def columns_grad(left, right, order, name):
        return weight_grad_columns(me, left, right, width, unit, [places[bit] for bit in order], name)

    down = weight_grad_rows(me, act, cotangent, g_away, width, ff // width * unit, "grad_down")
    down = [part.reshape(16, -1, width) for part in down]
    up = columns_grad(h2, du, UP, "grad_up")
    wo = columns_grad(mixed2, dbr, OUT, "grad_out")
    dmix = after(dmix.reshape(2, length, width), out)
    common = qkv4, mixed, dmix, logs, tables, cosine, sine
    if small:
        dqkv, down, up, wo, dgain_two = attend_back(
            *common, (down, up, wo), dgain_two, ((ff // width * share, width), (share, ff), (share, width))
        )
    else:
        dqkv, = attend_back(*common)
    dqkv3 = dqkv.reshape(3, 2 * length, width)
    if small:
        dx, wq, dgain_one = last(tokens, x_away, gain_one, w_qkv_all, dqkv3, dmid, hidden, share)
    else:
        dx_away, dgain_away = project_back(side_array, x_away, gain_one, w_qkv_all, dqkv3, dmid, True)
        dx, dgain_own = project_back(side_array, tokens, gain_one, w_qkv_all, dqkv3, dmid, False)
        dgain_one = dgain_own + dgain_away
        dx = place(dx, dx_away)
    dgain_one, dgain_two = (jnp.sum(g, axis=0, keepdims=True) for g in (dgain_one, dgain_two))
    if not small:

        def scatter(pair, order):
            slots = jnp.stack(pair, axis=1)
            natural = [arranged(n, order) for n in range(16)]
            slots = slots[jnp.array(natural)]
            by = folds(unit) if slots.shape[2] == 2 * unit else 1
            slots = slots.reshape(32, by, slots.shape[2] // by, -1, width // by).transpose(0, 2, 3, 1, 4)
            rows = slots.reshape(32 * slots.shape[1], -1)
            return lax.psum_scatter(rows, ("stream", "batch"), scatter_dimension=0, tiled=True).astype(f32)

        parts = [columns_grad(hidden, dqkv3[n], QKV[n], "grad_qkv") for n in range(3)]
        down, up, wo, *parts = (
            scatter(pair, [places[bit] for bit in order])
            for pair, order in zip((down, up, wo, *parts), (DOWN, UP, OUT, *QKV))
        )
        wq = jnp.concatenate(parts, axis=1)
        dgain_one, dgain_two = lax.psum((dgain_one, dgain_two), ("stream", "batch"))
    begin = index * share
    dgain_one, dgain_two = (lax.dynamic_slice(g[0], (begin,), (share,)) for g in (dgain_one, dgain_two))
    return out, dx, dgain_one, wq, wo, dgain_two, up, down


def solution(mesh):
    token = P("stream", "batch", None, None)
    vector, matrix = P("batch"), P("batch", None)
    out_vector, out_matrix = P(("stream", "batch")), P(("stream", "batch"), None)
    return jax.shard_map(
        shards,
        mesh=mesh,
        in_specs=(token, token, vector, vector, matrix, matrix, vector, matrix, matrix),
        out_specs=(token, token, out_vector, out_matrix, out_matrix, out_vector, out_matrix, out_matrix),
        check_vma=False,
    )
```

```python
import functools
import math

import jax
import jax.numpy as jnp
from jax import lax
from jax.experimental import pallas as pl
from jax.experimental.pallas import tpu as pltpu
from jax.sharding import PartitionSpec as P

HD = 64
BLOCK = 16
LANES = 128
TILE = 256
BIG = -1e30
f32, bf16 = jnp.float32, jnp.bfloat16


def mm(a, b):
    return lax.dot_general(a, b, (((1,), (0,)), ((), ())), preferred_element_type=f32)


def mm_t(a, b):
    return lax.dot_general(a, b, (((1,), (1,)), ((), ())), preferred_element_type=f32)


def t_mm(a, b):
    return lax.dot_general(a, b, (((0,), (0,)), ((), ())), preferred_element_type=f32)


def rotary_tables(length):
    half = HD // 2
    places = jnp.arange(length).astype(f32)
    rates = jnp.exp(jnp.arange(half).astype(f32) * (-2.0 * math.log(10000.0) / HD))
    angles = places[:, None] * rates[None, :]
    cosine, sine = jnp.cos(angles), jnp.sin(angles)
    return (
        jnp.concatenate([cosine] * 4, axis=1),
        jnp.concatenate([-sine, sine, -sine, sine], axis=1),
    )


def half_partner(x):
    lane = lax.broadcasted_iota(jnp.int32, x.shape, 1)
    low = lax.rem(lane, HD) < HD // 2
    return jnp.where(low, pltpu.roll(x, LANES - HD // 2, 1), pltpu.roll(x, HD // 2, 1))


MESH = pl.DeviceIdType.MESH


def partner(bit):
    side, at = lax.axis_index("stream"), lax.axis_index("batch")
    return (1 - side, at) if bit < 0 else (side, jnp.bitwise_xor(at, 1 << bit))


def greet(others):
    barrier = pltpu.get_barrier_semaphore()
    for other in others:
        pl.semaphore_signal(barrier, inc=1, device_id=other, device_id_type=MESH)
    pl.semaphore_wait(barrier, len(others))


def line_partners():
    side, at = lax.axis_index("stream"), lax.axis_index("batch")
    return [partner(-1)] + [(side, jnp.bitwise_xor(at, mask)) for mask in (1, 2, 4, 8, 12)]


class LineGather:
    SENDS = 37

    def __init__(self, chunks, send_sems, recv_sems, local_sems, across_first=()):
        self.across_first = across_first
        self.chunks, self.send_sems, self.recv_sems, self.local_sems = chunks, send_sems, recv_sems, local_sems
        self.side, self.at = lax.axis_index("stream"), lax.axis_index("batch")
        self.z = lax.div(self.at, 4)

    @staticmethod
    def scratch(count):
        return [
            pltpu.SemaphoreType.DMA((count, LineGather.SENDS)),
            pltpu.SemaphoreType.DMA((count, 16)),
            pltpu.SemaphoreType.DMA((count,)),
        ]

    def copy(self, chunk, shard, target, number, own=False):
        source, place = self.chunks[chunk]
        return pltpu.make_async_remote_copy(
            src_ref=source if own else place(shard),
            dst_ref=place(shard),
            send_sem=self.send_sems.at[chunk, number],
            recv_sem=self.recv_sems.at[chunk, shard],
            device_id=(self.side, target),
            device_id_type=MESH,
        )

    def local(self, chunk):
        source, place = self.chunks[chunk]
        return pltpu.make_async_copy(source, place(self.at), self.local_sems.at[chunk])

    def sends(self, chunk, phase):
        at, z = self.at, self.z
        across, core = jnp.bitwise_xor(at, 2), jnp.bitwise_xor(at, 1)
        up, down = (at + 4, z < 3), (at - 4, z > 0)
        other = jnp.bitwise_xor
        early = chunk in self.across_first
        if phase == 0:
            yield None, at, [(*up, 0), (*down, 1), (across, None, 2), (core, None, 3)]
        if 1 <= phase <= 3:
            n = 4 + 6 * (phase - 1)
            below, above = [(*up, n), (core, None, n + 2)], [(*down, n + 3), (core, None, n + 5)]
            if not early:
                below.append((across, None, n + 1))
                above.append((across, None, n + 4))
            yield z >= phase, at - 4 * phase, below
            yield z + phase <= 3, at + 4 * phase, above
        if phase == 1:
            yield None, across, [(*up, 22), (*down, 23), (core, None, 24)] if early else [(core, None, 24)]
        if 2 <= phase <= 4:
            d, n = phase - 1, 25 + 4 * (phase - 2)
            below, above = [(core, None, n + 1)], [(core, None, n + 3)]
            if early:
                below.append((*up, n))
                above.append((*down, n + 2))
            yield z >= d, other(at - 4 * d, 2), below
            yield z + d <= 3, other(at + 4 * d, 2), above

    def each(self, chunk, phase, act):
        for when, shard, sends in self.sends(chunk, phase):

            def run():
                act(shard, None, None)
                for target, whether, number in sends:
                    if whether is None:
                        act(shard, target, number)
                    else:
                        pl.when(whether)(lambda: act(shard, target, number))

            if when is None:
                run()
            else:
                pl.when(when)(run)

    def phase(self, chunk, phase):
        def act(shard, target, number):
            if target is None:
                if phase == 0:
                    self.local(chunk).start()
                else:
                    self.copy(chunk, shard, self.at, 0).wait_recv()
            else:
                self.copy(chunk, shard, target, number, own=phase == 0).start()

        self.each(chunk, phase, act)

    def finish(self):
        for chunk in range(len(self.chunks)):
            for n in range(8):
                shard = jnp.bitwise_xor(lax.rem(self.at, 2), 1) + 2 * n
                self.copy(chunk, shard, self.at, 0).wait_recv()
            self.local(chunk).wait()
            for phase in range(5):

                def act(shard, target, number):
                    if target is not None:
                        self.copy(chunk, shard, target, number, own=phase == 0).wait_send()

                self.each(chunk, phase, act)


class SlabSum:
    def __init__(self, order, keep, send, got, sems, load=None):
        self.order, self.keep, self.send, self.got, self.sems, self.load = (0, *order), keep, send, got, sems, load

    @staticmethod
    def scratch(slots, share, columns):
        steps = slots.bit_length()
        return [
            *[pltpu.VMEM((max(slots >> n, 1), share, columns), bf16) for n in (0, *range(steps))],
            pltpu.SemaphoreType.DMA((2 * steps + 1,)),
        ]

    def copy(self, step):
        count = self.got[step].shape[0]
        return pltpu.make_async_remote_copy(
            src_ref=self.send if step == 0 else self.keep.at[pl.ds(count, count)],
            dst_ref=self.got[step],
            send_sem=self.sems.at[2 * step],
            recv_sem=self.sems.at[2 * step + 1],
            device_id=partner(self.order[step]),
            device_id_type=MESH,
        )

    def loading(self):
        return pltpu.make_async_copy(self.load, self.keep, self.sems.at[2 * len(self.order)])

    def start(self):
        self.copy(0).start()
        if self.load is not None:
            self.loading().start()

    def step(self, step):
        if step == 1 and self.load is not None:
            self.loading().wait()
        self.copy(step - 1).wait_recv()
        got = self.got[step - 1]

        @pl.loop(0, got.shape[0])
        def _(n):
            self.keep[n] = (self.keep[n].astype(f32) + got[n].astype(f32)).astype(bf16)

        self.copy(step).start()

    def finish(self, out_ref, width, first=0):
        last = len(self.order) - 1
        self.copy(last).wait_recv()
        total = self.keep[0].astype(f32) + self.got[last][0].astype(f32)
        share = out_ref.shape[0]
        by = total.shape[0] // share
        block = out_ref.shape[1] if by == 1 else width // by
        for n in range(total.shape[1] // block):
            for i in range(by):
                at = first + (n * by + i) * block
                out_ref[:, at : at + block] = total[i * share : (i + 1) * share, n * block : (n + 1) * block]
        for step in range(len(self.order)):
            self.copy(step).wait_send()


ALL = (-1, 0, 1, 2, 3)
LATE = (0, 1, 2, 3, -1)


class GainSum:
    def __init__(self, bits, held, got, sems):
        self.bits, self.held, self.got, self.sems = bits, held, got, sems

    @staticmethod
    def scratch(bits, width):
        steps = len(bits)
        return [
            pltpu.VMEM((steps, 8, width), f32),
            pltpu.VMEM((steps, 8, width), f32),
            pltpu.SemaphoreType.DMA((2 * steps,)),
        ]

    def copy(self, step):
        return pltpu.make_async_remote_copy(
            src_ref=self.held.at[step],
            dst_ref=self.got.at[step],
            send_sem=self.sems.at[2 * step],
            recv_sem=self.sems.at[2 * step + 1],
            device_id=partner(self.bits[step]),
            device_id_type=MESH,
        )

    def start(self, value):
        self.held[0] = value
        self.copy(0).start()

    def step(self, step):
        self.copy(step - 1).wait_recv()
        self.held[step] = self.held[step - 1] + self.got[step - 1]
        self.copy(step).start()

    def finish(self, out_ref):
        last = len(self.bits) - 1
        self.copy(last).wait_recv()
        out_ref[...] = self.held[last] + self.got[last]
        for step in range(len(self.bits)):
            self.copy(step).wait_send()


def row_specs(tile, width, half):
    own = pl.BlockSpec((None, None, tile, width), lambda i, s: (0, s[0], jnp.minimum(i, half - 1), 0))
    away = pl.BlockSpec((tile, width), lambda i, s: (jnp.maximum(i - half, 0), 0))
    return own, away


def read_rows(own_ref, away_ref, half):
    return jnp.where(pl.program_id(0) < half, own_ref[...], away_ref[...])


def project_kernel(side_ref, own_ref, away_ref, gain_ref, w_ref, cos_ref, sin_ref, out_ref, hidden_ref, *, half):
    width = own_ref.shape[-1]
    project_tile(read_rows(own_ref, away_ref, half), gain_ref[...], lambda part: w_ref[:, part * width : (part + 1) * width],
                 cos_ref, sin_ref, out_ref, hidden_ref)


def project_tile(x, gain, weights, cos_ref, sin_ref, out_ref, hidden_ref):
    x = x.astype(f32)
    width = x.shape[1]
    center = x - jnp.mean(x, axis=1, keepdims=True)
    spread = jnp.mean(center * center, axis=1, keepdims=True)
    hidden = (center * lax.rsqrt(spread + 1e-5) * gain.astype(f32)).astype(bf16)
    hidden_ref[...] = hidden
    cosine, sine = cos_ref[...], sin_ref[...]
    for part in range(3):
        rows = mm(hidden, weights(part))
        for pair in range(width // LANES):
            cols = slice(pair * LANES, (pair + 1) * LANES)
            field = rows[:, cols]
            if part < 2:
                field = field * cosine + half_partner(field) * sine
            if part == 0:
                field = field * 0.125
            out_ref[part, :, cols] = field.astype(bf16)


def project(side, own, away, gain, w, cosine, sine, tile=512):
    length, width = away.shape
    tokens, half = 2 * length, length // tile
    table = pl.BlockSpec((tile, LANES), lambda i, s: (lax.rem(i, half), 0))
    return pl.pallas_call(
        functools.partial(project_kernel, half=half),
        name="project",
        grid_spec=pltpu.PrefetchScalarGridSpec(
            num_scalar_prefetch=1,
            grid=(2 * half,),
            in_specs=[
                *row_specs(tile, width, half),
                pl.BlockSpec((1, width), lambda i, s: (0, 0)),
                pl.BlockSpec((width, 3 * width), lambda i, s: (0, 0), pipeline_mode=pl.Buffered(1)),
                table,
                table,
            ],
            out_specs=[
                pl.BlockSpec((3, tile, width), lambda i, s: (0, i, 0)),
                pl.BlockSpec((tile, width), lambda i, s: (i, 0)),
            ],
        ),
        out_shape=[jax.ShapeDtypeStruct((3, tokens, width), bf16), jax.ShapeDtypeStruct((tokens, width), bf16)],
        compiler_params=pltpu.CompilerParams(vmem_limit_bytes=62 << 20),
        cost_estimate=pl.CostEstimate(
            flops=6 * tokens * width * width, bytes_accessed=tokens * width * 10 + 6 * width * width, transcendentals=0
        ),
    )(side, own, away, gain, w, cosine, sine)


def first_kernel(shard_ref, wo_ref, wu_ref, gain_ref, tokens_ref, own_ref, cos_ref, sin_ref,
                 qkv_ref, hidden_ref, away_out, w_out, wo_all, wu_all, gains_out,
                 w_all, away, rows, swap_sems, out_sems, *refs, half):
    side, at = lax.axis_index("stream"), lax.axis_index("batch")
    step = pl.program_id(0)
    width = own_ref.shape[-1]
    tile = own_ref.shape[-2]
    def swap(n):
        part = pl.ds(n * tile, tile)
        return pltpu.make_async_remote_copy(
            src_ref=tokens_ref.at[0, 1 - side, part],
            dst_ref=away.at[part],
            send_sem=swap_sems.at[0, n],
            recv_sem=swap_sems.at[1, n],
            device_id=(1 - side, at),
            device_id_type=MESH,
        )

    def chunk(n):
        cols = slice(n * width, (n + 1) * width)
        return shard_ref.at[:, cols], lambda shard: w_all.at[shard, :, cols]

    weights = LineGather([chunk(n) for n in range(3)], *refs[:3], across_first=(0,))
    part = wu_ref.at[:, : wu_all.shape[2]]
    others = LineGather([(wo_ref, lambda shard: wo_all.at[shard]), (part, lambda shard: wu_all.at[shard])], *refs[3:6])
    gain = GainSum((0, 1, 2, 3), *refs[6:])
    keeps = [
        pltpu.make_async_copy(w_all, w_out, out_sems.at[0]),
        pltpu.make_async_copy(away, away_out, out_sems.at[1]),
    ]

    @pl.when(step == 0)
    def _():
        greet(line_partners())
        for n in range(half):
            swap(n).start()
        gain.start(gain_ref[...])
        for phase in range(5):
            for n in range(3):
                weights.phase(n, phase)
            if 1 <= phase <= 3:
                gain.step(phase)
        gain.finish(gains_out)
        weights.finish()
        for n in range(2):
            others.phase(n, 0)
        keeps[0].start()

    for now in range(1, 4):

        @pl.when(step == now)
        def _():
            for n in range(2):
                others.phase(n, now)
            if now >= half:
                swap(now - half).wait()
            if now == 2 * half - 1:
                keeps[1].start()

    @pl.when(step < half)
    def _():
        rows[...] = own_ref[...]

    @pl.when(step >= half)
    def _():
        rows[...] = away[pl.ds(pl.multiple_of((step - half) * tile, tile), tile), :]

    project_tile(rows[...], gains_out[0:1, :], lambda part: w_all[:, :, part * width : (part + 1) * width].reshape(width, width),
                 cos_ref, sin_ref, qkv_ref, hidden_ref)

    @pl.when(step == pl.num_programs(0) - 1)
    def _():
        for n in range(2):
            others.phase(n, 4)
        others.finish()
        for keep in keeps:
            keep.wait()


def first(shard, wo, wu, cut, gain, tokens, cosine, sine, tile=512):
    _, _, length, width = tokens.shape
    rows = shard.shape[0]
    half = length // tile
    assert half == 2
    anywhere = pl.BlockSpec(memory_space=pl.ANY)
    table = pl.BlockSpec((tile, LANES), lambda i: (lax.rem(i, half), 0))
    small = pl.BlockSpec((8, width), lambda i: (0, 0))
    return pl.pallas_call(
        functools.partial(first_kernel, half=half),
        name="first",
        grid=(2 * half,),
        in_specs=[
            anywhere,
            anywhere,
            anywhere,
            small,
            anywhere,
            pl.BlockSpec((None, None, tile, width), lambda i: (0, lax.axis_index("stream"), jnp.minimum(i, half - 1), 0)),
            table,
            table,
        ],
        out_specs=[
            pl.BlockSpec((3, tile, width), lambda i: (0, i, 0)),
            pl.BlockSpec((tile, width), lambda i: (i, 0)),
            anywhere,
            anywhere,
            anywhere,
            anywhere,
            small,
        ],
        out_shape=[
            jax.ShapeDtypeStruct((3, 2 * length, width), bf16),
            jax.ShapeDtypeStruct((2 * length, width), bf16),
            jax.ShapeDtypeStruct((length, width), bf16),
            jax.ShapeDtypeStruct((16, rows, 3 * width), bf16),
            jax.ShapeDtypeStruct((16, rows, width), bf16),
            jax.ShapeDtypeStruct((16, rows, cut), bf16),
            jax.ShapeDtypeStruct((8, width), f32),
        ],
        scratch_shapes=[
            pltpu.VMEM((16, rows, 3 * width), bf16),
            pltpu.VMEM((length, width), bf16),
            pltpu.VMEM((tile, width), bf16),
            pltpu.SemaphoreType.DMA((2, half)),
            pltpu.SemaphoreType.DMA((2,)),
            *LineGather.scratch(3),
            *LineGather.scratch(2),
            *GainSum.scratch((0, 1, 2, 3), width),
        ],
        compiler_params=pltpu.CompilerParams(vmem_limit_bytes=62 << 20, collective_id=0, has_side_effects=True),
        cost_estimate=pl.CostEstimate(
            flops=12 * length * width * width, bytes_accessed=length * width * 24 + 12 * width * width, transcendentals=0
        ),
    )(shard, wo, wu, gain, tokens, tokens, cosine, sine)


def mask_tables(length, row_length):
    pos = jnp.arange(length)
    blk = (pos // BLOCK)[:, None]
    lane = (jnp.arange(LANES) % HD)[None, :]
    dead = (pos >= row_length)[:, None]
    clean_query = (lane == blk).astype(bf16)
    noisy_query = (lane == blk - 1).astype(bf16)
    main_key = jnp.where((blk > lane) | dead, BIG, 0.0).astype(bf16)
    diag_key = jnp.where((blk != lane) | dead, BIG, 0.0).astype(bf16)
    return clean_query, noisy_query, main_key, diag_key


def low_lanes(shape):
    return lax.broadcasted_iota(jnp.int32, shape, 1) < HD


def attend_gather_kernel(qkv_ref, cq_ref, nq_ref, mk_ref, dk_ref, wu_ref, wd_ref, grad_ref,
                         out_ref, log_ref, wu_all, wd_all, away_ref,
                         qa, ka, kd, va, s_scr, swap_sems, send_sems, recv_sems, local_sems):
    side, at = lax.axis_index("stream"), lax.axis_index("batch")
    step = pl.program_id(0)
    wide, tall = wu_all.shape[2] // 2, wd_ref.shape[0] // 2
    cut = wu_ref.shape[1] - 2 * wide

    def columns(n):
        cols = slice(n * wide, (n + 1) * wide)
        return wu_ref.at[:, cut + n * wide : cut + (n + 1) * wide], lambda shard: wu_all.at[shard, :, cols]

    def rows(n):
        part = slice(n * tall, (n + 1) * tall)
        return wd_ref.at[part, :], lambda shard: wd_all.at[shard, part, :]

    chunks = [columns(0), columns(1), rows(0), rows(1)]
    weights = LineGather(chunks, send_sems, recv_sems, local_sems, EARLY)
    swap = pltpu.make_async_remote_copy(
        src_ref=grad_ref.at[0, 1 - side],
        dst_ref=away_ref,
        send_sem=swap_sems.at[0],
        recv_sem=swap_sems.at[1],
        device_id=(1 - side, at),
        device_id_type=MESH,
    )
    slots = 2 * SLOT_STEPS
    plan = [[] for _ in range(slots + 1)]
    items = SLOT_ORDER
    for n, item in enumerate(items):
        plan[min(1 + n * SLOT_RATE // 16, slots)].append(item)

    @pl.when(step == 0)
    def _():
        greet(line_partners())
        for chunk in range(4):
            weights.phase(chunk, 0)
        swap.start()

    def pass_on(slot):
        for now in range(SLOT_STEPS):
            if plan[2 * now + slot]:

                @pl.when(step == now)
                def _():
                    for item in plan[2 * now + slot]:
                        weights.phase(*item)

    pass_on(0)
    attend_kernel(qkv_ref, cq_ref, nq_ref, mk_ref, dk_ref, out_ref, log_ref, qa, ka, kd, va, s_scr,
                  between=lambda: pass_on(1))

    @pl.when(step == pl.num_programs(0) - 1)
    def _():
        for item in plan[slots]:
            weights.phase(*item)
        weights.finish()
        swap.wait()


EARLY = (0,)
SLOT_STEPS = 6
SLOT_RATE = 14
SLOT_ORDER = [(chunk, phase) for phase in range(1, 5) for chunk in range(4)]


def attend_kernel(qkv_ref, cq_ref, nq_ref, mk_ref, dk_ref, out_ref, log_ref,
                  qa, ka, kd, va, s_scr, between=lambda: None):
    length = out_ref.shape[1]
    clean = lax.axis_index("stream")
    noisy = 1 - clean
    tiles = length // TILE
    low = low_lanes((length, LANES))
    ones = jnp.ones((16, length), bf16)
    vc_t = qkv_ref[2, clean].T
    vn_t = qkv_ref[2, noisy].T
    for head in range(2):
        pick = low if head == 0 else jnp.logical_not(low)
        qa[0, head] = jnp.where(pick, qkv_ref[0, clean], cq_ref[...])
        qa[1, head] = jnp.where(pick, qkv_ref[0, noisy], nq_ref[...])
        qa[2, head] = jnp.where(pick, qkv_ref[0, noisy], cq_ref[...])
        ka[head] = jnp.where(pick, qkv_ref[1, clean], mk_ref[...])
        kd[head] = jnp.where(pick, qkv_ref[1, noisy], dk_ref[...])
        va[0, head, :HD] = vc_t[head * HD : (head + 1) * HD]
        va[1, head, :HD] = vn_t[head * HD : (head + 1) * HD]
        va[0, head, HD:] = ones
        va[1, head, HD:] = ones
    for copy in range(2):
        if copy:
            between()
        where_to = clean if copy == 0 else noisy
        for tile in range(tiles):
            rows = slice(tile * TILE, (tile + 1) * TILE)
            parts = []
            for head in range(2):
                pieces = [(qa[copy, head, rows, :], ka, 0, t) for t in range(tile + 1)]
                if copy == 1:
                    pieces.append((qa[2, head, rows, :], kd, 1, tile))
                top = None
                for n, (query, keys, vi, t) in enumerate(pieces):
                    s = mm_t(keys[head, t * TILE : (t + 1) * TILE, :], query)
                    if copy == 1 and tile == 0 and n == 0:
                        first = lax.broadcasted_iota(jnp.int32, s.shape, 1) < BLOCK
                        s = jnp.where(first, BIG, s)
                    s_scr[head, n * TILE : (n + 1) * TILE, :] = s
                    m = jnp.max(s, axis=0, keepdims=True)
                    top = m if top is None else jnp.maximum(top, m)
                acc = None
                for n, (query, keys, vi, t) in enumerate(pieces):
                    p = jnp.exp(s_scr[head, n * TILE : (n + 1) * TILE, :] - top).astype(bf16)
                    o = mm(va[vi, head, :, t * TILE : (t + 1) * TILE], p)
                    acc = o if acc is None else acc + o
                total = acc[HD : HD + 1, :]
                parts.append(acc[:HD] / total)
                log_ref[where_to, 0, head : head + 1, rows] = top + jnp.log(total)
            out_ref[where_to, rows, :] = jnp.concatenate(parts, axis=0).T.astype(bf16)


def attend(qkv, tables, shards=None, cut=0, grad=None):
    _, copies, length, width = qkv.shape
    pairs = width // LANES
    table_spec = pl.BlockSpec((length, LANES), lambda i: (0, 0), pipeline_mode=pl.Buffered(1))
    more_in, more_shapes, more_scratch = [], [], []
    body, params = attend_kernel, {}
    if shards is not None:
        assert pairs == SLOT_STEPS
        body = attend_gather_kernel
        params = dict(collective_id=3, has_side_effects=True)
        more_in = [*shards, grad]
        up, down = (shard.shape for shard in shards)
        more_shapes = [jax.ShapeDtypeStruct(s, bf16) for s in ((16, up[0], up[1] - cut), (16, *down))]
        more_shapes.append(jax.ShapeDtypeStruct((length, width), bf16))
        more_scratch = [pltpu.SemaphoreType.DMA((2,)), *LineGather.scratch(4)]
    anywhere = pl.BlockSpec(memory_space=pl.ANY)
    return pl.pallas_call(
        body,
        name="attend",
        grid=(pairs,),
        in_specs=[pl.BlockSpec((3, copies, length, LANES), lambda i: (0, 0, 0, i)), *[table_spec] * 4,
                  *[anywhere] * len(more_in)],
        out_specs=[
            pl.BlockSpec((copies, length, LANES), lambda i: (0, 0, i)),
            pl.BlockSpec((copies, 1, 2, length), lambda i: (0, i, 0, 0)),
            *[anywhere] * len(more_shapes),
        ],
        scratch_shapes=[
            pltpu.VMEM((3, 2, length, LANES), bf16),
            pltpu.VMEM((2, length, LANES), bf16),
            pltpu.VMEM((2, length, LANES), bf16),
            pltpu.VMEM((2, 2, HD + 16, length), bf16),
            pltpu.VMEM((2, length + TILE, TILE), f32),
            *more_scratch,
        ],
        out_shape=[
            jax.ShapeDtypeStruct((copies, length, width), bf16),
            jax.ShapeDtypeStruct((copies, pairs, 2, length), f32),
            *more_shapes,
        ],
        compiler_params=pltpu.CompilerParams(vmem_limit_bytes=62 << 20, **params),
        cost_estimate=pl.CostEstimate(
            flops=8 * length * length * width, bytes_accessed=16 * length * width, transcendentals=length * length * 12
        ),
    )(qkv, *tables, *more_in)


DOWN, UP, OUT = (-1, 1, 2, 3), (1, -1, 2, 3), (2, -1, 1, 3)
QKV = ((1, 2, 3, -1), (2, 1, 3, -1), (1, 2, 3, -1))


def attend_back_sum_kernel(*refs, orders):
    count = len(orders)
    core, refs = refs[:10], refs[10:]
    pairs, gain_ref, refs = refs[: 2 * count], refs[2 * count], refs[2 * count + 1 :]
    dqkv_ref, refs = refs[0], refs[1:]
    outs, gain_out, refs = refs[:count], refs[count], refs[count + 1 :]
    own, refs = refs[:10], refs[10:]
    per = len(refs[:-3]) // count
    sums = []
    for n, order in enumerate(orders):
        keep, *got, sems = refs[n * per : (n + 1) * per]
        sums.append(SlabSum(order, keep, pairs[2 * n + 1], got, sems, load=pairs[2 * n]))
    gain = GainSum(ALL, *refs[-3:])
    down, up, wo = sums
    step = pl.program_id(0)

    @pl.when(step == 0)
    def _():
        greet([partner(bit) for bit in ALL])
        for one in sums:
            one.start()
        gain.start(gain_ref[...])

    for at, plan in {
        1: ((down, 1), (up, 1), (wo, 1), (gain, 1)),
        2: ((wo, 2), (gain, 2)),
        3: ((down, 2), (up, 2), (wo, 3), (gain, 3)),
        4: ((down, 3), (up, 3), (wo, 4), (gain, 4)),
        5: ((down, 4), (up, 4)),
    }.items():

        @pl.when(step == at)
        def _():
            for one, number in plan:
                one.step(number)

    attend_back_kernel(*core, dqkv_ref, *own)

    @pl.when(step == pl.num_programs(0) - 1)
    def _():
        for one, out_ref in zip(sums, outs):
            one.finish(out_ref, gain_ref.shape[1])
        gain.finish(gain_out)


def attend_back_kernel(qkv_ref, o_ref, do_ref, log_ref, cq_ref, nq_ref, mk_ref, dk_ref, cos_ref, sin_ref,
                       dqkv_ref, qa, qz, ka, kd, kt, doz, dsum, dq, dkc, dvc):
    length = o_ref.shape[1]
    clean = lax.axis_index("stream")
    noisy = 1 - clean
    tiles = length // TILE
    low = low_lanes((length, LANES))
    zero = jnp.zeros((length, LANES), bf16)
    for copy in range(2):
        at = clean if copy == 0 else noisy
        kt[copy] = qkv_ref[1, at].T
        prod = (o_ref[at].astype(f32) * do_ref[at].astype(f32)).T
        dsum[copy, 0:1] = jnp.sum(prod[:HD], axis=0, keepdims=True)
        dsum[copy, 1:2] = jnp.sum(prod[HD:], axis=0, keepdims=True)
        for head in range(2):
            pick = low if head == 0 else jnp.logical_not(low)
            qa[copy, head] = jnp.where(pick, qkv_ref[0, at], (cq_ref, nq_ref)[copy][...])
            qz[copy, head] = jnp.where(pick, qkv_ref[0, at], zero)
            doz[copy, head] = jnp.where(pick, do_ref[at], zero)
            if copy == 0:
                ka[head] = jnp.where(pick, qkv_ref[1, at], mk_ref[...])
            else:
                qa[2, head] = jnp.where(pick, qkv_ref[0, at], cq_ref[...])
                kd[head] = jnp.where(pick, qkv_ref[1, at], dk_ref[...])
    cosine, sine = cos_ref[...], sin_ref[...]

    def piece(copy, tile, query, keys, kv_copy, krows):
        rows = slice(tile * TILE, (tile + 1) * TILE)
        kv_at = clean if kv_copy == 0 else noisy
        at = clean if copy == 0 else noisy
        probs, raws, dqs = [], [], []
        for head in range(2):
            s = mm_t(keys[head, krows, :], qa[query, head, rows, :])
            p = jnp.exp(s - log_ref[at, 0, head : head + 1, rows])
            if kv_copy == 0 and copy == 1 and tile == 0:
                first = lax.broadcasted_iota(jnp.int32, s.shape, 1) < BLOCK
                p = jnp.where(first, 0.0, p)
            dp = mm_t(qkv_ref[2, kv_at, krows, :], doz[copy, head, rows, :])
            raw = (p * (dp - dsum[copy, head : head + 1, rows])).astype(bf16)
            dqs.append(mm(kt[kv_copy, head * HD : (head + 1) * HD, krows], raw))
            probs.append(p.astype(bf16))
            raws.append(raw)
        grads = [doz[copy, head, rows, :] for head in range(2)]
        queries = [qz[copy, head, rows, :] for head in range(2)]
        return jnp.concatenate(dqs, axis=0), (raws, queries), (probs, grads)

    def product(pair):
        return mm(jnp.concatenate(pair[0], axis=1), jnp.concatenate(pair[1], axis=0))

    def finish(field, rotate, scale):
        if rotate:
            c, s = cosine, sine
            field = field * c - half_partner(field) * s
        return (field * scale if scale != 1.0 else field).astype(bf16)

    for tile in range(tiles):
        rows = slice(tile * TILE, (tile + 1) * TILE)
        dq_t, dk_t, dv_t = piece(1, tile, 2, kd, 1, rows)
        dq[1, :, rows] = dq_t
        dkc[rows, :] = product(dk_t)
        dqkv_ref[2, noisy, rows, :] = product(dv_t).astype(bf16)
    dqkv_ref[1, noisy] = finish(dkc[...], True, 1.0)
    for tile in reversed(range(tiles)):
        rows = slice(tile * TILE, (tile + 1) * TILE)
        seen = slice(0, (tile + 1) * TILE)
        dq_t, dk_c, dv_c = piece(0, tile, 0, ka, 0, seen)
        dq[0, :, rows] = dq_t
        dq_t, dk_n, dv_n = piece(1, tile, 1, ka, 0, seen)
        dq[1, :, rows] += dq_t
        dk_t = product((dk_c[0] + dk_n[0], dk_c[1] + dk_n[1]))
        dv_t = product((dv_c[0] + dv_n[0], dv_c[1] + dv_n[1]))
        if tile == tiles - 1:
            dkc[...] = dk_t
            dvc[...] = dv_t
        else:
            dkc[seen, :] += dk_t
            dvc[seen, :] += dv_t
    dqkv_ref[2, clean] = dvc[...].astype(bf16)
    dqkv_ref[1, clean] = finish(dkc[...], True, 1.0)
    dqkv_ref[0, clean] = finish(dq[0].T, True, 0.125)
    dqkv_ref[0, noisy] = finish(dq[1].T, True, 0.125)


def attend_back(qkv, mixed, grad, logs, tables, cosine, sine, pairs=None, gain=None, slabs=()):
    _, copies, length, width = qkv.shape
    steps = width // LANES
    table_spec = pl.BlockSpec((length, LANES), lambda i: (0, 0), pipeline_mode=pl.Buffered(1))
    row_spec = pl.BlockSpec((copies, length, LANES), lambda i: (0, 0, i))
    three = pl.BlockSpec((3, copies, length, LANES), lambda i: (0, 0, 0, i))
    anywhere = pl.BlockSpec(memory_space=pl.ANY)

    def fixed(shape):
        return pl.BlockSpec(shape, lambda i: (0, 0), pipeline_mode=pl.Buffered(1))

    more_in, more_specs, more_shapes, more_out, more_scratch = [], [], [], [], []
    body, params = attend_back_kernel, {}
    if pairs is not None:
        assert steps == 6
        body = functools.partial(attend_back_sum_kernel, orders=(DOWN, UP, OUT))
        params = dict(collective_id=1, has_side_effects=True)
        for (keep, send), slab in zip(pairs, slabs):
            slots, share, columns = keep.shape
            more_in += [keep, send]
            more_specs += [anywhere] * 2
            more_shapes.append(jax.ShapeDtypeStruct(slab, f32))
            more_out.append(fixed(slab))
            more_scratch += SlabSum.scratch(slots, share, columns)
        more_in.append(gain)
        more_specs.append(fixed((8, width)))
        more_shapes.append(jax.ShapeDtypeStruct((8, width), f32))
        more_out.append(fixed((8, width)))
        more_scratch += GainSum.scratch(ALL, width)
    return pl.pallas_call(
        body,
        name="attend_back",
        grid_spec=pltpu.PrefetchScalarGridSpec(
            num_scalar_prefetch=0,
            grid=(steps,),
            in_specs=[three, row_spec, row_spec, pl.BlockSpec((copies, 1, 2, length), lambda i: (0, i, 0, 0))]
            + [table_spec] * 6
            + more_specs,
            out_specs=[three, *more_out],
            scratch_shapes=[
                pltpu.VMEM((3, 2, length, LANES), bf16),
                pltpu.VMEM((2, 2, length, LANES), bf16),
                pltpu.VMEM((2, length, LANES), bf16),
                pltpu.VMEM((2, length, LANES), bf16),
                pltpu.VMEM((2, LANES, length), bf16),
                pltpu.VMEM((2, 2, length, LANES), bf16),
                pltpu.VMEM((2, 2, length), f32),
                pltpu.VMEM((2, LANES, length), f32),
                pltpu.VMEM((length, LANES), f32),
                pltpu.VMEM((length, LANES), f32),
                *more_scratch,
            ],
        ),
        out_shape=[jax.ShapeDtypeStruct((3, copies, length, width), bf16), *more_shapes],
        compiler_params=pltpu.CompilerParams(vmem_limit_bytes=62 << 20, **params),
        cost_estimate=pl.CostEstimate(
            flops=20 * length * length * width, bytes_accessed=30 * length * width, transcendentals=length * length * 12
        ),
    )(qkv, mixed, grad, logs, *tables, cosine, sine, *more_in)


ROOT = math.sqrt(2.0 / math.pi)


def feed_kernel(side_ref, x_own, x_away, mixed_ref, g_own, g_away, gain_ref, wo_all, wu_all, wu_more, wd_all,
                out_own, out_away, act_ref, du_ref, h2_ref, dmid_ref, dbr_ref, dmix_ref, dgain_ref,
                wo_ref, wu_ref, wd_ref, sems, *, half):
    groups, rows, width = wo_ref.shape
    fold = wu_ref.shape[0]

    @pl.when(pl.program_id(0) == 0)
    def _():
        copies = [pltpu.make_async_copy(wo_all, wo_ref, sems.at[0])]
        begin = 0
        for array in (wu_all, wu_more):
            end = begin + array.shape[2]
            for n in range(fold):
                low, high = max(begin, n * width), min(end, (n + 1) * width)
                if low < high:
                    copies.append(
                        pltpu.make_async_copy(
                            array.at[:, :, low - begin : high - begin],
                            wu_ref.at[n, :, :, low - n * width : high - n * width],
                            sems.at[len(copies)],
                        )
                    )
            begin = end
        copies.append(pltpu.make_async_copy(wd_all, wd_ref, sems.at[len(copies)]))
        for copy in copies:
            copy.start()
        for copy in copies:
            copy.wait()

    def down(c):
        per = groups // fold
        return wd_ref[c * per : (c + 1) * per].reshape(width, width)

    wo = wo_ref[...].reshape(width, width)
    gain = gain_ref[...].astype(f32)
    middle = read_rows(x_own, x_away, half).astype(f32) + mm(mixed_ref[...], wo)
    center = middle - jnp.mean(middle, axis=1, keepdims=True)
    spread = jnp.mean(center * center, axis=1, keepdims=True)
    inv = lax.rsqrt(spread + 1e-5)
    norm = center * inv
    hidden = (norm * gain).astype(bf16)
    h2_ref[...] = hidden
    grad = read_rows(g_own, g_away, half)
    out = middle
    dh = jnp.zeros_like(middle)
    for c in range(fold):
        cols = slice(c * width, (c + 1) * width)
        up = wu_ref[c].reshape(width, width)
        u = mm(hidden, up)
        da = mm_t(grad, down(c)).astype(bf16).astype(f32)
        sq = u * u
        t = jnp.tanh(u * (ROOT + (ROOT * 0.044715) * sq))
        part = 0.5 + 0.5 * t
        wide = u * part
        act = wide.astype(bf16)
        slope = part + (wide * (1.0 - t)) * (ROOT + (3 * ROOT * 0.044715) * sq)
        du = (da * slope).astype(bf16)
        act_ref[:, cols] = act
        du_ref[:, cols] = du
        out = out + mm(act, down(c))
        dh = dh + mm_t(du, up)
    low = out.astype(bf16)

    @pl.when(pl.program_id(0) < half)
    def _():
        out_own[...] = low

    @pl.when(pl.program_id(0) >= half)
    def _():
        out_away[...] = low

    @pl.when(pl.program_id(0) == 0)
    def _():
        dgain_ref[...] = jnp.zeros_like(dgain_ref)

    dgain_ref[...] += jnp.sum((dh * norm).reshape(-1, 8, width), axis=0)
    e = dh * gain
    dmid = grad.astype(f32) + inv * (
        e - jnp.mean(e, axis=1, keepdims=True) - norm * jnp.mean(e * norm, axis=1, keepdims=True)
    )
    dmid_ref[...] = dmid
    dbr = dmid.astype(bf16)
    dbr_ref[...] = dbr
    dmix_ref[...] = mm_t(dbr, wo).astype(bf16)


def feed(side, x_own, x_away, mixed, g_own, g_away, gain, weights, tile=512):
    tokens, width = mixed.shape
    groups, rows, _ = weights[0].shape
    ff = weights[1].shape[2] + weights[2].shape[2]
    fold = ff // width
    half = tokens // 2 // tile
    row = pl.BlockSpec((tile, width), lambda i, s: (i, 0))
    wide = pl.BlockSpec((tile, ff), lambda i, s: (i, 0))
    own, away = row_specs(tile, width, half)

    def keep(shape):
        return pl.BlockSpec(shape, lambda i, s: (0, 0), pipeline_mode=pl.Buffered(1))

    return pl.pallas_call(
        functools.partial(feed_kernel, half=half),
        name="feed",
        grid_spec=pltpu.PrefetchScalarGridSpec(
            num_scalar_prefetch=1,
            grid=(2 * half,),
            in_specs=[own, away, row, own, away, keep((1, width)), *[pl.BlockSpec(memory_space=pl.ANY)] * 4],
            out_specs=[own, away, wide, wide, row, row, row, row, pl.BlockSpec((8, width), lambda i, s: (0, 0))],
            scratch_shapes=[
                pltpu.VMEM((groups, rows, width), bf16),
                pltpu.VMEM((fold, groups, rows, width), bf16),
                pltpu.VMEM((groups, fold * rows, width), bf16),
                pltpu.SemaphoreType.DMA((3 + fold,)),
            ],
        ),
        out_shape=[
            jax.ShapeDtypeStruct((1, 2, tokens // 2, width), bf16),
            jax.ShapeDtypeStruct((tokens // 2, width), bf16),
            jax.ShapeDtypeStruct((tokens, ff), bf16),
            jax.ShapeDtypeStruct((tokens, ff), bf16),
            jax.ShapeDtypeStruct((tokens, width), bf16),
            jax.ShapeDtypeStruct((tokens, width), f32),
            jax.ShapeDtypeStruct((tokens, width), bf16),
            jax.ShapeDtypeStruct((tokens, width), bf16),
            jax.ShapeDtypeStruct((8, width), f32),
        ],
        compiler_params=pltpu.CompilerParams(vmem_limit_bytes=62 << 20),
        cost_estimate=pl.CostEstimate(
            flops=tokens * width * (4 * width + 8 * ff), bytes_accessed=tokens * (width * 18 + ff * 4),
            transcendentals=tokens * ff
        ),
    )(side, x_own, x_away, mixed, g_own, g_away, gain, *weights)


def folds(share):
    return 1 if share % 16 == 0 else 2


def fold(slab):
    if folds(slab.shape[0]) == 1:
        return slab
    middle = slab.shape[1] // 2
    return jnp.concatenate([slab[:, :middle], slab[:, middle:]], axis=0)


def arranged(slot, order):
    return sum((slot >> bit & 1) << (len(order) - 1 - n) for n, bit in enumerate(order))


def weight_kernel(me_ref, left_ref, *refs, share, split, order):
    weight_slabs(me_ref[0], left_ref, *refs, share=share, split=split, order=order)


def weight_slabs(me, left_ref, *refs, share, split, order):
    right_refs, (keep_ref, send_ref, scr) = refs[:-3], refs[-3:]
    if split:
        own_ref, away_ref = right_refs
        half = own_ref.shape[0]
        total = t_mm(left_ref[:half], own_ref[...]) + t_mm(left_ref[half:], away_ref[...])
    else:
        total = t_mm(left_ref[...], right_refs[0][...])
    slabs = total.shape[0] // share
    scr[...] = total.reshape(scr.shape)
    low_me = lax.rem(me, slabs)
    for slot in range(slabs):
        source = jnp.bitwise_xor(low_me, slot)
        into = send_ref if slot % 2 else keep_ref
        into[arranged(slot // 2, order)] = fold(scr[source]).astype(bf16)


def weight_grad_columns(me, left, right, block, share, order, name):
    tokens, dl = left.shape
    dr = right.shape[1]
    peers = dl // share
    by = folds(share)
    shape = (peers // 2, share * by, dr // by)
    out = pl.BlockSpec((peers // 2, share * by, block // by), lambda j, m: (0, 0, j))
    return pl.pallas_call(
        functools.partial(weight_kernel, share=share, split=False, order=order),
        name=name,
        grid_spec=pltpu.PrefetchScalarGridSpec(
            num_scalar_prefetch=1,
            grid=(dr // block,),
            in_specs=[
                pl.BlockSpec((tokens, dl), lambda j, m: (0, 0), pipeline_mode=pl.Buffered(1)),
                pl.BlockSpec((tokens, block), lambda j, m: (0, j)),
            ],
            out_specs=[out, out],
            scratch_shapes=[pltpu.VMEM((peers, share, block), f32)],
        ),
        out_shape=[jax.ShapeDtypeStruct(shape, bf16)] * 2,
        compiler_params=pltpu.CompilerParams(vmem_limit_bytes=62 << 20),
        cost_estimate=pl.CostEstimate(
            flops=2 * tokens * dl * dr, bytes_accessed=2 * tokens * (dl + dr) + 2 * dl * dr, transcendentals=0
        ),
    )(me, left, right)


def weight_grad_rows(me, left, own, away, block, share, name):
    tokens, dl = left.shape
    length, dr = away.shape
    slabs = block // share
    steps = dl // block
    assert steps == 4
    shape = (2, slabs // 2, 2, share, dr)
    out = pl.BlockSpec((None, slabs // 2, None, share, dr), lambda j, m: (lax.div(j, 2), 0, lax.rem(j, 2), 0, 0))
    bits = (slabs // 2).bit_length() - 1

    def place(j, m):
        return (0, jnp.bitwise_xor(j, lax.div(m[0], slabs)))

    return pl.pallas_call(
        functools.partial(weight_kernel, share=share, split=True, order=tuple(range(bits))),
        name=name,
        grid_spec=pltpu.PrefetchScalarGridSpec(
            num_scalar_prefetch=1,
            grid=(steps,),
            in_specs=[
                pl.BlockSpec((tokens, block), place),
                pl.BlockSpec((None, None, length, dr), lambda j, m: (0, m[1], 0, 0), pipeline_mode=pl.Buffered(1)),
                pl.BlockSpec((length, dr), lambda j, m: (0, 0), pipeline_mode=pl.Buffered(1)),
            ],
            out_specs=[out, out],
            scratch_shapes=[pltpu.VMEM((slabs, share, dr), f32)],
        ),
        out_shape=[jax.ShapeDtypeStruct(shape, bf16)] * 2,
        compiler_params=pltpu.CompilerParams(vmem_limit_bytes=62 << 20),
        cost_estimate=pl.CostEstimate(
            flops=2 * tokens * dl * dr, bytes_accessed=2 * tokens * (dl + dr) + 2 * dl * dr, transcendentals=0
        ),
    )(me, left, own, away)


def last_kernel(x_own, x_away, gain_ref, w_hbm, dqkv_hbm, dmid_hbm, hidden_hbm,
                dx_ref, dw_ref, gain_out,
                xv, w_ref, dqkv, dmid, hidden, send, land, dgain, scr,
                load_sems, tile_sems, send_sems, recv_sems, out_sems, *refs, share):
    count = len(QKV)
    per = len(refs[:-3]) // count
    sums = []
    for n, order in enumerate(QKV):
        first, keep, *got, sems = refs[n * per : (n + 1) * per]
        sums.append(SlabSum(order, keep, first, got, sems))
    gain = GainSum(LATE, *refs[-3:])
    side, at = lax.axis_index("stream"), lax.axis_index("batch")
    me = side * lax.axis_size("batch") + at
    step = pl.program_id(0)
    width = w_ref.shape[0]
    length = land.shape[0]
    tiles = pl.num_programs(0)
    tile = 2 * length // 8
    half = 4

    def rows_of(t, base=0):
        return pl.ds(pl.multiple_of((t - base) * tile, tile), tile)

    loads = [
        pltpu.make_async_copy(w_hbm, w_ref, load_sems.at[0]),
        pltpu.make_async_copy(x_away, xv.at[pl.ds(length, length)], load_sems.at[1]),
        pltpu.make_async_copy(hidden_hbm, hidden, load_sems.at[2]),
        pltpu.make_async_copy(x_own.at[0, side], xv.at[pl.ds(0, length)], load_sems.at[3]),
    ]

    def load_grad(t):
        return pltpu.make_async_copy(dqkv_hbm.at[:, rows_of(t), :], dqkv.at[:, rows_of(t), :], tile_sems.at[0, t])

    def load_middle(t):
        return pltpu.make_async_copy(dmid_hbm.at[rows_of(t), :], dmid.at[rows_of(t), :], tile_sems.at[1, t])

    def away(t):
        return pltpu.make_async_remote_copy(
            src_ref=send.at[rows_of(t, half), :],
            dst_ref=land.at[rows_of(t, half), :],
            send_sem=send_sems.at[t - half],
            recv_sem=recv_sems.at[t - half],
            device_id=(1 - side, at),
            device_id_type=MESH,
        )

    def result(t, row):
        return pltpu.make_async_copy(
            dmid.at[rows_of(t), :],
            dx_ref.at[0, row, pl.ds(pl.multiple_of(lax.rem(t, half) * tile, tile), tile), :],
            out_sems.at[t],
        )

    @pl.when(step == 0)
    def _():
        loads[0].start()
        loads[1].start()
        load_grad(4).start()
        load_middle(4).start()
        loads[2].start()
        for t in (5, 6, 7, 0, 1, 2, 3):
            load_grad(t).start()
        loads[3].start()
        for t in (5, 6, 7, 0, 1, 2, 3):
            load_middle(t).start()
        dgain[...] = jnp.zeros_like(dgain)
        greet([partner(bit) for bit in ALL])
        loads[0].wait()
        loads[1].wait()
        load_grad(4).wait()
        load_middle(4).wait()

    @pl.when(step > 0)
    def _():
        load_middle(lax.rem(step + half, 8)).wait()

    @pl.when(step == half)
    def _():
        loads[3].wait()

    for now, plan in {
        1: ((0, 1), (1, 1)),
        2: ((0, 2), (2, 1)),
        3: ((1, 2),),
        4: ((0, 3),),
        6: ((2, 2), (1, 3)),
        7: ((0, 4),),
    }.items():

        @pl.when(step == now)
        def _():
            for n, number in plan:
                sums[n].step(number)

    t = lax.rem(step + half, 8)
    rows = rows_of(t)
    x = xv[rows, :].astype(f32)
    center = x - jnp.mean(x, axis=1, keepdims=True)
    spread = jnp.mean(center * center, axis=1, keepdims=True)
    inv = lax.rsqrt(spread + 1e-5)
    norm = center * inv
    dh = mm_t(dqkv[0, rows, :], w_ref[:, :width])
    dh = dh + mm_t(dqkv[1, rows, :], w_ref[:, width : 2 * width])
    dh = dh + mm_t(dqkv[2, rows, :], w_ref[:, 2 * width :])
    dgain[...] += jnp.sum((dh * norm).reshape(-1, 8, width), axis=0)
    e = dh * gain_ref[...]
    dx = dmid[rows, :] + inv * (
        e - jnp.mean(e, axis=1, keepdims=True) - norm * jnp.mean(e * norm, axis=1, keepdims=True)
    )

    @pl.when(step < half)
    def _():
        send[rows_of(step), :] = dx.astype(bf16)
        away(t).start()

    @pl.when(step >= half)
    def _():
        dmid[rows, :] = dx
        result(t, side).start()

    def part(n):
        order = tuple({-1: 3, 1: 0, 2: 1, 3: 2}[bit] for bit in QKV[n])
        weight_slabs(me, hidden, dqkv.at[n], sums[n].keep, sums[n].send, scr, share=share, split=False, order=order)
        sums[n].start()

    @pl.when(step == 0)
    def _():
        loads[2].wait()
        for other in (5, 6, 7, 0, 1, 2, 3):
            load_grad(other).wait()
        part(0)
        part(1)

    @pl.when(step == 1)
    def _():
        part(2)

    @pl.when(step == tiles - 1)
    def _():
        gain.start(dgain[...])
        sums[2].step(3)
        sums[1].step(4)
        sums[0].finish(dw_ref, width, 0)
        gain.step(1)
        sums[2].step(4)
        gain.step(2)
        sums[1].finish(dw_ref, width, width)
        gain.step(3)
        sums[2].finish(dw_ref, width, 2 * width)
        gain.step(4)
        for other in range(half, 8):
            away(other).wait()
            dmid[rows_of(other), :] = land[rows_of(other, half), :].astype(f32)
            result(other, 1 - side).start()
        gain.finish(gain_out)
        for other in range(8):
            result(other, side).wait()


def last(tokens, x_away, gain, w, dqkv, dmid, hidden, share):
    tokens_all, width = hidden.shape
    length = tokens_all // 2
    slots = width // share // 2
    anywhere = pl.BlockSpec(memory_space=pl.ANY)

    def fixed(shape):
        return pl.BlockSpec(shape, lambda i: (0, 0), pipeline_mode=pl.Buffered(1))

    scratch = []
    for _ in range(3):
        by = folds(share)
        scratch += [
            pltpu.VMEM((slots, share * by, width // by), bf16),
            *SlabSum.scratch(slots, share * by, width // by),
        ]
    return pl.pallas_call(
        functools.partial(last_kernel, share=share),
        name="last",
        grid=(8,),
        in_specs=[anywhere, anywhere, fixed((1, width)), *[anywhere] * 4],
        out_specs=[anywhere, fixed((share, 3 * width)), fixed((8, width))],
        out_shape=[
            jax.ShapeDtypeStruct((1, 2, length, width), f32),
            jax.ShapeDtypeStruct((share, 3 * width), f32),
            jax.ShapeDtypeStruct((8, width), f32),
        ],
        scratch_shapes=[
            pltpu.VMEM((2 * length, width), bf16),
            pltpu.VMEM((width, 3 * width), bf16),
            pltpu.VMEM((3, 2 * length, width), bf16),
            pltpu.VMEM((2 * length, width), f32),
            pltpu.VMEM((2 * length, width), bf16),
            pltpu.VMEM((length, width), bf16),
            pltpu.VMEM((length, width), bf16),
            pltpu.VMEM((8, width), f32),
            pltpu.VMEM((2 * slots, share, width), f32),
            pltpu.SemaphoreType.DMA((4,)),
            pltpu.SemaphoreType.DMA((2, 8)),
            pltpu.SemaphoreType.DMA((4,)),
            pltpu.SemaphoreType.DMA((4,)),
            pltpu.SemaphoreType.DMA((8,)),
            *scratch,
            *GainSum.scratch(LATE, width),
        ],
        compiler_params=pltpu.CompilerParams(vmem_limit_bytes=62 << 20, collective_id=2, has_side_effects=True),
        cost_estimate=pl.CostEstimate(
            flops=24 * length * width * width, bytes_accessed=36 * length * width, transcendentals=0
        ),
    )(tokens, x_away, gain, w, dqkv, dmid, hidden)


def project_back_kernel(side_ref, x_ref, gain_ref, w_ref, dqkv_ref, dmid_ref, dx_ref, dgain_ref):
    x = x_ref[...].astype(f32)
    width = x.shape[1]
    center = x - jnp.mean(x, axis=1, keepdims=True)
    spread = jnp.mean(center * center, axis=1, keepdims=True)
    inv = lax.rsqrt(spread + 1e-5)
    norm = center * inv
    dh = mm_t(dqkv_ref[0], w_ref[:, :width])
    dh = dh + mm_t(dqkv_ref[1], w_ref[:, width : 2 * width])
    dh = dh + mm_t(dqkv_ref[2], w_ref[:, 2 * width :])

    @pl.when(pl.program_id(0) == 0)
    def _():
        dgain_ref[...] = jnp.zeros_like(dgain_ref)

    dgain_ref[...] += jnp.sum((dh * norm).reshape(-1, 8, width), axis=0)
    e = dh * gain_ref[...].astype(f32)
    dx_ref[...] = (dmid_ref[...] + inv * (
        e - jnp.mean(e, axis=1, keepdims=True) - norm * jnp.mean(e * norm, axis=1, keepdims=True)
    )).astype(dx_ref.dtype)


def project_back(side, x, gain, w, dqkv, dmid, away, tile=256):
    width = x.shape[-1]
    length = dmid.shape[0] // 2
    half = length // tile
    first = half if away else 0
    if away:
        x_spec = pl.BlockSpec((tile, width), lambda i, s: (i, 0))
        out_spec, out_shape = x_spec, jax.ShapeDtypeStruct((length, width), bf16)
    else:
        x_spec = pl.BlockSpec((None, None, tile, width), lambda i, s: (0, s[0], i, 0))
        out_spec, out_shape = x_spec, jax.ShapeDtypeStruct((1, 2, length, width), f32)
    return pl.pallas_call(
        project_back_kernel,
        name="project_back_away" if away else "project_back_own",
        grid_spec=pltpu.PrefetchScalarGridSpec(
            num_scalar_prefetch=1,
            grid=(half,),
            in_specs=[
                x_spec,
                pl.BlockSpec((1, width), lambda i, s: (0, 0)),
                pl.BlockSpec((width, 3 * width), lambda i, s: (0, 0), pipeline_mode=pl.Buffered(1)),
                pl.BlockSpec((3, tile, width), lambda i, s: (0, i + first, 0)),
                pl.BlockSpec((tile, width), lambda i, s: (i + first, 0)),
            ],
            out_specs=[out_spec, pl.BlockSpec((8, width), lambda i, s: (0, 0))],
        ),
        out_shape=[out_shape, jax.ShapeDtypeStruct((8, width), f32)],
        compiler_params=pltpu.CompilerParams(vmem_limit_bytes=62 << 20),
        cost_estimate=pl.CostEstimate(
            flops=6 * length * width * width, bytes_accessed=length * width * 16, transcendentals=0
        ),
    )(side, x, gain, w, dqkv, dmid)


def flip(x, bit):
    axis, by = ("stream", 1) if bit < 0 else ("batch", 1 << bit)
    return lax.ppermute(x, axis, [(i, i ^ by) for i in range(lax.axis_size(axis))])


def after(value, *others):
    return lax.optimization_barrier((value, *others))[0]


def shards(tokens, cotangent, lengths, ln1_gain, w_qkv, w_out, ln2_gain, w_up, w_down):
    side = lax.axis_index("stream")
    at = lax.axis_index("batch")
    _, rows_dev, length, width = tokens.shape
    assert rows_dev == 2
    ff = w_up.shape[1]
    peers = lax.axis_size("batch")
    small = peers == 16 and width % (16 * peers) == 0
    side_array = side.reshape(1).astype(jnp.int32)
    index = side * peers + at
    me = jnp.stack([index if small else 0 * index, side]).astype(jnp.int32)
    share = width // (2 * peers)
    cut = ff // 3 // LANES * LANES

    cosine, sine = rotary_tables(length)
    tables = mask_tables(length, jnp.take(lengths, side))
    if small:
        rows = width // peers
        gains = jnp.zeros((8, width), f32)
        gains = lax.dynamic_update_slice(gains, jnp.stack([ln1_gain, ln2_gain]).astype(f32), (0, at * rows))
        qkv, hidden, x_away, w_qkv_all, wo_all, wu_all, gains = first(
            w_qkv, w_out, w_up, cut, gains, tokens, cosine, sine
        )
        qkv4 = qkv.reshape(3, 2, length, width)
        w_qkv_all = w_qkv_all.reshape(width, 3 * width)
        gain_one, gain_two = gains[0:1], gains[1:2]
        mixed, logs, wu_more, wd_all, g_away = attend(qkv4, tables, (w_up, w_down), cut, cotangent)
        weights = [wo_all, wu_all, wu_more, wd_all]
    else:

        def whole(x):
            return lax.all_gather(x, "batch", axis=0, tiled=True)

        x_away = flip(lax.dynamic_index_in_dim(tokens[0], 1 - side, 0, False), -1)
        g_away = flip(lax.dynamic_index_in_dim(cotangent[0], 1 - side, 0, False), -1)
        w_qkv_all = whole(w_qkv)
        gain_one, gain_two = (whole(gain)[None].astype(f32) for gain in (ln1_gain, ln2_gain))
        weights = [whole(w).reshape(16, -1, w.shape[1]) for w in (w_out, w_up, w_down)]
        weights[1:2] = [weights[1][:, :, :cut], weights[1][:, :, cut:]]
        qkv, hidden = project(side_array, tokens, x_away, gain_one, w_qkv_all, cosine, sine)
        qkv4 = qkv.reshape(3, 2, length, width)
        mixed, logs = attend(qkv4, tables)
    mixed2 = mixed.reshape(2 * length, width)
    out, out_away, act, du, h2, dmid, dbr, dmix, dgain_two = feed(
        side_array, tokens, x_away, mixed2, cotangent, g_away, gain_two, weights
    )

    def place(result, away):
        away = flip(away, -1).astype(result.dtype)
        return lax.dynamic_update_slice(result, away[None, None], (0, 1 - side, 0, 0))

    out = place(out, out_away)
    unit = share if small else width // 32
    places = {-1: 3, 1: 0, 2: 1, 3: 2}

    def columns_grad(left, right, order, name):
        return weight_grad_columns(me, left, right, width, unit, [places[bit] for bit in order], name)

    down = weight_grad_rows(me, act, cotangent, g_away, width, ff // width * unit, "grad_down")
    down = [part.reshape(16, -1, width) for part in down]
    up = columns_grad(h2, du, UP, "grad_up")
    wo = columns_grad(mixed2, dbr, OUT, "grad_out")
    dmix = after(dmix.reshape(2, length, width), out)
    common = qkv4, mixed, dmix, logs, tables, cosine, sine
    if small:
        dqkv, down, up, wo, dgain_two = attend_back(
            *common, (down, up, wo), dgain_two, ((ff // width * share, width), (share, ff), (share, width))
        )
    else:
        dqkv, = attend_back(*common)
    dqkv3 = dqkv.reshape(3, 2 * length, width)
    if small:
        dx, wq, dgain_one = last(tokens, x_away, gain_one, w_qkv_all, dqkv3, dmid, hidden, share)
    else:
        dx_away, dgain_away = project_back(side_array, x_away, gain_one, w_qkv_all, dqkv3, dmid, True)
        dx, dgain_own = project_back(side_array, tokens, gain_one, w_qkv_all, dqkv3, dmid, False)
        dgain_one = dgain_own + dgain_away
        dx = place(dx, dx_away)
    dgain_one, dgain_two = (jnp.sum(g, axis=0, keepdims=True) for g in (dgain_one, dgain_two))
    if not small:

        def scatter(pair, order):
            slots = jnp.stack(pair, axis=1)
            natural = [arranged(n, order) for n in range(16)]
            slots = slots[jnp.array(natural)]
            by = folds(unit) if slots.shape[2] == 2 * unit else 1
            slots = slots.reshape(32, by, slots.shape[2] // by, -1, width // by).transpose(0, 2, 3, 1, 4)
            rows = slots.reshape(32 * slots.shape[1], -1)
            return lax.psum_scatter(rows, ("stream", "batch"), scatter_dimension=0, tiled=True).astype(f32)

        parts = [columns_grad(hidden, dqkv3[n], QKV[n], "grad_qkv") for n in range(3)]
        down, up, wo, *parts = (
            scatter(pair, [places[bit] for bit in order])
            for pair, order in zip((down, up, wo, *parts), (DOWN, UP, OUT, *QKV))
        )
        wq = jnp.concatenate(parts, axis=1)
        dgain_one, dgain_two = lax.psum((dgain_one, dgain_two), ("stream", "batch"))
    begin = index * share
    dgain_one, dgain_two = (lax.dynamic_slice(g[0], (begin,), (share,)) for g in (dgain_one, dgain_two))
    return out, dx, dgain_one, wq, wo, dgain_two, up, down


def solution(mesh):
    token = P("stream", "batch", None, None)
    vector, matrix = P("batch"), P("batch", None)
    out_vector, out_matrix = P(("stream", "batch")), P(("stream", "batch"), None)
    return jax.shard_map(
        shards,
        mesh=mesh,
        in_specs=(token, token, vector, vector, matrix, matrix, vector, matrix, matrix),
        out_specs=(token, token, out_vector, out_matrix, out_matrix, out_vector, out_matrix, out_matrix),
        check_vma=False,
    )
```

```python
import functools
import math

import jax
import jax.numpy as jnp
from jax import lax
from jax.experimental import pallas as pl
from jax.experimental.pallas import tpu as pltpu
from jax.sharding import PartitionSpec as P

HD = 64
BLOCK = 16
LANES = 128
TILE = 256
BIG = -1e30
f32, bf16 = jnp.float32, jnp.bfloat16


def mm(a, b):
    return lax.dot_general(a, b, (((1,), (0,)), ((), ())), preferred_element_type=f32)


def mm_t(a, b):
    return lax.dot_general(a, b, (((1,), (1,)), ((), ())), preferred_element_type=f32)


def t_mm(a, b):
    return lax.dot_general(a, b, (((0,), (0,)), ((), ())), preferred_element_type=f32)


def rotary_tables(length):
    half = HD // 2
    places = jnp.arange(length).astype(f32)
    rates = jnp.exp(jnp.arange(half).astype(f32) * (-2.0 * math.log(10000.0) / HD))
    angles = places[:, None] * rates[None, :]
    cosine, sine = jnp.cos(angles), jnp.sin(angles)
    return (
        jnp.concatenate([cosine] * 4, axis=1),
        jnp.concatenate([-sine, sine, -sine, sine], axis=1),
    )


def half_partner(x):
    lane = lax.broadcasted_iota(jnp.int32, x.shape, 1)
    low = lax.rem(lane, HD) < HD // 2
    return jnp.where(low, pltpu.roll(x, LANES - HD // 2, 1), pltpu.roll(x, HD // 2, 1))


MESH = pl.DeviceIdType.MESH


def partner(bit):
    side, at = lax.axis_index("stream"), lax.axis_index("batch")
    return (1 - side, at) if bit < 0 else (side, jnp.bitwise_xor(at, 1 << bit))


def greet(others):
    barrier = pltpu.get_barrier_semaphore()
    for other in others:
        pl.semaphore_signal(barrier, inc=1, device_id=other, device_id_type=MESH)
    pl.semaphore_wait(barrier, len(others))


def line_partners():
    side, at = lax.axis_index("stream"), lax.axis_index("batch")
    return [partner(-1)] + [(side, jnp.bitwise_xor(at, mask)) for mask in (1, 2, 4, 8, 12)]


class LineGather:
    SENDS = 37

    def __init__(self, chunks, send_sems, recv_sems, local_sems, across_first=()):
        self.across_first = across_first
        self.chunks, self.send_sems, self.recv_sems, self.local_sems = chunks, send_sems, recv_sems, local_sems
        self.side, self.at = lax.axis_index("stream"), lax.axis_index("batch")
        self.z = lax.div(self.at, 4)

    @staticmethod
    def scratch(count):
        return [
            pltpu.SemaphoreType.DMA((count, LineGather.SENDS)),
            pltpu.SemaphoreType.DMA((count, 16)),
            pltpu.SemaphoreType.DMA((count,)),
        ]

    def copy(self, chunk, shard, target, number, own=False):
        source, place = self.chunks[chunk]
        return pltpu.make_async_remote_copy(
            src_ref=source if own else place(shard),
            dst_ref=place(shard),
            send_sem=self.send_sems.at[chunk, number],
            recv_sem=self.recv_sems.at[chunk, shard],
            device_id=(self.side, target),
            device_id_type=MESH,
        )

    def local(self, chunk):
        source, place = self.chunks[chunk]
        return pltpu.make_async_copy(source, place(self.at), self.local_sems.at[chunk])

    def sends(self, chunk, phase):
        at, z = self.at, self.z
        across, core = jnp.bitwise_xor(at, 2), jnp.bitwise_xor(at, 1)
        up, down = (at + 4, z < 3), (at - 4, z > 0)
        other = jnp.bitwise_xor
        early = chunk in self.across_first
        if phase == 0:
            yield None, at, [(*up, 0), (*down, 1), (across, None, 2), (core, None, 3)]
        if 1 <= phase <= 3:
            n = 4 + 6 * (phase - 1)
            below, above = [(*up, n), (core, None, n + 2)], [(*down, n + 3), (core, None, n + 5)]
            if not early:
                below.append((across, None, n + 1))
                above.append((across, None, n + 4))
            yield z >= phase, at - 4 * phase, below
            yield z + phase <= 3, at + 4 * phase, above
        if phase == 1:
            yield None, across, [(*up, 22), (*down, 23), (core, None, 24)] if early else [(core, None, 24)]
        if 2 <= phase <= 4:
            d, n = phase - 1, 25 + 4 * (phase - 2)
            below, above = [(core, None, n + 1)], [(core, None, n + 3)]
            if early:
                below.append((*up, n))
                above.append((*down, n + 2))
            yield z >= d, other(at - 4 * d, 2), below
            yield z + d <= 3, other(at + 4 * d, 2), above

    def each(self, chunk, phase, act):
        for when, shard, sends in self.sends(chunk, phase):

            def run():
                act(shard, None, None)
                for target, whether, number in sends:
                    if whether is None:
                        act(shard, target, number)
                    else:
                        pl.when(whether)(lambda: act(shard, target, number))

            if when is None:
                run()
            else:
                pl.when(when)(run)

    def phase(self, chunk, phase):
        def act(shard, target, number):
            if target is None:
                if phase == 0:
                    self.local(chunk).start()
                else:
                    self.copy(chunk, shard, self.at, 0).wait_recv()
            else:
                self.copy(chunk, shard, target, number, own=phase == 0).start()

        self.each(chunk, phase, act)

    def finish(self):
        for chunk in range(len(self.chunks)):
            for n in range(8):
                shard = jnp.bitwise_xor(lax.rem(self.at, 2), 1) + 2 * n
                self.copy(chunk, shard, self.at, 0).wait_recv()
            self.local(chunk).wait()
            for phase in range(5):

                def act(shard, target, number):
                    if target is not None:
                        self.copy(chunk, shard, target, number, own=phase == 0).wait_send()

                self.each(chunk, phase, act)


class SlabSum:
    def __init__(self, order, keep, send, got, sems, load=None):
        self.order, self.keep, self.send, self.got, self.sems, self.load = (0, *order), keep, send, got, sems, load

    @staticmethod
    def scratch(slots, share, columns):
        steps = slots.bit_length()
        return [
            *[pltpu.VMEM((max(slots >> n, 1), share, columns), bf16) for n in (0, *range(steps))],
            pltpu.SemaphoreType.DMA((2 * steps + 1,)),
        ]

    def copy(self, step):
        count = self.got[step].shape[0]
        return pltpu.make_async_remote_copy(
            src_ref=self.send if step == 0 else self.keep.at[pl.ds(count, count)],
            dst_ref=self.got[step],
            send_sem=self.sems.at[2 * step],
            recv_sem=self.sems.at[2 * step + 1],
            device_id=partner(self.order[step]),
            device_id_type=MESH,
        )

    def loading(self):
        return pltpu.make_async_copy(self.load, self.keep, self.sems.at[2 * len(self.order)])

    def start(self):
        self.copy(0).start()
        if self.load is not None:
            self.loading().start()

    def step(self, step):
        if step == 1 and self.load is not None:
            self.loading().wait()
        self.copy(step - 1).wait_recv()
        got = self.got[step - 1]

        @pl.loop(0, got.shape[0])
        def _(n):
            self.keep[n] = (self.keep[n].astype(f32) + got[n].astype(f32)).astype(bf16)

        self.copy(step).start()

    def finish(self, out_ref, width, first=0):
        last = len(self.order) - 1
        self.copy(last).wait_recv()
        total = self.keep[0].astype(f32) + self.got[last][0].astype(f32)
        share = out_ref.shape[0]
        by = total.shape[0] // share
        block = out_ref.shape[1] if by == 1 else width // by
        for n in range(total.shape[1] // block):
            for i in range(by):
                at = first + (n * by + i) * block
                out_ref[:, at : at + block] = total[i * share : (i + 1) * share, n * block : (n + 1) * block]
        for step in range(len(self.order)):
            self.copy(step).wait_send()


ALL = (-1, 0, 1, 2, 3)
LATE = (0, 1, 2, 3, -1)


class GainSum:
    def __init__(self, bits, held, got, sems):
        self.bits, self.held, self.got, self.sems = bits, held, got, sems

    @staticmethod
    def scratch(bits, width):
        steps = len(bits)
        return [
            pltpu.VMEM((steps, 8, width), f32),
            pltpu.VMEM((steps, 8, width), f32),
            pltpu.SemaphoreType.DMA((2 * steps,)),
        ]

    def copy(self, step):
        return pltpu.make_async_remote_copy(
            src_ref=self.held.at[step],
            dst_ref=self.got.at[step],
            send_sem=self.sems.at[2 * step],
            recv_sem=self.sems.at[2 * step + 1],
            device_id=partner(self.bits[step]),
            device_id_type=MESH,
        )

    def start(self, value):
        self.held[0] = value
        self.copy(0).start()

    def step(self, step):
        self.copy(step - 1).wait_recv()
        self.held[step] = self.held[step - 1] + self.got[step - 1]
        self.copy(step).start()

    def finish(self, out_ref):
        last = len(self.bits) - 1
        self.copy(last).wait_recv()
        out_ref[...] = self.held[last] + self.got[last]
        for step in range(len(self.bits)):
            self.copy(step).wait_send()


def row_specs(tile, width, half):
    own = pl.BlockSpec((None, None, tile, width), lambda i, s: (0, s[0], jnp.minimum(i, half - 1), 0))
    away = pl.BlockSpec((tile, width), lambda i, s: (jnp.maximum(i - half, 0), 0))
    return own, away


def read_rows(own_ref, away_ref, half):
    return jnp.where(pl.program_id(0) < half, own_ref[...], away_ref[...])


def project_kernel(side_ref, own_ref, away_ref, gain_ref, w_ref, cos_ref, sin_ref, out_ref, hidden_ref, *, half):
    width = own_ref.shape[-1]
    project_tile(read_rows(own_ref, away_ref, half), gain_ref[...], lambda part: w_ref[:, part * width : (part + 1) * width],
                 cos_ref, sin_ref, out_ref, hidden_ref)


def project_tile(x, gain, weights, cos_ref, sin_ref, out_ref, hidden_ref):
    x = x.astype(f32)
    width = x.shape[1]
    center = x - jnp.mean(x, axis=1, keepdims=True)
    spread = jnp.mean(center * center, axis=1, keepdims=True)
    hidden = (center * lax.rsqrt(spread + 1e-5) * gain.astype(f32)).astype(bf16)
    hidden_ref[...] = hidden
    cosine, sine = cos_ref[...], sin_ref[...]
    for part in range(3):
        rows = mm(hidden, weights(part))
        for pair in range(width // LANES):
            cols = slice(pair * LANES, (pair + 1) * LANES)
            field = rows[:, cols]
            if part < 2:
                field = field * cosine + half_partner(field) * sine
            if part == 0:
                field = field * 0.125
            out_ref[part, :, cols] = field.astype(bf16)


def project(side, own, away, gain, w, cosine, sine, tile=512):
    length, width = away.shape
    tokens, half = 2 * length, length // tile
    table = pl.BlockSpec((tile, LANES), lambda i, s: (lax.rem(i, half), 0))
    return pl.pallas_call(
        functools.partial(project_kernel, half=half),
        name="project",
        grid_spec=pltpu.PrefetchScalarGridSpec(
            num_scalar_prefetch=1,
            grid=(2 * half,),
            in_specs=[
                *row_specs(tile, width, half),
                pl.BlockSpec((1, width), lambda i, s: (0, 0)),
                pl.BlockSpec((width, 3 * width), lambda i, s: (0, 0), pipeline_mode=pl.Buffered(1)),
                table,
                table,
            ],
            out_specs=[
                pl.BlockSpec((3, tile, width), lambda i, s: (0, i, 0)),
                pl.BlockSpec((tile, width), lambda i, s: (i, 0)),
            ],
        ),
        out_shape=[jax.ShapeDtypeStruct((3, tokens, width), bf16), jax.ShapeDtypeStruct((tokens, width), bf16)],
        compiler_params=pltpu.CompilerParams(vmem_limit_bytes=62 << 20),
        cost_estimate=pl.CostEstimate(
            flops=6 * tokens * width * width, bytes_accessed=tokens * width * 10 + 6 * width * width, transcendentals=0
        ),
    )(side, own, away, gain, w, cosine, sine)


def first_kernel(shard_ref, wo_ref, wu_ref, gain_ref, tokens_ref, own_ref, cos_ref, sin_ref,
                 qkv_ref, hidden_ref, away_out, w_out, wo_all, wu_all, gains_out,
                 w_all, away, rows, swap_sems, out_sems, *refs, half):
    side, at = lax.axis_index("stream"), lax.axis_index("batch")
    step = pl.program_id(0)
    width = own_ref.shape[-1]
    tile = own_ref.shape[-2]
    def swap(n):
        part = pl.ds(n * tile, tile)
        return pltpu.make_async_remote_copy(
            src_ref=tokens_ref.at[0, 1 - side, part],
            dst_ref=away.at[part],
            send_sem=swap_sems.at[0, n],
            recv_sem=swap_sems.at[1, n],
            device_id=(1 - side, at),
            device_id_type=MESH,
        )

    def chunk(n):
        cols = slice(n * width, (n + 1) * width)
        return shard_ref.at[:, cols], lambda shard: w_all.at[shard, :, cols]

    weights = LineGather([chunk(n) for n in range(3)], *refs[:3])
    part = wu_ref.at[:, : wu_all.shape[2]]
    others = LineGather([(wo_ref, lambda shard: wo_all.at[shard]), (part, lambda shard: wu_all.at[shard])], *refs[3:6])
    gain = GainSum((0, 1, 2, 3), *refs[6:])
    keeps = [
        pltpu.make_async_copy(w_all, w_out, out_sems.at[0]),
        pltpu.make_async_copy(away, away_out, out_sems.at[1]),
    ]

    @pl.when(step == 0)
    def _():
        greet(line_partners())
        for n in range(half):
            swap(n).start()
        gain.start(gain_ref[...])
        for phase in range(5):
            for n in range(3):
                weights.phase(n, phase)
            if 1 <= phase <= 3:
                gain.step(phase)
        gain.finish(gains_out)
        weights.finish()
        for n in range(2):
            others.phase(n, 0)
        keeps[0].start()

    for now in range(1, 4):

        @pl.when(step == now)
        def _():
            for n in range(2):
                others.phase(n, now)
            if now >= half:
                swap(now - half).wait()
            if now == 2 * half - 1:
                keeps[1].start()

    @pl.when(step < half)
    def _():
        rows[...] = own_ref[...]

    @pl.when(step >= half)
    def _():
        rows[...] = away[pl.ds(pl.multiple_of((step - half) * tile, tile), tile), :]

    project_tile(rows[...], gains_out[0:1, :], lambda part: w_all[:, :, part * width : (part + 1) * width].reshape(width, width),
                 cos_ref, sin_ref, qkv_ref, hidden_ref)

    @pl.when(step == pl.num_programs(0) - 1)
    def _():
        for n in range(2):
            others.phase(n, 4)
        others.finish()
        for keep in keeps:
            keep.wait()


def first(shard, wo, wu, cut, gain, tokens, cosine, sine, tile=512):
    _, _, length, width = tokens.shape
    rows = shard.shape[0]
    half = length // tile
    assert half == 2
    anywhere = pl.BlockSpec(memory_space=pl.ANY)
    table = pl.BlockSpec((tile, LANES), lambda i: (lax.rem(i, half), 0))
    small = pl.BlockSpec((8, width), lambda i: (0, 0))
    return pl.pallas_call(
        functools.partial(first_kernel, half=half),
        name="first",
        grid=(2 * half,),
        in_specs=[
            anywhere,
            anywhere,
            anywhere,
            small,
            anywhere,
            pl.BlockSpec((None, None, tile, width), lambda i: (0, lax.axis_index("stream"), jnp.minimum(i, half - 1), 0)),
            table,
            table,
        ],
        out_specs=[
            pl.BlockSpec((3, tile, width), lambda i: (0, i, 0)),
            pl.BlockSpec((tile, width), lambda i: (i, 0)),
            anywhere,
            anywhere,
            anywhere,
            anywhere,
            small,
        ],
        out_shape=[
            jax.ShapeDtypeStruct((3, 2 * length, width), bf16),
            jax.ShapeDtypeStruct((2 * length, width), bf16),
            jax.ShapeDtypeStruct((length, width), bf16),
            jax.ShapeDtypeStruct((16, rows, 3 * width), bf16),
            jax.ShapeDtypeStruct((16, rows, width), bf16),
            jax.ShapeDtypeStruct((16, rows, cut), bf16),
            jax.ShapeDtypeStruct((8, width), f32),
        ],
        scratch_shapes=[
            pltpu.VMEM((16, rows, 3 * width), bf16),
            pltpu.VMEM((length, width), bf16),
            pltpu.VMEM((tile, width), bf16),
            pltpu.SemaphoreType.DMA((2, half)),
            pltpu.SemaphoreType.DMA((2,)),
            *LineGather.scratch(3),
            *LineGather.scratch(2),
            *GainSum.scratch((0, 1, 2, 3), width),
        ],
        compiler_params=pltpu.CompilerParams(vmem_limit_bytes=62 << 20, collective_id=0, has_side_effects=True),
        cost_estimate=pl.CostEstimate(
            flops=12 * length * width * width, bytes_accessed=length * width * 24 + 12 * width * width, transcendentals=0
        ),
    )(shard, wo, wu, gain, tokens, tokens, cosine, sine)


def mask_tables(length, row_length):
    pos = jnp.arange(length)
    blk = (pos // BLOCK)[:, None]
    lane = (jnp.arange(LANES) % HD)[None, :]
    dead = (pos >= row_length)[:, None]
    clean_query = (lane == blk).astype(bf16)
    noisy_query = (lane == blk - 1).astype(bf16)
    main_key = jnp.where((blk > lane) | dead, BIG, 0.0).astype(bf16)
    diag_key = jnp.where((blk != lane) | dead, BIG, 0.0).astype(bf16)
    return clean_query, noisy_query, main_key, diag_key


def low_lanes(shape):
    return lax.broadcasted_iota(jnp.int32, shape, 1) < HD


def attend_gather_kernel(qkv_ref, cq_ref, nq_ref, mk_ref, dk_ref, wu_ref, wd_ref, grad_ref,
                         out_ref, log_ref, wu_all, wd_all, away_ref,
                         qa, ka, kd, va, s_scr, swap_sems, send_sems, recv_sems, local_sems):
    side, at = lax.axis_index("stream"), lax.axis_index("batch")
    step = pl.program_id(0)
    wide, tall = wu_all.shape[2] // 2, wd_ref.shape[0] // 2
    cut = wu_ref.shape[1] - 2 * wide

    def columns(n):
        cols = slice(n * wide, (n + 1) * wide)
        return wu_ref.at[:, cut + n * wide : cut + (n + 1) * wide], lambda shard: wu_all.at[shard, :, cols]

    def rows(n):
        part = slice(n * tall, (n + 1) * tall)
        return wd_ref.at[part, :], lambda shard: wd_all.at[shard, part, :]

    chunks = [columns(0), columns(1), rows(0), rows(1)]
    weights = LineGather(chunks, send_sems, recv_sems, local_sems, EARLY)
    swap = pltpu.make_async_remote_copy(
        src_ref=grad_ref.at[0, 1 - side],
        dst_ref=away_ref,
        send_sem=swap_sems.at[0],
        recv_sem=swap_sems.at[1],
        device_id=(1 - side, at),
        device_id_type=MESH,
    )
    slots = 2 * SLOT_STEPS
    plan = [[] for _ in range(slots + 1)]
    items = SLOT_ORDER
    for n, item in enumerate(items):
        plan[min(1 + n * SLOT_RATE // 16, slots)].append(item)

    @pl.when(step == 0)
    def _():
        greet(line_partners())
        for chunk in range(4):
            weights.phase(chunk, 0)
        swap.start()

    def pass_on(slot):
        for now in range(SLOT_STEPS):
            if plan[2 * now + slot]:

                @pl.when(step == now)
                def _():
                    for item in plan[2 * now + slot]:
                        weights.phase(*item)

    pass_on(0)
    attend_kernel(qkv_ref, cq_ref, nq_ref, mk_ref, dk_ref, out_ref, log_ref, qa, ka, kd, va, s_scr,
                  between=lambda: pass_on(1))

    @pl.when(step == pl.num_programs(0) - 1)
    def _():
        for item in plan[slots]:
            weights.phase(*item)
        weights.finish()
        swap.wait()


EARLY = (0,)
SLOT_STEPS = 6
SLOT_RATE = 14
SLOT_ORDER = [(chunk, phase) for phase in range(1, 5) for chunk in range(4)]


def attend_kernel(qkv_ref, cq_ref, nq_ref, mk_ref, dk_ref, out_ref, log_ref,
                  qa, ka, kd, va, s_scr, between=lambda: None):
    length = out_ref.shape[1]
    clean = lax.axis_index("stream")
    noisy = 1 - clean
    tiles = length // TILE
    low = low_lanes((length, LANES))
    ones = jnp.ones((16, length), bf16)
    vc_t = qkv_ref[2, clean].T
    vn_t = qkv_ref[2, noisy].T
    for head in range(2):
        pick = low if head == 0 else jnp.logical_not(low)
        qa[0, head] = jnp.where(pick, qkv_ref[0, clean], cq_ref[...])
        qa[1, head] = jnp.where(pick, qkv_ref[0, noisy], nq_ref[...])
        qa[2, head] = jnp.where(pick, qkv_ref[0, noisy], cq_ref[...])
        ka[head] = jnp.where(pick, qkv_ref[1, clean], mk_ref[...])
        kd[head] = jnp.where(pick, qkv_ref[1, noisy], dk_ref[...])
        va[0, head, :HD] = vc_t[head * HD : (head + 1) * HD]
        va[1, head, :HD] = vn_t[head * HD : (head + 1) * HD]
        va[0, head, HD:] = ones
        va[1, head, HD:] = ones
    for copy in range(2):
        if copy:
            between()
        where_to = clean if copy == 0 else noisy
        for tile in range(tiles):
            rows = slice(tile * TILE, (tile + 1) * TILE)
            parts = []
            for head in range(2):
                pieces = [(qa[copy, head, rows, :], ka, 0, t) for t in range(tile + 1)]
                if copy == 1:
                    pieces.append((qa[2, head, rows, :], kd, 1, tile))
                top = None
                for n, (query, keys, vi, t) in enumerate(pieces):
                    s = mm_t(keys[head, t * TILE : (t + 1) * TILE, :], query)
                    if copy == 1 and tile == 0 and n == 0:
                        first = lax.broadcasted_iota(jnp.int32, s.shape, 1) < BLOCK
                        s = jnp.where(first, BIG, s)
                    s_scr[head, n * TILE : (n + 1) * TILE, :] = s
                    m = jnp.max(s, axis=0, keepdims=True)
                    top = m if top is None else jnp.maximum(top, m)
                acc = None
                for n, (query, keys, vi, t) in enumerate(pieces):
                    p = jnp.exp(s_scr[head, n * TILE : (n + 1) * TILE, :] - top).astype(bf16)
                    o = mm(va[vi, head, :, t * TILE : (t + 1) * TILE], p)
                    acc = o if acc is None else acc + o
                total = acc[HD : HD + 1, :]
                parts.append(acc[:HD] / total)
                log_ref[where_to, 0, head : head + 1, rows] = top + jnp.log(total)
            out_ref[where_to, rows, :] = jnp.concatenate(parts, axis=0).T.astype(bf16)


def attend(qkv, tables, shards=None, cut=0, grad=None):
    _, copies, length, width = qkv.shape
    pairs = width // LANES
    table_spec = pl.BlockSpec((length, LANES), lambda i: (0, 0), pipeline_mode=pl.Buffered(1))
    more_in, more_shapes, more_scratch = [], [], []
    body, params = attend_kernel, {}
    if shards is not None:
        assert pairs == SLOT_STEPS
        body = attend_gather_kernel
        params = dict(collective_id=3, has_side_effects=True)
        more_in = [*shards, grad]
        up, down = (shard.shape for shard in shards)
        more_shapes = [jax.ShapeDtypeStruct(s, bf16) for s in ((16, up[0], up[1] - cut), (16, *down))]
        more_shapes.append(jax.ShapeDtypeStruct((length, width), bf16))
        more_scratch = [pltpu.SemaphoreType.DMA((2,)), *LineGather.scratch(4)]
    anywhere = pl.BlockSpec(memory_space=pl.ANY)
    return pl.pallas_call(
        body,
        name="attend",
        grid=(pairs,),
        in_specs=[pl.BlockSpec((3, copies, length, LANES), lambda i: (0, 0, 0, i)), *[table_spec] * 4,
                  *[anywhere] * len(more_in)],
        out_specs=[
            pl.BlockSpec((copies, length, LANES), lambda i: (0, 0, i)),
            pl.BlockSpec((copies, 1, 2, length), lambda i: (0, i, 0, 0)),
            *[anywhere] * len(more_shapes),
        ],
        scratch_shapes=[
            pltpu.VMEM((3, 2, length, LANES), bf16),
            pltpu.VMEM((2, length, LANES), bf16),
            pltpu.VMEM((2, length, LANES), bf16),
            pltpu.VMEM((2, 2, HD + 16, length), bf16),
            pltpu.VMEM((2, length + TILE, TILE), f32),
            *more_scratch,
        ],
        out_shape=[
            jax.ShapeDtypeStruct((copies, length, width), bf16),
            jax.ShapeDtypeStruct((copies, pairs, 2, length), f32),
            *more_shapes,
        ],
        compiler_params=pltpu.CompilerParams(vmem_limit_bytes=62 << 20, **params),
        cost_estimate=pl.CostEstimate(
            flops=8 * length * length * width, bytes_accessed=16 * length * width, transcendentals=length * length * 12
        ),
    )(qkv, *tables, *more_in)


DOWN, UP, OUT = (-1, 1, 2, 3), (1, -1, 2, 3), (2, -1, 1, 3)
QKV = ((1, 2, 3, -1), (2, 1, 3, -1), (1, 2, 3, -1))


def attend_back_sum_kernel(*refs, orders):
    count = len(orders)
    core, refs = refs[:10], refs[10:]
    pairs, gain_ref, refs = refs[: 2 * count], refs[2 * count], refs[2 * count + 1 :]
    dqkv_ref, refs = refs[0], refs[1:]
    outs, gain_out, refs = refs[:count], refs[count], refs[count + 1 :]
    own, refs = refs[:10], refs[10:]
    per = len(refs[:-3]) // count
    sums = []
    for n, order in enumerate(orders):
        keep, *got, sems = refs[n * per : (n + 1) * per]
        sums.append(SlabSum(order, keep, pairs[2 * n + 1], got, sems, load=pairs[2 * n]))
    gain = GainSum(ALL, *refs[-3:])
    down, up, wo = sums
    step = pl.program_id(0)

    @pl.when(step == 0)
    def _():
        greet([partner(bit) for bit in ALL])
        for one in sums:
            one.start()
        gain.start(gain_ref[...])

    for at, plan in {
        1: ((down, 1), (up, 1), (wo, 1), (gain, 1)),
        2: ((wo, 2), (gain, 2)),
        3: ((down, 2), (up, 2), (wo, 3), (gain, 3)),
        4: ((down, 3), (up, 3), (wo, 4), (gain, 4)),
        5: ((down, 4), (up, 4)),
    }.items():

        @pl.when(step == at)
        def _():
            for one, number in plan:
                one.step(number)

    attend_back_kernel(*core, dqkv_ref, *own)

    @pl.when(step == pl.num_programs(0) - 1)
    def _():
        for one, out_ref in zip(sums, outs):
            one.finish(out_ref, gain_ref.shape[1])
        gain.finish(gain_out)


def attend_back_kernel(qkv_ref, o_ref, do_ref, log_ref, cq_ref, nq_ref, mk_ref, dk_ref, cos_ref, sin_ref,
                       dqkv_ref, qa, qz, ka, kd, kt, doz, dsum, dq, dkc, dvc):
    length = o_ref.shape[1]
    clean = lax.axis_index("stream")
    noisy = 1 - clean
    tiles = length // TILE
    low = low_lanes((length, LANES))
    zero = jnp.zeros((length, LANES), bf16)
    for copy in range(2):
        at = clean if copy == 0 else noisy
        kt[copy] = qkv_ref[1, at].T
        prod = (o_ref[at].astype(f32) * do_ref[at].astype(f32)).T
        dsum[copy, 0:1] = jnp.sum(prod[:HD], axis=0, keepdims=True)
        dsum[copy, 1:2] = jnp.sum(prod[HD:], axis=0, keepdims=True)
        for head in range(2):
            pick = low if head == 0 else jnp.logical_not(low)
            qa[copy, head] = jnp.where(pick, qkv_ref[0, at], (cq_ref, nq_ref)[copy][...])
            qz[copy, head] = jnp.where(pick, qkv_ref[0, at], zero)
            doz[copy, head] = jnp.where(pick, do_ref[at], zero)
            if copy == 0:
                ka[head] = jnp.where(pick, qkv_ref[1, at], mk_ref[...])
            else:
                qa[2, head] = jnp.where(pick, qkv_ref[0, at], cq_ref[...])
                kd[head] = jnp.where(pick, qkv_ref[1, at], dk_ref[...])
    cosine, sine = cos_ref[...], sin_ref[...]

    def piece(copy, tile, query, keys, kv_copy, krows):
        rows = slice(tile * TILE, (tile + 1) * TILE)
        kv_at = clean if kv_copy == 0 else noisy
        at = clean if copy == 0 else noisy
        probs, raws, dqs = [], [], []
        for head in range(2):
            s = mm_t(keys[head, krows, :], qa[query, head, rows, :])
            p = jnp.exp(s - log_ref[at, 0, head : head + 1, rows])
            if kv_copy == 0 and copy == 1 and tile == 0:
                first = lax.broadcasted_iota(jnp.int32, s.shape, 1) < BLOCK
                p = jnp.where(first, 0.0, p)
            dp = mm_t(qkv_ref[2, kv_at, krows, :], doz[copy, head, rows, :])
            raw = (p * (dp - dsum[copy, head : head + 1, rows])).astype(bf16)
            dqs.append(mm(kt[kv_copy, head * HD : (head + 1) * HD, krows], raw))
            probs.append(p.astype(bf16))
            raws.append(raw)
        grads = [doz[copy, head, rows, :] for head in range(2)]
        queries = [qz[copy, head, rows, :] for head in range(2)]
        return jnp.concatenate(dqs, axis=0), (raws, queries), (probs, grads)

    def product(pair):
        return mm(jnp.concatenate(pair[0], axis=1), jnp.concatenate(pair[1], axis=0))

    def finish(field, rotate, scale):
        if rotate:
            c, s = cosine, sine
            field = field * c - half_partner(field) * s
        return (field * scale if scale != 1.0 else field).astype(bf16)

    for tile in range(tiles):
        rows = slice(tile * TILE, (tile + 1) * TILE)
        dq_t, dk_t, dv_t = piece(1, tile, 2, kd, 1, rows)
        dq[1, :, rows] = dq_t
        dkc[rows, :] = product(dk_t)
        dqkv_ref[2, noisy, rows, :] = product(dv_t).astype(bf16)
    dqkv_ref[1, noisy] = finish(dkc[...], True, 1.0)
    for tile in reversed(range(tiles)):
        rows = slice(tile * TILE, (tile + 1) * TILE)
        seen = slice(0, (tile + 1) * TILE)
        dq_t, dk_c, dv_c = piece(0, tile, 0, ka, 0, seen)
        dq[0, :, rows] = dq_t
        dq_t, dk_n, dv_n = piece(1, tile, 1, ka, 0, seen)
        dq[1, :, rows] += dq_t
        dk_t = product((dk_c[0] + dk_n[0], dk_c[1] + dk_n[1]))
        dv_t = product((dv_c[0] + dv_n[0], dv_c[1] + dv_n[1]))
        if tile == tiles - 1:
            dkc[...] = dk_t
            dvc[...] = dv_t
        else:
            dkc[seen, :] += dk_t
            dvc[seen, :] += dv_t
    dqkv_ref[2, clean] = dvc[...].astype(bf16)
    dqkv_ref[1, clean] = finish(dkc[...], True, 1.0)
    dqkv_ref[0, clean] = finish(dq[0].T, True, 0.125)
    dqkv_ref[0, noisy] = finish(dq[1].T, True, 0.125)


def attend_back(qkv, mixed, grad, logs, tables, cosine, sine, pairs=None, gain=None, slabs=()):
    _, copies, length, width = qkv.shape
    steps = width // LANES
    table_spec = pl.BlockSpec((length, LANES), lambda i: (0, 0), pipeline_mode=pl.Buffered(1))
    row_spec = pl.BlockSpec((copies, length, LANES), lambda i: (0, 0, i))
    three = pl.BlockSpec((3, copies, length, LANES), lambda i: (0, 0, 0, i))
    anywhere = pl.BlockSpec(memory_space=pl.ANY)

    def fixed(shape):
        return pl.BlockSpec(shape, lambda i: (0, 0), pipeline_mode=pl.Buffered(1))

    more_in, more_specs, more_shapes, more_out, more_scratch = [], [], [], [], []
    body, params = attend_back_kernel, {}
    if pairs is not None:
        assert steps == 6
        body = functools.partial(attend_back_sum_kernel, orders=(DOWN, UP, OUT))
        params = dict(collective_id=1, has_side_effects=True)
        for (keep, send), slab in zip(pairs, slabs):
            slots, share, columns = keep.shape
            more_in += [keep, send]
            more_specs += [anywhere] * 2
            more_shapes.append(jax.ShapeDtypeStruct(slab, f32))
            more_out.append(fixed(slab))
            more_scratch += SlabSum.scratch(slots, share, columns)
        more_in.append(gain)
        more_specs.append(fixed((8, width)))
        more_shapes.append(jax.ShapeDtypeStruct((8, width), f32))
        more_out.append(fixed((8, width)))
        more_scratch += GainSum.scratch(ALL, width)
    return pl.pallas_call(
        body,
        name="attend_back",
        grid_spec=pltpu.PrefetchScalarGridSpec(
            num_scalar_prefetch=0,
            grid=(steps,),
            in_specs=[three, row_spec, row_spec, pl.BlockSpec((copies, 1, 2, length), lambda i: (0, i, 0, 0))]
            + [table_spec] * 6
            + more_specs,
            out_specs=[three, *more_out],
            scratch_shapes=[
                pltpu.VMEM((3, 2, length, LANES), bf16),
                pltpu.VMEM((2, 2, length, LANES), bf16),
                pltpu.VMEM((2, length, LANES), bf16),
                pltpu.VMEM((2, length, LANES), bf16),
                pltpu.VMEM((2, LANES, length), bf16),
                pltpu.VMEM((2, 2, length, LANES), bf16),
                pltpu.VMEM((2, 2, length), f32),
                pltpu.VMEM((2, LANES, length), f32),
                pltpu.VMEM((length, LANES), f32),
                pltpu.VMEM((length, LANES), f32),
                *more_scratch,
            ],
        ),
        out_shape=[jax.ShapeDtypeStruct((3, copies, length, width), bf16), *more_shapes],
        compiler_params=pltpu.CompilerParams(vmem_limit_bytes=62 << 20, **params),
        cost_estimate=pl.CostEstimate(
            flops=20 * length * length * width, bytes_accessed=30 * length * width, transcendentals=length * length * 12
        ),
    )(qkv, mixed, grad, logs, *tables, cosine, sine, *more_in)


ROOT = math.sqrt(2.0 / math.pi)


def feed_kernel(side_ref, x_own, x_away, mixed_ref, g_own, g_away, gain_ref, wo_all, wu_all, wu_more, wd_all,
                out_own, out_away, act_ref, du_ref, h2_ref, dmid_ref, dbr_ref, dmix_ref, dgain_ref,
                wo_ref, wu_ref, wd_ref, sems, *, half):
    groups, rows, width = wo_ref.shape
    fold = wu_ref.shape[0]

    @pl.when(pl.program_id(0) == 0)
    def _():
        copies = [pltpu.make_async_copy(wo_all, wo_ref, sems.at[0])]
        begin = 0
        for array in (wu_all, wu_more):
            end = begin + array.shape[2]
            for n in range(fold):
                low, high = max(begin, n * width), min(end, (n + 1) * width)
                if low < high:
                    copies.append(
                        pltpu.make_async_copy(
                            array.at[:, :, low - begin : high - begin],
                            wu_ref.at[n, :, :, low - n * width : high - n * width],
                            sems.at[len(copies)],
                        )
                    )
            begin = end
        copies.append(pltpu.make_async_copy(wd_all, wd_ref, sems.at[len(copies)]))
        for copy in copies:
            copy.start()
        for copy in copies:
            copy.wait()

    def down(c):
        per = groups // fold
        return wd_ref[c * per : (c + 1) * per].reshape(width, width)

    wo = wo_ref[...].reshape(width, width)
    gain = gain_ref[...].astype(f32)
    middle = read_rows(x_own, x_away, half).astype(f32) + mm(mixed_ref[...], wo)
    center = middle - jnp.mean(middle, axis=1, keepdims=True)
    spread = jnp.mean(center * center, axis=1, keepdims=True)
    inv = lax.rsqrt(spread + 1e-5)
    norm = center * inv
    hidden = (norm * gain).astype(bf16)
    h2_ref[...] = hidden
    grad = read_rows(g_own, g_away, half)
    out = middle
    dh = jnp.zeros_like(middle)
    for c in range(fold):
        cols = slice(c * width, (c + 1) * width)
        up = wu_ref[c].reshape(width, width)
        u = mm(hidden, up)
        da = mm_t(grad, down(c)).astype(bf16).astype(f32)
        sq = u * u
        t = jnp.tanh(u * (ROOT + (ROOT * 0.044715) * sq))
        part = 0.5 + 0.5 * t
        act = (u * part).astype(bf16)
        slope = part + (u * (part * (1.0 - t))) * (ROOT + (3 * ROOT * 0.044715) * sq)
        du = (da * slope).astype(bf16)
        act_ref[:, cols] = act
        du_ref[:, cols] = du
        out = out + mm(act, down(c))
        dh = dh + mm_t(du, up)
    low = out.astype(bf16)

    @pl.when(pl.program_id(0) < half)
    def _():
        out_own[...] = low

    @pl.when(pl.program_id(0) >= half)
    def _():
        out_away[...] = low

    @pl.when(pl.program_id(0) == 0)
    def _():
        dgain_ref[...] = jnp.zeros_like(dgain_ref)

    dgain_ref[...] += jnp.sum((dh * norm).reshape(-1, 8, width), axis=0)
    e = dh * gain
    dmid = grad.astype(f32) + inv * (
        e - jnp.mean(e, axis=1, keepdims=True) - norm * jnp.mean(e * norm, axis=1, keepdims=True)
    )
    dmid_ref[...] = dmid
    dbr = dmid.astype(bf16)
    dbr_ref[...] = dbr
    dmix_ref[...] = mm_t(dbr, wo).astype(bf16)


def feed(side, x_own, x_away, mixed, g_own, g_away, gain, weights, tile=512):
    tokens, width = mixed.shape
    groups, rows, _ = weights[0].shape
    ff = weights[1].shape[2] + weights[2].shape[2]
    fold = ff // width
    half = tokens // 2 // tile
    row = pl.BlockSpec((tile, width), lambda i, s: (i, 0))
    wide = pl.BlockSpec((tile, ff), lambda i, s: (i, 0))
    own, away = row_specs(tile, width, half)

    def keep(shape):
        return pl.BlockSpec(shape, lambda i, s: (0, 0), pipeline_mode=pl.Buffered(1))

    return pl.pallas_call(
        functools.partial(feed_kernel, half=half),
        name="feed",
        grid_spec=pltpu.PrefetchScalarGridSpec(
            num_scalar_prefetch=1,
            grid=(2 * half,),
            in_specs=[own, away, row, own, away, keep((1, width)), *[pl.BlockSpec(memory_space=pl.ANY)] * 4],
            out_specs=[own, away, wide, wide, row, row, row, row, pl.BlockSpec((8, width), lambda i, s: (0, 0))],
            scratch_shapes=[
                pltpu.VMEM((groups, rows, width), bf16),
                pltpu.VMEM((fold, groups, rows, width), bf16),
                pltpu.VMEM((groups, fold * rows, width), bf16),
                pltpu.SemaphoreType.DMA((3 + fold,)),
            ],
        ),
        out_shape=[
            jax.ShapeDtypeStruct((1, 2, tokens // 2, width), bf16),
            jax.ShapeDtypeStruct((tokens // 2, width), bf16),
            jax.ShapeDtypeStruct((tokens, ff), bf16),
            jax.ShapeDtypeStruct((tokens, ff), bf16),
            jax.ShapeDtypeStruct((tokens, width), bf16),
            jax.ShapeDtypeStruct((tokens, width), f32),
            jax.ShapeDtypeStruct((tokens, width), bf16),
            jax.ShapeDtypeStruct((tokens, width), bf16),
            jax.ShapeDtypeStruct((8, width), f32),
        ],
        compiler_params=pltpu.CompilerParams(vmem_limit_bytes=62 << 20),
        cost_estimate=pl.CostEstimate(
            flops=tokens * width * (4 * width + 8 * ff), bytes_accessed=tokens * (width * 18 + ff * 4),
            transcendentals=tokens * ff
        ),
    )(side, x_own, x_away, mixed, g_own, g_away, gain, *weights)


def folds(share):
    return 1 if share % 16 == 0 else 2


def fold(slab):
    if folds(slab.shape[0]) == 1:
        return slab
    middle = slab.shape[1] // 2
    return jnp.concatenate([slab[:, :middle], slab[:, middle:]], axis=0)


def arranged(slot, order):
    return sum((slot >> bit & 1) << (len(order) - 1 - n) for n, bit in enumerate(order))


def weight_kernel(me_ref, left_ref, *refs, share, split, order):
    weight_slabs(me_ref[0], left_ref, *refs, share=share, split=split, order=order)


def weight_slabs(me, left_ref, *refs, share, split, order):
    right_refs, (keep_ref, send_ref, scr) = refs[:-3], refs[-3:]
    if split:
        own_ref, away_ref = right_refs
        half = own_ref.shape[0]
        total = t_mm(left_ref[:half], own_ref[...]) + t_mm(left_ref[half:], away_ref[...])
    else:
        total = t_mm(left_ref[...], right_refs[0][...])
    slabs = total.shape[0] // share
    scr[...] = total.reshape(scr.shape)
    low_me = lax.rem(me, slabs)
    for slot in range(slabs):
        source = jnp.bitwise_xor(low_me, slot)
        into = send_ref if slot % 2 else keep_ref
        into[arranged(slot // 2, order)] = fold(scr[source]).astype(bf16)


def weight_grad_columns(me, left, right, block, share, order, name):
    tokens, dl = left.shape
    dr = right.shape[1]
    peers = dl // share
    by = folds(share)
    shape = (peers // 2, share * by, dr // by)
    out = pl.BlockSpec((peers // 2, share * by, block // by), lambda j, m: (0, 0, j))
    return pl.pallas_call(
        functools.partial(weight_kernel, share=share, split=False, order=order),
        name=name,
        grid_spec=pltpu.PrefetchScalarGridSpec(
            num_scalar_prefetch=1,
            grid=(dr // block,),
            in_specs=[
                pl.BlockSpec((tokens, dl), lambda j, m: (0, 0), pipeline_mode=pl.Buffered(1)),
                pl.BlockSpec((tokens, block), lambda j, m: (0, j)),
            ],
            out_specs=[out, out],
            scratch_shapes=[pltpu.VMEM((peers, share, block), f32)],
        ),
        out_shape=[jax.ShapeDtypeStruct(shape, bf16)] * 2,
        compiler_params=pltpu.CompilerParams(vmem_limit_bytes=62 << 20),
        cost_estimate=pl.CostEstimate(
            flops=2 * tokens * dl * dr, bytes_accessed=2 * tokens * (dl + dr) + 2 * dl * dr, transcendentals=0
        ),
    )(me, left, right)


def weight_grad_rows(me, left, own, away, block, share, name):
    tokens, dl = left.shape
    length, dr = away.shape
    slabs = block // share
    steps = dl // block
    assert steps == 4
    shape = (2, slabs // 2, 2, share, dr)
    out = pl.BlockSpec((None, slabs // 2, None, share, dr), lambda j, m: (lax.div(j, 2), 0, lax.rem(j, 2), 0, 0))
    bits = (slabs // 2).bit_length() - 1

    def place(j, m):
        return (0, jnp.bitwise_xor(j, lax.div(m[0], slabs)))

    return pl.pallas_call(
        functools.partial(weight_kernel, share=share, split=True, order=tuple(range(bits))),
        name=name,
        grid_spec=pltpu.PrefetchScalarGridSpec(
            num_scalar_prefetch=1,
            grid=(steps,),
            in_specs=[
                pl.BlockSpec((tokens, block), place),
                pl.BlockSpec((None, None, length, dr), lambda j, m: (0, m[1], 0, 0), pipeline_mode=pl.Buffered(1)),
                pl.BlockSpec((length, dr), lambda j, m: (0, 0), pipeline_mode=pl.Buffered(1)),
            ],
            out_specs=[out, out],
            scratch_shapes=[pltpu.VMEM((slabs, share, dr), f32)],
        ),
        out_shape=[jax.ShapeDtypeStruct(shape, bf16)] * 2,
        compiler_params=pltpu.CompilerParams(vmem_limit_bytes=62 << 20),
        cost_estimate=pl.CostEstimate(
            flops=2 * tokens * dl * dr, bytes_accessed=2 * tokens * (dl + dr) + 2 * dl * dr, transcendentals=0
        ),
    )(me, left, own, away)


def last_kernel(x_own, x_away, gain_ref, w_hbm, dqkv_hbm, dmid_hbm, hidden_hbm,
                dx_ref, dw_ref, gain_out,
                xv, w_ref, dqkv, dmid, hidden, send, land, dgain, scr,
                load_sems, tile_sems, send_sems, recv_sems, out_sems, *refs, share):
    count = len(QKV)
    per = len(refs[:-3]) // count
    sums = []
    for n, order in enumerate(QKV):
        first, keep, *got, sems = refs[n * per : (n + 1) * per]
        sums.append(SlabSum(order, keep, first, got, sems))
    gain = GainSum(LATE, *refs[-3:])
    side, at = lax.axis_index("stream"), lax.axis_index("batch")
    me = side * lax.axis_size("batch") + at
    step = pl.program_id(0)
    width = w_ref.shape[0]
    length = land.shape[0]
    tiles = pl.num_programs(0)
    tile = 2 * length // 8
    half = 4

    def rows_of(t, base=0):
        return pl.ds(pl.multiple_of((t - base) * tile, tile), tile)

    loads = [
        pltpu.make_async_copy(w_hbm, w_ref, load_sems.at[0]),
        pltpu.make_async_copy(x_away, xv.at[pl.ds(length, length)], load_sems.at[1]),
        pltpu.make_async_copy(hidden_hbm, hidden, load_sems.at[2]),
        pltpu.make_async_copy(x_own.at[0, side], xv.at[pl.ds(0, length)], load_sems.at[3]),
    ]

    def load_grad(t):
        return pltpu.make_async_copy(dqkv_hbm.at[:, rows_of(t), :], dqkv.at[:, rows_of(t), :], tile_sems.at[0, t])

    def load_middle(t):
        return pltpu.make_async_copy(dmid_hbm.at[rows_of(t), :], dmid.at[rows_of(t), :], tile_sems.at[1, t])

    def away(t):
        return pltpu.make_async_remote_copy(
            src_ref=send.at[rows_of(t, half), :],
            dst_ref=land.at[rows_of(t, half), :],
            send_sem=send_sems.at[t - half],
            recv_sem=recv_sems.at[t - half],
            device_id=(1 - side, at),
            device_id_type=MESH,
        )

    def result(t, row):
        return pltpu.make_async_copy(
            dmid.at[rows_of(t), :],
            dx_ref.at[0, row, pl.ds(pl.multiple_of(lax.rem(t, half) * tile, tile), tile), :],
            out_sems.at[t],
        )

    @pl.when(step == 0)
    def _():
        loads[0].start()
        loads[1].start()
        load_grad(4).start()
        load_middle(4).start()
        loads[2].start()
        for t in (5, 6, 7, 0, 1, 2, 3):
            load_grad(t).start()
        loads[3].start()
        for t in (5, 6, 7, 0, 1, 2, 3):
            load_middle(t).start()
        dgain[...] = jnp.zeros_like(dgain)
        greet([partner(bit) for bit in ALL])
        loads[0].wait()
        loads[1].wait()
        load_grad(4).wait()
        load_middle(4).wait()

    @pl.when(step > 0)
    def _():
        load_middle(lax.rem(step + half, 8)).wait()

    @pl.when(step == half)
    def _():
        loads[3].wait()

    for now, plan in {
        1: ((0, 1), (1, 1)),
        2: ((0, 2), (2, 1)),
        3: ((1, 2),),
        4: ((0, 3),),
        6: ((2, 2), (1, 3)),
        7: ((0, 4),),
    }.items():

        @pl.when(step == now)
        def _():
            for n, number in plan:
                sums[n].step(number)

    t = lax.rem(step + half, 8)
    rows = rows_of(t)
    x = xv[rows, :].astype(f32)
    center = x - jnp.mean(x, axis=1, keepdims=True)
    spread = jnp.mean(center * center, axis=1, keepdims=True)
    inv = lax.rsqrt(spread + 1e-5)
    norm = center * inv
    dh = mm_t(dqkv[0, rows, :], w_ref[:, :width])
    dh = dh + mm_t(dqkv[1, rows, :], w_ref[:, width : 2 * width])
    dh = dh + mm_t(dqkv[2, rows, :], w_ref[:, 2 * width :])
    dgain[...] += jnp.sum((dh * norm).reshape(-1, 8, width), axis=0)
    e = dh * gain_ref[...]
    dx = dmid[rows, :] + inv * (
        e - jnp.mean(e, axis=1, keepdims=True) - norm * jnp.mean(e * norm, axis=1, keepdims=True)
    )

    @pl.when(step < half)
    def _():
        send[rows_of(step), :] = dx.astype(bf16)
        away(t).start()

    @pl.when(step >= half)
    def _():
        dmid[rows, :] = dx
        result(t, side).start()

    def part(n):
        order = tuple({-1: 3, 1: 0, 2: 1, 3: 2}[bit] for bit in QKV[n])
        weight_slabs(me, hidden, dqkv.at[n], sums[n].keep, sums[n].send, scr, share=share, split=False, order=order)
        sums[n].start()

    @pl.when(step == 0)
    def _():
        loads[2].wait()
        for other in (5, 6, 7, 0, 1, 2, 3):
            load_grad(other).wait()
        part(0)
        part(1)

    @pl.when(step == 1)
    def _():
        part(2)

    @pl.when(step == tiles - 1)
    def _():
        gain.start(dgain[...])
        sums[2].step(3)
        sums[1].step(4)
        sums[0].finish(dw_ref, width, 0)
        gain.step(1)
        sums[2].step(4)
        gain.step(2)
        sums[1].finish(dw_ref, width, width)
        gain.step(3)
        sums[2].finish(dw_ref, width, 2 * width)
        gain.step(4)
        for other in range(half, 8):
            away(other).wait()
            dmid[rows_of(other), :] = land[rows_of(other, half), :].astype(f32)
            result(other, 1 - side).start()
        gain.finish(gain_out)
        for other in range(8):
            result(other, side).wait()


def last(tokens, x_away, gain, w, dqkv, dmid, hidden, share):
    tokens_all, width = hidden.shape
    length = tokens_all // 2
    slots = width // share // 2
    anywhere = pl.BlockSpec(memory_space=pl.ANY)

    def fixed(shape):
        return pl.BlockSpec(shape, lambda i: (0, 0), pipeline_mode=pl.Buffered(1))

    scratch = []
    for _ in range(3):
        by = folds(share)
        scratch += [
            pltpu.VMEM((slots, share * by, width // by), bf16),
            *SlabSum.scratch(slots, share * by, width // by),
        ]
    return pl.pallas_call(
        functools.partial(last_kernel, share=share),
        name="last",
        grid=(8,),
        in_specs=[anywhere, anywhere, fixed((1, width)), *[anywhere] * 4],
        out_specs=[anywhere, fixed((share, 3 * width)), fixed((8, width))],
        out_shape=[
            jax.ShapeDtypeStruct((1, 2, length, width), f32),
            jax.ShapeDtypeStruct((share, 3 * width), f32),
            jax.ShapeDtypeStruct((8, width), f32),
        ],
        scratch_shapes=[
            pltpu.VMEM((2 * length, width), bf16),
            pltpu.VMEM((width, 3 * width), bf16),
            pltpu.VMEM((3, 2 * length, width), bf16),
            pltpu.VMEM((2 * length, width), f32),
            pltpu.VMEM((2 * length, width), bf16),
            pltpu.VMEM((length, width), bf16),
            pltpu.VMEM((length, width), bf16),
            pltpu.VMEM((8, width), f32),
            pltpu.VMEM((2 * slots, share, width), f32),
            pltpu.SemaphoreType.DMA((4,)),
            pltpu.SemaphoreType.DMA((2, 8)),
            pltpu.SemaphoreType.DMA((4,)),
            pltpu.SemaphoreType.DMA((4,)),
            pltpu.SemaphoreType.DMA((8,)),
            *scratch,
            *GainSum.scratch(LATE, width),
        ],
        compiler_params=pltpu.CompilerParams(vmem_limit_bytes=62 << 20, collective_id=2, has_side_effects=True),
        cost_estimate=pl.CostEstimate(
            flops=24 * length * width * width, bytes_accessed=36 * length * width, transcendentals=0
        ),
    )(tokens, x_away, gain, w, dqkv, dmid, hidden)


def project_back_kernel(side_ref, x_ref, gain_ref, w_ref, dqkv_ref, dmid_ref, dx_ref, dgain_ref):
    x = x_ref[...].astype(f32)
    width = x.shape[1]
    center = x - jnp.mean(x, axis=1, keepdims=True)
    spread = jnp.mean(center * center, axis=1, keepdims=True)
    inv = lax.rsqrt(spread + 1e-5)
    norm = center * inv
    dh = mm_t(dqkv_ref[0], w_ref[:, :width])
    dh = dh + mm_t(dqkv_ref[1], w_ref[:, width : 2 * width])
    dh = dh + mm_t(dqkv_ref[2], w_ref[:, 2 * width :])

    @pl.when(pl.program_id(0) == 0)
    def _():
        dgain_ref[...] = jnp.zeros_like(dgain_ref)

    dgain_ref[...] += jnp.sum((dh * norm).reshape(-1, 8, width), axis=0)
    e = dh * gain_ref[...].astype(f32)
    dx_ref[...] = (dmid_ref[...] + inv * (
        e - jnp.mean(e, axis=1, keepdims=True) - norm * jnp.mean(e * norm, axis=1, keepdims=True)
    )).astype(dx_ref.dtype)


def project_back(side, x, gain, w, dqkv, dmid, away, tile=256):
    width = x.shape[-1]
    length = dmid.shape[0] // 2
    half = length // tile
    first = half if away else 0
    if away:
        x_spec = pl.BlockSpec((tile, width), lambda i, s: (i, 0))
        out_spec, out_shape = x_spec, jax.ShapeDtypeStruct((length, width), bf16)
    else:
        x_spec = pl.BlockSpec((None, None, tile, width), lambda i, s: (0, s[0], i, 0))
        out_spec, out_shape = x_spec, jax.ShapeDtypeStruct((1, 2, length, width), f32)
    return pl.pallas_call(
        project_back_kernel,
        name="project_back_away" if away else "project_back_own",
        grid_spec=pltpu.PrefetchScalarGridSpec(
            num_scalar_prefetch=1,
            grid=(half,),
            in_specs=[
                x_spec,
                pl.BlockSpec((1, width), lambda i, s: (0, 0)),
                pl.BlockSpec((width, 3 * width), lambda i, s: (0, 0), pipeline_mode=pl.Buffered(1)),
                pl.BlockSpec((3, tile, width), lambda i, s: (0, i + first, 0)),
                pl.BlockSpec((tile, width), lambda i, s: (i + first, 0)),
            ],
            out_specs=[out_spec, pl.BlockSpec((8, width), lambda i, s: (0, 0))],
        ),
        out_shape=[out_shape, jax.ShapeDtypeStruct((8, width), f32)],
        compiler_params=pltpu.CompilerParams(vmem_limit_bytes=62 << 20),
        cost_estimate=pl.CostEstimate(
            flops=6 * length * width * width, bytes_accessed=length * width * 16, transcendentals=0
        ),
    )(side, x, gain, w, dqkv, dmid)


def flip(x, bit):
    axis, by = ("stream", 1) if bit < 0 else ("batch", 1 << bit)
    return lax.ppermute(x, axis, [(i, i ^ by) for i in range(lax.axis_size(axis))])


def after(value, *others):
    return lax.optimization_barrier((value, *others))[0]


def shards(tokens, cotangent, lengths, ln1_gain, w_qkv, w_out, ln2_gain, w_up, w_down):
    side = lax.axis_index("stream")
    at = lax.axis_index("batch")
    _, rows_dev, length, width = tokens.shape
    assert rows_dev == 2
    ff = w_up.shape[1]
    peers = lax.axis_size("batch")
    small = peers == 16 and width % (16 * peers) == 0
    side_array = side.reshape(1).astype(jnp.int32)
    index = side * peers + at
    me = jnp.stack([index if small else 0 * index, side]).astype(jnp.int32)
    share = width // (2 * peers)
    cut = ff // 4 // LANES * LANES

    cosine, sine = rotary_tables(length)
    tables = mask_tables(length, jnp.take(lengths, side))
    if small:
        rows = width // peers
        gains = jnp.zeros((8, width), f32)
        gains = lax.dynamic_update_slice(gains, jnp.stack([ln1_gain, ln2_gain]).astype(f32), (0, at * rows))
        qkv, hidden, x_away, w_qkv_all, wo_all, wu_all, gains = first(
            w_qkv, w_out, w_up, cut, gains, tokens, cosine, sine
        )
        qkv4 = qkv.reshape(3, 2, length, width)
        w_qkv_all = w_qkv_all.reshape(width, 3 * width)
        gain_one, gain_two = gains[0:1], gains[1:2]
        mixed, logs, wu_more, wd_all, g_away = attend(qkv4, tables, (w_up, w_down), cut, cotangent)
        weights = [wo_all, wu_all, wu_more, wd_all]
    else:

        def whole(x):
            return lax.all_gather(x, "batch", axis=0, tiled=True)

        x_away = flip(lax.dynamic_index_in_dim(tokens[0], 1 - side, 0, False), -1)
        g_away = flip(lax.dynamic_index_in_dim(cotangent[0], 1 - side, 0, False), -1)
        w_qkv_all = whole(w_qkv)
        gain_one, gain_two = (whole(gain)[None].astype(f32) for gain in (ln1_gain, ln2_gain))
        weights = [whole(w).reshape(16, -1, w.shape[1]) for w in (w_out, w_up, w_down)]
        weights[1:2] = [weights[1][:, :, :cut], weights[1][:, :, cut:]]
        qkv, hidden = project(side_array, tokens, x_away, gain_one, w_qkv_all, cosine, sine)
        qkv4 = qkv.reshape(3, 2, length, width)
        mixed, logs = attend(qkv4, tables)
    mixed2 = mixed.reshape(2 * length, width)
    out, out_away, act, du, h2, dmid, dbr, dmix, dgain_two = feed(
        side_array, tokens, x_away, mixed2, cotangent, g_away, gain_two, weights
    )

    def place(result, away):
        away = flip(away, -1).astype(result.dtype)
        return lax.dynamic_update_slice(result, away[None, None], (0, 1 - side, 0, 0))

    out = place(out, out_away)
    unit = share if small else width // 32
    places = {-1: 3, 1: 0, 2: 1, 3: 2}

    def columns_grad(left, right, order, name):
        return weight_grad_columns(me, left, right, width, unit, [places[bit] for bit in order], name)

    down = weight_grad_rows(me, act, cotangent, g_away, width, ff // width * unit, "grad_down")
    down = [part.reshape(16, -1, width) for part in down]
    up = columns_grad(h2, du, UP, "grad_up")
    wo = columns_grad(mixed2, dbr, OUT, "grad_out")
    dmix = after(dmix.reshape(2, length, width), out)
    common = qkv4, mixed, dmix, logs, tables, cosine, sine
    if small:
        dqkv, down, up, wo, dgain_two = attend_back(
            *common, (down, up, wo), dgain_two, ((ff // width * share, width), (share, ff), (share, width))
        )
    else:
        dqkv, = attend_back(*common)
    dqkv3 = dqkv.reshape(3, 2 * length, width)
    if small:
        dx, wq, dgain_one = last(tokens, x_away, gain_one, w_qkv_all, dqkv3, dmid, hidden, share)
    else:
        dx_away, dgain_away = project_back(side_array, x_away, gain_one, w_qkv_all, dqkv3, dmid, True)
        dx, dgain_own = project_back(side_array, tokens, gain_one, w_qkv_all, dqkv3, dmid, False)
        dgain_one = dgain_own + dgain_away
        dx = place(dx, dx_away)
    dgain_one, dgain_two = (jnp.sum(g, axis=0, keepdims=True) for g in (dgain_one, dgain_two))
    if not small:

        def scatter(pair, order):
            slots = jnp.stack(pair, axis=1)
            natural = [arranged(n, order) for n in range(16)]
            slots = slots[jnp.array(natural)]
            by = folds(unit) if slots.shape[2] == 2 * unit else 1
            slots = slots.reshape(32, by, slots.shape[2] // by, -1, width // by).transpose(0, 2, 3, 1, 4)
            rows = slots.reshape(32 * slots.shape[1], -1)
            return lax.psum_scatter(rows, ("stream", "batch"), scatter_dimension=0, tiled=True).astype(f32)

        parts = [columns_grad(hidden, dqkv3[n], QKV[n], "grad_qkv") for n in range(3)]
        down, up, wo, *parts = (
            scatter(pair, [places[bit] for bit in order])
            for pair, order in zip((down, up, wo, *parts), (DOWN, UP, OUT, *QKV))
        )
        wq = jnp.concatenate(parts, axis=1)
        dgain_one, dgain_two = lax.psum((dgain_one, dgain_two), ("stream", "batch"))
    begin = index * share
    dgain_one, dgain_two = (lax.dynamic_slice(g[0], (begin,), (share,)) for g in (dgain_one, dgain_two))
    return out, dx, dgain_one, wq, wo, dgain_two, up, down


def solution(mesh):
    token = P("stream", "batch", None, None)
    vector, matrix = P("batch"), P("batch", None)
    out_vector, out_matrix = P(("stream", "batch")), P(("stream", "batch"), None)
    return jax.shard_map(
        shards,
        mesh=mesh,
        in_specs=(token, token, vector, vector, matrix, matrix, vector, matrix, matrix),
        out_specs=(token, token, out_vector, out_matrix, out_matrix, out_vector, out_matrix, out_matrix),
        check_vma=False,
    )
```
